32 devices in a mesh: expert: 8 (over z, y), shard: 4 (over x, core).
Axes of the slice: x: 2, y: 2, z: 4, core: 2. Of those that a mesh axis runs over, the one named last changes fastest.
Arguments:
- hidden: bfloat16 [8, 512, 2048], P('expert', 'shard'), may hold values from -12 to 12
- cotangent: bfloat16 [8, 512, 2048], P('expert', 'shard'), may hold values from -6 to 6
- segments: int32 [8, 512], P('expert'), may hold values from 0 to 3, as said below
- routes: int32 [8, 512, 6], P('expert', 'shard'), may hold values from 0 to 31, all different within a row; in each aligned block of 128 rows (0 to 127, 128 to 255, ..., all dimensions but the last counted through in order) at most 32 rows name the same one
- w_query: bfloat16 [2048, 3072], P('shard'), may hold values from -0.125 to 0.125
- w_latent: bfloat16 [2048, 576], P('shard'), may hold values from -0.125 to 0.125
- g_latent: bfloat16 [512], P('shard'), may hold values from 0.099609375 to 1.8984375
- w_expand: bfloat16 [512, 4096], P('shard'), may hold values from -0.25 to 0.25
- w_out: bfloat16 [2048, 2048], P('shard'), may hold values from -1 to 1
- g_attn: bfloat16 [2048], P('shard'), may hold values from 0.099609375 to 1.8984375
- g_ffn: bfloat16 [2048], P('shard'), may hold values from 0.099609375 to 1.8984375
- w_router: bfloat16 [2048, 32], P('shard'), may hold values from -0.125 to 0.125
- s_gate: bfloat16 [2048, 2816], P('shard'), may hold values from -0.125 to 0.125
- s_up: bfloat16 [2048, 2816], P('shard'), may hold values from -0.125 to 0.125
- s_down: bfloat16 [2816, 2048], P('shard'), may hold values from -0.109375 to 0.109375
- e_gate: bfloat16 [32, 2048, 1408], P('expert', None, 'shard'), may hold values from -0.125 to 0.125
- expert_up_weight: bfloat16 [32, 2048, 1408], P('expert', None, 'shard'), may hold values from -0.125 to 0.125
- e_down: bfloat16 [32, 1408, 2048], P('expert', 'shard'), may hold values from -0.15625 to 0.15625
Outputs:
- output: bfloat16 [8, 512, 2048], P('expert', 'shard')
- d_hidden: float32 [8, 512, 2048], P('expert', 'shard')
- d_query: float32 [2048, 3072], P('shard')
- d_latent: float32 [2048, 576], P('shard')
- d_glatent: float32 [512], P('shard')
- d_expand: float32 [512, 4096], P('shard')
- d_out: float32 [2048, 2048], P('shard')
- d_gattn: float32 [2048], P('shard')
- d_gffn: float32 [2048], P('shard')
- d_router: float32 [2048, 32], P('shard')
- d_sgate: float32 [2048, 2816], P('shard')
- d_sup: float32 [2048, 2816], P('shard')
- d_sdown: float32 [2816, 2048], P('shard')
- d_egate: float32 [32, 2048, 1408], P('expert', None, 'shard')
- grad_expert_up: float32 [32, 2048, 1408], P('expert', None, 'shard')
- d_edown: float32 [32, 1408, 2048], P('expert', 'shard')
The draws below stay inside these ranges and needn't reach their ends.
Inputs may be any that keep to these rules, and one draw needn't show every extreme that they name: `segments`: along each sequence the ids start at 0 and rise by one at each document boundary; each sequence holds 2 to 4 documents of 102 positions or more, and some sequence holds 4. `routes`: each token names 6 different experts; among the rows of one device no expert is named by more than 32 of them, a bound that some block reaches of one device.
All inputs are finite; a program needn't handle non-finite values.
Results may differ from the reference program's by a relative error of at most 0.019.
Values may be sent and summed in bfloat16 or wider, within the bound.
No kernel may reach another device: no remote copies, remote signals or barrier semaphores. Data moves between devices by JAX's collectives and lax.ppermute only.
A program may use at most 640 MiB of HBM per device.

```python
import math
import jax
import jax.numpy as jnp
import numpy as np
from jax import lax

D = 2048
H = 16
DN = 128
DR = 64
DV = 128
KVR = 512
FF = 1408
FS = 2816
TOP = 6
TOK_DEV = 128
EXPERTS = 32
LENGTH = 512
SEQS = 8
TOKENS = 4096
CAP = 32
DOC_MIN = 102
N_EXPERT = 8
N_SHARD = 4


def draw_hidden(key, part):
    key_base, key_rows, key_cols = jax.random.split(key, 3)
    base_vals = jax.random.normal(key_base, (SEQS, LENGTH, D), jnp.float32)
    row_scale = jnp.exp(jax.random.uniform(key_rows, (SEQS, LENGTH, 1), jnp.float32, math.log(0.3), math.log(3.0)))
    col_scale = jnp.exp(jax.random.uniform(key_cols, (1, 1, D), jnp.float32, math.log(0.5), math.log(2.0)))
    return jnp.clip(base_vals * row_scale * col_scale, -12.0, 12.0).astype(jnp.bfloat16)


def draw_segments(key, part):
    key_count, key_pick, key_cuts = jax.random.split(jax.random.fold_in(key, 7), 3)
    doc_counts = 2 + jax.random.randint(key_count, (SEQS,), 0, 3)
    picked = jax.random.randint(key_pick, (), 0, SEQS)
    doc_counts = jnp.where(jnp.arange(SEQS) == picked, 4, doc_counts).astype(jnp.int32)
    spare_room = LENGTH - doc_counts * DOC_MIN
    cut_points = jax.random.randint(key_cuts, (SEQS, 3), 0, spare_room[:, None] + 1)
    cut_points = jnp.sort(cut_points, axis=1)
    index_vals = jnp.arange(1, 4).astype(jnp.int32)
    doc_bounds = index_vals[None, :] * DOC_MIN + cut_points
    active_cut = index_vals[None, :] <= doc_counts[:, None] - 1
    positions = jnp.arange(LENGTH).astype(jnp.int32)
    crossed = active_cut[:, None, :] & (positions[None, :, None] >= doc_bounds[:, None, :])
    return jnp.sum(crossed.astype(jnp.int32), axis=2).astype(jnp.int32)


def level_of(own_key, extent, cuts, low, largest):
    level, own = 1.0, jax.random.fold_in(own_key, 6)
    for position, blocks in cuts:
        draws = jnp.exp(jax.random.uniform(jax.random.fold_in(own, position), (blocks,), jnp.float32, low / len(cuts), largest / len(cuts)))
        level = level * jnp.repeat(draws, extent[position] // blocks).reshape([-1 if axis == position else 1 for axis in range(len(extent))])
    return level


def deal_out(stream_key, own, number, rows, amount, top, bound, skew):
    order = jax.random.permutation(stream_key, amount)
    crowded, ordinary = portions_of(amount, rows * top, bound, skew, True), portions_of(amount, rows * top, bound, skew, False)
    places = jnp.arange(amount)

    def named(tallies, offset_by):
        used = int((tallies > 0).sum())
        fixed = max(1, used // 4)
        passed = fixed + (places - fixed + offset_by * (used - fixed)) % max(1, amount - fixed)
        return jnp.zeros((amount,), jnp.int32).at[order[jnp.where(places < fixed, places, passed)]].set(jnp.asarray(tallies, jnp.int32))

    tallies = jnp.where(number % 4 == 0, named(crowded, number // 4), named(ordinary, number - number // 4 - 1))
    mixed = jax.random.permutation(jax.random.fold_in(own, 3), amount)
    source_of, sink = mixed[0:amount // 2 * 2:2], mixed[1:amount // 2 * 2:2]
    room = jnp.minimum(tallies[source_of] - 1, bound - tallies[sink]) // 2
    room = jnp.where((source_of == order[0]) | (sink == order[0]) | (tallies[sink] == 0), 0, jnp.maximum(room, 0))
    passed = jax.random.randint(jax.random.fold_in(own, 4), (amount // 2,), 0, 1 << 20) % (room + 1)
    tallies = tallies.at[source_of].add(-passed).at[sink].add(passed)
    members = jnp.searchsorted(jnp.cumsum(tallies), jnp.arange(rows * top), side="right").astype(jnp.int32)
    table = members.reshape(top, rows).T
    table = table[jax.random.permutation(jax.random.fold_in(own, 1), rows)]
    offset_by = jax.random.randint(jax.random.fold_in(own, 2), (rows, 1), 0, top)
    return jnp.take_along_axis(table, (jnp.arange(top)[None, :] + offset_by) % top, axis=1)


def portions_of(count, total, limit, lean, full):
    weights = [(1 << 20) // math.isqrt(rank ** lean) + 1 for rank in range(1, count + 1)]
    largest = limit if full else min(limit, max(-(-total // count), total * weights[0] // sum(weights)))
    least = 1 if total - largest >= count - 1 else 0
    given, surplus = [largest] + [least] * (count - 1), total - largest - least * (count - 1)
    while surplus > 0:
        movable = [i for i in range(1, count) if given[i] < largest] or [i for i in range(1, count) if given[i] < limit]
        pool, remaining = sum([weights[i] for i in movable]), surplus
        for i in movable:
            extra = min(limit - given[i], max(1, remaining * weights[i] // pool), surplus)
            given[i] = given[i] + extra
            surplus = surplus - extra
    return np.array(given)


def gaussian(stream_key, extent, width, bound, cuts=(), kind=jnp.bfloat16):
    drawn = jax.random.normal(stream_key, extent, jnp.float32) * width
    if len(cuts) > 0:
        drawn = level_of(stream_key, extent, cuts, -0.22, 0.18) * drawn
    return jnp.clip(drawn, min=-bound, max=bound).astype(kind)


def setup_inputs(seed: int = 0) -> dict:
    keys = jax.random.split(jax.random.key(seed), 19)
    hidden = draw_hidden(jax.random.fold_in(keys[18], 71), 0)
    cotangent = gaussian(keys[1], (SEQS, LENGTH, D), 1.0, 6.0, ((0, 8), (1, 4)))
    segments = draw_segments(jax.random.fold_in(keys[18], 71), 0)
    routes_keys = jax.random.split(jax.random.fold_in(keys[3], 1), SEQS * LENGTH // TOK_DEV)
    routes_turns = jax.random.permutation(jax.random.fold_in(keys[3], 3), SEQS * LENGTH // TOK_DEV)
    routes = jax.vmap(lambda own, number: deal_out(jax.random.fold_in(keys[3], 2), own, number, TOK_DEV, EXPERTS, TOP, CAP, 1))(routes_keys, routes_turns).reshape((SEQS, LENGTH, TOP))
    w_query = gaussian(keys[4], (D, H * (DN + DR)), D ** -0.5, 0.125, ((0, 4),))
    w_latent = gaussian(keys[5], (D, KVR + DR), D ** -0.5, 0.125, ((0, 4),))
    g_latent = jnp.clip(1.0 + 0.18 * jax.random.normal(keys[6], (KVR,), jnp.float32), 0.099609375, 1.8984375).astype(jnp.bfloat16)
    w_expand = gaussian(keys[7], (KVR, H * (DN + DV)), KVR ** -0.5, 0.25, ((0, 4),))
    w_out = gaussian(keys[8], (H * DV, D), (H * DV // 64) ** -0.5, 1.0, ((0, 4),))
    g_attn = jnp.clip(1.0 + 0.18 * jax.random.normal(keys[9], (D,), jnp.float32), 0.099609375, 1.8984375).astype(jnp.bfloat16)
    g_ffn = jnp.clip(1.0 + 0.18 * jax.random.normal(keys[10], (D,), jnp.float32), 0.099609375, 1.8984375).astype(jnp.bfloat16)
    w_router = gaussian(keys[11], (D, EXPERTS), D ** -0.5, 0.125, ((0, 4),))
    s_gate = gaussian(keys[12], (D, FS), D ** -0.5, 0.125, ((0, 4),))
    s_up = gaussian(keys[13], (D, FS), D ** -0.5, 0.125, ((0, 4),))
    s_down = gaussian(keys[14], (FS, D), FS ** -0.5, 0.109375, ((0, 4),))
    e_gate = gaussian(keys[15], (EXPERTS, D, FF), D ** -0.5, 0.125, ((0, 8), (2, 4)))
    expert_up_weight = gaussian(keys[16], (EXPERTS, D, FF), D ** -0.5, 0.125, ((0, 8), (2, 4)))
    e_down = gaussian(keys[17], (EXPERTS, FF, D), FF ** -0.5, 0.15625, ((0, 8), (1, 4)))
    return dict(hidden=hidden, cotangent=cotangent, segments=segments, routes=routes, w_query=w_query, w_latent=w_latent, g_latent=g_latent, w_expand=w_expand, w_out=w_out, g_attn=g_attn, g_ffn=g_ffn, w_router=w_router, s_gate=s_gate, s_up=s_up, s_down=s_down, e_gate=e_gate, expert_up_weight=expert_up_weight, e_down=e_down)


@jax.custom_vjp
def low(v):
    return lax.optimization_barrier(v.astype(jnp.bfloat16)).astype(jnp.float32)

@jax.custom_vjp
def low_back(v):
    return v

def low_keep(v):
    return (low(v), None)

def low_pass(kept, grad):
    return (grad,)

def back_keep(v):
    return (v, None)

def back_low(kept, grad):
    return (low(grad),)
low.defvjp(low_keep, low_pass)
low_back.defvjp(back_keep, back_low)
EPS = 1e-06
ROUTE_SCALE = 2.446
ROPE_BASE = 50000.0
PRECISE = lax.Precision.HIGHEST

def round_both(values):
    return low(low_back(values))

def matmul(first_op, second_op):
    return jnp.dot(first_op, second_op, precision=PRECISE, preferred_element_type=jnp.float32)

def rms_norm(values, gain_vec):
    return values * lax.rsqrt(lax.optimization_barrier(jnp.mean(values * values, axis=-1, keepdims=True)) + EPS) * gain_vec

def rope_angles(positions):
    half_width = DR // 2
    inverse = ROPE_BASE ** (-jnp.arange(half_width).astype(jnp.float32) / half_width)
    angles = positions.astype(jnp.float32)[:, None] * inverse[None, :]
    return (jnp.cos(angles), jnp.sin(angles))

def rotate(values, cosine, sine_vals):
    half_width = values.shape[-1] // 2
    first_half = values[..., :half_width]
    second_half = values[..., half_width:]
    return jnp.concatenate([first_half * cosine - second_half * sine_vals, second_half * cosine + first_half * sine_vals], axis=-1)

def route_ranks(route_block):
    flat_routes = route_block.reshape(-1)
    hit_table = (flat_routes[:, None] == jnp.arange(EXPERTS).astype(jnp.int32)[None, :]).astype(jnp.int32)
    before = jnp.cumsum(hit_table, axis=0) - hit_table
    return lax.optimization_barrier(jnp.sum(before * hit_table, axis=1)).astype(jnp.int32)

def reference(hidden, cotangent, segments, routes, w_query, w_latent, g_latent, w_expand, w_out, g_attn, g_ffn, w_router, s_gate, s_up, s_down, e_gate, expert_up_weight, e_down):
    devices = N_EXPERT * N_SHARD
    per_expert = devices * CAP
    blocks = routes.reshape(devices, TOK_DEV * TOP).astype(jnp.int32)
    slot_rank = jax.vmap(route_ranks)(blocks)
    owner_base = (jnp.arange(devices).astype(jnp.int32) * CAP)[:, None]
    slot_of = (blocks * per_expert + owner_base + slot_rank).reshape(-1)
    pair_count = TOKENS * TOP
    pair_of_slot = jnp.full((EXPERTS * per_expert,), pair_count, jnp.int32).at[slot_of].set(jnp.arange(pair_count).astype(jnp.int32))
    token_of_slot = pair_of_slot // TOP
    flat_routes = routes.reshape(TOKENS, TOP).astype(jnp.int32)
    positions = jnp.arange(LENGTH).astype(jnp.int32)
    cosine, sine_vals = rope_angles(positions)
    score_scale = (DN + DR) ** (-0.5)

    def sequence_attention(normed_seq, seg_row, query_weight, latent_weight, latent_norm_gain, expand_weight):
        query_all = low_back(matmul(normed_seq, query_weight)).reshape(LENGTH, H, DN + DR)
        query_all = low(jnp.concatenate([query_all[..., :DN], rotate(query_all[..., DN:], cosine[:, None, :], sine_vals[:, None, :])], axis=-1))
        compressed = low_back(matmul(normed_seq, latent_weight))
        latent_all = low(jnp.concatenate([rms_norm(compressed[:, :KVR], latent_norm_gain), rotate(compressed[:, KVR:], cosine, sine_vals)], axis=1))
        key_rope = latent_all[:, KVR:]

        def query_block(start_row):
            expanded = round_both(matmul(latent_all[:, :KVR], expand_weight)).reshape(LENGTH, H, DN + DV)
            query_rows = lax.dynamic_slice_in_dim(query_all, start_row, TOK_DEV, 0)
            seg_rows = lax.dynamic_slice_in_dim(seg_row, start_row, TOK_DEV, 0)
            pos_rows = lax.dynamic_slice_in_dim(positions, start_row, TOK_DEV, 0)
            raw_scores = jnp.einsum('qhd,khd->hqk', query_rows[..., :DN], expanded[..., :DN], precision=PRECISE) + jnp.einsum('qhd,kd->hqk', query_rows[..., DN:], key_rope, precision=PRECISE)
            scores = low_back(raw_scores) * score_scale
            allowed = (seg_rows[:, None] == seg_row[None, :]) & (positions[None, :] <= pos_rows[:, None])
            scores = jnp.where(allowed[None], scores, -1e+30)
            weights_f = jax.nn.softmax(scores, axis=-1)
            mixed_rows = jnp.einsum('hqk,khd->qhd', low(weights_f), expanded[..., DN:], precision=PRECISE)
            return round_both(mixed_rows).reshape(TOK_DEV, H * DV)
        starts = (jnp.arange(N_SHARD) * TOK_DEV).astype(jnp.int32)
        return lax.map(jax.checkpoint(query_block), starts).reshape(LENGTH, H * DV)

    def apply_routed_expert(operands):
        routed_expert_rows, gate_w, up_w, down_w = operands
        gate_preactivation = low_back(matmul(routed_expert_rows, gate_w))
        up_preactivation = low_back(matmul(routed_expert_rows, up_w))
        inner_act = low(jax.nn.silu(gate_preactivation) * up_preactivation)
        return round_both(matmul(inner_act, down_w))

    def layer_function(inputs_float, query_weight, latent_weight, latent_norm_gain, expand_weight, output_weight, first_norm_gain, second_norm_gain, router_weight, shared_gate_weight, shared_up_weight, shared_down_weight, expert_gate_weight, expert_up_matrix, expert_down_weight):
        normed = low(rms_norm(inputs_float, first_norm_gain))
        mixed_all = lax.map(jax.checkpoint(lambda seq_pair: sequence_attention(seq_pair[0], seq_pair[1], query_weight, latent_weight, latent_norm_gain, expand_weight)), (normed, segments))
        attn_out = low_back(matmul(mixed_all.reshape(TOKENS, H * DV), output_weight))
        residual_mid = inputs_float.reshape(TOKENS, D) + attn_out
        normed_two = low(rms_norm(residual_mid, second_norm_gain))
        logits = low_back(matmul(normed_two, router_weight))
        probs_r = jax.nn.sigmoid(logits)
        chosen = jnp.take_along_axis(probs_r, flat_routes, axis=1)
        route_weights = chosen / lax.optimization_barrier(jnp.sum(chosen, axis=1, keepdims=True)) * ROUTE_SCALE
        padded_rows = jnp.concatenate([normed_two, jnp.zeros((1, D), jnp.float32)], axis=0)
        holding_rows_buffer = low_back(jnp.take(padded_rows, token_of_slot, axis=0)).reshape(EXPERTS, per_expert, D)
        routed_expert_output = lax.map(apply_routed_expert, (holding_rows_buffer, expert_gate_weight, expert_up_matrix, expert_down_weight))
        picked_rows = jnp.take(routed_expert_output.reshape(-1, D), slot_of, axis=0).reshape(TOKENS, TOP, D)
        routed = lax.optimization_barrier(jnp.sum(route_weights[:, :, None] * picked_rows, axis=1))
        shared_gate = low_back(matmul(normed_two, shared_gate_weight))
        shared_up = low_back(matmul(normed_two, shared_up_weight))
        shared_inner = low(jax.nn.silu(shared_gate) * shared_up)
        shared_out = matmul(shared_inner, shared_down_weight)
        result_rows = residual_mid + routed + shared_out
        return result_rows.reshape(SEQS, LENGTH, D)
    floats = [array_in.astype(jnp.float32) for array_in in (hidden, w_query, w_latent, g_latent, w_expand, w_out, g_attn, g_ffn, w_router, s_gate, s_up, s_down, e_gate, expert_up_weight, e_down)]
    output, pullback = jax.vjp(layer_function, *floats)
    gradients = pullback(cotangent.astype(jnp.float32))
    return (output.astype(jnp.bfloat16), gradients[0], gradients[1], gradients[2], gradients[3], gradients[4], gradients[5], gradients[6], gradients[7], gradients[8], gradients[9], gradients[10], gradients[11], gradients[12], gradients[13], gradients[14])
```

```python
import functools

import jax
import jax.numpy as jnp
from jax import lax
from jax.experimental import pallas as pl
from jax.experimental.pallas import tpu as pltpu
from jax.sharding import PartitionSpec as P

H = 16
DN = 128
DR = 64
DV = 128
KVR = 512
TOP = 6
EXP_DEV = 4

EPS = 1e-06
ROUTE_SCALE = 2.446
ROPE_BASE = 50000.0
SCORE_SCALE = (DN + DR) ** (-0.5)
BF = jnp.bfloat16
F32 = jnp.float32
BOTH = ("expert", "shard")
VMEM_BYTES = 56 * 1024 * 1024


def mm(a, b):
    return jnp.dot(a, b, preferred_element_type=F32)


def mm_tn(a, b):
    return lax.dot_general(a, b, (((0,), (0,)), ((), ())), preferred_element_type=F32)


def mm_nt(a, b):
    return lax.dot_general(a, b, (((1,), (1,)), ((), ())), preferred_element_type=F32)


def rope_angles(positions):
    half_width = DR // 2
    inverse = ROPE_BASE ** (-jnp.arange(half_width).astype(F32) / half_width)
    angles = positions.astype(F32)[:, None] * inverse[None, :]
    return (jnp.cos(angles), jnp.sin(angles))


def rotate(values, cosine, sine_vals):
    half_width = DR // 2
    first_half = values[..., :half_width]
    second_half = values[..., half_width:]
    return jnp.concatenate(
        [
            first_half * cosine - second_half * sine_vals,
            second_half * cosine + first_half * sine_vals,
        ],
        axis=-1,
    )


def norm_forward(values):
    factor = lax.rsqrt(jnp.mean(values * values, axis=-1, keepdims=True) + EPS)
    return values * factor, factor


def norm_backward(grad_out, gain_vec, unit_vals, factor):
    grad_unit = grad_out * gain_vec
    grad_in = factor * (
        grad_unit - unit_vals * jnp.mean(grad_unit * unit_vals, axis=-1, keepdims=True)
    )
    return (grad_in, jnp.sum(grad_out * unit_vals, axis=0))


def swish_parts(gate, up):
    sig = jax.nn.sigmoid(gate)
    silu = gate * sig
    return silu * up, up * sig * (1.0 + gate * (1.0 - sig)), silu


def exchange(values, axis):
    return lax.all_to_all(values, axis, split_axis=0, concat_axis=0, tiled=True)


def gather_shard(values, shards):
    copies = jnp.broadcast_to(values[None], (shards,) + values.shape)
    got = exchange(copies, "shard")
    return got.reshape((shards * values.shape[0],) + values.shape[1:])


def sum_shard(values, shards):
    rows = values.shape[0] // shards
    got = exchange(values.reshape((shards, rows) + values.shape[1:]), "shard")
    return jnp.sum(got.astype(F32), axis=0)


def params(**kw):
    return pltpu.CompilerParams(vmem_limit_bytes=VMEM_BYTES, **kw)


def allowed_mask(seg_col, seg_row):
    length = seg_row.shape[1]
    rows = lax.broadcasted_iota(jnp.int32, (length, length), 0)
    cols = lax.broadcasted_iota(jnp.int32, (length, length), 1)
    return (seg_col == seg_row) & (cols <= rows)


def attention_forward_kernel(
    n1_ref, wq_ref, lat_ref, we_ref, cos_ref, sin_ref, segc_ref, segr_ref,
    o_ref, q_ref, kv_ref, lse_ref,
):
    width = n1_ref.shape[1]
    query = mm(n1_ref[...], wq_ref[...].reshape(width, DN + DR))
    query = jnp.concatenate(
        [query[:, :DN], rotate(query[:, DN:], cos_ref[...], sin_ref[...])], axis=1
    ).astype(BF)
    q_ref[0] = query
    kv = mm(lat_ref[:, :KVR], we_ref[...].reshape(KVR, DN + DV)).astype(BF)
    kv_ref[0] = kv
    scores = mm_nt(query[:, :DN], kv[:, :DN]) + mm_nt(query[:, DN:], lat_ref[:, KVR:])
    ok = allowed_mask(segc_ref[...], segr_ref[...])
    scores = jnp.where(ok, scores * SCORE_SCALE, -1e30)
    top = jnp.max(scores, axis=1, keepdims=True)
    expo = jnp.exp(scores - top)
    total = jnp.sum(expo, axis=1, keepdims=True)
    lse_ref[0] = top + jnp.log(total)
    weights = (expo / total).astype(BF)
    o_ref[...] = mm(weights, kv[:, DN:]).astype(BF)


def attention_forward(n1, wq, latent, we, cosine, sine_vals, seg_col, seg_row):
    length, width = n1.shape
    shards, heads = wq.shape[0], wq.shape[1]
    whole = lambda shape: pl.BlockSpec(shape, lambda h: (0,) * len(shape))
    return pl.pallas_call(
        attention_forward_kernel,
        grid=(heads,),
        in_specs=[
            whole((length, width)),
            pl.BlockSpec((shards, 1, width // shards, DN + DR), lambda h: (0, h, 0, 0)),
            whole((length, KVR + DR)),
            pl.BlockSpec((shards, 1, KVR // shards, DN + DV), lambda h: (0, h, 0, 0)),
            whole((length, DR // 2)),
            whole((length, DR // 2)),
            whole((length, 1)),
            whole((1, length)),
        ],
        out_specs=[
            pl.BlockSpec((length, DV), lambda h: (0, h)),
            pl.BlockSpec((1, length, DN + DR), lambda h: (h, 0, 0)),
            pl.BlockSpec((1, length, DN + DV), lambda h: (h, 0, 0)),
            pl.BlockSpec((1, length, 1), lambda h: (h, 0, 0)),
        ],
        out_shape=[
            jax.ShapeDtypeStruct((length, heads * DV), BF),
            jax.ShapeDtypeStruct((heads, length, DN + DR), BF),
            jax.ShapeDtypeStruct((heads, length, DN + DV), BF),
            jax.ShapeDtypeStruct((heads, length, 1), F32),
        ],
        compiler_params=params(),
        name="attention_forward",
    )(n1, wq, latent, we, cosine, sine_vals, seg_col, seg_row)


def attention_backward_kernel(
    dh_ref, wo_ref, o_ref, q_ref, kv_ref, lse_ref, lat_ref, we_ref, wq_ref, n1_ref,
    cos_ref, sin_ref, segc_ref, segr_ref,
    dn1_ref, dlat_ref, dwq_ref, dwe_ref, dwo_ref,
):
    head = pl.program_id(0)
    width = n1_ref.shape[1]
    shards = wq_ref.shape[0]
    query, kv = q_ref[0], kv_ref[0]
    grad_o = mm_nt(dh_ref[...], wo_ref[...]).astype(BF)
    dwo_ref[...] = mm_tn(o_ref[...], dh_ref[...]).astype(BF)
    scores = mm_nt(query[:, :DN], kv[:, :DN]) + mm_nt(query[:, DN:], lat_ref[:, KVR:])
    ok = allowed_mask(segc_ref[...], segr_ref[...])
    weights = jnp.where(ok, jnp.exp(scores * SCORE_SCALE - lse_ref[0]), 0.0)
    grad_w = mm_nt(grad_o, kv[:, DN:])
    delta = jnp.sum(weights * grad_w, axis=1, keepdims=True)
    grad_s = (weights * (grad_w - delta) * SCORE_SCALE).astype(BF)
    grad_qr = mm(grad_s, lat_ref[:, KVR:])
    grad_q = jnp.concatenate(
        [mm(grad_s, kv[:, :DN]), rotate(grad_qr, cos_ref[...], -sin_ref[...])], axis=1
    ).astype(BF)
    grad_kv = jnp.concatenate(
        [mm_tn(grad_s, query[:, :DN]), mm_tn(weights.astype(BF), grad_o)], axis=1
    ).astype(BF)
    grad_kr = mm_tn(grad_s, query[:, DN:])
    dwq_ref[...] = mm_tn(n1_ref[...], grad_q).astype(BF).reshape(dwq_ref.shape)
    dwe_ref[...] = mm_tn(lat_ref[:, :KVR], grad_kv).astype(BF).reshape(dwe_ref.shape)
    part_n1 = mm_nt(grad_q, wq_ref[...].reshape(width, DN + DR))
    part_lat = mm_nt(grad_kv, we_ref[...].reshape(KVR, DN + DV))

    @pl.when(head == 0)
    def _():
        dn1_ref[...] = part_n1
        dlat_ref[:, :KVR] = part_lat
        dlat_ref[:, KVR:] = grad_kr

    @pl.when(head > 0)
    def _():
        dn1_ref[...] += part_n1
        dlat_ref[:, :KVR] += part_lat
        dlat_ref[:, KVR:] += grad_kr


def attention_backward(
    dh, wo, o, query, kv, lse, latent, we, wq, n1, cosine, sine_vals, seg_col, seg_row
):
    length, width = n1.shape
    shards, heads = wq.shape[0], wq.shape[1]
    whole = lambda shape: pl.BlockSpec(shape, lambda h: (0,) * len(shape))
    wq_spec = pl.BlockSpec((shards, 1, width // shards, DN + DR), lambda h: (0, h, 0, 0))
    we_spec = pl.BlockSpec((shards, 1, KVR // shards, DN + DV), lambda h: (0, h, 0, 0))
    return pl.pallas_call(
        attention_backward_kernel,
        grid=(heads,),
        in_specs=[
            whole((length, width)),
            pl.BlockSpec((DV, width), lambda h: (h, 0)),
            pl.BlockSpec((length, DV), lambda h: (0, h)),
            pl.BlockSpec((1, length, DN + DR), lambda h: (h, 0, 0)),
            pl.BlockSpec((1, length, DN + DV), lambda h: (h, 0, 0)),
            pl.BlockSpec((1, length, 1), lambda h: (h, 0, 0)),
            whole((length, KVR + DR)),
            we_spec,
            wq_spec,
            whole((length, width)),
            whole((length, DR // 2)),
            whole((length, DR // 2)),
            whole((length, 1)),
            whole((1, length)),
        ],
        out_specs=[
            whole((length, width)),
            whole((length, KVR + DR)),
            wq_spec,
            we_spec,
            pl.BlockSpec((DV, width), lambda h: (h, 0)),
        ],
        out_shape=[
            jax.ShapeDtypeStruct((length, width), F32),
            jax.ShapeDtypeStruct((length, KVR + DR), F32),
            jax.ShapeDtypeStruct(wq.shape, BF),
            jax.ShapeDtypeStruct(we.shape, BF),
            jax.ShapeDtypeStruct((heads * DV, width), BF),
        ],
        compiler_params=params(),
        name="attention_backward",
    )(dh, wo, o, query, kv, lse, latent, we, wq, n1, cosine, sine_vals, seg_col, seg_row)


def pick_kernel(pick_ref, x_ref, out_ref):
    rows = mm(pick_ref[0], x_ref[0]).astype(BF)
    out_ref[...] = rows.reshape(out_ref.shape)


def pick_rows(pick, x_all, capacity):
    devices, slots, tokens = pick.shape
    width = x_all.shape[2]
    return pl.pallas_call(
        pick_kernel,
        grid=(devices,),
        in_specs=[
            pl.BlockSpec((1, slots, tokens), lambda d: (d, 0, 0)),
            pl.BlockSpec((1, tokens, width), lambda d: (d, 0, 0)),
        ],
        out_specs=pl.BlockSpec((EXP_DEV, capacity, width), lambda d: (0, d, 0)),
        out_shape=jax.ShapeDtypeStruct((EXP_DEV, devices * capacity, width), BF),
        compiler_params=params(),
        name="pick_rows",
    )(pick, x_all)


def place_kernel(pick_ref, rows_ref, left_ref, right_ref, out_ref):
    slots = pick_ref.shape[1]
    rows = rows_ref[...].reshape(slots, rows_ref.shape[2])
    total = mm_tn(pick_ref[0], rows) + mm(left_ref[0], right_ref[...])
    out_ref[0] = total.astype(BF)


def place_rows(pick, rows, left, right, capacity):
    devices, slots, tokens = pick.shape
    width = rows.shape[2]
    inner = left.shape[2]
    return pl.pallas_call(
        place_kernel,
        grid=(devices,),
        in_specs=[
            pl.BlockSpec((1, slots, tokens), lambda d: (d, 0, 0)),
            pl.BlockSpec((EXP_DEV, capacity, width), lambda d: (0, d, 0)),
            pl.BlockSpec((1, tokens, inner), lambda d: (d, 0, 0)),
            pl.BlockSpec((inner, width), lambda d: (0, 0)),
        ],
        out_specs=pl.BlockSpec((1, tokens, width), lambda d: (d, 0, 0)),
        out_shape=jax.ShapeDtypeStruct((devices, tokens, width), BF),
        compiler_params=params(),
        name="place_rows",
    )(pick, rows, left, right)


def body(
    hidden,
    cotangent,
    segments,
    routes,
    w_query,
    w_latent,
    g_latent,
    w_expand,
    w_out,
    g_attn,
    g_ffn,
    w_router,
    s_gate,
    s_up,
    s_down,
    e_gate,
    expert_up_weight,
    e_down,
):
    tokens = hidden.shape[1]
    width = hidden.shape[2]
    shards = lax.axis_size("shard")
    groups = lax.axis_size("expert")
    devices = groups * shards
    experts = EXP_DEV * groups
    capacity = max(2, tokens * TOP * 4 // (3 * experts))
    heads = H // shards
    length = tokens * shards
    part = width // shards
    my_shard = lax.axis_index("shard")
    my_group = lax.axis_index("expert")
    hid_shard = s_down.shape[0]
    hid = hid_shard // groups

    hidden_all = gather_shard(hidden[0], shards)
    wq = exchange(
        w_query.reshape(part, H, DN + DR).transpose(1, 0, 2), "shard"
    ).reshape(shards, heads, part, DN + DR)
    we = exchange(
        w_expand.reshape(KVR // shards, H, DN + DV).transpose(1, 0, 2), "shard"
    ).reshape(shards, heads, KVR // shards, DN + DV)
    full_latent = lax.all_gather(w_latent, "shard", axis=0, tiled=True)
    gain_pack = lax.all_gather(
        jnp.concatenate([g_attn, g_ffn, g_latent]), "shard", axis=0, tiled=False
    )
    gattn = gain_pack[:, :part].reshape(width).astype(F32)
    gffn = gain_pack[:, part : 2 * part].reshape(width).astype(F32)
    glatent = gain_pack[:, 2 * part :].reshape(KVR).astype(F32)
    full_router = lax.all_gather(w_router, "shard", axis=0, tiled=True)
    g_all = lax.all_gather(cotangent[0], BOTH, axis=0, tiled=False)

    mine = lambda w: lax.dynamic_slice_in_dim(
        w.reshape(part, shards, hid_shard), my_group * hid, hid, 2
    )
    gate_up = jnp.concatenate([mine(s_gate), mine(s_up)], axis=2).transpose(1, 0, 2)
    shared_in = exchange(gate_up, "shard").reshape(width, 2 * hid)
    shared_down = lax.dynamic_slice_in_dim(s_down, my_group * hid, hid, 0)

    local_routes = routes[0]
    flat_routes = local_routes.reshape(-1)
    choose = local_routes[:, :, None] == jnp.arange(experts, dtype=jnp.int32)[None, None, :]
    hits = choose.reshape(-1, experts).astype(F32)
    pair_count = tokens * TOP
    lower = (
        lax.broadcasted_iota(jnp.int32, (pair_count, pair_count), 1)
        < lax.broadcasted_iota(jnp.int32, (pair_count, pair_count), 0)
    ).astype(BF)
    before = mm(lower, hits.astype(BF))
    slot_rank = jnp.sum(before * hits, axis=1).astype(jnp.int32)
    slot_of = (flat_routes * capacity + slot_rank).reshape(tokens, TOP)
    slots = EXP_DEV * capacity
    slots_all = lax.all_gather(slot_of, BOTH, axis=0, tiled=False)
    slot_ids = my_group * slots + jnp.arange(slots, dtype=jnp.int32)
    match = slots_all[:, None, :, :] == slot_ids[None, :, None, None]
    pick = jnp.any(match, axis=3).astype(BF)

    residual_all = hidden_all.astype(F32)
    unit_all, factor_all = norm_forward(residual_all)
    n1 = (unit_all * gattn).astype(BF)
    cosine, sine_vals = rope_angles(jnp.arange(length, dtype=jnp.int32))
    compressed = mm(n1, full_latent)
    latent_unit, latent_factor = norm_forward(compressed[:, :KVR])
    latent = jnp.concatenate(
        [latent_unit * glatent, rotate(compressed[:, KVR:], cosine, sine_vals)], axis=1
    ).astype(BF)
    seg_row = segments
    seg_col = segments.reshape(length, 1)
    attended, query, kv, lse = attention_forward(
        n1, wq, latent, we, cosine, sine_vals, seg_col, seg_row
    )
    attn_out = sum_shard(mm(attended, w_out).astype(BF), shards)
    residual_in = hidden[0].astype(F32)
    residual_mid = residual_in + attn_out
    unit_two, factor_two = norm_forward(residual_mid)
    normed_two = (unit_two * gffn).astype(BF)

    n2_all = lax.all_gather(normed_two, BOTH, axis=0, tiled=False)
    probs = jax.nn.sigmoid(mm(normed_two, full_router))
    chosen = jnp.sum(jnp.where(choose, probs[:, None, :], 0.0), axis=-1)
    chosen_total = jnp.sum(chosen, axis=1, keepdims=True)
    route_weights = chosen / chosen_total * ROUTE_SCALE
    weights_all = lax.all_gather(route_weights, BOTH, axis=0, tiled=False)
    slot_weight = jnp.sum(
        jnp.where(match, weights_all[:, None, :, :], 0.0), axis=(2, 3)
    )
    by_expert = lambda v: v.reshape(devices, EXP_DEV, capacity).transpose(1, 0, 2).reshape(
        EXP_DEV, devices * capacity
    )
    row_weight = by_expert(slot_weight)[:, :, None]

    grad_rows = pick_rows(pick, g_all, capacity)
    grad_inner = jnp.einsum("jmd,jfd->jmf", grad_rows, e_down, preferred_element_type=F32)
    shared_grad_inner = mm_nt(g_all.reshape(-1, width), shared_down)
    rows = pick_rows(pick, n2_all, capacity)
    gate = jnp.einsum("jmd,jdf->jmf", rows, e_gate, preferred_element_type=F32)
    up = jnp.einsum("jmd,jdf->jmf", rows, expert_up_weight, preferred_element_type=F32)
    inner, slope_gate, slope_up = swish_parts(gate, up)
    weighted_grad = row_weight * grad_inner
    grad_gate_b = (weighted_grad * slope_gate).astype(BF)
    grad_up_b = (weighted_grad * slope_up).astype(BF)
    inner_w = (row_weight * inner).astype(BF)
    grad_slot_weight = jnp.sum(inner.astype(BF).astype(F32) * grad_inner, axis=2)

    shared_pre = mm(n2_all.reshape(-1, width), shared_in)
    s_inner, s_slope_gate, s_slope_up = swish_parts(shared_pre[:, :hid], shared_pre[:, hid:])
    shared_inner = s_inner.astype(BF)
    shared_grads = jnp.concatenate(
        [shared_grad_inner * s_slope_gate, shared_grad_inner * s_slope_up], axis=1
    ).astype(BF)

    dz = (
        jnp.einsum("jmf,jdf->jmd", grad_gate_b, e_gate, preferred_element_type=F32)
        + jnp.einsum("jmf,jdf->jmd", grad_up_b, expert_up_weight, preferred_element_type=F32)
    ).astype(BF)
    dn2_part = place_rows(
        pick, dz, shared_grads.reshape(devices, tokens, 2 * hid), shared_in.T, capacity
    )
    dn2 = lax.psum_scatter(dn2_part, BOTH, scatter_dimension=0, tiled=False).astype(F32)
    weighted_out = jnp.einsum(
        "jmf,jfd->jmd", inner_w, e_down, preferred_element_type=F32
    ).astype(BF)
    out_part = place_rows(
        pick, weighted_out, shared_inner.reshape(devices, tokens, hid), shared_down, capacity
    )
    routed_shared = lax.psum_scatter(
        out_part, BOTH, scatter_dimension=0, tiled=False
    ).astype(F32)
    output_rows = residual_mid + routed_shared

    d_edown = jnp.einsum("jmf,jmd->jfd", inner_w, grad_rows, preferred_element_type=F32)
    d_egate = jnp.einsum("jmd,jmf->jdf", rows, grad_gate_b, preferred_element_type=F32)
    grad_expert_up = jnp.einsum("jmd,jmf->jdf", rows, grad_up_b, preferred_element_type=F32)

    slot_back = grad_slot_weight.reshape(EXP_DEV, devices, capacity).transpose(1, 0, 2)
    got = exchange(slot_back.reshape(devices, slots), BOTH)
    slot_grads = jnp.sum(got.reshape(groups, shards, slots), axis=1).reshape(-1)
    at_slot = slot_of[:, :, None] == jnp.arange(experts * capacity, dtype=jnp.int32)
    grad_weights = jnp.sum(jnp.where(at_slot, slot_grads, 0.0), axis=2)
    grad_chosen = ROUTE_SCALE * (
        grad_weights / chosen_total
        - jnp.sum(grad_weights * chosen, axis=1, keepdims=True) / (chosen_total * chosen_total)
    )
    grad_probs = jnp.sum(jnp.where(choose, grad_chosen[:, :, None], 0.0), axis=1)
    grad_logits = (grad_probs * probs * (1.0 - probs)).astype(BF)

    d_shared_in = mm_tn(shared_grads, n2_all.reshape(-1, width)).astype(BF)
    d_shared_down = mm_tn(shared_inner, g_all.reshape(-1, width)).astype(BF)
    in_pieces = exchange(
        d_shared_in.reshape(2 * hid, shards, part).transpose(1, 0, 2), "shard"
    )
    in_all = lax.all_gather(in_pieces, "expert", axis=0, tiled=False)
    in_all = in_all.reshape(groups, shards, 2, hid, part).astype(F32)
    in_all = in_all.transpose(2, 1, 0, 3, 4).reshape(2, shards * groups * hid, part)
    part_sgate = in_all[0].T
    part_sup = in_all[1].T
    part_sdown = lax.all_gather(d_shared_down, "expert", axis=0, tiled=True).astype(F32)

    grad_normed_two = dn2 + mm_nt(grad_logits, full_router)
    grad_mid_norm, d_gffn = norm_backward(grad_normed_two, gffn, unit_two, factor_two)
    grad_mid = cotangent[0].astype(F32) + grad_mid_norm
    grad_attn = gather_shard(grad_mid.astype(BF), shards)
    d_router_part = mm_tn(normed_two, grad_logits)

    dn1_heads, dlat, dwq, dwe, d_out = attention_backward(
        grad_attn, w_out, attended, query, kv, lse, latent, we, wq, n1,
        cosine, sine_vals, seg_col, seg_row,
    )
    grad_comp_norm, d_glatent = norm_backward(dlat[:, :KVR], glatent, latent_unit, latent_factor)
    grad_compressed = jnp.concatenate(
        [grad_comp_norm, rotate(dlat[:, KVR:], cosine, -sine_vals)], axis=1
    ).astype(BF)
    grad_normed = sum_shard(
        (dn1_heads + mm_nt(grad_compressed, full_latent)).astype(BF), shards
    )
    unit_one, factor_one = norm_forward(residual_in)
    grad_input_norm, d_gattn = norm_backward(grad_normed, gattn, unit_one, factor_one)
    grad_input = grad_mid + grad_input_norm

    rows_query = exchange(dwq.reshape(H, part, DN + DR), "shard")
    rows_expand = exchange(dwe.reshape(H, KVR // shards, DN + DV), "shard")
    rows_latent = sum_shard(mm_tn(n1, grad_compressed).astype(BF), shards).astype(BF)
    sum_query, sum_latent, sum_expand, sum_out = lax.psum(
        (rows_query, rows_latent, rows_expand, d_out), "expert"
    )
    small = lax.psum(
        jnp.concatenate([d_router_part.reshape(-1), d_gattn, d_gffn, d_glatent]), BOTH
    )
    count = width * experts
    d_router = lax.dynamic_slice_in_dim(
        small[:count].reshape(width, experts), my_shard * part, part, 0
    )
    gains = small[count:]
    own = lambda v, n: lax.dynamic_slice_in_dim(v, my_shard * n, n, 0)
    part_gattn = own(gains[:width], part)
    part_gffn = own(gains[width : 2 * width], part)
    part_glatent = own(gains[2 * width :], KVR // shards)
    part_query = sum_query.transpose(1, 0, 2).reshape(part, H * (DN + DR)).astype(F32)
    part_expand = (
        sum_expand.transpose(1, 0, 2).reshape(KVR // shards, H * (DN + DV)).astype(F32)
    )
    return (
        output_rows.astype(BF)[None],
        grad_input[None],
        part_query,
        sum_latent.astype(F32),
        part_glatent,
        part_expand,
        sum_out.astype(F32),
        part_gattn,
        part_gffn,
        d_router,
        part_sgate,
        part_sup,
        part_sdown,
        d_egate,
        grad_expert_up,
        d_edown,
    )


def solution(mesh):
    return jax.shard_map(
        body,
        mesh=mesh,
        in_specs=(
            P("expert", "shard", None),
            P("expert", "shard", None),
            P("expert", None),
            P("expert", "shard", None),
            P("shard", None),
            P("shard", None),
            P("shard"),
            P("shard", None),
            P("shard", None),
            P("shard"),
            P("shard"),
            P("shard", None),
            P("shard", None),
            P("shard", None),
            P("shard", None),
            P("expert", None, "shard"),
            P("expert", None, "shard"),
            P("expert", "shard", None),
        ),
        out_specs=(
            P("expert", "shard", None),
            P("expert", "shard", None),
            P("shard", None),
            P("shard", None),
            P("shard"),
            P("shard", None),
            P("shard", None),
            P("shard"),
            P("shard"),
            P("shard", None),
            P("shard", None),
            P("shard", None),
            P("shard", None),
            P("expert", None, "shard"),
            P("expert", None, "shard"),
            P("expert", "shard", None),
        ),
        check_vma=False,
    )
```

```python
import functools

import jax
import jax.numpy as jnp
from jax import lax
from jax.experimental import pallas as pl
from jax.experimental.pallas import tpu as pltpu
from jax.sharding import PartitionSpec as P

H = 16
DN = 128
DR = 64
DV = 128
KVR = 512
TOP = 6
EXP_DEV = 4

EPS = 1e-06
ROUTE_SCALE = 2.446
ROPE_BASE = 50000.0
SCORE_SCALE = (DN + DR) ** (-0.5)
BF = jnp.bfloat16
F32 = jnp.float32
BOTH = ("expert", "shard")
VMEM_BYTES = 56 * 1024 * 1024


def mm(a, b):
    return jnp.dot(a, b, preferred_element_type=F32)


def mm_tn(a, b):
    return lax.dot_general(a, b, (((0,), (0,)), ((), ())), preferred_element_type=F32)


def mm_nt(a, b):
    return lax.dot_general(a, b, (((1,), (1,)), ((), ())), preferred_element_type=F32)


def rope_angles(positions):
    half_width = DR // 2
    inverse = ROPE_BASE ** (-jnp.arange(half_width).astype(F32) / half_width)
    angles = positions.astype(F32)[:, None] * inverse[None, :]
    return (jnp.cos(angles), jnp.sin(angles))


def rotate(values, cosine, sine_vals):
    half_width = DR // 2
    first_half = values[..., :half_width]
    second_half = values[..., half_width:]
    return jnp.concatenate(
        [
            first_half * cosine - second_half * sine_vals,
            second_half * cosine + first_half * sine_vals,
        ],
        axis=-1,
    )


def norm_forward(values):
    factor = lax.rsqrt(jnp.mean(values * values, axis=-1, keepdims=True) + EPS)
    return values * factor, factor


def norm_backward(grad_out, gain_vec, unit_vals, factor):
    grad_unit = grad_out * gain_vec
    grad_in = factor * (
        grad_unit - unit_vals * jnp.mean(grad_unit * unit_vals, axis=-1, keepdims=True)
    )
    return (grad_in, jnp.sum(grad_out * unit_vals, axis=0))


def swish_parts(gate, up):
    sig = jax.nn.sigmoid(gate)
    silu = gate * sig
    return silu * up, up * sig * (1.0 + gate * (1.0 - sig)), silu


def exchange(values, axis):
    return lax.all_to_all(values, axis, split_axis=0, concat_axis=0, tiled=True)


class Links:
    def __init__(self):
        self.groups = lax.axis_size("expert")
        self.shards = lax.axis_size("shard")
        self.rows = self.shards // 2
        n = self.groups
        self.ring = list(range(0, n, 2)) + list(range(n - 1, 0, -2))
        shard = lax.axis_index("shard")
        self.x = shard // 2
        self.core = shard % 2
        group = lax.axis_index("expert")
        places = [self.ring.index(e) for e in range(n)]
        self.place = jnp.sum(
            jnp.where(jnp.arange(n) == group, jnp.array(places, jnp.int32), 0)
        )

    def send(self, values, target):
        pairs = []
        for e in range(self.groups):
            for s in range(self.shards):
                pairs.append((e * self.shards + s, target(e, s)))
        return lax.ppermute(values, BOTH, pairs)

    def around(self, values, step):
        n = self.groups
        return self.send(
            values,
            lambda e, s: self.ring[(self.ring.index(e) + step) % n] * self.shards + s,
        )

    def along_x(self, values, step):
        return self.send(
            values,
            lambda e, s: e * self.shards + ((s // 2 + step) % self.rows) * 2 + s % 2,
        )

    def partner(self, values):
        return self.send(values, lambda e, s: e * self.shards + (s ^ 1))

    def from_x(self, step):
        return (self.x - step) % self.rows

    def put_shard(self, own, other):
        out = jnp.zeros((self.shards,) + own[0].shape, own[0].dtype)
        zeros = (0,) * own[0].ndim
        for k in range(self.rows):
            at = self.from_x(k) * 2
            out = lax.dynamic_update_slice(out, own[k][None], (at + self.core,) + zeros)
            out = lax.dynamic_update_slice(
                out, other[k][None], (at + 1 - self.core,) + zeros
            )
        return out

    def gather_shard(self, values):
        own = [values] + [self.along_x(values, k) for k in range(1, self.rows)]
        other = [self.partner(v) for v in own]
        return self.put_shard(own, other)

    def exchange_shard(self, values):
        pairs = values.reshape((self.rows, 2) + values.shape[1:])
        take = lambda v, i, axis: lax.dynamic_index_in_dim(v, i, axis, keepdims=False)
        own, other = [], []
        for k in range(self.rows):
            got = take(pairs, (self.x + k) % self.rows, 0)
            got = got if k == 0 else self.along_x(got, k)
            own.append(take(got, self.core, 0))
            other.append(self.partner(take(got, 1 - self.core, 0)))
        return self.put_shard(own, other)

    def sum_shard(self, values):
        pairs = values.reshape((self.rows, 2) + values.shape[1:])
        take = lambda v, i, axis: lax.dynamic_index_in_dim(v, i, axis, keepdims=False)
        both = take(pairs, self.core, 1).astype(F32) + self.partner(
            take(pairs, 1 - self.core, 1)
        ).astype(F32)
        total = take(both, self.x, 0)
        for k in range(1, self.rows):
            far = take(both, (self.x + k) % self.rows, 0).astype(BF)
            total = total + self.along_x(far, k).astype(F32)
        return total

    def ring_gather(self, values, plus):
        n = self.groups
        out = [values] + [None] * (n - 1)
        ahead, back = values, values
        for r in range(1, n):
            if r <= plus:
                ahead = self.around(ahead, 1)
                out[r] = ahead
            if r <= n - 1 - plus:
                back = self.around(back, -1)
                out[n - r] = back
        return out

    def ring_reduce(self, parts, plus):
        n = self.groups
        minus = n - 1 - plus
        ahead, back = parts[plus], parts[n - minus]
        for r in range(max(plus, minus), 0, -1):
            if r <= plus:
                ahead = self.around(ahead, -1)
                if r > 1:
                    ahead = (ahead.astype(F32) + parts[r - 1].astype(F32)).astype(BF)
            if r <= minus:
                back = self.around(back, 1)
                if r > 1:
                    back = (back.astype(F32) + parts[n - r + 1].astype(F32)).astype(BF)
        return parts[0].astype(F32) + ahead.astype(F32) + back.astype(F32)

    def block(self, values, r):
        return lax.dynamic_index_in_dim(
            values, (self.place - r) % self.groups, 0, keepdims=False
        )

    def put_ring(self, blocks):
        out = jnp.zeros((self.groups,) + blocks[0].shape, blocks[0].dtype)
        zeros = (0,) * blocks[0].ndim
        for r in range(self.groups):
            at = (self.place - r) % self.groups
            out = lax.dynamic_update_slice(out, blocks[r][None], (at,) + zeros)
        return out

    def order(self):
        n, rows = self.groups, self.rows
        ring = jnp.array(self.ring, jnp.int32)
        places = (self.place - jnp.arange(n, dtype=jnp.int32)) % n
        groups = jnp.sum(
            jnp.where(places[:, None] == jnp.arange(n)[None, :], ring[None, :], 0), axis=1
        )
        xs = (self.x - jnp.arange(rows, dtype=jnp.int32)) % rows
        cores = jnp.stack([self.core, 1 - self.core]).astype(jnp.int32)
        all_of = (
            groups[:, None, None] * self.shards + xs[None, None, :] * 2 + cores[None, :, None]
        )
        return all_of.reshape(-1).astype(jnp.int32)

    def gather_all(self, values):
        n, rows = self.groups, self.rows
        tokens, width = values.shape
        half = tokens // 2
        first, second = values[:half], values[half:]
        spread = jnp.stack([first] + [self.along_x(first, k) for k in range(1, rows)])
        upper = self.ring_gather(spread, n // 2)
        lower = self.ring_gather(second, (n - 1) // 2)
        out = jnp.zeros((n, 2, rows, tokens, width), values.dtype)
        steps = [0] + [r for k in range(1, n // 2 + 1) for r in dict.fromkeys((k, n - k))]
        for r in steps:
            low = jnp.stack(
                [lower[r]] + [self.along_x(lower[r], k) for k in range(1, rows)]
            )
            own = jnp.concatenate([upper[r], low], axis=1)
            both = jnp.stack([own, self.partner(own)])[None]
            out = lax.dynamic_update_slice(out, both, (r, 0, 0, 0, 0))
        return out

    def sum_all(self, values):
        n, rows = self.groups, self.rows
        half = values.shape[3] // 2
        upper, lower = [None] * n, [None] * n
        steps = [r for k in range(n // 2, 0, -1) for r in dict.fromkeys((k, n - k))] + [0]
        for r in steps:
            both = values[r, 0].astype(F32) + self.partner(values[r, 1]).astype(F32)
            upper[r] = both[:, :half].astype(BF)
            low = both[0, half:]
            for k in range(1, rows):
                low = low + self.along_x(both[k, half:].astype(BF), -k).astype(F32)
            lower[r] = low.astype(BF)
        top = self.ring_reduce(upper, n // 2)
        bottom = self.ring_reduce(lower, (n - 1) // 2)
        total = top[0]
        for k in range(1, rows):
            total = total + self.along_x(top[k].astype(BF), -k).astype(F32)
        return jnp.concatenate([total, bottom], axis=0)


def params(**kw):
    return pltpu.CompilerParams(vmem_limit_bytes=VMEM_BYTES, **kw)


def allowed_mask(seg_col, seg_row):
    length = seg_row.shape[1]
    rows = lax.broadcasted_iota(jnp.int32, (length, length), 0)
    cols = lax.broadcasted_iota(jnp.int32, (length, length), 1)
    return (seg_col == seg_row) & (cols <= rows)


def attention_forward_kernel(
    n1_ref, wq_ref, lat_ref, we_ref, wo_ref, cos_ref, sin_ref, segc_ref, segr_ref,
    out_ref, o_ref, q_ref, kv_ref, lse_ref,
):
    width = n1_ref.shape[1]
    heads = q_ref.shape[0]
    queries = mm(n1_ref[...], wq_ref[...].reshape(width, heads * (DN + DR)))
    kv_all = mm(lat_ref[:, :KVR], we_ref[...].reshape(KVR, heads * (DN + DV)))
    kv_ref[...] = kv_all.astype(BF)
    ok = allowed_mask(segc_ref[...], segr_ref[...])
    key_rot = lat_ref[:, KVR:]
    for h in range(heads):
        at = h * (DN + DR)
        query = jnp.concatenate(
            [
                queries[:, at : at + DN],
                rotate(queries[:, at + DN : at + DN + DR], cos_ref[...], sin_ref[...]),
            ],
            axis=1,
        ).astype(BF)
        q_ref[h] = query
        at = h * (DN + DV)
        keys = kv_ref[:, at : at + DN]
        values = kv_ref[:, at + DN : at + DN + DV]
        scores = mm_nt(query[:, :DN], keys) + mm_nt(query[:, DN:], key_rot)
        scores = jnp.where(ok, scores * SCORE_SCALE, -1e30)
        top = jnp.max(scores, axis=1, keepdims=True)
        expo = jnp.exp(scores - top)
        total = jnp.sum(expo, axis=1, keepdims=True)
        lse_ref[h] = top + jnp.log(total)
        weights = (expo / total).astype(BF)
        o_ref[:, h * DV : (h + 1) * DV] = mm(weights, values).astype(BF)
    out_ref[...] = mm(o_ref[...], wo_ref[...]).astype(BF)


def attention_forward(n1, wq, latent, we, wo, cosine, sine_vals, seg_col, seg_row):
    length, width = n1.shape
    heads = wo.shape[0] // DV
    return pl.pallas_call(
        attention_forward_kernel,
        out_shape=[
            jax.ShapeDtypeStruct((length, width), BF),
            jax.ShapeDtypeStruct((length, heads * DV), BF),
            jax.ShapeDtypeStruct((heads, length, DN + DR), BF),
            jax.ShapeDtypeStruct((length, heads * (DN + DV)), BF),
            jax.ShapeDtypeStruct((heads, length, 1), F32),
        ],
        compiler_params=params(),
        name="attention_forward",
    )(n1, wq, latent, we, wo, cosine, sine_vals, seg_col, seg_row)


def attention_backward_kernel(
    dh_ref, wo_ref, o_ref, q_ref, kv_ref, lse_ref, lat_ref, we_ref, wq_ref, n1_ref,
    cos_ref, sin_ref, segc_ref, segr_ref,
    dn1_ref, dlat_ref, dwq_ref, dwe_ref, dwo_ref,
    go_ref, gq_ref, gkv_ref,
):
    width = n1_ref.shape[1]
    heads = q_ref.shape[0]
    go_ref[...] = mm_nt(dh_ref[...], wo_ref[...]).astype(BF)
    dwo_ref[...] = mm_tn(o_ref[...], dh_ref[...]).astype(BF)
    ok = allowed_mask(segc_ref[...], segr_ref[...])
    key_rot = lat_ref[:, KVR:]
    grad_kr = None
    for h in range(heads):
        at = h * (DN + DV)
        keys = kv_ref[:, at : at + DN]
        values = kv_ref[:, at + DN : at + DN + DV]
        query = q_ref[h]
        grad_o = go_ref[:, h * DV : (h + 1) * DV]
        scores = mm_nt(query[:, :DN], keys) + mm_nt(query[:, DN:], key_rot)
        weights = jnp.where(ok, jnp.exp(scores * SCORE_SCALE - lse_ref[h]), 0.0)
        grad_w = mm_nt(grad_o, values)
        delta = jnp.sum(weights * grad_w, axis=1, keepdims=True)
        grad_s = (weights * (grad_w - delta) * SCORE_SCALE).astype(BF)
        gkv_ref[:, at : at + DN] = mm_tn(grad_s, query[:, :DN]).astype(BF)
        gkv_ref[:, at + DN : at + DN + DV] = mm_tn(weights.astype(BF), grad_o).astype(BF)
        part_kr = mm_tn(grad_s, query[:, DN:])
        grad_kr = part_kr if h == 0 else grad_kr + part_kr
        at = h * (DN + DR)
        grad_qr = rotate(mm(grad_s, key_rot), cos_ref[...], -sin_ref[...])
        gq_ref[:, at : at + DN + DR] = jnp.concatenate(
            [mm(grad_s, keys), grad_qr], axis=1
        ).astype(BF)
    dwq_ref[...] = mm_tn(n1_ref[...], gq_ref[...]).astype(BF).reshape(dwq_ref.shape)
    dwe_ref[...] = mm_tn(lat_ref[:, :KVR], gkv_ref[...]).astype(BF).reshape(dwe_ref.shape)
    dn1_ref[...] = mm_nt(gq_ref[...], wq_ref[...].reshape(width, heads * (DN + DR)))
    dlat_ref[:, :KVR] = mm_nt(gkv_ref[...], we_ref[...].reshape(KVR, heads * (DN + DV)))
    dlat_ref[:, KVR:] = grad_kr


def attention_backward(
    dh, wo, o, query, kv, lse, latent, we, wq, n1, cosine, sine_vals, seg_col, seg_row
):
    length, width = n1.shape
    heads = query.shape[0]
    return pl.pallas_call(
        attention_backward_kernel,
        out_shape=[
            jax.ShapeDtypeStruct((length, width), F32),
            jax.ShapeDtypeStruct((length, KVR + DR), F32),
            jax.ShapeDtypeStruct(wq.shape, BF),
            jax.ShapeDtypeStruct(we.shape, BF),
            jax.ShapeDtypeStruct((heads * DV, width), BF),
        ],
        scratch_shapes=[
            pltpu.VMEM((length, heads * DV), BF),
            pltpu.VMEM((length, heads * (DN + DR)), BF),
            pltpu.VMEM((length, heads * (DN + DV)), BF),
        ],
        compiler_params=params(),
        name="attention_backward",
    )(dh, wo, o, query, kv, lse, latent, we, wq, n1, cosine, sine_vals, seg_col, seg_row)


STEP = 4


def pick_kernel(order_ref, pick_ref, *refs):
    out_ref = refs[STEP]
    capacity = out_ref.shape[1] // STEP
    for i in range(STEP):
        rows = mm(pick_ref[i], refs[i][0]).astype(BF)
        out_ref[:, i * capacity : (i + 1) * capacity, :] = rows.reshape(
            EXP_DEV, capacity, rows.shape[1]
        )


def pick_rows(pick, x_all, order, capacity):
    devices, slots, tokens = pick.shape
    width = x_all.shape[2]
    at = lambda i: pl.BlockSpec((1, tokens, width), lambda d, o: (o[d * STEP + i], 0, 0))
    return pl.pallas_call(
        pick_kernel,
        grid_spec=pltpu.PrefetchScalarGridSpec(
            num_scalar_prefetch=1,
            grid=(devices // STEP,),
            in_specs=[pl.BlockSpec((STEP, slots, tokens), lambda d, o: (d, 0, 0))]
            + [at(i) for i in range(STEP)],
            out_specs=pl.BlockSpec(
                (EXP_DEV, STEP * capacity, width), lambda d, o: (0, d, 0)
            ),
        ),
        out_shape=jax.ShapeDtypeStruct((EXP_DEV, devices * capacity, width), BF),
        compiler_params=params(),
        name="pick_rows",
    )(order, pick, *([x_all] * STEP))


def place_kernel(order_ref, pick_ref, rows_ref, left_ref, right_ref, out_ref):
    step, slots = pick_ref.shape[0], pick_ref.shape[1]
    capacity = rows_ref.shape[1] // step
    for i in range(step):
        rows = rows_ref[:, i * capacity : (i + 1) * capacity, :]
        rows = rows.reshape(slots, rows.shape[2])
        total = mm_tn(pick_ref[i], rows) + mm(left_ref[i], right_ref[...])
        out_ref[i] = total.astype(BF)


def place_rows(pick, rows, left, right, order, capacity, step):
    devices, slots, tokens = pick.shape
    width = rows.shape[2]
    inner = left.shape[2]
    where = (lambda d, o: (d, 0, 0)) if step > 1 else (lambda d, o: (o[d], 0, 0))
    return pl.pallas_call(
        place_kernel,
        grid_spec=pltpu.PrefetchScalarGridSpec(
            num_scalar_prefetch=1,
            grid=(devices // step,),
            in_specs=[
                pl.BlockSpec((step, slots, tokens), lambda d, o: (d, 0, 0)),
                pl.BlockSpec((EXP_DEV, step * capacity, width), lambda d, o: (0, d, 0)),
                pl.BlockSpec((step, tokens, inner), lambda d, o: (d, 0, 0)),
                pl.BlockSpec((inner, width), lambda d, o: (0, 0)),
            ],
            out_specs=pl.BlockSpec((step, tokens, width), where),
        ),
        out_shape=jax.ShapeDtypeStruct((devices, tokens, width), BF),
        compiler_params=params(),
        name="place_rows",
    )(order, pick, rows, left, right)


def body(
    hidden,
    cotangent,
    segments,
    routes,
    w_query,
    w_latent,
    g_latent,
    w_expand,
    w_out,
    g_attn,
    g_ffn,
    w_router,
    s_gate,
    s_up,
    s_down,
    e_gate,
    expert_up_weight,
    e_down,
):
    tokens = hidden.shape[1]
    width = hidden.shape[2]
    links = Links()
    shards, groups = links.shards, links.groups
    devices = groups * shards
    experts = EXP_DEV * groups
    capacity = max(2, tokens * TOP * 4 // (3 * experts))
    heads = H // shards
    length = tokens * shards
    part = width // shards
    my_shard = lax.axis_index("shard")
    my_group = lax.axis_index("expert")
    hid_shard = s_down.shape[0]
    hid = hid_shard // groups
    latent_part = KVR // shards

    g_all = lax.all_gather(cotangent[0], BOTH, axis=0, tiled=False)
    router_rows = part * experts // width
    small_rows = jnp.concatenate([g_attn, g_ffn, g_latent])
    small_rows = jnp.pad(small_rows, (0, -small_rows.shape[0] % width)).reshape(-1, width)
    packed = jnp.concatenate([hidden[0], w_router.reshape(router_rows, width), small_rows])
    packed = jnp.pad(packed, ((0, -packed.shape[0] % 16), (0, 0)))
    packed = links.gather_shard(packed)
    full_latent = links.gather_shard(w_latent).reshape(width, KVR + DR)
    wq = links.exchange_shard(
        w_query.reshape(part, shards, heads * (DN + DR)).transpose(1, 0, 2)
    )
    we = links.exchange_shard(
        w_expand.reshape(latent_part, shards, heads * (DN + DV)).transpose(1, 0, 2)
    )
    hidden_all = packed[:, :tokens].reshape(length, width)
    full_router = packed[:, tokens : tokens + router_rows].reshape(width, experts)
    gains_in = packed[:, tokens + router_rows :].reshape(shards, -1)
    gattn = gains_in[:, :part].reshape(width).astype(F32)
    gffn = gains_in[:, part : 2 * part].reshape(width).astype(F32)
    glatent = gains_in[:, 2 * part : 2 * part + latent_part].reshape(KVR).astype(F32)

    mine = lambda w: lax.dynamic_slice_in_dim(
        w.reshape(part, shards, hid_shard), my_group * hid, hid, 2
    )
    gate_up = jnp.concatenate([mine(s_gate), mine(s_up)], axis=2).transpose(1, 0, 2)
    shared_in = links.exchange_shard(gate_up).reshape(width, 2 * hid)
    shared_down = lax.dynamic_slice_in_dim(s_down, my_group * hid, hid, 0)

    order = links.order()
    same = jnp.arange(devices, dtype=jnp.int32)
    back_order = jnp.sum(
        jnp.where(order[:, None] == same[None, :], same[:, None], 0), axis=0
    ).astype(jnp.int32)
    local_routes = routes[0]
    flat_routes = local_routes.reshape(-1)
    choose = local_routes[:, :, None] == jnp.arange(experts, dtype=jnp.int32)[None, None, :]
    hits = choose.reshape(-1, experts).astype(F32)
    pair_count = tokens * TOP
    before_it = (
        lax.broadcasted_iota(jnp.int32, (pair_count, pair_count), 1)
        < lax.broadcasted_iota(jnp.int32, (pair_count, pair_count), 0)
    ).astype(BF)
    before = mm(before_it, hits.astype(BF))
    slot_rank = jnp.sum(before * hits, axis=1).astype(jnp.int32)
    slot_of = (flat_routes * capacity + slot_rank).reshape(tokens, TOP)
    slots = EXP_DEV * capacity
    slot_rows = jnp.pad(slot_of.T, ((0, 8 - TOP), (0, 0)), constant_values=-1)
    slots_all = exchange(jnp.broadcast_to(slot_rows[None], (devices, 8, tokens)), BOTH)
    slots_all = jnp.take(slots_all, order, axis=0)[:, :TOP]
    slot_ids = my_group * slots + jnp.arange(slots, dtype=jnp.int32)
    pick = jnp.any(
        slots_all[:, None] == slot_ids[None, :, None, None], axis=2
    ).astype(BF)

    residual_all = hidden_all.astype(F32)
    unit_all, _ = norm_forward(residual_all)
    n1 = (unit_all * gattn).astype(BF)
    cosine, sine_vals = rope_angles(jnp.arange(length, dtype=jnp.int32))
    compressed = mm(n1, full_latent)
    latent_unit, latent_factor = norm_forward(compressed[:, :KVR])
    latent = jnp.concatenate(
        [latent_unit * glatent, rotate(compressed[:, KVR:], cosine, sine_vals)], axis=1
    ).astype(BF)
    seg_row = segments
    seg_col = segments.reshape(length, 1)
    attn_part, attended, query, kv, lse = attention_forward(
        n1, wq, latent, we, w_out, cosine, sine_vals, seg_col, seg_row
    )
    attn_out = links.sum_shard(attn_part.reshape(shards, tokens, width))
    residual_in = hidden[0].astype(F32)
    residual_mid = residual_in + attn_out
    unit_two, factor_two = norm_forward(residual_mid)
    normed_two = (unit_two * gffn).astype(BF)

    n2_all = links.gather_all(normed_two).reshape(devices, tokens, width)
    probs = jax.nn.sigmoid(mm(normed_two, full_router))
    chosen = jnp.sum(jnp.where(choose, probs[:, None, :], 0.0), axis=-1)
    chosen_total = jnp.sum(chosen, axis=1, keepdims=True)

    grad_rows = pick_rows(pick, g_all, order, capacity)
    grad_inner = jnp.einsum("jmd,jfd->jmf", grad_rows, e_down, preferred_element_type=F32)
    shared_grad_inner = mm_nt(g_all.reshape(-1, width), shared_down)
    shared_grad_inner = jnp.take(
        shared_grad_inner.reshape(devices, tokens, hid), order, axis=0
    ).reshape(-1, hid)

    shared_pre = mm(
        n2_all.reshape(-1, width), jnp.concatenate([shared_in, full_router], axis=1)
    )
    probs_all = jax.nn.sigmoid(
        shared_pre[:, 2 * hid :].reshape(devices, tokens, experts).transpose(0, 2, 1)
    )
    named = jnp.any(
        (slots_all // capacity)[:, None]
        == jnp.arange(experts, dtype=jnp.int32)[None, :, None, None],
        axis=2,
    )
    totals = jnp.sum(jnp.where(named, probs_all, 0.0), axis=1, keepdims=True)
    local_probs = lax.dynamic_slice_in_dim(probs_all, my_group * EXP_DEV, EXP_DEV, 1)
    local_weights = local_probs / totals * ROUTE_SCALE
    slot_weight = jnp.sum(
        jnp.where(
            pick.reshape(devices, EXP_DEV, capacity, tokens) > 0,
            local_weights[:, :, None, :],
            0.0,
        ),
        axis=3,
    )
    row_weight = slot_weight.transpose(1, 0, 2).reshape(EXP_DEV, devices * capacity, 1)

    rows = pick_rows(pick, n2_all, same, capacity)
    gate = jnp.einsum("jmd,jdf->jmf", rows, e_gate, preferred_element_type=F32)
    up = jnp.einsum("jmd,jdf->jmf", rows, expert_up_weight, preferred_element_type=F32)
    inner, slope_gate, slope_up = swish_parts(gate, up)
    weighted_grad = row_weight * grad_inner
    grad_gate_b = (weighted_grad * slope_gate).astype(BF)
    grad_up_b = (weighted_grad * slope_up).astype(BF)
    inner_w = (row_weight * inner).astype(BF)
    grad_slot_weight = jnp.sum(inner.astype(BF).astype(F32) * grad_inner, axis=2)

    s_inner, s_slope_gate, s_slope_up = swish_parts(
        shared_pre[:, :hid], shared_pre[:, hid : 2 * hid]
    )
    shared_inner = s_inner.astype(BF)
    shared_grads = jnp.concatenate(
        [shared_grad_inner * s_slope_gate, shared_grad_inner * s_slope_up], axis=1
    ).astype(BF)

    dz = (
        jnp.einsum("jmf,jdf->jmd", grad_gate_b, e_gate, preferred_element_type=F32)
        + jnp.einsum("jmf,jdf->jmd", grad_up_b, expert_up_weight, preferred_element_type=F32)
    ).astype(BF)
    dn2_part = place_rows(
        pick, dz, shared_grads.reshape(devices, tokens, 2 * hid), shared_in.T, same,
        capacity, STEP,
    )
    dn2 = links.sum_all(dn2_part.reshape(groups, 2, shards // 2, tokens, width))
    weighted_out = jnp.einsum(
        "jmf,jfd->jmd", inner_w, e_down, preferred_element_type=F32
    ).astype(BF)
    out_part = place_rows(
        pick, weighted_out, shared_inner.reshape(devices, tokens, hid), shared_down, order,
        capacity, 1,
    )
    routed_shared = lax.psum_scatter(
        out_part, BOTH, scatter_dimension=0, tiled=False
    ).astype(F32)
    output_rows = residual_mid + routed_shared

    d_edown = jnp.einsum("jmf,jmd->jfd", inner_w, grad_rows, preferred_element_type=F32)
    d_egate = jnp.einsum("jmd,jmf->jdf", rows, grad_gate_b, preferred_element_type=F32)
    grad_expert_up = jnp.einsum("jmd,jmf->jdf", rows, grad_up_b, preferred_element_type=F32)

    slot_back = grad_slot_weight.reshape(EXP_DEV, devices, capacity).transpose(1, 0, 2)
    slot_back = jnp.take(slot_back.reshape(devices, slots), back_order, axis=0)
    got = exchange(slot_back, BOTH)
    slot_grads = jnp.sum(got.reshape(groups, shards, slots), axis=1).reshape(-1)
    at_slot = slot_of[:, :, None] == jnp.arange(experts * capacity, dtype=jnp.int32)
    grad_weights = jnp.sum(jnp.where(at_slot, slot_grads, 0.0), axis=2)
    grad_chosen = ROUTE_SCALE * (
        grad_weights / chosen_total
        - jnp.sum(grad_weights * chosen, axis=1, keepdims=True) / (chosen_total * chosen_total)
    )
    grad_probs = jnp.sum(jnp.where(choose, grad_chosen[:, :, None], 0.0), axis=1)
    grad_logits = (grad_probs * probs * (1.0 - probs)).astype(BF)
    logits_back = exchange(
        jnp.broadcast_to(grad_logits.T[None], (devices, experts, tokens)), BOTH
    )
    logits_back = jnp.take(logits_back, order, axis=0)
    own_columns = lax.dynamic_slice_in_dim(n2_all, my_shard * part, part, 2)
    d_router = mm(
        logits_back.transpose(1, 0, 2).reshape(experts, -1), own_columns.reshape(-1, part)
    ).T

    d_shared_in = mm_tn(shared_grads, n2_all.reshape(-1, width)).astype(BF)
    shared_inner_back = jnp.take(
        shared_inner.reshape(devices, tokens, hid), back_order, axis=0
    ).reshape(-1, hid)
    d_shared_down = mm_tn(shared_inner_back, g_all.reshape(-1, width)).astype(BF)
    in_pieces = links.exchange_shard(
        d_shared_in.reshape(2 * hid, shards, part).transpose(1, 0, 2)
    )
    in_all = lax.all_gather(in_pieces, "expert", axis=0, tiled=False)
    in_all = in_all.reshape(groups, shards, 2, hid, part).astype(F32)
    in_all = in_all.transpose(2, 1, 0, 3, 4).reshape(2, shards * groups * hid, part)
    part_sgate = in_all[0].T
    part_sup = in_all[1].T
    part_sdown = lax.all_gather(d_shared_down, "expert", axis=0, tiled=True).astype(F32)

    grad_normed_two = dn2 + mm_nt(grad_logits, full_router)
    grad_mid_norm, d_gffn = norm_backward(grad_normed_two, gffn, unit_two, factor_two)
    grad_mid = cotangent[0].astype(F32) + grad_mid_norm
    grad_attn = links.gather_shard(grad_mid.astype(BF)).reshape(length, width)

    dn1_heads, dlat, dwq, dwe, d_out = attention_backward(
        grad_attn, w_out, attended, query, kv, lse, latent, we, wq, n1,
        cosine, sine_vals, seg_col, seg_row,
    )
    grad_comp_norm, d_glatent = norm_backward(dlat[:, :KVR], glatent, latent_unit, latent_factor)
    grad_compressed = jnp.concatenate(
        [grad_comp_norm, rotate(dlat[:, KVR:], cosine, -sine_vals)], axis=1
    ).astype(BF)
    grad_normed = links.sum_shard(
        (dn1_heads + mm_nt(grad_compressed, full_latent)).astype(BF).reshape(
            shards, tokens, width
        )
    )
    unit_one, factor_one = norm_forward(residual_in)
    grad_input_norm, d_gattn = norm_backward(grad_normed, gattn, unit_one, factor_one)
    grad_input = grad_mid + grad_input_norm

    rows_latent = links.sum_shard(
        mm_tn(n1, grad_compressed).astype(BF).reshape(shards, part, KVR + DR)
    ).astype(BF)
    cut = part // groups
    cut_latent = latent_part // groups
    by_heads = jnp.concatenate(
        [
            dwq.reshape(shards, groups, cut, -1),
            dwe.reshape(shards, groups, cut_latent, cut // cut_latent, -1)
            .transpose(0, 1, 3, 2, 4)
            .reshape(shards, groups, cut, -1),
        ],
        axis=3,
    ).transpose(1, 0, 2, 3)
    by_rows = jnp.concatenate(
        [d_out.reshape(groups, cut, width), rows_latent.reshape(groups, cut, KVR + DR)], axis=2
    )
    slots_r = range(groups)
    sum_heads = links.ring_reduce([links.block(by_heads, r) for r in slots_r], groups // 2)
    sum_rows = links.ring_reduce([links.block(by_rows, r) for r in slots_r], (groups - 1) // 2)
    sum_heads = links.exchange_shard(sum_heads.astype(BF))
    all_heads = links.put_ring(links.ring_gather(sum_heads, groups // 2))
    all_rows = links.put_ring(links.ring_gather(sum_rows.astype(BF), (groups - 1) // 2))
    query_wide = heads * (DN + DR)
    part_query = (
        all_heads[..., :query_wide].transpose(0, 2, 1, 3).reshape(part, H * (DN + DR))
    ).astype(F32)
    part_expand = (
        all_heads[..., query_wide:]
        .reshape(groups, shards, cut // cut_latent, cut_latent, -1)
        .transpose(0, 3, 1, 2, 4)
        .reshape(latent_part, H * (DN + DV))
    ).astype(F32)
    all_rows = all_rows.reshape(part, width + KVR + DR).astype(F32)

    gain_grads = jnp.concatenate(
        [
            d_gattn.reshape(shards, part),
            d_gffn.reshape(shards, part),
            d_glatent.reshape(shards, latent_part),
        ],
        axis=1,
    )
    got = exchange(
        jnp.broadcast_to(gain_grads[None], (groups,) + gain_grads.shape).reshape(devices, -1),
        BOTH,
    )
    gains = jnp.sum(got, axis=0)
    return (
        output_rows.astype(BF)[None],
        grad_input[None],
        part_query,
        all_rows[:, width:],
        gains[2 * part :],
        part_expand,
        all_rows[:, :width],
        gains[:part],
        gains[part : 2 * part],
        d_router,
        part_sgate,
        part_sup,
        part_sdown,
        d_egate,
        grad_expert_up,
        d_edown,
    )


def solution(mesh):
    return jax.shard_map(
        body,
        mesh=mesh,
        in_specs=(
            P("expert", "shard", None),
            P("expert", "shard", None),
            P("expert", None),
            P("expert", "shard", None),
            P("shard", None),
            P("shard", None),
            P("shard"),
            P("shard", None),
            P("shard", None),
            P("shard"),
            P("shard"),
            P("shard", None),
            P("shard", None),
            P("shard", None),
            P("shard", None),
            P("expert", None, "shard"),
            P("expert", None, "shard"),
            P("expert", "shard", None),
        ),
        out_specs=(
            P("expert", "shard", None),
            P("expert", "shard", None),
            P("shard", None),
            P("shard", None),
            P("shard"),
            P("shard", None),
            P("shard", None),
            P("shard"),
            P("shard"),
            P("shard", None),
            P("shard", None),
            P("shard", None),
            P("shard", None),
            P("expert", None, "shard"),
            P("expert", None, "shard"),
            P("expert", "shard", None),
        ),
        check_vma=False,
    )
```

```python
import functools

import jax
import jax.numpy as jnp
from jax import lax
from jax.experimental import pallas as pl
from jax.experimental.pallas import tpu as pltpu
from jax.sharding import PartitionSpec as P

H = 16
DN = 128
DR = 64
DV = 128
KVR = 512
TOP = 6
EXP_DEV = 4

EPS = 1e-06
ROUTE_SCALE = 2.446
ROPE_BASE = 50000.0
SCORE_SCALE = (DN + DR) ** (-0.5)
BF = jnp.bfloat16
F32 = jnp.float32
BOTH = ("expert", "shard")
VMEM_BYTES = 56 * 1024 * 1024


def mm(a, b):
    return jnp.dot(a, b, preferred_element_type=F32)


def mm_tn(a, b):
    return lax.dot_general(a, b, (((0,), (0,)), ((), ())), preferred_element_type=F32)


def mm_nt(a, b):
    return lax.dot_general(a, b, (((1,), (1,)), ((), ())), preferred_element_type=F32)


def rope_angles(positions):
    half_width = DR // 2
    inverse = ROPE_BASE ** (-jnp.arange(half_width).astype(F32) / half_width)
    angles = positions.astype(F32)[:, None] * inverse[None, :]
    return (jnp.cos(angles), jnp.sin(angles))


def rotate(values, cosine, sine_vals):
    half_width = DR // 2
    first_half = values[..., :half_width]
    second_half = values[..., half_width:]
    return jnp.concatenate(
        [
            first_half * cosine - second_half * sine_vals,
            second_half * cosine + first_half * sine_vals,
        ],
        axis=-1,
    )


def norm_forward(values):
    factor = lax.rsqrt(jnp.mean(values * values, axis=-1, keepdims=True) + EPS)
    return values * factor, factor


def norm_backward(grad_out, gain_vec, unit_vals, factor):
    grad_unit = grad_out * gain_vec
    grad_in = factor * (
        grad_unit - unit_vals * jnp.mean(grad_unit * unit_vals, axis=-1, keepdims=True)
    )
    return (grad_in, jnp.sum(grad_out * unit_vals, axis=0))


def swish_parts(gate, up):
    sig = jax.nn.sigmoid(gate)
    silu = gate * sig
    return silu * up, up * sig * (1.0 + gate * (1.0 - sig)), silu


def exchange(values, axis):
    return lax.all_to_all(values, axis, split_axis=0, concat_axis=0, tiled=True)


def tie(streams, extra):
    return lax.optimization_barrier((streams, extra))


class Fill:
    def __init__(self, work, *inputs):
        self.work, self.inputs, self.result = work, inputs, None


class Links:
    def __init__(self):
        self.groups = lax.axis_size("expert")
        self.shards = lax.axis_size("shard")
        self.rows = self.shards // 2
        n = self.groups
        self.ring = list(range(0, n, 2)) + list(range(n - 1, 0, -2))
        shard = lax.axis_index("shard")
        self.x = shard // 2
        self.core = shard % 2
        group = lax.axis_index("expert")
        places = [self.ring.index(e) for e in range(n)]
        self.place = jnp.sum(
            jnp.where(jnp.arange(n) == group, jnp.array(places, jnp.int32), 0)
        )

    def send(self, values, target):
        pairs = []
        for e in range(self.groups):
            for s in range(self.shards):
                pairs.append((e * self.shards + s, target(e, s)))
        return lax.ppermute(values, BOTH, pairs)

    def around(self, values, step):
        n = self.groups
        return self.send(
            values,
            lambda e, s: self.ring[(self.ring.index(e) + step) % n] * self.shards + s,
        )

    def along_x(self, values, step):
        return self.send(
            values,
            lambda e, s: e * self.shards + ((s // 2 + step) % self.rows) * 2 + s % 2,
        )

    def partner(self, values):
        return self.send(values, lambda e, s: e * self.shards + (s ^ 1))

    def shard_at(self):
        xs = (self.x - jnp.arange(self.rows, dtype=jnp.int32)) % self.rows
        cores = jnp.stack([self.core, 1 - self.core]).astype(jnp.int32)
        return (xs[:, None] * 2 + cores[None, :]).reshape(-1).astype(jnp.int32)

    def slot_at(self):
        shard = jnp.arange(self.shards, dtype=jnp.int32)
        back = (self.x - shard // 2) % self.rows
        return (back * 2 + (shard % 2 != self.core)).astype(jnp.int32)

    def gather_shard(self, values):
        out = []
        for k in range(self.rows):
            own = values if k == 0 else self.along_x(values, k)
            out += [own, self.partner(own)]
        return jnp.stack(out)

    def spread_shard(self, pieces):
        take = lambda v, i: lax.dynamic_index_in_dim(v, i, 0, keepdims=False)
        pairs = pieces.reshape((self.rows, 2) + pieces.shape[1:])
        out = []
        for k in range(self.rows):
            got = take(pairs, (self.x + k) % self.rows)
            got = got if k == 0 else self.along_x(got, k)
            out += [take(got, self.core), self.partner(take(got, 1 - self.core))]
        return jnp.stack(out)

    def exchange_shard(self, values):
        pairs = values.reshape((self.rows, 2) + values.shape[1:])
        out = []
        for k in range(self.rows):
            got = pairs[k] if k == 0 else self.along_x(pairs[k], -k)
            out += [got[0], self.partner(got[1])]
        xs = (self.x + jnp.arange(self.rows, dtype=jnp.int32)) % self.rows
        shard = jnp.arange(self.shards, dtype=jnp.int32)
        ahead = (shard // 2 - self.x) % self.rows
        slot = ahead * 2 + (shard % 2 != self.core)
        return jnp.take(jnp.stack(out), slot, axis=0)

    def sum_shard(self, values):
        pairs = values.reshape((self.rows, 2) + values.shape[1:])
        total = None
        for k in range(self.rows):
            both = pairs[k, 0].astype(F32) + self.partner(pairs[k, 1]).astype(F32)
            if k > 0:
                both = self.along_x(both.astype(BF), -k).astype(F32)
            total = both if total is None else total + both
        return total

    def ring_gather(self, values, pluses, fills=()):
        n = self.groups
        fills = dict(fills)
        outs = [[v] + [None] * (n - 1) for v in values]
        ahead, back = list(values), list(values)
        for r in range(1, n):
            moves = [(i, 1) for i, p in enumerate(pluses) if r <= p]
            moves += [(i, -1) for i, p in enumerate(pluses) if r <= n - 1 - p]
            if not moves:
                break
            streams = [ahead[i] if step > 0 else back[i] for i, step in moves]
            streams = self.step(streams, [step for _, step in moves], fills.get(r))
            for (i, step), got in zip(moves, streams):
                if step > 0:
                    ahead[i] = outs[i][r] = got
                else:
                    back[i] = outs[i][n - r] = got
        return outs

    def step(self, streams, steps, fill):
        if fill is None:
            return [self.around(v, s) for v, s in zip(streams, steps)]
        streams, inputs = tie(streams, fill.inputs)
        streams = [self.around(v, s) for v, s in zip(streams, steps)]
        streams, fill.result = tie(streams, fill.work(*inputs))
        return streams

    def ring_reduce(self, parts, pluses, fills=()):
        n = self.groups
        fills = dict(fills)
        ahead = [p[plus] for p, plus in zip(parts, pluses)]
        back = [p[plus + 1] for p, plus in zip(parts, pluses)]
        most = max(max(p, n - 1 - p) for p in pluses)
        for r in range(most, 0, -1):
            moves = [(i, 1) for i, p in enumerate(pluses) if r <= p]
            moves += [(i, -1) for i, p in enumerate(pluses) if r <= n - 1 - p]
            streams = [ahead[i] if step > 0 else back[i] for i, step in moves]
            streams = self.step(streams, [-step for _, step in moves], fills.get(r))
            for (i, step), got in zip(moves, streams):
                here = parts[i][r - 1 if step > 0 else (n - r + 1) % n]
                if r > 1:
                    got = (got.astype(F32) + here.astype(F32)).astype(BF)
                if step > 0:
                    ahead[i] = got
                else:
                    back[i] = got
        return [
            p[0].astype(F32) + a.astype(F32) + b.astype(F32)
            for p, a, b in zip(parts, ahead, back)
        ]

    def block_at(self):
        return (self.place - jnp.arange(self.groups, dtype=jnp.int32)) % self.groups

    def blocks(self, values):
        return [
            lax.dynamic_index_in_dim(
                values, (self.place - r) % self.groups, 0, keepdims=False
            )
            for r in range(self.groups)
        ]

    def order(self):
        n = self.groups
        ring = jnp.array(self.ring, jnp.int32)
        groups = jnp.sum(
            jnp.where(self.block_at()[:, None] == jnp.arange(n)[None, :], ring[None, :], 0),
            axis=1,
        )
        all_of = groups[:, None] * self.shards + self.shard_at()[None, :]
        return all_of.reshape(-1).astype(jnp.int32)

    def gather_all(self, values, fills=()):
        n, rows = self.groups, self.rows
        tokens, width = values.shape
        half = tokens // 2
        first, second = values[:half], values[half:]
        spread = jnp.stack([first] + [self.along_x(first, k) for k in range(1, rows)])
        upper, lower = self.ring_gather(
            [spread, second], [n // 2, (n - 1) // 2], fills
        )
        out = jnp.zeros((n, rows, 2, tokens, width), values.dtype)
        steps = [0] + [r for k in range(1, n // 2 + 1) for r in dict.fromkeys((k, n - k))]
        for r in steps:
            low = jnp.stack(
                [lower[r]] + [self.along_x(lower[r], k) for k in range(1, rows)]
            )
            own = jnp.concatenate([upper[r], low], axis=1)
            both = jnp.stack([own, self.partner(own)], axis=1)[None]
            out = lax.dynamic_update_slice(out, both, (r, 0, 0, 0, 0))
        return out

    def sum_all(self, values, fills=()):
        n, rows = self.groups, self.rows
        half = values.shape[3] // 2
        upper, lower = [None] * n, [None] * n
        steps = [r for k in range(n // 2, 0, -1) for r in dict.fromkeys((k, n - k))] + [0]
        for r in steps:
            both = values[r, :, 0].astype(F32) + self.partner(values[r, :, 1]).astype(F32)
            upper[r] = both[:, :half].astype(BF)
            low = both[0, half:]
            for k in range(1, rows):
                low = low + self.along_x(both[k, half:].astype(BF), -k).astype(F32)
            lower[r] = low.astype(BF)
        top, bottom = self.ring_reduce([upper, lower], [n // 2, (n - 1) // 2], fills)
        total = top[0]
        for k in range(1, rows):
            total = total + self.along_x(top[k].astype(BF), -k).astype(F32)
        return jnp.concatenate([total, bottom], axis=0)


def params(**kw):
    return pltpu.CompilerParams(vmem_limit_bytes=VMEM_BYTES, **kw)


SMEM = pl.BlockSpec(memory_space=pltpu.SMEM)
VMEM = pl.BlockSpec(memory_space=pltpu.VMEM)


def allowed_mask(seg_col, seg_row, pos_col, pos_row):
    return (seg_col == seg_row) & (pos_row <= pos_col)


def attention_forward_kernel(
    slot_ref, x_ref, gattn_ref, glat_ref, wq_ref, wl_ref, we_ref, wo_ref,
    cos_ref, sin_ref, col_ref, row_ref,
    out_ref, n1_ref, c_ref, lat_ref, o_ref, q_ref, kv_ref, lse_ref,
):
    shards, part = wq_ref.shape[0], wq_ref.shape[1]
    heads = q_ref.shape[0]
    tokens = x_ref.shape[0] // shards
    for b in range(shards):
        at = slice(b * tokens, (b + 1) * tokens)
        unit, _ = norm_forward(x_ref[at].astype(F32))
        n1_ref[at] = (unit * gattn_ref[...]).astype(BF)
    queries, compressed, kv_all = None, None, None
    for s in range(shards):
        left = n1_ref[:, s * part : (s + 1) * part]
        one = mm(left, wq_ref[slot_ref[s]])
        queries = one if s == 0 else queries + one
        one = mm_nt(left, wl_ref[slot_ref[s]])
        compressed = one if s == 0 else compressed + one
    c_ref[...] = compressed
    unit, _ = norm_forward(compressed[:, :KVR])
    lat_ref[:, :KVR] = (unit * glat_ref[...]).astype(BF)
    lat_ref[:, KVR:] = rotate(compressed[:, KVR:], cos_ref[...], sin_ref[...]).astype(BF)
    part = KVR // shards
    for s in range(shards):
        one = mm(lat_ref[:, s * part : (s + 1) * part], we_ref[slot_ref[s]])
        kv_all = one if s == 0 else kv_all + one
    kv_ref[...] = kv_all.astype(BF)
    ok = allowed_mask(
        col_ref[:, :1], row_ref[:1, :], col_ref[:, 1:2], row_ref[1:2, :]
    )
    key_rot = lat_ref[:, KVR:]
    for h in range(heads):
        at = h * (DN + DR)
        query = jnp.concatenate(
            [
                queries[:, at : at + DN],
                rotate(queries[:, at + DN : at + DN + DR], cos_ref[...], sin_ref[...]),
            ],
            axis=1,
        ).astype(BF)
        q_ref[h] = query
        at = h * (DN + DV)
        keys = kv_ref[:, at : at + DN]
        values = kv_ref[:, at + DN : at + DN + DV]
        scores = mm_nt(query[:, :DN], keys) + mm_nt(query[:, DN:], key_rot)
        scores = jnp.where(ok, scores * SCORE_SCALE, -1e30)
        top = jnp.max(scores, axis=1, keepdims=True)
        expo = jnp.exp(scores - top)
        total = jnp.sum(expo, axis=1, keepdims=True)
        lse_ref[h] = top + jnp.log(total)
        weights = (expo / total).astype(BF)
        o_ref[:, h * DV : (h + 1) * DV] = mm(weights, values).astype(BF)
    out_ref[...] = mm(o_ref[...], wo_ref[...]).astype(BF)


def attention_forward(slot, x, gattn, glat, wq, wl, we, wo, cosine, sine_vals, col, row):
    length, width = x.shape
    heads = wo.shape[0] // DV
    return pl.pallas_call(
        attention_forward_kernel,
        in_specs=[SMEM] + [VMEM] * 11,
        out_shape=[
            jax.ShapeDtypeStruct((length, width), BF),
            jax.ShapeDtypeStruct((length, width), BF),
            jax.ShapeDtypeStruct((length, KVR + DR), F32),
            jax.ShapeDtypeStruct((length, KVR + DR), BF),
            jax.ShapeDtypeStruct((length, heads * DV), BF),
            jax.ShapeDtypeStruct((heads, length, DN + DR), BF),
            jax.ShapeDtypeStruct((length, heads * (DN + DV)), BF),
            jax.ShapeDtypeStruct((heads, length, 1), F32),
        ],
        compiler_params=params(),
        name="attention_forward",
    )(slot, x, gattn, glat, wq, wl, we, wo, cosine, sine_vals, col, row)


def attention_backward_kernel(
    slot_ref, dh_ref, glat_ref, wo_ref, o_ref, q_ref, kv_ref, lse_ref, lat_ref, c_ref,
    we_ref, wl_ref, wq_ref, n1_ref, cos_ref, sin_ref, col_ref, row_ref,
    dn1_ref, dw_ref, dwl_ref, dwo_ref, dgl_ref,
    go_ref, gq_ref, gkv_ref, gc_ref,
):
    shards, part = wq_ref.shape[0], wq_ref.shape[1]
    heads = q_ref.shape[0]
    go_ref[...] = mm_nt(dh_ref[...], wo_ref[...]).astype(BF)
    dwo_ref[...] = mm_tn(o_ref[...], dh_ref[...]).astype(BF)
    ok = allowed_mask(
        col_ref[:, :1], row_ref[:1, :], col_ref[:, 1:2], row_ref[1:2, :]
    )
    key_rot = lat_ref[:, KVR:]
    grad_kr = None
    for h in range(heads):
        at = h * (DN + DV)
        keys = kv_ref[:, at : at + DN]
        values = kv_ref[:, at + DN : at + DN + DV]
        query = q_ref[h]
        grad_o = go_ref[:, h * DV : (h + 1) * DV]
        scores = mm_nt(query[:, :DN], keys) + mm_nt(query[:, DN:], key_rot)
        weights = jnp.where(ok, jnp.exp(scores * SCORE_SCALE - lse_ref[h]), 0.0)
        grad_w = mm_nt(grad_o, values)
        delta = jnp.sum(weights * grad_w, axis=1, keepdims=True)
        grad_s = (weights * (grad_w - delta) * SCORE_SCALE).astype(BF)
        gkv_ref[:, at : at + DN] = mm_tn(grad_s, query[:, :DN]).astype(BF)
        gkv_ref[:, at + DN : at + DN + DV] = mm_tn(weights.astype(BF), grad_o).astype(BF)
        one = mm_tn(grad_s, query[:, DN:])
        grad_kr = one if h == 0 else grad_kr + one
        at = h * (DN + DR)
        grad_qr = rotate(mm(grad_s, key_rot), cos_ref[...], -sin_ref[...])
        gq_ref[:, at : at + DN + DR] = jnp.concatenate(
            [mm(grad_s, keys), grad_qr], axis=1
        ).astype(BF)
    latent_part = KVR // shards
    query_wide = heads * (DN + DR)
    ratio = part // latent_part
    piece = heads * (DN + DV) // ratio
    grad_lat = []
    for s in range(shards):
        at = slice(s * latent_part, (s + 1) * latent_part)
        grad_lat.append(mm_nt(gkv_ref[...], we_ref[slot_ref[s]]))
        one = mm_tn(lat_ref[:, at], gkv_ref[...]).astype(BF)
        for i in range(ratio):
            dw_ref[slot_ref[s], i * latent_part : (i + 1) * latent_part, query_wide:] = one[
                :, i * piece : (i + 1) * piece
            ]
    grad_lat = jnp.concatenate(grad_lat, axis=1)
    unit, factor = norm_forward(c_ref[:, :KVR])
    grad_norm, grad_gain = norm_backward(grad_lat, glat_ref[...], unit, factor)
    dgl_ref[...] = grad_gain.reshape(1, KVR)
    gc_ref[:, :KVR] = grad_norm.astype(BF)
    gc_ref[:, KVR:] = rotate(grad_kr, cos_ref[...], -sin_ref[...]).astype(BF)
    for s in range(shards):
        at = slice(s * part, (s + 1) * part)
        dn1_ref[:, at] = (
            mm_nt(gq_ref[...], wq_ref[slot_ref[s]]) + mm(gc_ref[...], wl_ref[slot_ref[s]])
        ).astype(BF)
        dw_ref[slot_ref[s], :, :query_wide] = mm_tn(n1_ref[:, at], gq_ref[...]).astype(BF)
        dwl_ref[slot_ref[s]] = mm_tn(gc_ref[...], n1_ref[:, at]).astype(BF)


def attention_backward(
    slot, dh, glat, wo, o, query, kv, lse, latent, compressed, we, wl, wq, n1,
    cosine, sine_vals, col, row,
):
    length, width = n1.shape
    heads = query.shape[0]
    shards, part = wq.shape[0], wq.shape[1]
    wide = heads * (DN + DR) + heads * (DN + DV) * KVR // width
    return pl.pallas_call(
        attention_backward_kernel,
        in_specs=[SMEM] + [VMEM] * 17,
        out_shape=[
            jax.ShapeDtypeStruct((length, width), BF),
            jax.ShapeDtypeStruct((shards, part, wide), BF),
            jax.ShapeDtypeStruct(wl.shape, BF),
            jax.ShapeDtypeStruct((heads * DV, width), BF),
            jax.ShapeDtypeStruct((1, KVR), F32),
        ],
        scratch_shapes=[
            pltpu.VMEM((length, heads * DV), BF),
            pltpu.VMEM((length, heads * (DN + DR)), BF),
            pltpu.VMEM((length, heads * (DN + DV)), BF),
            pltpu.VMEM((length, KVR + DR), BF),
        ],
        compiler_params=params(),
        name="attention_backward",
    )(
        slot, dh, glat, wo, o, query, kv, lse, latent, compressed, we, wl, wq, n1,
        cosine, sine_vals, col, row,
    )


def finish_kernel(groups, shards, per, piece, *refs):
    place_ref = refs[0]
    by_head, by_row = (refs[1 + i * groups : 1 + (i + 1) * groups] for i in range(2))
    query_ref, expand_ref, out_ref = refs[1 + 2 * groups :]
    cut = by_row[0].shape[0]
    wide = by_head[0].shape[2] - piece
    expand_wide = expand_ref.shape[1] // shards
    for r in range(groups):
        at = place_ref[r]
        rows = pl.ds(pl.multiple_of(at * cut, cut), cut)
        out_ref[rows, :] = by_row[r][...].astype(F32)
        low = pl.ds(pl.multiple_of((at % per) * cut, cut), cut)
        for s in range(shards):
            query_ref[rows, s * wide : (s + 1) * wide] = by_head[r][s, :, :wide].astype(F32)
            lanes = pl.ds(
                pl.multiple_of(s * expand_wide + (at // per) * piece, piece), piece
            )
            expand_ref[low, lanes] = by_head[r][s, :, wide:].astype(F32)


def finish(place, by_head, by_row, heads, width):
    groups, shards = len(by_head), by_head[0].shape[0]
    latent_part = KVR // shards
    part = width // shards
    per = groups * latent_part // part
    piece = heads * (DN + DV) * latent_part // part
    return pl.pallas_call(
        functools.partial(finish_kernel, groups, shards, per, piece),
        in_specs=[SMEM] + [VMEM] * (2 * groups),
        out_shape=[
            jax.ShapeDtypeStruct((part, H * (DN + DR)), F32),
            jax.ShapeDtypeStruct((latent_part, H * (DN + DV)), F32),
            jax.ShapeDtypeStruct((part, width), F32),
        ],
        compiler_params=params(),
        name="finish",
    )(place, *by_head, *by_row)


def shared_finish_kernel(x_ref, gate_ref, up_ref, hold_ref):
    groups, shards, hid = x_ref.shape[0], x_ref.shape[1], x_ref.shape[2] // 2
    for i, out_ref in ((0, gate_ref), (1, up_ref)):
        for s in range(shards):
            for g in range(groups):
                at = (s * groups + g) * hid
                hold_ref[at : at + hid] = x_ref[g, s, i * hid : (i + 1) * hid].astype(F32)
        out_ref[...] = hold_ref[...].T


def shared_finish(pieces):
    groups, shards, two, part = pieces.shape
    wide = groups * shards * two // 2
    return pl.pallas_call(
        shared_finish_kernel,
        in_specs=[VMEM],
        out_shape=[jax.ShapeDtypeStruct((part, wide), F32)] * 2,
        scratch_shapes=[pltpu.VMEM((wide, part), F32)],
        compiler_params=params(),
        name="shared_finish",
    )(pieces)


STEP = 4


def pick_kernel(order_ref, pick_ref, *refs):
    out_ref = refs[STEP]
    capacity = out_ref.shape[1] // STEP
    for i in range(STEP):
        rows = mm(pick_ref[i], refs[i][0]).astype(BF)
        out_ref[:, i * capacity : (i + 1) * capacity, :] = rows.reshape(
            EXP_DEV, capacity, rows.shape[1]
        )


def pick_rows(pick, x_all, order, capacity):
    devices, slots, tokens = pick.shape
    width = x_all.shape[2]
    at = lambda i: pl.BlockSpec((1, tokens, width), lambda d, o: (o[d * STEP + i], 0, 0))
    return pl.pallas_call(
        pick_kernel,
        grid_spec=pltpu.PrefetchScalarGridSpec(
            num_scalar_prefetch=1,
            grid=(devices // STEP,),
            in_specs=[pl.BlockSpec((STEP, slots, tokens), lambda d, o: (d, 0, 0))]
            + [at(i) for i in range(STEP)],
            out_specs=pl.BlockSpec(
                (EXP_DEV, STEP * capacity, width), lambda d, o: (0, d, 0)
            ),
        ),
        out_shape=jax.ShapeDtypeStruct((EXP_DEV, devices * capacity, width), BF),
        compiler_params=params(),
        name="pick_rows",
    )(order, pick, *([x_all] * STEP))


def place_kernel(order_ref, pick_ref, rows_ref, left_ref, right_ref, out_ref):
    step, slots = pick_ref.shape[0], pick_ref.shape[1]
    capacity = rows_ref.shape[1] // step
    for i in range(step):
        rows = rows_ref[:, i * capacity : (i + 1) * capacity, :]
        rows = rows.reshape(slots, rows.shape[2])
        total = mm_tn(pick_ref[i], rows) + mm(left_ref[i], right_ref[...])
        out_ref[i] = total.astype(BF)


def place_rows(pick, rows, left, right, order, capacity, step):
    devices, slots, tokens = pick.shape
    width = rows.shape[2]
    inner = left.shape[2]
    where = (lambda d, o: (d, 0, 0)) if step > 1 else (lambda d, o: (o[d], 0, 0))
    return pl.pallas_call(
        place_kernel,
        grid_spec=pltpu.PrefetchScalarGridSpec(
            num_scalar_prefetch=1,
            grid=(devices // step,),
            in_specs=[
                pl.BlockSpec((step, slots, tokens), lambda d, o: (d, 0, 0)),
                pl.BlockSpec((EXP_DEV, step * capacity, width), lambda d, o: (0, d, 0)),
                pl.BlockSpec((step, tokens, inner), lambda d, o: (d, 0, 0)),
                pl.BlockSpec((inner, width), lambda d, o: (0, 0)),
            ],
            out_specs=pl.BlockSpec((step, tokens, width), where),
        ),
        out_shape=jax.ShapeDtypeStruct((devices, tokens, width), BF),
        compiler_params=params(),
        name="place_rows",
    )(order, pick, rows, left, right)


def body(
    hidden,
    cotangent,
    segments,
    routes,
    w_query,
    w_latent,
    g_latent,
    w_expand,
    w_out,
    g_attn,
    g_ffn,
    w_router,
    s_gate,
    s_up,
    s_down,
    e_gate,
    expert_up_weight,
    e_down,
):
    tokens = hidden.shape[1]
    width = hidden.shape[2]
    links = Links()
    shards, groups = links.shards, links.groups
    devices = groups * shards
    experts = EXP_DEV * groups
    capacity = max(2, tokens * TOP * 4 // (3 * experts))
    heads = H // shards
    length = tokens * shards
    part = width // shards
    my_shard = lax.axis_index("shard")
    my_group = lax.axis_index("expert")
    hid_shard = s_down.shape[0]
    hid = hid_shard // groups
    latent_part = KVR // shards
    shard_at, slot_at = links.shard_at(), links.slot_at()

    g_all = lax.all_gather(cotangent[0], BOTH, axis=0, tiled=False)
    router_rows = part * experts // width
    small_rows = jnp.concatenate([g_attn, g_ffn, g_latent])
    small_rows = jnp.pad(small_rows, (0, -small_rows.shape[0] % width)).reshape(-1, width)
    packed = jnp.concatenate([w_router.reshape(router_rows, width), small_rows])
    packed = links.gather_shard(jnp.pad(packed, ((0, -packed.shape[0] % 16), (0, 0))))
    hidden_all = links.gather_shard(hidden[0]).reshape(length, width)
    pieces = lambda w: jnp.stack(jnp.split(w, shards, axis=1))
    wl = links.gather_shard(w_latent.T)
    wq = links.spread_shard(pieces(w_query))
    we = links.spread_shard(pieces(w_expand))
    packed = jnp.take(packed, slot_at, axis=0)
    full_router = packed[:, :router_rows].reshape(width, experts)
    gains_in = packed[:, router_rows:].reshape(shards, -1)
    gattn = gains_in[:, :part].reshape(1, width).astype(F32)
    gffn = gains_in[:, part : 2 * part].reshape(width).astype(F32)
    glatent = gains_in[:, 2 * part : 2 * part + latent_part].reshape(1, KVR).astype(F32)

    order = links.order()
    same = jnp.arange(devices, dtype=jnp.int32)
    back_order = jnp.sum(
        jnp.where(order[:, None] == same[None, :], same[:, None], 0), axis=0
    ).astype(jnp.int32)
    local_routes = routes[0]
    flat_routes = local_routes.reshape(-1)
    choose = local_routes[:, :, None] == jnp.arange(experts, dtype=jnp.int32)[None, None, :]
    hits = choose.reshape(-1, experts).astype(F32)
    pair_count = tokens * TOP
    before_it = (
        lax.broadcasted_iota(jnp.int32, (pair_count, pair_count), 1)
        < lax.broadcasted_iota(jnp.int32, (pair_count, pair_count), 0)
    ).astype(BF)
    before = mm(before_it, hits.astype(BF))
    slot_rank = jnp.sum(before * hits, axis=1).astype(jnp.int32)
    slot_of = (flat_routes * capacity + slot_rank).reshape(tokens, TOP)
    slots = EXP_DEV * capacity
    slot_rows = jnp.pad(slot_of.T, ((0, 8 - TOP), (0, 0)), constant_values=-1)
    slots_all = exchange(jnp.broadcast_to(slot_rows[None], (devices, 8, tokens)), BOTH)
    slots_all = jnp.take(slots_all, order, axis=0)[:, :TOP]
    slot_ids = my_group * slots + jnp.arange(slots, dtype=jnp.int32)
    pick = jnp.any(
        slots_all[:, None] == slot_ids[None, :, None, None], axis=2
    ).astype(BF)

    positions = (shard_at[:, None] * tokens + jnp.arange(tokens, dtype=jnp.int32)).reshape(-1)
    cosine, sine_vals = rope_angles(positions)
    segs = jnp.take(segments.reshape(shards, tokens), shard_at, axis=0).reshape(-1)
    col = jnp.stack([segs, positions], axis=1)
    row = jnp.stack([segs, positions], axis=0)
    attn_part, n1, compressed, latent, attended, query, kv, lse = attention_forward(
        slot_at, hidden_all, gattn, glatent, wq, wl, we, w_out, cosine, sine_vals, col, row
    )
    (s_gate, s_up, s_down), attn_part = tie((s_gate, s_up, s_down), attn_part)
    attn_out = links.sum_shard(attn_part.reshape(shards, tokens, width))

    mine = lambda w: lax.dynamic_slice_in_dim(
        w.reshape(part, shards, hid_shard), my_group * hid, hid, 2
    )
    gate_up = jnp.concatenate([mine(s_gate), mine(s_up)], axis=2).transpose(1, 0, 2)
    shared_down = lax.dynamic_slice_in_dim(s_down, my_group * hid, hid, 0)

    residual_in = hidden[0].astype(F32)
    residual_mid = residual_in + attn_out
    unit_two, factor_two = norm_forward(residual_mid)
    normed_two = (unit_two * gffn).astype(BF)

    work_g = Fill(lambda p, g: pick_rows(p, g, order, capacity), pick, g_all)
    n2_all = links.gather_all(normed_two, [(groups // 2, work_g)]).reshape(
        devices, tokens, width
    )
    grad_rows = work_g.result
    shared_in = links.spread_shard(gate_up)
    shared_in = jnp.take(shared_in, slot_at, axis=0).reshape(width, 2 * hid)
    probs = jax.nn.sigmoid(mm(normed_two, full_router))
    chosen = jnp.sum(jnp.where(choose, probs[:, None, :], 0.0), axis=-1)
    chosen_total = jnp.sum(chosen, axis=1, keepdims=True)

    grad_inner = jnp.einsum("jmd,jfd->jmf", grad_rows, e_down, preferred_element_type=F32)
    shared_grad_inner = mm_nt(g_all.reshape(-1, width), shared_down)
    shared_grad_inner = jnp.take(
        shared_grad_inner.reshape(devices, tokens, hid), order, axis=0
    ).reshape(-1, hid)

    shared_pre = mm(
        n2_all.reshape(-1, width), jnp.concatenate([shared_in, full_router], axis=1)
    )
    probs_all = jax.nn.sigmoid(
        shared_pre[:, 2 * hid :].reshape(devices, tokens, experts).transpose(0, 2, 1)
    )
    named = jnp.any(
        (slots_all // capacity)[:, None]
        == jnp.arange(experts, dtype=jnp.int32)[None, :, None, None],
        axis=2,
    )
    totals = jnp.sum(jnp.where(named, probs_all, 0.0), axis=1, keepdims=True)
    local_probs = lax.dynamic_slice_in_dim(probs_all, my_group * EXP_DEV, EXP_DEV, 1)
    local_weights = local_probs / totals * ROUTE_SCALE
    slot_weight = jnp.sum(
        jnp.where(
            pick.reshape(devices, EXP_DEV, capacity, tokens) > 0,
            local_weights[:, :, None, :],
            0.0,
        ),
        axis=3,
    )
    row_weight = slot_weight.transpose(1, 0, 2).reshape(EXP_DEV, devices * capacity, 1)

    rows = pick_rows(pick, n2_all, same, capacity)
    gate = jnp.einsum("jmd,jdf->jmf", rows, e_gate, preferred_element_type=F32)
    up = jnp.einsum("jmd,jdf->jmf", rows, expert_up_weight, preferred_element_type=F32)
    inner, slope_gate, slope_up = swish_parts(gate, up)
    weighted_grad = row_weight * grad_inner
    grad_gate_b = (weighted_grad * slope_gate).astype(BF)
    grad_up_b = (weighted_grad * slope_up).astype(BF)
    inner_w = (row_weight * inner).astype(BF)
    grad_slot_weight = jnp.sum(inner.astype(BF).astype(F32) * grad_inner, axis=2)

    s_inner, s_slope_gate, s_slope_up = swish_parts(
        shared_pre[:, :hid], shared_pre[:, hid : 2 * hid]
    )
    shared_inner = s_inner.astype(BF)
    shared_grads = jnp.concatenate(
        [shared_grad_inner * s_slope_gate, shared_grad_inner * s_slope_up], axis=1
    ).astype(BF)

    dz = (
        jnp.einsum("jmf,jdf->jmd", grad_gate_b, e_gate, preferred_element_type=F32)
        + jnp.einsum("jmf,jdf->jmd", grad_up_b, expert_up_weight, preferred_element_type=F32)
    ).astype(BF)
    dn2_part = place_rows(
        pick, dz, shared_grads.reshape(devices, tokens, 2 * hid), shared_in.T, same,
        capacity, STEP,
    )

    d_shared_in = mm_tn(shared_grads, n2_all.reshape(-1, width)).astype(BF)
    shared_inner_back = jnp.take(
        shared_inner.reshape(devices, tokens, hid), back_order, axis=0
    ).reshape(-1, hid)
    d_shared_down = mm_tn(shared_inner_back, g_all.reshape(-1, width)).astype(BF)
    in_pieces = exchange(
        d_shared_in.reshape(2 * hid, shards, part).transpose(1, 0, 2), "shard"
    )
    in_all = lax.all_gather(in_pieces, "expert", axis=0, tiled=False)
    down_all = lax.all_gather(d_shared_down, "expert", axis=0, tiled=True)

    slot_back = grad_slot_weight.reshape(EXP_DEV, devices, capacity).transpose(1, 0, 2)
    slot_back = jnp.take(slot_back.reshape(devices, slots), back_order, axis=0)
    got = exchange(slot_back, BOTH)
    slot_grads = jnp.sum(got.reshape(groups, shards, slots), axis=1).reshape(-1)
    at_slot = slot_of[:, :, None] == jnp.arange(experts * capacity, dtype=jnp.int32)
    grad_weights = jnp.sum(jnp.where(at_slot, slot_grads, 0.0), axis=2)
    grad_chosen = ROUTE_SCALE * (
        grad_weights / chosen_total
        - jnp.sum(grad_weights * chosen, axis=1, keepdims=True) / (chosen_total * chosen_total)
    )
    grad_probs = jnp.sum(jnp.where(choose, grad_chosen[:, :, None], 0.0), axis=1)
    grad_logits = (grad_probs * probs * (1.0 - probs)).astype(BF)
    logits_back = exchange(
        jnp.broadcast_to(grad_logits.T[None], (devices, experts, tokens)), BOTH
    )
    logits_back = jnp.take(logits_back, order, axis=0)

    def outputs(inner_of, shared_of):
        weighted_out = jnp.einsum(
            "jmf,jfd->jmd", inner_of, e_down, preferred_element_type=F32
        ).astype(BF)
        return place_rows(
            pick, weighted_out, shared_of.reshape(devices, tokens, hid), shared_down, order,
            capacity, 1,
        )

    weight_grad = lambda a, b: jnp.einsum("jmd,jmf->jdf", a, b, preferred_element_type=F32)
    down_grad = lambda a, b: jnp.einsum("jmf,jmd->jfd", a, b, preferred_element_type=F32)
    work = [
        Fill(weight_grad, rows, grad_gate_b),
        Fill(weight_grad, rows, grad_up_b),
        Fill(outputs, inner_w, shared_inner),
        Fill(down_grad, inner_w, grad_rows),
    ]
    dn2 = links.sum_all(
        dn2_part.reshape(groups, shards // 2, 2, tokens, width),
        [(groups // 2 - i, w) for i, w in enumerate(work)],
    )
    d_egate, grad_expert_up, out_part, d_edown = (w.result for w in work)
    dn2, (out_part, in_all, down_all) = tie(dn2, (out_part, in_all, down_all))
    routed_shared = lax.psum_scatter(
        out_part, BOTH, scatter_dimension=0, tiled=False
    ).astype(F32)
    output_rows = residual_mid + routed_shared

    grad_normed_two = dn2 + mm_nt(grad_logits, full_router)
    grad_mid_norm, d_gffn = norm_backward(grad_normed_two, gffn, unit_two, factor_two)
    grad_mid = cotangent[0].astype(F32) + grad_mid_norm
    grad_attn = links.gather_shard(grad_mid.astype(BF)).reshape(length, width)
    own_columns = lax.dynamic_slice_in_dim(n2_all, my_shard * part, part, 2)
    d_router = mm(
        logits_back.transpose(1, 0, 2).reshape(experts, -1), own_columns.reshape(-1, part)
    ).T

    dn1, dw, dwl, d_out, d_glatent = attention_backward(
        slot_at, grad_attn, glatent, w_out, attended, query, kv, lse, latent, compressed,
        we, wl, wq, n1, cosine, sine_vals, col, row,
    )
    (dn1, dw, dwl, d_out), in_all = tie((dn1, dw, dwl, d_out), in_all)
    grad_normed = links.sum_shard(dn1.reshape(shards, tokens, width))
    unit_one, factor_one = norm_forward(residual_in)
    grad_input_norm, d_gattn = norm_backward(
        grad_normed, gattn.reshape(width), unit_one, factor_one
    )
    grad_input = grad_mid + grad_input_norm

    cut = part // groups
    lat = links.sum_shard(dwl).astype(BF).reshape(groups, (KVR + DR) // groups, part)
    by_head = links.blocks(dw.reshape(shards, groups, cut, -1).transpose(1, 0, 2, 3))
    by_row = links.blocks(d_out.reshape(groups, cut, width))
    pluses = [groups // 2, (groups - 1) // 2, (groups - 1) // 2]
    work_s = Fill(shared_finish, in_all)
    sum_head, sum_row, sum_lat = links.ring_reduce(
        [by_head, by_row, links.blocks(lat)], pluses, [(groups // 2, work_s)]
    )
    part_sgate, part_sup = work_s.result
    sum_head = links.exchange_shard(sum_head.astype(BF))
    all_head, all_row, all_lat = links.ring_gather(
        [sum_head, sum_row.astype(BF), sum_lat.astype(BF)], pluses
    )
    part_query, part_expand, part_out = finish(
        links.block_at(), all_head, all_row, heads, width
    )
    part_latent = jnp.take(jnp.stack(all_lat), links.block_at(), axis=0)
    part_latent = part_latent.reshape(KVR + DR, part).astype(F32)

    gain_grads = jnp.concatenate(
        [
            d_gattn.reshape(shards, part),
            d_gffn.reshape(shards, part),
            d_glatent.reshape(shards, latent_part),
        ],
        axis=1,
    )
    got = exchange(
        jnp.broadcast_to(gain_grads[None], (groups,) + gain_grads.shape).reshape(devices, -1),
        BOTH,
    )
    gains = jnp.sum(got, axis=0)
    return (
        output_rows.astype(BF)[None],
        grad_input[None],
        part_query,
        part_latent.T,
        gains[2 * part :],
        part_expand,
        part_out,
        gains[:part],
        gains[part : 2 * part],
        d_router,
        part_sgate,
        part_sup,
        down_all.astype(F32),
        d_egate,
        grad_expert_up,
        d_edown,
    )


def solution(mesh):
    return jax.shard_map(
        body,
        mesh=mesh,
        in_specs=(
            P("expert", "shard", None),
            P("expert", "shard", None),
            P("expert", None),
            P("expert", "shard", None),
            P("shard", None),
            P("shard", None),
            P("shard"),
            P("shard", None),
            P("shard", None),
            P("shard"),
            P("shard"),
            P("shard", None),
            P("shard", None),
            P("shard", None),
            P("shard", None),
            P("expert", None, "shard"),
            P("expert", None, "shard"),
            P("expert", "shard", None),
        ),
        out_specs=(
            P("expert", "shard", None),
            P("expert", "shard", None),
            P("shard", None),
            P("shard", None),
            P("shard"),
            P("shard", None),
            P("shard", None),
            P("shard"),
            P("shard"),
            P("shard", None),
            P("shard", None),
            P("shard", None),
            P("shard", None),
            P("expert", None, "shard"),
            P("expert", None, "shard"),
            P("expert", "shard", None),
        ),
        check_vma=False,
    )
```

```python
import functools

import jax
import jax.numpy as jnp
from jax import lax
from jax.experimental import pallas as pl
from jax.experimental.pallas import tpu as pltpu
from jax.sharding import PartitionSpec as P

H = 16
DN = 128
DR = 64
DV = 128
KVR = 512
TOP = 6
EXP_DEV = 4

EPS = 1e-06
ROUTE_SCALE = 2.446
ROPE_BASE = 50000.0
SCORE_SCALE = (DN + DR) ** (-0.5)
BF = jnp.bfloat16
F32 = jnp.float32
BOTH = ("expert", "shard")
VMEM_BYTES = 56 * 1024 * 1024


def mm(a, b):
    return jnp.dot(a, b, preferred_element_type=F32)


def mm_tn(a, b):
    return lax.dot_general(a, b, (((0,), (0,)), ((), ())), preferred_element_type=F32)


def mm_nt(a, b):
    return lax.dot_general(a, b, (((1,), (1,)), ((), ())), preferred_element_type=F32)


def rope_angles(positions):
    half_width = DR // 2
    inverse = ROPE_BASE ** (-jnp.arange(half_width).astype(F32) / half_width)
    angles = positions.astype(F32)[:, None] * inverse[None, :]
    return (jnp.cos(angles), jnp.sin(angles))


def rotate(values, cosine, sine_vals):
    half_width = DR // 2
    first_half = values[..., :half_width]
    second_half = values[..., half_width:]
    return jnp.concatenate(
        [
            first_half * cosine - second_half * sine_vals,
            second_half * cosine + first_half * sine_vals,
        ],
        axis=-1,
    )


def norm_forward(values):
    factor = lax.rsqrt(jnp.mean(values * values, axis=-1, keepdims=True) + EPS)
    return values * factor, factor


def norm_backward(grad_out, gain_vec, unit_vals, factor):
    grad_unit = grad_out * gain_vec
    grad_in = factor * (
        grad_unit - unit_vals * jnp.mean(grad_unit * unit_vals, axis=-1, keepdims=True)
    )
    return (grad_in, jnp.sum(grad_out * unit_vals, axis=0))


def swish_parts(gate, up):
    sig = jax.nn.sigmoid(gate)
    silu = gate * sig
    return silu * up, up * sig * (1.0 + gate * (1.0 - sig)), silu


def exchange(values, axis):
    return lax.all_to_all(values, axis, split_axis=0, concat_axis=0, tiled=True)


def tie(streams, extra):
    return lax.optimization_barrier((streams, extra))


class Fill:
    def __init__(self, work, *inputs):
        self.work, self.inputs, self.result = work, inputs, None


class Links:
    def __init__(self):
        self.groups = lax.axis_size("expert")
        self.shards = lax.axis_size("shard")
        self.rows = self.shards // 2
        n = self.groups
        self.ring = list(range(0, n, 2)) + list(range(n - 1, 0, -2))
        shard = lax.axis_index("shard")
        self.x = shard // 2
        self.core = shard % 2
        group = lax.axis_index("expert")
        places = [self.ring.index(e) for e in range(n)]
        self.place = jnp.sum(
            jnp.where(jnp.arange(n) == group, jnp.array(places, jnp.int32), 0)
        )

    def send(self, values, target):
        pairs = []
        for e in range(self.groups):
            for s in range(self.shards):
                pairs.append((e * self.shards + s, target(e, s)))
        return lax.ppermute(values, BOTH, pairs)

    def around(self, values, step):
        n = self.groups
        return self.send(
            values,
            lambda e, s: self.ring[(self.ring.index(e) + step) % n] * self.shards + s,
        )

    def along_x(self, values, step):
        return self.send(
            values,
            lambda e, s: e * self.shards + ((s // 2 + step) % self.rows) * 2 + s % 2,
        )

    def partner(self, values):
        return self.send(values, lambda e, s: e * self.shards + (s ^ 1))

    def shard_at(self):
        xs = (self.x - jnp.arange(self.rows, dtype=jnp.int32)) % self.rows
        cores = jnp.stack([self.core, 1 - self.core]).astype(jnp.int32)
        return (xs[:, None] * 2 + cores[None, :]).reshape(-1).astype(jnp.int32)

    def slot_at(self):
        shard = jnp.arange(self.shards, dtype=jnp.int32)
        back = (self.x - shard // 2) % self.rows
        return (back * 2 + (shard % 2 != self.core)).astype(jnp.int32)

    def gather_shard(self, values):
        out = []
        for k in range(self.rows):
            own = values if k == 0 else self.along_x(values, k)
            out += [own, self.partner(own)]
        return jnp.stack(out)

    def spread_shard(self, pieces):
        take = lambda v, i: lax.dynamic_index_in_dim(v, i, 0, keepdims=False)
        pairs = pieces.reshape((self.rows, 2) + pieces.shape[1:])
        out = []
        for k in range(self.rows):
            got = take(pairs, (self.x + k) % self.rows)
            got = got if k == 0 else self.along_x(got, k)
            out += [take(got, self.core), self.partner(take(got, 1 - self.core))]
        return jnp.stack(out)

    def exchange_shard(self, values):
        pairs = values.reshape((self.rows, 2) + values.shape[1:])
        out = []
        for k in range(self.rows):
            got = pairs[k] if k == 0 else self.along_x(pairs[k], -k)
            out += [got[0], self.partner(got[1])]
        xs = (self.x + jnp.arange(self.rows, dtype=jnp.int32)) % self.rows
        shard = jnp.arange(self.shards, dtype=jnp.int32)
        ahead = (shard // 2 - self.x) % self.rows
        slot = ahead * 2 + (shard % 2 != self.core)
        return jnp.take(jnp.stack(out), slot, axis=0)

    def sum_shard(self, values, fill=None):
        pairs = values.reshape((self.rows, 2) + values.shape[1:])
        both = [
            pairs[k, 0].astype(F32) + self.partner(pairs[k, 1]).astype(F32)
            for k in range(self.rows)
        ]
        far = [v.astype(BF) for v in both[1:]]
        if fill is not None:
            far, inputs = tie(far, fill.inputs)
        far = [self.along_x(v, -k - 1) for k, v in enumerate(far)]
        if fill is not None:
            far, fill.result = tie(far, fill.work(*inputs))
        total = both[0]
        for v in far:
            total = total + v.astype(F32)
        return total

    def ring_gather(self, values, pluses, fills=()):
        n = self.groups
        fills = dict(fills)
        outs = [[v] + [None] * (n - 1) for v in values]
        ahead, back = list(values), list(values)
        for r in range(1, n):
            moves = [(i, 1) for i, p in enumerate(pluses) if r <= p]
            moves += [(i, -1) for i, p in enumerate(pluses) if r <= n - 1 - p]
            if not moves:
                break
            streams = [ahead[i] if step > 0 else back[i] for i, step in moves]
            streams = self.step(streams, [step for _, step in moves], fills.get(r))
            for (i, step), got in zip(moves, streams):
                if step > 0:
                    ahead[i] = outs[i][r] = got
                else:
                    back[i] = outs[i][n - r] = got
        return outs

    def step(self, streams, steps, fill):
        if fill is None:
            return [self.around(v, s) for v, s in zip(streams, steps)]
        streams, inputs = tie(streams, fill.inputs)
        streams = [self.around(v, s) for v, s in zip(streams, steps)]
        streams, fill.result = tie(streams, fill.work(*inputs))
        return streams

    def ring_reduce(self, parts, pluses, fills=()):
        n = self.groups
        fills = dict(fills)
        ahead = [p[plus] for p, plus in zip(parts, pluses)]
        back = [p[plus + 1] for p, plus in zip(parts, pluses)]
        most = max(max(p, n - 1 - p) for p in pluses)
        for r in range(most, 0, -1):
            moves = [(i, 1) for i, p in enumerate(pluses) if r <= p]
            moves += [(i, -1) for i, p in enumerate(pluses) if r <= n - 1 - p]
            streams = [ahead[i] if step > 0 else back[i] for i, step in moves]
            streams = self.step(streams, [-step for _, step in moves], fills.get(r))
            for (i, step), got in zip(moves, streams):
                here = parts[i][r - 1 if step > 0 else (n - r + 1) % n]
                if r > 1:
                    got = (got.astype(F32) + here.astype(F32)).astype(BF)
                if step > 0:
                    ahead[i] = got
                else:
                    back[i] = got
        return [
            p[0].astype(F32) + a.astype(F32) + b.astype(F32)
            for p, a, b in zip(parts, ahead, back)
        ]

    def block_at(self):
        return (self.place - jnp.arange(self.groups, dtype=jnp.int32)) % self.groups

    def blocks(self, values):
        return [
            lax.dynamic_index_in_dim(
                values, (self.place - r) % self.groups, 0, keepdims=False
            )
            for r in range(self.groups)
        ]

    def order(self):
        n = self.groups
        ring = jnp.array(self.ring, jnp.int32)
        groups = jnp.sum(
            jnp.where(self.block_at()[:, None] == jnp.arange(n)[None, :], ring[None, :], 0),
            axis=1,
        )
        all_of = groups[:, None] * self.shards + self.shard_at()[None, :]
        return all_of.reshape(-1).astype(jnp.int32)

    def gather_all(self, values, fills=()):
        n, rows = self.groups, self.rows
        tokens, width = values.shape
        half = tokens // 2
        first, second = values[:half], values[half:]
        spread = jnp.stack([first] + [self.along_x(first, k) for k in range(1, rows)])
        upper, lower = self.ring_gather(
            [spread, second], [n // 2, (n - 1) // 2], fills
        )
        out = jnp.zeros((n, rows, 2, tokens, width), values.dtype)
        steps = [0] + [r for k in range(1, n // 2 + 1) for r in dict.fromkeys((k, n - k))]
        for r in steps:
            low = jnp.stack(
                [lower[r]] + [self.along_x(lower[r], k) for k in range(1, rows)]
            )
            own = jnp.concatenate([upper[r], low], axis=1)
            both = jnp.stack([own, self.partner(own)], axis=1)[None]
            out = lax.dynamic_update_slice(out, both, (r, 0, 0, 0, 0))
        return out

    def gather_plain(self, values):
        n, rows = self.groups, self.rows
        spread = jnp.stack([values] + [self.along_x(values, k) for k in range(1, rows)])
        (got,) = self.ring_gather([spread], [n // 2])
        out = jnp.zeros((n, rows, 2) + values.shape, values.dtype)
        for r in [0] + [r for k in range(1, n // 2 + 1) for r in dict.fromkeys((k, n - k))]:
            both = jnp.stack([got[r], self.partner(got[r])], axis=1)[None]
            out = lax.dynamic_update_slice(out, both, (r, 0, 0, 0, 0))
        return out

    def sum_all(self, own, other, fills=()):
        n, rows = self.groups, self.rows
        both = (own.astype(F32) + self.partner(other).astype(F32)).astype(BF)
        (top,) = self.ring_reduce([[both[r] for r in range(n)]], [n // 2], fills)
        total = top[0]
        for k in range(1, rows):
            total = total + self.along_x(top[k].astype(BF), -k).astype(F32)
        return total


def params(**kw):
    return pltpu.CompilerParams(vmem_limit_bytes=VMEM_BYTES, **kw)


SMEM = pl.BlockSpec(memory_space=pltpu.SMEM)
VMEM = pl.BlockSpec(memory_space=pltpu.VMEM)


def allowed_mask(seg_col, seg_row, pos_col, pos_row):
    return (seg_col == seg_row) & (pos_row <= pos_col)


def attention_forward_kernel(
    slot_ref, x_ref, gattn_ref, glat_ref, wq_ref, wl_ref, we_ref, wo_ref,
    cos_ref, sin_ref, col_ref, row_ref,
    out_ref, n1_ref, c_ref, lat_ref, o_ref, q_ref, kv_ref, lse_ref,
):
    shards, part = wq_ref.shape[0], wq_ref.shape[1]
    heads = q_ref.shape[0]
    tokens = x_ref.shape[0] // shards
    for b in range(shards):
        at = slice(b * tokens, (b + 1) * tokens)
        unit, _ = norm_forward(x_ref[at].astype(F32))
        n1_ref[at] = (unit * gattn_ref[...]).astype(BF)
    queries, compressed, kv_all = None, None, None
    for s in range(shards):
        left = n1_ref[:, s * part : (s + 1) * part]
        one = mm(left, wq_ref[slot_ref[s]])
        queries = one if s == 0 else queries + one
        one = mm_nt(left, wl_ref[slot_ref[s]])
        compressed = one if s == 0 else compressed + one
    c_ref[...] = compressed
    unit, _ = norm_forward(compressed[:, :KVR])
    lat_ref[:, :KVR] = (unit * glat_ref[...]).astype(BF)
    lat_ref[:, KVR:] = rotate(compressed[:, KVR:], cos_ref[...], sin_ref[...]).astype(BF)
    part = KVR // shards
    for s in range(shards):
        one = mm(lat_ref[:, s * part : (s + 1) * part], we_ref[slot_ref[s]])
        kv_all = one if s == 0 else kv_all + one
    kv_ref[...] = kv_all.astype(BF)
    ok = allowed_mask(
        col_ref[:, :1], row_ref[:1, :], col_ref[:, 1:2], row_ref[1:2, :]
    )
    key_rot = lat_ref[:, KVR:]
    for h in range(heads):
        at = h * (DN + DR)
        query = jnp.concatenate(
            [
                queries[:, at : at + DN],
                rotate(queries[:, at + DN : at + DN + DR], cos_ref[...], sin_ref[...]),
            ],
            axis=1,
        ).astype(BF)
        q_ref[h] = query
        at = h * (DN + DV)
        keys = kv_ref[:, at : at + DN]
        values = kv_ref[:, at + DN : at + DN + DV]
        scores = mm_nt(query[:, :DN], keys) + mm_nt(query[:, DN:], key_rot)
        scores = jnp.where(ok, scores * SCORE_SCALE, -1e30)
        top = jnp.max(scores, axis=1, keepdims=True)
        expo = jnp.exp(scores - top)
        total = jnp.sum(expo, axis=1, keepdims=True)
        lse_ref[h] = top + jnp.log(total)
        weights = (expo / total).astype(BF)
        o_ref[:, h * DV : (h + 1) * DV] = mm(weights, values).astype(BF)
    out_ref[...] = mm(o_ref[...], wo_ref[...]).astype(BF)


def attention_forward(slot, x, gattn, glat, wq, wl, we, wo, cosine, sine_vals, col, row):
    length, width = x.shape
    heads = wo.shape[0] // DV
    return pl.pallas_call(
        attention_forward_kernel,
        in_specs=[SMEM] + [VMEM] * 11,
        out_shape=[
            jax.ShapeDtypeStruct((length, width), BF),
            jax.ShapeDtypeStruct((length, width), BF),
            jax.ShapeDtypeStruct((length, KVR + DR), F32),
            jax.ShapeDtypeStruct((length, KVR + DR), BF),
            jax.ShapeDtypeStruct((length, heads * DV), BF),
            jax.ShapeDtypeStruct((heads, length, DN + DR), BF),
            jax.ShapeDtypeStruct((length, heads * (DN + DV)), BF),
            jax.ShapeDtypeStruct((heads, length, 1), F32),
        ],
        compiler_params=params(),
        name="attention_forward",
    )(slot, x, gattn, glat, wq, wl, we, wo, cosine, sine_vals, col, row)


def attention_backward_kernel(
    slot_ref, dh_ref, glat_ref, wo_ref, o_ref, q_ref, kv_ref, lse_ref, lat_ref, c_ref,
    we_ref, wl_ref, wq_ref, n1_ref, cos_ref, sin_ref, col_ref, row_ref,
    dn1_ref, dw_ref, dwl_ref, dwo_ref, dgl_ref,
    go_ref, gq_ref, gkv_ref, gc_ref,
):
    shards, part = wq_ref.shape[0], wq_ref.shape[1]
    heads = q_ref.shape[0]
    go_ref[...] = mm_nt(dh_ref[...], wo_ref[...]).astype(BF)
    dwo_ref[...] = mm_tn(o_ref[...], dh_ref[...]).astype(BF)
    ok = allowed_mask(
        col_ref[:, :1], row_ref[:1, :], col_ref[:, 1:2], row_ref[1:2, :]
    )
    key_rot = lat_ref[:, KVR:]
    grad_kr = None
    for h in range(heads):
        at = h * (DN + DV)
        keys = kv_ref[:, at : at + DN]
        values = kv_ref[:, at + DN : at + DN + DV]
        query = q_ref[h]
        grad_o = go_ref[:, h * DV : (h + 1) * DV]
        scores = mm_nt(query[:, :DN], keys) + mm_nt(query[:, DN:], key_rot)
        weights = jnp.where(ok, jnp.exp(scores * SCORE_SCALE - lse_ref[h]), 0.0)
        grad_w = mm_nt(grad_o, values)
        delta = jnp.sum(weights * grad_w, axis=1, keepdims=True)
        grad_s = (weights * (grad_w - delta) * SCORE_SCALE).astype(BF)
        gkv_ref[:, at : at + DN] = mm_tn(grad_s, query[:, :DN]).astype(BF)
        gkv_ref[:, at + DN : at + DN + DV] = mm_tn(weights.astype(BF), grad_o).astype(BF)
        one = mm_tn(grad_s, query[:, DN:])
        grad_kr = one if h == 0 else grad_kr + one
        at = h * (DN + DR)
        grad_qr = rotate(mm(grad_s, key_rot), cos_ref[...], -sin_ref[...])
        gq_ref[:, at : at + DN + DR] = jnp.concatenate(
            [mm(grad_s, keys), grad_qr], axis=1
        ).astype(BF)
    latent_part = KVR // shards
    query_wide = heads * (DN + DR)
    ratio = part // latent_part
    piece = heads * (DN + DV) // ratio
    grad_lat = []
    for s in range(shards):
        at = slice(s * latent_part, (s + 1) * latent_part)
        grad_lat.append(mm_nt(gkv_ref[...], we_ref[slot_ref[s]]))
        one = mm_tn(lat_ref[:, at], gkv_ref[...]).astype(BF)
        for i in range(ratio):
            dw_ref[slot_ref[s], i * latent_part : (i + 1) * latent_part, query_wide:] = one[
                :, i * piece : (i + 1) * piece
            ]
    grad_lat = jnp.concatenate(grad_lat, axis=1)
    unit, factor = norm_forward(c_ref[:, :KVR])
    grad_norm, grad_gain = norm_backward(grad_lat, glat_ref[...], unit, factor)
    dgl_ref[...] = grad_gain.reshape(1, KVR)
    gc_ref[:, :KVR] = grad_norm.astype(BF)
    gc_ref[:, KVR:] = rotate(grad_kr, cos_ref[...], -sin_ref[...]).astype(BF)
    for s in range(shards):
        at = slice(s * part, (s + 1) * part)
        dn1_ref[:, at] = (
            mm_nt(gq_ref[...], wq_ref[slot_ref[s]]) + mm(gc_ref[...], wl_ref[slot_ref[s]])
        ).astype(BF)
        dw_ref[slot_ref[s], :, :query_wide] = mm_tn(n1_ref[:, at], gq_ref[...]).astype(BF)
        dwl_ref[slot_ref[s]] = mm_tn(gc_ref[...], n1_ref[:, at]).astype(BF)


def attention_backward(
    slot, dh, glat, wo, o, query, kv, lse, latent, compressed, we, wl, wq, n1,
    cosine, sine_vals, col, row,
):
    length, width = n1.shape
    heads = query.shape[0]
    shards, part = wq.shape[0], wq.shape[1]
    wide = heads * (DN + DR) + heads * (DN + DV) * KVR // width
    return pl.pallas_call(
        attention_backward_kernel,
        in_specs=[SMEM] + [VMEM] * 17,
        out_shape=[
            jax.ShapeDtypeStruct((length, width), BF),
            jax.ShapeDtypeStruct((shards, part, wide), BF),
            jax.ShapeDtypeStruct(wl.shape, BF),
            jax.ShapeDtypeStruct((heads * DV, width), BF),
            jax.ShapeDtypeStruct((1, KVR), F32),
        ],
        scratch_shapes=[
            pltpu.VMEM((length, heads * DV), BF),
            pltpu.VMEM((length, heads * (DN + DR)), BF),
            pltpu.VMEM((length, heads * (DN + DV)), BF),
            pltpu.VMEM((length, KVR + DR), BF),
        ],
        compiler_params=params(),
        name="attention_backward",
    )(
        slot, dh, glat, wo, o, query, kv, lse, latent, compressed, we, wl, wq, n1,
        cosine, sine_vals, col, row,
    )


def finish_kernel(groups, shards, per, piece, *refs):
    place_ref = refs[0]
    by_head, by_row = (refs[1 + i * groups : 1 + (i + 1) * groups] for i in range(2))
    query_ref, expand_ref, out_ref = refs[1 + 2 * groups :]
    cut = by_row[0].shape[0]
    wide = by_head[0].shape[2] - piece
    expand_wide = expand_ref.shape[1] // shards
    for r in range(groups):
        at = place_ref[r]
        rows = pl.ds(pl.multiple_of(at * cut, cut), cut)
        out_ref[rows, :] = by_row[r][...].astype(F32)
        low = pl.ds(pl.multiple_of((at % per) * cut, cut), cut)
        for s in range(shards):
            query_ref[rows, s * wide : (s + 1) * wide] = by_head[r][s, :, :wide].astype(F32)
            lanes = pl.ds(
                pl.multiple_of(s * expand_wide + (at // per) * piece, piece), piece
            )
            expand_ref[low, lanes] = by_head[r][s, :, wide:].astype(F32)


def finish(place, by_head, by_row, heads, width):
    groups, shards = len(by_head), by_head[0].shape[0]
    latent_part = KVR // shards
    part = width // shards
    per = groups * latent_part // part
    piece = heads * (DN + DV) * latent_part // part
    return pl.pallas_call(
        functools.partial(finish_kernel, groups, shards, per, piece),
        in_specs=[SMEM] + [VMEM] * (2 * groups),
        out_shape=[
            jax.ShapeDtypeStruct((part, H * (DN + DR)), F32),
            jax.ShapeDtypeStruct((latent_part, H * (DN + DV)), F32),
            jax.ShapeDtypeStruct((part, width), F32),
        ],
        compiler_params=params(),
        name="finish",
    )(place, *by_head, *by_row)


def shared_finish_kernel(x_ref, gate_ref, up_ref, hold_ref):
    groups, shards, hid = x_ref.shape[0], x_ref.shape[1], x_ref.shape[2] // 2
    for i, out_ref in ((0, gate_ref), (1, up_ref)):
        for s in range(shards):
            for g in range(groups):
                at = (s * groups + g) * hid
                hold_ref[at : at + hid] = x_ref[g, s, i * hid : (i + 1) * hid].astype(F32)
        out_ref[...] = hold_ref[...].T


def shared_finish(pieces):
    groups, shards, two, part = pieces.shape
    wide = groups * shards * two // 2
    return pl.pallas_call(
        shared_finish_kernel,
        in_specs=[VMEM],
        out_shape=[jax.ShapeDtypeStruct((part, wide), F32)] * 2,
        scratch_shapes=[pltpu.VMEM((wide, part), F32)],
        compiler_params=params(),
        name="shared_finish",
    )(pieces)


STEP = 8
PAD = 128


def pick_into(out_ref, pick, rows_of, i, step):
    capacity = out_ref.shape[1] // step
    rows = mm(pick, rows_of).astype(BF)
    out_ref[:, i * capacity : (i + 1) * capacity, :] = rows.reshape(
        EXP_DEV, capacity, rows.shape[1]
    )


def place_from(rows_ref, pick, i, step):
    capacity = rows_ref.shape[1] // step
    rows = rows_ref[:, i * capacity : (i + 1) * capacity, :]
    return mm_tn(pick, rows.reshape(EXP_DEV * capacity, rows.shape[2]))


def resident(shape):
    return pl.BlockSpec(
        shape, lambda *_: (0,) * len(shape), pipeline_mode=pl.Buffered(1)
    )


def grad_rows_kernel(pick_ref, g_ref, down_ref, rows_ref, inner_ref):
    inner = down_ref.shape[1]
    for i in range(STEP):
        pick_into(rows_ref, pick_ref[i], g_ref[i], i, STEP)
    for j in range(EXP_DEV):
        inner_ref[j, :, :inner] = mm_nt(rows_ref[j], down_ref[j])


def grad_rows_of(pick, g_all, down, capacity):
    devices, slots, tokens = pick.shape
    width, inner = g_all.shape[2], down.shape[1]
    lanes = inner + -inner % PAD
    rows = STEP * capacity
    return pl.pallas_call(
        grad_rows_kernel,
        grid=(devices // STEP,),
        in_specs=[
            pl.BlockSpec((STEP, slots, tokens), lambda d: (d, 0, 0)),
            pl.BlockSpec((STEP, tokens, width), lambda d: (d, 0, 0)),
            resident(down.shape),
        ],
        out_specs=[
            pl.BlockSpec((EXP_DEV, rows, width), lambda d: (0, d, 0)),
            pl.BlockSpec((EXP_DEV, rows, lanes), lambda d: (0, d, 0)),
        ],
        out_shape=[
            jax.ShapeDtypeStruct((EXP_DEV, devices * capacity, width), BF),
            jax.ShapeDtypeStruct((EXP_DEV, devices * capacity, lanes), F32),
        ],
        compiler_params=params(),
        name="grad_rows",
    )(pick, g_all, down)


def inner_kernel(
    pick_ref, x_ref, w_ref, weight_ref, grad_ref,
    rows_ref, inner_ref, grads_ref, slot_ref,
):
    lanes = grad_ref.shape[2]
    inner = inner_ref.shape[2]
    for i in range(STEP):
        pick_into(rows_ref, pick_ref[i], x_ref[i], i, STEP)
    for j in range(EXP_DEV):
        both = mm(rows_ref[j], w_ref[j])
        gate, up = both[:, :inner], both[:, lanes : lanes + inner]
        act, slope_gate, slope_up = swish_parts(gate, up)
        weight = weight_ref[j]
        grad = grad_ref[j, :, :inner]
        slot_ref[j] = jnp.sum(act.astype(BF).astype(F32) * grad, axis=1, keepdims=True)
        inner_ref[j] = (weight * act).astype(BF)
        grad = weight * grad
        if lanes > inner:
            grads_ref[j] = jnp.zeros(grads_ref.shape[1:], BF)
        grads_ref[j, :, :inner] = (grad * slope_gate).astype(BF)
        grads_ref[j, :, lanes : lanes + inner] = (grad * slope_up).astype(BF)


def inner_of(pick, x_all, both, weight, grad, inner, capacity):
    devices, slots, tokens = pick.shape
    width, lanes = x_all.shape[2], grad.shape[2]
    rows = STEP * capacity
    total = devices * capacity
    by_rows = lambda n: pl.BlockSpec((EXP_DEV, rows, n), lambda d: (0, d, 0))
    return pl.pallas_call(
        inner_kernel,
        grid=(devices // STEP,),
        in_specs=[
            pl.BlockSpec((STEP, slots, tokens), lambda d: (d, 0, 0)),
            pl.BlockSpec((STEP, tokens, width), lambda d: (d, 0, 0)),
            resident(both.shape),
            by_rows(1),
            by_rows(lanes),
        ],
        out_specs=[by_rows(width), by_rows(inner), by_rows(2 * lanes), by_rows(1)],
        out_shape=[
            jax.ShapeDtypeStruct((EXP_DEV, total, width), BF),
            jax.ShapeDtypeStruct((EXP_DEV, total, inner), BF),
            jax.ShapeDtypeStruct((EXP_DEV, total, 2 * lanes), BF),
            jax.ShapeDtypeStruct((EXP_DEV, total, 1), F32),
        ],
        compiler_params=params(),
        name="inner",
    )(pick, x_all, both, weight, grad)


def back_kernel(
    pick_ref, grads_ref, w_ref, left_ref, right_ref, own_ref, other_ref, hold_ref
):
    for j in range(EXP_DEV):
        hold_ref[j] = mm_nt(grads_ref[j], w_ref[j]).astype(BF)
    for i in range(STEP):
        total = place_from(hold_ref, pick_ref[i], i, STEP) + mm(left_ref[i], right_ref[...])
        out_ref = own_ref if i % 2 == 0 else other_ref
        out_ref[i // 2] = total.astype(BF)


def back_rows(pick, grads, both, left, right, capacity):
    devices, slots, tokens = pick.shape
    width, inner = both.shape[1], left.shape[2]
    rows = STEP * capacity
    return pl.pallas_call(
        back_kernel,
        grid=(devices // STEP,),
        in_specs=[
            pl.BlockSpec((STEP, slots, tokens), lambda d: (d, 0, 0)),
            pl.BlockSpec((EXP_DEV, rows, grads.shape[2]), lambda d: (0, d, 0)),
            resident(both.shape),
            pl.BlockSpec((STEP, tokens, inner), lambda d: (d, 0, 0)),
            resident(right.shape),
        ],
        out_specs=[pl.BlockSpec((STEP // 2, tokens, width), lambda d: (d, 0, 0))] * 2,
        out_shape=[jax.ShapeDtypeStruct((devices // 2, tokens, width), BF)] * 2,
        scratch_shapes=[pltpu.VMEM((EXP_DEV, rows, width), BF)],
        compiler_params=params(),
        name="back_rows",
    )(pick, grads, both, left, right)


def place_kernel(order_ref, pick_ref, rows_ref, left_ref, right_ref, out_ref):
    total = place_from(rows_ref, pick_ref[0], 0, 1) + mm(left_ref[0], right_ref[...])
    out_ref[0] = total.astype(BF)


def place_rows(pick, rows, left, right, order, capacity):
    devices, slots, tokens = pick.shape
    width = rows.shape[2]
    inner = left.shape[2]
    return pl.pallas_call(
        place_kernel,
        grid_spec=pltpu.PrefetchScalarGridSpec(
            num_scalar_prefetch=1,
            grid=(devices,),
            in_specs=[
                pl.BlockSpec((1, slots, tokens), lambda d, o: (d, 0, 0)),
                pl.BlockSpec((EXP_DEV, capacity, width), lambda d, o: (0, d, 0)),
                pl.BlockSpec((1, tokens, inner), lambda d, o: (d, 0, 0)),
                pl.BlockSpec((inner, width), lambda d, o: (0, 0)),
            ],
            out_specs=pl.BlockSpec((1, tokens, width), lambda d, o: (o[d], 0, 0)),
        ),
        out_shape=jax.ShapeDtypeStruct((devices, tokens, width), BF),
        compiler_params=params(),
        name="place_rows",
    )(order, pick, rows, left, right)


def gate_up_kernel(rows_ref, grads_ref, gate_ref, up_ref):
    inner = gate_ref.shape[2]
    both = mm_tn(rows_ref[0], grads_ref[0])
    gate_ref[0] = both[:, :inner]
    at = grads_ref.shape[2] // 2
    up_ref[0] = both[:, at : at + inner]


def gate_up_grads(rows, grads, inner):
    _, total, width = rows.shape
    tile = width // 4
    out = pl.BlockSpec((1, tile, inner), lambda j, i: (j, i, 0))
    return pl.pallas_call(
        gate_up_kernel,
        grid=(EXP_DEV, 4),
        in_specs=[
            pl.BlockSpec((1, total, tile), lambda j, i: (j, 0, i)),
            pl.BlockSpec((1, total, grads.shape[2]), lambda j, i: (j, 0, 0)),
        ],
        out_specs=[out, out],
        out_shape=[jax.ShapeDtypeStruct((EXP_DEV, width, inner), F32)] * 2,
        compiler_params=params(),
        name="gate_up_grads",
    )(rows, grads)


def body(
    hidden,
    cotangent,
    segments,
    routes,
    w_query,
    w_latent,
    g_latent,
    w_expand,
    w_out,
    g_attn,
    g_ffn,
    w_router,
    s_gate,
    s_up,
    s_down,
    e_gate,
    expert_up_weight,
    e_down,
):
    tokens = hidden.shape[1]
    width = hidden.shape[2]
    links = Links()
    shards, groups = links.shards, links.groups
    devices = groups * shards
    experts = EXP_DEV * groups
    capacity = max(2, tokens * TOP * 4 // (3 * experts))
    heads = H // shards
    length = tokens * shards
    part = width // shards
    my_shard = lax.axis_index("shard")
    my_group = lax.axis_index("expert")
    hid_shard = s_down.shape[0]
    hid = hid_shard // groups
    latent_part = KVR // shards
    shard_at, slot_at = links.shard_at(), links.slot_at()

    router_rows = part * experts // width
    small_rows = jnp.concatenate([g_attn, g_ffn, g_latent])
    small_rows = jnp.pad(small_rows, (0, -small_rows.shape[0] % width)).reshape(-1, width)
    packed = jnp.concatenate([w_router.reshape(router_rows, width), small_rows])
    packed = links.gather_shard(jnp.pad(packed, ((0, -packed.shape[0] % 16), (0, 0))))
    hidden_all = links.gather_shard(hidden[0]).reshape(length, width)
    pieces = lambda w: jnp.stack(jnp.split(w, shards, axis=1))
    wl = links.gather_shard(w_latent.T)
    wq = links.spread_shard(pieces(w_query))
    we = links.spread_shard(pieces(w_expand))
    g_all = links.gather_plain(cotangent[0]).reshape(devices, tokens, width)
    packed = jnp.take(packed, slot_at, axis=0)
    full_router = packed[:, :router_rows].reshape(width, experts)
    gains_in = packed[:, router_rows:].reshape(shards, -1)
    gattn = gains_in[:, :part].reshape(1, width).astype(F32)
    gffn = gains_in[:, part : 2 * part].reshape(width).astype(F32)
    glatent = gains_in[:, 2 * part : 2 * part + latent_part].reshape(1, KVR).astype(F32)

    order = links.order()
    same = jnp.arange(devices, dtype=jnp.int32)
    back_order = jnp.sum(
        jnp.where(order[:, None] == same[None, :], same[:, None], 0), axis=0
    ).astype(jnp.int32)
    local_routes = routes[0]
    flat_routes = local_routes.reshape(-1)
    choose = local_routes[:, :, None] == jnp.arange(experts, dtype=jnp.int32)[None, None, :]
    hits = choose.reshape(-1, experts).astype(F32)
    pair_count = tokens * TOP
    before_it = (
        lax.broadcasted_iota(jnp.int32, (pair_count, pair_count), 1)
        < lax.broadcasted_iota(jnp.int32, (pair_count, pair_count), 0)
    ).astype(BF)
    before = mm(before_it, hits.astype(BF))
    slot_rank = jnp.sum(before * hits, axis=1).astype(jnp.int32)
    slot_of = (flat_routes * capacity + slot_rank).reshape(tokens, TOP)
    slots = EXP_DEV * capacity
    slot_rows = jnp.pad(slot_of.T, ((0, 8 - TOP), (0, 0)), constant_values=-1)
    slots_all = exchange(jnp.broadcast_to(slot_rows[None], (devices, 8, tokens)), BOTH)
    slots_all = jnp.take(slots_all, order, axis=0)[:, :TOP]
    slot_ids = my_group * slots + jnp.arange(slots, dtype=jnp.int32)
    pick = jnp.any(
        slots_all[:, None] == slot_ids[None, :, None, None], axis=2
    ).astype(BF)

    positions = (shard_at[:, None] * tokens + jnp.arange(tokens, dtype=jnp.int32)).reshape(-1)
    cosine, sine_vals = rope_angles(positions)
    segs = jnp.take(segments.reshape(shards, tokens), shard_at, axis=0).reshape(-1)
    col = jnp.stack([segs, positions], axis=1)
    row = jnp.stack([segs, positions], axis=0)
    attn_part, n1, compressed, latent, attended, query, kv, lse = attention_forward(
        slot_at, hidden_all, gattn, glatent, wq, wl, we, w_out, cosine, sine_vals, col, row
    )
    inner_units = e_gate.shape[2]
    work_g = Fill(lambda p, g, w: grad_rows_of(p, g, w, capacity), pick, g_all, e_down)
    attn_out = links.sum_shard(attn_part.reshape(shards, tokens, width), work_g)
    grad_rows, grad_inner = work_g.result

    residual_in = hidden[0].astype(F32)
    residual_mid = residual_in + attn_out
    unit_two, factor_two = norm_forward(residual_mid)
    normed_two = (unit_two * gffn).astype(BF)

    def shared_pieces(gate_of, up_of):
        mine = lambda w: lax.dynamic_slice_in_dim(
            w.reshape(part, shards, hid_shard), my_group * hid, hid, 2
        )
        return jnp.concatenate([mine(gate_of), mine(up_of)], axis=2).transpose(1, 0, 2)

    def pad_lanes(gate_of, up_of):
        lane_pad = ((0, 0), (0, 0), (0, -inner_units % PAD))
        return jnp.concatenate([jnp.pad(gate_of, lane_pad), jnp.pad(up_of, lane_pad)], axis=2)

    shared_down = lax.dynamic_slice_in_dim(s_down, my_group * hid, hid, 0)
    work = [
        Fill(shared_pieces, s_gate, s_up),
        Fill(pad_lanes, e_gate, expert_up_weight),
        Fill(lambda g, w: mm_nt(g.reshape(-1, width), w), g_all, shared_down),
    ]
    n2_all = links.gather_all(normed_two, list(enumerate(work, 1))).reshape(
        devices, tokens, width
    )
    gate_up, both_weights, shared_grad_inner = (w.result for w in work)
    shared_in = links.spread_shard(gate_up)
    shared_in = jnp.take(shared_in, slot_at, axis=0).reshape(width, 2 * hid)
    probs = jax.nn.sigmoid(mm(normed_two, full_router))
    chosen = jnp.sum(jnp.where(choose, probs[:, None, :], 0.0), axis=-1)
    chosen_total = jnp.sum(chosen, axis=1, keepdims=True)

    shared_pre = mm(
        n2_all.reshape(-1, width), jnp.concatenate([shared_in, full_router], axis=1)
    )
    probs_all = jax.nn.sigmoid(
        shared_pre[:, 2 * hid :].reshape(devices, tokens, experts).transpose(0, 2, 1)
    )
    named = jnp.any(
        (slots_all // capacity)[:, None]
        == jnp.arange(experts, dtype=jnp.int32)[None, :, None, None],
        axis=2,
    )
    totals = jnp.sum(jnp.where(named, probs_all, 0.0), axis=1, keepdims=True)
    local_probs = lax.dynamic_slice_in_dim(probs_all, my_group * EXP_DEV, EXP_DEV, 1)
    local_weights = local_probs / totals * ROUTE_SCALE
    slot_weight = jnp.sum(
        jnp.where(
            pick.reshape(devices, EXP_DEV, capacity, tokens) > 0,
            local_weights[:, :, None, :],
            0.0,
        ),
        axis=3,
    )
    row_weight = slot_weight.transpose(1, 0, 2).reshape(EXP_DEV, devices * capacity, 1)

    rows, inner_w, grads_b, grad_slot_weight = inner_of(
        pick, n2_all, both_weights, row_weight, grad_inner, inner_units, capacity
    )

    s_inner, s_slope_gate, s_slope_up = swish_parts(
        shared_pre[:, :hid], shared_pre[:, hid : 2 * hid]
    )
    shared_inner = s_inner.astype(BF)
    shared_grads = jnp.concatenate(
        [shared_grad_inner * s_slope_gate, shared_grad_inner * s_slope_up], axis=1
    ).astype(BF)

    dn2_own, dn2_other = back_rows(
        pick, grads_b, both_weights, shared_grads.reshape(devices, tokens, 2 * hid),
        shared_in.T, capacity,
    )

    d_shared_down = mm_tn(shared_inner, g_all.reshape(-1, width)).astype(BF)
    down_all = lax.all_gather(d_shared_down, "expert", axis=0, tiled=True)

    def shared_grads_of(grads_of, rows_of):
        out = mm_tn(grads_of, rows_of.reshape(-1, width)).astype(BF)
        return out.reshape(2 * hid, shards, part).transpose(1, 0, 2)

    def router_back(slot_sums):
        slot_back = slot_sums.reshape(EXP_DEV, devices, capacity).transpose(1, 0, 2)
        slot_back = jnp.take(slot_back.reshape(devices, slots), back_order, axis=0)
        got = exchange(slot_back, BOTH)
        slot_grads = jnp.sum(got.reshape(groups, shards, slots), axis=1).reshape(-1)
        at_slot = slot_of[:, :, None] == jnp.arange(experts * capacity, dtype=jnp.int32)
        grad_weights = jnp.sum(jnp.where(at_slot, slot_grads, 0.0), axis=2)
        grad_chosen = ROUTE_SCALE * (
            grad_weights / chosen_total
            - jnp.sum(grad_weights * chosen, axis=1, keepdims=True)
            / (chosen_total * chosen_total)
        )
        grad_probs = jnp.sum(jnp.where(choose, grad_chosen[:, :, None], 0.0), axis=1)
        return (grad_probs * probs * (1.0 - probs)).astype(BF)

    def outputs(inner_of, shared_of):
        weighted_out = jnp.einsum(
            "jmf,jfd->jmd", inner_of, e_down, preferred_element_type=F32
        ).astype(BF)
        return place_rows(
            pick, weighted_out, shared_of.reshape(devices, tokens, hid), shared_down, order,
            capacity,
        )

    down_grad = lambda a, b: jnp.einsum("jmf,jmd->jfd", a, b, preferred_element_type=F32)
    ring_shape = (groups, shards // 2, tokens, width)
    work = [
        Fill(
            lambda a, b, c: (shared_grads_of(a, b), router_back(c)),
            shared_grads, n2_all, grad_slot_weight,
        ),
        Fill(outputs, inner_w, shared_inner),
        Fill(lambda a, b: gate_up_grads(a, b, inner_units), rows, grads_b),
        Fill(down_grad, inner_w, grad_rows),
    ]
    dn2 = links.sum_all(
        dn2_own.reshape(ring_shape),
        dn2_other.reshape(ring_shape),
        [(groups // 2 - i, w) for i, w in enumerate(work)],
    )
    (shared_out, grad_logits), out_part, (d_egate, grad_expert_up), d_edown = (
        w.result for w in work
    )
    logits_back = exchange(
        jnp.broadcast_to(grad_logits.T[None], (devices, experts, tokens)), BOTH
    )
    logits_back = jnp.take(logits_back, order, axis=0)
    in_pieces = jnp.take(links.spread_shard(shared_out), slot_at, axis=0)
    in_all = lax.all_gather(in_pieces, "expert", axis=0, tiled=False)

    grad_normed_two = dn2 + mm_nt(grad_logits, full_router)
    grad_mid_norm, d_gffn = norm_backward(grad_normed_two, gffn, unit_two, factor_two)
    grad_mid = cotangent[0].astype(F32) + grad_mid_norm
    grad_attn = links.gather_shard(grad_mid.astype(BF)).reshape(length, width)
    grad_attn, out_part = tie(grad_attn, out_part)
    routed_shared = lax.psum_scatter(
        out_part, BOTH, scatter_dimension=0, tiled=False
    ).astype(F32)
    output_rows = residual_mid + routed_shared
    own_columns = lax.dynamic_slice_in_dim(n2_all, my_shard * part, part, 2)
    d_router = mm(
        logits_back.transpose(1, 0, 2).reshape(experts, -1), own_columns.reshape(-1, part)
    ).T

    dn1, dw, dwl, d_out, d_glatent = attention_backward(
        slot_at, grad_attn, glatent, w_out, attended, query, kv, lse, latent, compressed,
        we, wl, wq, n1, cosine, sine_vals, col, row,
    )
    (dn1, dw, dwl, d_out), (in_all, down_all) = tie(
        (dn1, dw, dwl, d_out), (in_all, down_all)
    )
    grad_normed = links.sum_shard(dn1.reshape(shards, tokens, width))
    unit_one, factor_one = norm_forward(residual_in)
    grad_input_norm, d_gattn = norm_backward(
        grad_normed, gattn.reshape(width), unit_one, factor_one
    )
    grad_input = grad_mid + grad_input_norm

    cut = part // groups
    lat = links.sum_shard(dwl).astype(BF).reshape(groups, (KVR + DR) // groups, part)
    by_head = links.blocks(dw.reshape(shards, groups, cut, -1).transpose(1, 0, 2, 3))
    by_row = links.blocks(d_out.reshape(groups, cut, width))
    pluses = [groups // 2, (groups - 1) // 2]
    work_s = Fill(shared_finish, in_all)
    sum_head, sum_row = links.ring_reduce(
        [by_head, by_row], pluses, [(groups // 2 - 1, work_s)]
    )
    (sum_lat,) = links.ring_reduce([links.blocks(lat)], pluses[1:])
    part_sgate, part_sup = work_s.result
    sum_head = links.exchange_shard(sum_head.astype(BF))
    all_head, all_row = links.ring_gather([sum_head, sum_row.astype(BF)], pluses)
    (all_lat,) = links.ring_gather([sum_lat.astype(BF)], pluses[1:])
    part_query, part_expand, part_out = finish(
        links.block_at(), all_head, all_row, heads, width
    )
    part_latent = jnp.take(jnp.stack(all_lat), links.block_at(), axis=0)
    part_latent = part_latent.reshape(KVR + DR, part).astype(F32)

    gain_grads = jnp.concatenate(
        [
            d_gattn.reshape(shards, part),
            d_gffn.reshape(shards, part),
            d_glatent.reshape(shards, latent_part),
        ],
        axis=1,
    )
    got = exchange(
        jnp.broadcast_to(gain_grads[None], (groups,) + gain_grads.shape).reshape(devices, -1),
        BOTH,
    )
    gains = jnp.sum(got, axis=0)
    return (
        output_rows.astype(BF)[None],
        grad_input[None],
        part_query,
        part_latent.T,
        gains[2 * part :],
        part_expand,
        part_out,
        gains[:part],
        gains[part : 2 * part],
        d_router,
        part_sgate,
        part_sup,
        down_all.astype(F32),
        d_egate,
        grad_expert_up,
        d_edown,
    )


def solution(mesh):
    return jax.shard_map(
        body,
        mesh=mesh,
        in_specs=(
            P("expert", "shard", None),
            P("expert", "shard", None),
            P("expert", None),
            P("expert", "shard", None),
            P("shard", None),
            P("shard", None),
            P("shard"),
            P("shard", None),
            P("shard", None),
            P("shard"),
            P("shard"),
            P("shard", None),
            P("shard", None),
            P("shard", None),
            P("shard", None),
            P("expert", None, "shard"),
            P("expert", None, "shard"),
            P("expert", "shard", None),
        ),
        out_specs=(
            P("expert", "shard", None),
            P("expert", "shard", None),
            P("shard", None),
            P("shard", None),
            P("shard"),
            P("shard", None),
            P("shard", None),
            P("shard"),
            P("shard"),
            P("shard", None),
            P("shard", None),
            P("shard", None),
            P("shard", None),
            P("expert", None, "shard"),
            P("expert", None, "shard"),
            P("expert", "shard", None),
        ),
        check_vma=False,
    )
```

```python
import functools

import jax
import jax.numpy as jnp
from jax import lax
from jax.experimental import pallas as pl
from jax.experimental.pallas import tpu as pltpu
from jax.sharding import PartitionSpec as P

H = 16
DN = 128
DR = 64
DV = 128
KVR = 512
TOP = 6
EXP_DEV = 4

EPS = 1e-06
ROUTE_SCALE = 2.446
ROPE_BASE = 50000.0
SCORE_SCALE = (DN + DR) ** (-0.5)
BF = jnp.bfloat16
F32 = jnp.float32
BOTH = ("expert", "shard")
VMEM_BYTES = 56 * 1024 * 1024


def mm(a, b):
    return jnp.dot(a, b, preferred_element_type=F32)


def mm_tn(a, b):
    return lax.dot_general(a, b, (((0,), (0,)), ((), ())), preferred_element_type=F32)


def mm_nt(a, b):
    return lax.dot_general(a, b, (((1,), (1,)), ((), ())), preferred_element_type=F32)


def rope_angles(positions):
    half_width = DR // 2
    inverse = ROPE_BASE ** (-jnp.arange(half_width).astype(F32) / half_width)
    angles = positions.astype(F32)[:, None] * inverse[None, :]
    return (jnp.cos(angles), jnp.sin(angles))


def rotate(values, cosine, sine_vals):
    half_width = DR // 2
    first_half = values[..., :half_width]
    second_half = values[..., half_width:]
    return jnp.concatenate(
        [
            first_half * cosine - second_half * sine_vals,
            second_half * cosine + first_half * sine_vals,
        ],
        axis=-1,
    )


def norm_forward(values):
    factor = lax.rsqrt(jnp.mean(values * values, axis=-1, keepdims=True) + EPS)
    return values * factor, factor


def norm_backward(grad_out, gain_vec, unit_vals, factor):
    grad_unit = grad_out * gain_vec
    grad_in = factor * (
        grad_unit - unit_vals * jnp.mean(grad_unit * unit_vals, axis=-1, keepdims=True)
    )
    return (grad_in, jnp.sum(grad_out * unit_vals, axis=0))


def swish_parts(gate, up):
    sig = jax.nn.sigmoid(gate)
    silu = gate * sig
    return silu * up, up * sig * (1.0 + gate * (1.0 - sig)), silu


def exchange(values, axis):
    return lax.all_to_all(values, axis, split_axis=0, concat_axis=0, tiled=True)


def tie(streams, extra):
    return lax.optimization_barrier((streams, extra))


class Fill:
    def __init__(self, work, *inputs):
        self.work, self.inputs, self.result = work, inputs, None


class Links:
    def __init__(self):
        self.groups = lax.axis_size("expert")
        self.shards = lax.axis_size("shard")
        self.rows = self.shards // 2
        n = self.groups
        self.ring = list(range(0, n, 2)) + list(range(n - 1, 0, -2))
        shard = lax.axis_index("shard")
        self.x = shard // 2
        self.core = shard % 2
        group = lax.axis_index("expert")
        places = [self.ring.index(e) for e in range(n)]
        self.place = jnp.sum(
            jnp.where(jnp.arange(n) == group, jnp.array(places, jnp.int32), 0)
        )

    def send(self, values, target):
        pairs = []
        for e in range(self.groups):
            for s in range(self.shards):
                pairs.append((e * self.shards + s, target(e, s)))
        return lax.ppermute(values, BOTH, pairs)

    def around(self, values, step):
        n = self.groups
        return self.send(
            values,
            lambda e, s: self.ring[(self.ring.index(e) + step) % n] * self.shards + s,
        )

    def along_x(self, values, step):
        return self.send(
            values,
            lambda e, s: e * self.shards + ((s // 2 + step) % self.rows) * 2 + s % 2,
        )

    def partner(self, values):
        return self.send(values, lambda e, s: e * self.shards + (s ^ 1))

    def shard_at(self):
        xs = (self.x - jnp.arange(self.rows, dtype=jnp.int32)) % self.rows
        cores = jnp.stack([self.core, 1 - self.core]).astype(jnp.int32)
        return (xs[:, None] * 2 + cores[None, :]).reshape(-1).astype(jnp.int32)

    def slot_at(self):
        shard = jnp.arange(self.shards, dtype=jnp.int32)
        back = (self.x - shard // 2) % self.rows
        return (back * 2 + (shard % 2 != self.core)).astype(jnp.int32)

    def gather_shard(self, values):
        out = []
        for k in range(self.rows):
            own = values if k == 0 else self.along_x(values, k)
            out += [own, self.partner(own)]
        return jnp.stack(out)

    def spread_shard(self, pieces):
        take = lambda v, i: lax.dynamic_index_in_dim(v, i, 0, keepdims=False)
        pairs = pieces.reshape((self.rows, 2) + pieces.shape[1:])
        out = []
        for k in range(self.rows):
            got = take(pairs, (self.x + k) % self.rows)
            got = got if k == 0 else self.along_x(got, k)
            out += [take(got, self.core), self.partner(take(got, 1 - self.core))]
        return jnp.stack(out)

    def spread_shard_ring(self, pieces):
        n, rows = self.groups, self.rows
        take = lambda v, i, axis: lax.dynamic_index_in_dim(v, i, axis, keepdims=False)
        part, wide = pieces.shape[1:]
        pairs = pieces.reshape(rows, 2, n, part // n, wide)
        mine = take(pairs, self.place, 2)
        out = []
        for k in range(rows):
            if k == 0:
                got = take(pairs, self.x, 0)
            else:
                far = self.along_x(take(mine, (self.x + k) % rows, 0), k)
                (far,) = self.ring_gather([far], [n // 2])
                got = jnp.take(jnp.stack(far, axis=1), self.block_at(), axis=1)
            got = got.reshape(2, part, wide)
            out += [take(got, self.core, 0), self.partner(take(got, 1 - self.core, 0))]
        return jnp.stack(out)

    def exchange_shard(self, values):
        pairs = values.reshape((self.rows, 2) + values.shape[1:])
        out = []
        for k in range(self.rows):
            got = pairs[k] if k == 0 else self.along_x(pairs[k], -k)
            out += [got[0], self.partner(got[1])]
        xs = (self.x + jnp.arange(self.rows, dtype=jnp.int32)) % self.rows
        shard = jnp.arange(self.shards, dtype=jnp.int32)
        ahead = (shard // 2 - self.x) % self.rows
        slot = ahead * 2 + (shard % 2 != self.core)
        return jnp.take(jnp.stack(out), slot, axis=0)

    def sum_shard(self, values, fill=None):
        pairs = values.reshape((self.rows, 2) + values.shape[1:])
        both = [
            pairs[k, 0].astype(F32) + self.partner(pairs[k, 1]).astype(F32)
            for k in range(self.rows)
        ]
        far = [v.astype(BF) for v in both[1:]]
        if fill is not None:
            _, inputs = tie(far, fill.inputs)
        far = [self.along_x(v, -k - 1) for k, v in enumerate(far)]
        if fill is not None:
            far, fill.result = tie(far, fill.work(*inputs))
        total = both[0]
        for v in far:
            total = total + v.astype(F32)
        return total

    def ring_gather(self, values, pluses, fills=()):
        n = self.groups
        fills = dict(fills)
        outs = [[v] + [None] * (n - 1) for v in values]
        ahead, back = list(values), list(values)
        for r in range(1, n):
            moves = [(i, 1) for i, p in enumerate(pluses) if r <= p]
            moves += [(i, -1) for i, p in enumerate(pluses) if r <= n - 1 - p]
            if not moves:
                break
            streams = [ahead[i] if step > 0 else back[i] for i, step in moves]
            streams = self.step(streams, [step for _, step in moves], fills.get(r))
            for (i, step), got in zip(moves, streams):
                if step > 0:
                    ahead[i] = outs[i][r] = got
                else:
                    back[i] = outs[i][n - r] = got
        return outs

    def step(self, streams, steps, fill):
        if fill is None:
            return [self.around(v, s) for v, s in zip(streams, steps)]
        streams, inputs = tie(streams, fill.inputs)
        streams = [self.around(v, s) for v, s in zip(streams, steps)]
        streams, fill.result = tie(streams, fill.work(*inputs))
        return streams

    def ring_reduce(self, parts, pluses, fills=()):
        n = self.groups
        fills = dict(fills)
        ahead = [p[plus] for p, plus in zip(parts, pluses)]
        back = [p[plus + 1] for p, plus in zip(parts, pluses)]
        most = max(max(p, n - 1 - p) for p in pluses)
        for r in range(most, 0, -1):
            moves = [(i, 1) for i, p in enumerate(pluses) if r <= p]
            moves += [(i, -1) for i, p in enumerate(pluses) if r <= n - 1 - p]
            streams = [ahead[i] if step > 0 else back[i] for i, step in moves]
            streams = self.step(streams, [-step for _, step in moves], fills.get(r))
            for (i, step), got in zip(moves, streams):
                here = parts[i][r - 1 if step > 0 else (n - r + 1) % n]
                if r > 1:
                    got = (got.astype(F32) + here.astype(F32)).astype(BF)
                if step > 0:
                    ahead[i] = got
                else:
                    back[i] = got
        return [
            p[0].astype(F32) + a.astype(F32) + b.astype(F32)
            for p, a, b in zip(parts, ahead, back)
        ]

    def block_at(self):
        return (self.place - jnp.arange(self.groups, dtype=jnp.int32)) % self.groups

    def blocks(self, values):
        return [
            lax.dynamic_index_in_dim(
                values, (self.place - r) % self.groups, 0, keepdims=False
            )
            for r in range(self.groups)
        ]

    def order(self):
        n = self.groups
        ring = jnp.array(self.ring, jnp.int32)
        groups = jnp.sum(
            jnp.where(self.block_at()[:, None] == jnp.arange(n)[None, :], ring[None, :], 0),
            axis=1,
        )
        shard = self.shard_at().reshape(self.rows, 2).T.reshape(-1)
        all_of = groups[:, None] * self.shards + shard[None, :]
        return all_of.reshape(-1).astype(jnp.int32)

    def gather_all(self, values, fills=()):
        n, rows = self.groups, self.rows
        tokens, width = values.shape
        half = tokens // 2
        first, second = values[:half], values[half:]
        spread = jnp.stack([first] + [self.along_x(first, k) for k in range(1, rows)])
        upper, lower = self.ring_gather(
            [spread, second], [n // 2, (n - 1) // 2], fills
        )
        out = jnp.zeros((n, 2, rows, tokens, width), values.dtype)
        steps = [0] + [r for k in range(1, n // 2 + 1) for r in dict.fromkeys((k, n - k))]
        for r in steps:
            low = jnp.stack(
                [lower[r]] + [self.along_x(lower[r], k) for k in range(1, rows)]
            )
            own = jnp.concatenate([upper[r], low], axis=1)
            out = lax.dynamic_update_slice(out, own[None, None], (r, 0, 0, 0, 0))
            out = lax.dynamic_update_slice(
                out, self.partner(own)[None, None], (r, 1, 0, 0, 0)
            )
        return out

    def sum_all(self, own, other, fills=()):
        n, rows = self.groups, self.rows
        both = (own.astype(F32) + self.partner(other).astype(F32)).astype(BF)
        (top,) = self.ring_reduce([[both[r] for r in range(n)]], [n // 2], fills)
        total = top[0]
        for k in range(1, rows):
            total = total + self.along_x(top[k].astype(BF), -k).astype(F32)
        return total


def params(**kw):
    return pltpu.CompilerParams(vmem_limit_bytes=VMEM_BYTES, **kw)


SMEM = pl.BlockSpec(memory_space=pltpu.SMEM)
VMEM = pl.BlockSpec(memory_space=pltpu.VMEM)


def allowed_mask(seg_col, seg_row, pos_col, pos_row):
    return (seg_col == seg_row) & (pos_row <= pos_col)


def attention_forward_kernel(
    slot_ref, x_ref, gattn_ref, glat_ref, wq_ref, wl_ref, we_ref, wo_ref,
    cos_ref, sin_ref, col_ref, row_ref,
    out_ref, n1_ref, c_ref, lat_ref, o_ref, q_ref, kv_ref, lse_ref,
):
    shards, part = wq_ref.shape[0], wq_ref.shape[1]
    heads = q_ref.shape[0]
    tokens = x_ref.shape[0] // shards
    for b in range(shards):
        at = slice(b * tokens, (b + 1) * tokens)
        unit, _ = norm_forward(x_ref[at].astype(F32))
        n1_ref[at] = (unit * gattn_ref[...]).astype(BF)
    queries, compressed, kv_all = None, None, None
    for s in range(shards):
        left = n1_ref[:, s * part : (s + 1) * part]
        one = mm(left, wq_ref[slot_ref[s]])
        queries = one if s == 0 else queries + one
        one = mm_nt(left, wl_ref[slot_ref[s]])
        compressed = one if s == 0 else compressed + one
    c_ref[...] = compressed
    unit, _ = norm_forward(compressed[:, :KVR])
    lat_ref[:, :KVR] = (unit * glat_ref[...]).astype(BF)
    lat_ref[:, KVR:] = rotate(compressed[:, KVR:], cos_ref[...], sin_ref[...]).astype(BF)
    part = KVR // shards
    for s in range(shards):
        one = mm(lat_ref[:, s * part : (s + 1) * part], we_ref[slot_ref[s]])
        kv_all = one if s == 0 else kv_all + one
    kv_ref[...] = kv_all.astype(BF)
    ok = allowed_mask(
        col_ref[:, :1], row_ref[:1, :], col_ref[:, 1:2], row_ref[1:2, :]
    )
    key_rot = lat_ref[:, KVR:]
    for h in range(heads):
        at = h * (DN + DR)
        query = jnp.concatenate(
            [
                queries[:, at : at + DN],
                rotate(queries[:, at + DN : at + DN + DR], cos_ref[...], sin_ref[...]),
            ],
            axis=1,
        ).astype(BF)
        q_ref[h] = query
        at = h * (DN + DV)
        keys = kv_ref[:, at : at + DN]
        values = kv_ref[:, at + DN : at + DN + DV]
        scores = mm_nt(query[:, :DN], keys) + mm_nt(query[:, DN:], key_rot)
        scores = jnp.where(ok, scores * SCORE_SCALE, -1e30)
        top = jnp.max(scores, axis=1, keepdims=True)
        expo = jnp.exp(scores - top)
        total = jnp.sum(expo, axis=1, keepdims=True)
        lse_ref[h] = top + jnp.log(total)
        weights = (expo / total).astype(BF)
        o_ref[:, h * DV : (h + 1) * DV] = mm(weights, values).astype(BF)
    out_ref[...] = mm(o_ref[...], wo_ref[...]).astype(BF)


def attention_forward(slot, x, gattn, glat, wq, wl, we, wo, cosine, sine_vals, col, row):
    length, width = x.shape
    heads = wo.shape[0] // DV
    return pl.pallas_call(
        attention_forward_kernel,
        in_specs=[SMEM] + [VMEM] * 11,
        out_shape=[
            jax.ShapeDtypeStruct((length, width), BF),
            jax.ShapeDtypeStruct((length, width), BF),
            jax.ShapeDtypeStruct((length, KVR + DR), F32),
            jax.ShapeDtypeStruct((length, KVR + DR), BF),
            jax.ShapeDtypeStruct((length, heads * DV), BF),
            jax.ShapeDtypeStruct((heads, length, DN + DR), BF),
            jax.ShapeDtypeStruct((length, heads * (DN + DV)), BF),
            jax.ShapeDtypeStruct((heads, length, 1), F32),
        ],
        compiler_params=params(),
        name="attention_forward",
    )(slot, x, gattn, glat, wq, wl, we, wo, cosine, sine_vals, col, row)


def attention_backward_kernel(
    slot_ref, dh_ref, glat_ref, wo_ref, o_ref, q_ref, kv_ref, lse_ref, lat_ref, c_ref,
    we_ref, wl_ref, wq_ref, n1_ref, cos_ref, sin_ref, col_ref, row_ref,
    dn1_ref, dw_ref, dwl_ref, dwo_ref, dgl_ref,
    go_ref, gq_ref, gkv_ref, gc_ref,
):
    shards, part = wq_ref.shape[0], wq_ref.shape[1]
    heads = q_ref.shape[0]
    go_ref[...] = mm_nt(dh_ref[...], wo_ref[...]).astype(BF)
    dwo_ref[...] = mm_tn(o_ref[...], dh_ref[...]).astype(BF)
    ok = allowed_mask(
        col_ref[:, :1], row_ref[:1, :], col_ref[:, 1:2], row_ref[1:2, :]
    )
    key_rot = lat_ref[:, KVR:]
    grad_kr = None
    for h in range(heads):
        at = h * (DN + DV)
        keys = kv_ref[:, at : at + DN]
        values = kv_ref[:, at + DN : at + DN + DV]
        query = q_ref[h]
        grad_o = go_ref[:, h * DV : (h + 1) * DV]
        scores = mm_nt(query[:, :DN], keys) + mm_nt(query[:, DN:], key_rot)
        weights = jnp.where(ok, jnp.exp(scores * SCORE_SCALE - lse_ref[h]), 0.0)
        grad_w = mm_nt(grad_o, values)
        delta = jnp.sum(weights * grad_w, axis=1, keepdims=True)
        grad_s = (weights * (grad_w - delta) * SCORE_SCALE).astype(BF)
        gkv_ref[:, at : at + DN] = mm_tn(grad_s, query[:, :DN]).astype(BF)
        gkv_ref[:, at + DN : at + DN + DV] = mm_tn(weights.astype(BF), grad_o).astype(BF)
        one = mm_tn(grad_s, query[:, DN:])
        grad_kr = one if h == 0 else grad_kr + one
        at = h * (DN + DR)
        grad_qr = rotate(mm(grad_s, key_rot), cos_ref[...], -sin_ref[...])
        gq_ref[:, at : at + DN + DR] = jnp.concatenate(
            [mm(grad_s, keys), grad_qr], axis=1
        ).astype(BF)
    latent_part = KVR // shards
    query_wide = heads * (DN + DR)
    ratio = part // latent_part
    piece = heads * (DN + DV) // ratio
    grad_lat = []
    for s in range(shards):
        at = slice(s * latent_part, (s + 1) * latent_part)
        grad_lat.append(mm_nt(gkv_ref[...], we_ref[slot_ref[s]]))
        one = mm_tn(lat_ref[:, at], gkv_ref[...]).astype(BF)
        for i in range(ratio):
            dw_ref[slot_ref[s], i * latent_part : (i + 1) * latent_part, query_wide:] = one[
                :, i * piece : (i + 1) * piece
            ]
    grad_lat = jnp.concatenate(grad_lat, axis=1)
    unit, factor = norm_forward(c_ref[:, :KVR])
    grad_norm, grad_gain = norm_backward(grad_lat, glat_ref[...], unit, factor)
    dgl_ref[...] = grad_gain.reshape(1, KVR)
    gc_ref[:, :KVR] = grad_norm.astype(BF)
    gc_ref[:, KVR:] = rotate(grad_kr, cos_ref[...], -sin_ref[...]).astype(BF)
    for s in range(shards):
        at = slice(s * part, (s + 1) * part)
        dn1_ref[:, at] = (
            mm_nt(gq_ref[...], wq_ref[slot_ref[s]]) + mm(gc_ref[...], wl_ref[slot_ref[s]])
        ).astype(BF)
        dw_ref[slot_ref[s], :, :query_wide] = mm_tn(n1_ref[:, at], gq_ref[...]).astype(BF)
        dwl_ref[slot_ref[s]] = mm_tn(gc_ref[...], n1_ref[:, at]).astype(BF)


def attention_backward(
    slot, dh, glat, wo, o, query, kv, lse, latent, compressed, we, wl, wq, n1,
    cosine, sine_vals, col, row,
):
    length, width = n1.shape
    heads = query.shape[0]
    shards, part = wq.shape[0], wq.shape[1]
    wide = heads * (DN + DR) + heads * (DN + DV) * KVR // width
    return pl.pallas_call(
        attention_backward_kernel,
        in_specs=[SMEM] + [VMEM] * 17,
        out_shape=[
            jax.ShapeDtypeStruct((length, width), BF),
            jax.ShapeDtypeStruct((shards, part, wide), BF),
            jax.ShapeDtypeStruct(wl.shape, BF),
            jax.ShapeDtypeStruct((heads * DV, width), BF),
            jax.ShapeDtypeStruct((1, KVR), F32),
        ],
        scratch_shapes=[
            pltpu.VMEM((length, heads * DV), BF),
            pltpu.VMEM((length, heads * (DN + DR)), BF),
            pltpu.VMEM((length, heads * (DN + DV)), BF),
            pltpu.VMEM((length, KVR + DR), BF),
        ],
        compiler_params=params(),
        name="attention_backward",
    )(
        slot, dh, glat, wo, o, query, kv, lse, latent, compressed, we, wl, wq, n1,
        cosine, sine_vals, col, row,
    )


def finish_kernel(groups, shards, per, piece, *refs):
    place_ref = refs[0]
    by_head, by_row = (refs[1 + i * groups : 1 + (i + 1) * groups] for i in range(2))
    query_ref, expand_ref, out_ref = refs[1 + 2 * groups :]
    cut = by_row[0].shape[0]
    wide = by_head[0].shape[2] - piece
    expand_wide = expand_ref.shape[1] // shards
    for r in range(groups):
        at = place_ref[r]
        rows = pl.ds(pl.multiple_of(at * cut, cut), cut)
        out_ref[rows, :] = by_row[r][...].astype(F32)
        low = pl.ds(pl.multiple_of((at % per) * cut, cut), cut)
        for s in range(shards):
            query_ref[rows, s * wide : (s + 1) * wide] = by_head[r][s, :, :wide].astype(F32)
            lanes = pl.ds(
                pl.multiple_of(s * expand_wide + (at // per) * piece, piece), piece
            )
            expand_ref[low, lanes] = by_head[r][s, :, wide:].astype(F32)


def finish(place, by_head, by_row, heads, width):
    groups, shards = len(by_head), by_head[0].shape[0]
    latent_part = KVR // shards
    part = width // shards
    per = groups * latent_part // part
    piece = heads * (DN + DV) * latent_part // part
    return pl.pallas_call(
        functools.partial(finish_kernel, groups, shards, per, piece),
        in_specs=[SMEM] + [VMEM] * (2 * groups),
        out_shape=[
            jax.ShapeDtypeStruct((part, H * (DN + DR)), F32),
            jax.ShapeDtypeStruct((latent_part, H * (DN + DV)), F32),
            jax.ShapeDtypeStruct((part, width), F32),
        ],
        compiler_params=params(),
        name="finish",
    )(place, *by_head, *by_row)


def shared_finish_kernel(x_ref, gate_ref, up_ref, hold_ref):
    groups, shards, hid = x_ref.shape[0], x_ref.shape[1], x_ref.shape[2] // 2
    for i, out_ref in ((0, gate_ref), (1, up_ref)):
        for s in range(shards):
            for g in range(groups):
                at = (s * groups + g) * hid
                hold_ref[at : at + hid] = x_ref[g, s, i * hid : (i + 1) * hid].astype(F32)
        out_ref[...] = hold_ref[...].T


def shared_finish(pieces):
    groups, shards, two, part = pieces.shape
    wide = groups * shards * two // 2
    return pl.pallas_call(
        shared_finish_kernel,
        in_specs=[VMEM],
        out_shape=[jax.ShapeDtypeStruct((part, wide), F32)] * 2,
        scratch_shapes=[pltpu.VMEM((wide, part), F32)],
        compiler_params=params(),
        name="shared_finish",
    )(pieces)


STEP = 8
PAD = 128


def pick_into(out_ref, pick, rows_of, i, step):
    capacity = out_ref.shape[1] // step
    rows = mm(pick, rows_of).astype(BF)
    out_ref[:, i * capacity : (i + 1) * capacity, :] = rows.reshape(
        EXP_DEV, capacity, rows.shape[1]
    )


def place_from(rows_ref, pick, i, step):
    capacity = rows_ref.shape[1] // step
    rows = rows_ref[:, i * capacity : (i + 1) * capacity, :]
    return mm_tn(pick, rows.reshape(EXP_DEV * capacity, rows.shape[2]))


def resident(shape):
    return pl.BlockSpec(
        shape, lambda *_: (0,) * len(shape), pipeline_mode=pl.Buffered(1)
    )


def grad_rows_kernel(pick_ref, g_ref, down_ref, rows_ref, inner_ref):
    inner = down_ref.shape[1]
    for i in range(STEP):
        pick_into(rows_ref, pick_ref[i], g_ref[i], i, STEP)
    for j in range(EXP_DEV):
        inner_ref[j, :, :inner] = mm_nt(rows_ref[j], down_ref[j])


def grad_rows_of(pick, g_all, down, capacity):
    devices, slots, tokens = pick.shape
    width, inner = g_all.shape[2], down.shape[1]
    lanes = inner + -inner % PAD
    rows = STEP * capacity
    return pl.pallas_call(
        grad_rows_kernel,
        grid=(devices // STEP,),
        in_specs=[
            pl.BlockSpec((STEP, slots, tokens), lambda d: (d, 0, 0)),
            pl.BlockSpec((STEP, tokens, width), lambda d: (d, 0, 0)),
            resident(down.shape),
        ],
        out_specs=[
            pl.BlockSpec((EXP_DEV, rows, width), lambda d: (0, d, 0)),
            pl.BlockSpec((EXP_DEV, rows, lanes), lambda d: (0, d, 0)),
        ],
        out_shape=[
            jax.ShapeDtypeStruct((EXP_DEV, devices * capacity, width), BF),
            jax.ShapeDtypeStruct((EXP_DEV, devices * capacity, lanes), F32),
        ],
        compiler_params=params(),
        name="grad_rows",
    )(pick, g_all, down)


def stack_weights(w_ref, gate_ref, up_ref):
    inner, lanes = gate_ref.shape[1], w_ref.shape[1] // 2

    @pl.when(pl.program_id(0) == 0)
    def _():
        for j in range(EXP_DEV):
            for i, ref in ((0, gate_ref), (1, up_ref)):
                w_ref[j, i * lanes : i * lanes + inner] = ref[j]
                if lanes > inner:
                    w_ref[j, i * lanes + inner : (i + 1) * lanes] = jnp.zeros(
                        (lanes - inner, w_ref.shape[2]), BF
                    )


def inner_kernel(
    pick_ref, x_ref, gate_ref, up_ref, weight_ref, grad_ref,
    rows_ref, inner_ref, grads_ref, slot_ref, w_ref,
):
    lanes = grad_ref.shape[2]
    inner = inner_ref.shape[2]
    stack_weights(w_ref, gate_ref, up_ref)
    for i in range(STEP):
        pick_into(rows_ref, pick_ref[i], x_ref[i], i, STEP)
    for j in range(EXP_DEV):
        both = mm_nt(rows_ref[j], w_ref[j])
        gate, up = both[:, :inner], both[:, lanes : lanes + inner]
        act, slope_gate, slope_up = swish_parts(gate, up)
        weight = weight_ref[j]
        grad = grad_ref[j, :, :inner]
        slot_ref[j] = jnp.sum(act.astype(BF).astype(F32) * grad, axis=1, keepdims=True)
        inner_ref[j] = (weight * act).astype(BF)
        grad = weight * grad
        if lanes > inner:
            grads_ref[j] = jnp.zeros(grads_ref.shape[1:], BF)
        grads_ref[j, :, :inner] = (grad * slope_gate).astype(BF)
        grads_ref[j, :, lanes : lanes + inner] = (grad * slope_up).astype(BF)


def inner_of(pick, x_all, gate, up, weight, grad, capacity):
    devices, slots, tokens = pick.shape
    width, lanes, inner = x_all.shape[2], grad.shape[2], gate.shape[1]
    rows = STEP * capacity
    total = devices * capacity
    by_rows = lambda n: pl.BlockSpec((EXP_DEV, rows, n), lambda d: (0, d, 0))
    return pl.pallas_call(
        inner_kernel,
        grid=(devices // STEP,),
        in_specs=[
            pl.BlockSpec((STEP, slots, tokens), lambda d: (d, 0, 0)),
            pl.BlockSpec((STEP, tokens, width), lambda d: (d, 0, 0)),
            resident(gate.shape),
            resident(up.shape),
            by_rows(1),
            by_rows(lanes),
        ],
        out_specs=[by_rows(width), by_rows(inner), by_rows(2 * lanes), by_rows(1)],
        out_shape=[
            jax.ShapeDtypeStruct((EXP_DEV, total, width), BF),
            jax.ShapeDtypeStruct((EXP_DEV, total, inner), BF),
            jax.ShapeDtypeStruct((EXP_DEV, total, 2 * lanes), BF),
            jax.ShapeDtypeStruct((EXP_DEV, total, 1), F32),
        ],
        scratch_shapes=[pltpu.VMEM((EXP_DEV, 2 * lanes, width), BF)],
        compiler_params=params(),
        name="inner",
    )(pick, x_all, gate, up, weight, grad)


def back_kernel(
    rows, pick_ref, grads_ref, gate_ref, up_ref, left_ref, right_ref,
    own_ref, other_ref, hold_ref, w_ref,
):
    stack_weights(w_ref, gate_ref, up_ref)
    for j in range(EXP_DEV):
        hold_ref[j] = mm(grads_ref[j], w_ref[j]).astype(BF)
    for i in range(STEP):
        total = place_from(hold_ref, pick_ref[i], i, STEP) + mm(left_ref[i], right_ref[...])
        out_ref = own_ref if i // rows % 2 == 0 else other_ref
        out_ref[i // (2 * rows) * rows + i % rows] = total.astype(BF)


def back_rows(pick, grads, gate, up, left, right, capacity, x_rows):
    devices, slots, tokens = pick.shape
    width, inner = gate.shape[2], left.shape[2]
    rows = STEP * capacity
    return pl.pallas_call(
        functools.partial(back_kernel, x_rows),
        grid=(devices // STEP,),
        in_specs=[
            pl.BlockSpec((STEP, slots, tokens), lambda d: (d, 0, 0)),
            pl.BlockSpec((EXP_DEV, rows, grads.shape[2]), lambda d: (0, d, 0)),
            resident(gate.shape),
            resident(up.shape),
            pl.BlockSpec((STEP, tokens, inner), lambda d: (d, 0, 0)),
            resident(right.shape),
        ],
        out_specs=[pl.BlockSpec((STEP // 2, tokens, width), lambda d: (d, 0, 0))] * 2,
        out_shape=[jax.ShapeDtypeStruct((devices // 2, tokens, width), BF)] * 2,
        scratch_shapes=[
            pltpu.VMEM((EXP_DEV, rows, width), BF),
            pltpu.VMEM((EXP_DEV, grads.shape[2], width), BF),
        ],
        compiler_params=params(),
        name="back_rows",
    )(pick, grads, gate, up, left, right)


def gate_up_kernel(rows_ref, grads_ref, gate_ref, up_ref):
    inner = gate_ref.shape[1]
    both = mm_tn(grads_ref[0], rows_ref[0])
    gate_ref[0] = both[:inner]
    at = grads_ref.shape[2] // 2
    up_ref[0] = both[at : at + inner]


def gate_up_grads(rows, grads, inner):
    _, total, width = rows.shape
    tile = width // 4
    out = pl.BlockSpec((1, inner, tile), lambda j, i: (j, 0, i))
    return pl.pallas_call(
        gate_up_kernel,
        grid=(EXP_DEV, 4),
        in_specs=[
            pl.BlockSpec((1, total, tile), lambda j, i: (j, 0, i)),
            pl.BlockSpec((1, total, grads.shape[2]), lambda j, i: (j, 0, 0)),
        ],
        out_specs=[out, out],
        out_shape=[jax.ShapeDtypeStruct((EXP_DEV, inner, width), F32)] * 2,
        compiler_params=params(),
        name="gate_up_grads",
    )(rows, grads)


def output_kernel(
    x_rows, pick_ref, inner_ref, down_ref, left_ref, right_ref, own_ref, other_ref, hold_ref
):
    for j in range(EXP_DEV):
        hold_ref[j] = mm(inner_ref[j], down_ref[j]).astype(BF)
    for i in range(STEP):
        total = place_from(hold_ref, pick_ref[i], i, STEP) + mm(left_ref[i], right_ref[...])
        out_ref = own_ref if i // x_rows % 2 == 0 else other_ref
        out_ref[i // (2 * x_rows) * x_rows + i % x_rows] = total.astype(BF)


def output_rows_of(pick, inner, down, left, right, capacity, x_rows):
    devices, slots, tokens = pick.shape
    width = down.shape[2]
    rows = STEP * capacity
    return pl.pallas_call(
        functools.partial(output_kernel, x_rows),
        grid=(devices // STEP,),
        in_specs=[
            pl.BlockSpec((STEP, slots, tokens), lambda d: (d, 0, 0)),
            pl.BlockSpec((EXP_DEV, rows, inner.shape[2]), lambda d: (0, d, 0)),
            resident(down.shape),
            pl.BlockSpec((STEP, tokens, left.shape[2]), lambda d: (d, 0, 0)),
            resident(right.shape),
        ],
        out_specs=[pl.BlockSpec((STEP // 2, tokens, width), lambda d: (d, 0, 0))] * 2,
        out_shape=[jax.ShapeDtypeStruct((devices // 2, tokens, width), BF)] * 2,
        scratch_shapes=[pltpu.VMEM((EXP_DEV, rows, width), BF)],
        compiler_params=params(),
        name="output_rows",
    )(pick, inner, down, left, right)


def body(
    hidden,
    cotangent,
    segments,
    routes,
    w_query,
    w_latent,
    g_latent,
    w_expand,
    w_out,
    g_attn,
    g_ffn,
    w_router,
    s_gate,
    s_up,
    s_down,
    e_gate,
    expert_up_weight,
    e_down,
):
    tokens = hidden.shape[1]
    width = hidden.shape[2]
    links = Links()
    shards, groups = links.shards, links.groups
    devices = groups * shards
    experts = EXP_DEV * groups
    capacity = max(2, tokens * TOP * 4 // (3 * experts))
    heads = H // shards
    length = tokens * shards
    part = width // shards
    my_shard = lax.axis_index("shard")
    my_group = lax.axis_index("expert")
    hid_shard = s_down.shape[0]
    hid = hid_shard // groups
    latent_part = KVR // shards
    shard_at, slot_at = links.shard_at(), links.slot_at()

    router_rows = part * experts // width
    small_rows = jnp.concatenate([g_attn, g_ffn, g_latent])
    small_rows = jnp.pad(small_rows, (0, -small_rows.shape[0] % width)).reshape(-1, width)
    packed = jnp.concatenate([w_router.reshape(router_rows, width), small_rows])
    packed = links.gather_shard(jnp.pad(packed, ((0, -packed.shape[0] % 16), (0, 0))))
    hidden_all = links.gather_shard(hidden[0]).reshape(length, width)
    pieces = lambda w: jnp.stack(jnp.split(w, shards, axis=1))
    wl = links.gather_shard(w_latent.T)
    wq = links.spread_shard_ring(pieces(w_query))
    we = links.spread_shard(pieces(w_expand))
    (wl, wq, we), grad_top = tie((wl, wq, we), cotangent[0])
    g_all = links.gather_all(grad_top).reshape(devices, tokens, width)
    packed = jnp.take(packed, slot_at, axis=0)
    full_router = packed[:, :router_rows].reshape(width, experts)
    gains_in = packed[:, router_rows:].reshape(shards, -1)
    gattn = gains_in[:, :part].reshape(1, width).astype(F32)
    gffn = gains_in[:, part : 2 * part].reshape(width).astype(F32)
    glatent = gains_in[:, 2 * part : 2 * part + latent_part].reshape(1, KVR).astype(F32)

    order = links.order()
    same = jnp.arange(devices, dtype=jnp.int32)
    back_order = jnp.sum(
        jnp.where(order[:, None] == same[None, :], same[:, None], 0), axis=0
    ).astype(jnp.int32)
    local_routes = routes[0]
    flat_routes = local_routes.reshape(-1)
    choose = local_routes[:, :, None] == jnp.arange(experts, dtype=jnp.int32)[None, None, :]
    hits = choose.reshape(-1, experts).astype(F32)
    pair_count = tokens * TOP
    before_it = (
        lax.broadcasted_iota(jnp.int32, (pair_count, pair_count), 1)
        < lax.broadcasted_iota(jnp.int32, (pair_count, pair_count), 0)
    ).astype(BF)
    before = mm(before_it, hits.astype(BF))
    slot_rank = jnp.sum(before * hits, axis=1).astype(jnp.int32)
    slot_of = (flat_routes * capacity + slot_rank).reshape(tokens, TOP)
    slots = EXP_DEV * capacity
    slot_rows = jnp.pad(slot_of.T, ((0, 8 - TOP), (0, 0)), constant_values=-1)
    slots_all = exchange(jnp.broadcast_to(slot_rows[None], (devices, 8, tokens)), BOTH)
    slots_all = jnp.take(slots_all, order, axis=0)[:, :TOP]
    slot_ids = my_group * slots + jnp.arange(slots, dtype=jnp.int32)
    pick = jnp.any(
        slots_all[:, None] == slot_ids[None, :, None, None], axis=2
    ).astype(BF)

    positions = (shard_at[:, None] * tokens + jnp.arange(tokens, dtype=jnp.int32)).reshape(-1)
    cosine, sine_vals = rope_angles(positions)
    segs = jnp.take(segments.reshape(shards, tokens), shard_at, axis=0).reshape(-1)
    col = jnp.stack([segs, positions], axis=1)
    row = jnp.stack([segs, positions], axis=0)
    attn_part, n1, compressed, latent, attended, query, kv, lse = attention_forward(
        slot_at, hidden_all, gattn, glatent, wq, wl, we, w_out, cosine, sine_vals, col, row
    )
    inner_units = e_gate.shape[2]
    gate_t, up_t = jnp.swapaxes(e_gate, 1, 2), jnp.swapaxes(expert_up_weight, 1, 2)
    attn_out = links.sum_shard(attn_part.reshape(shards, tokens, width))

    residual_in = hidden[0].astype(F32)
    residual_mid = residual_in + attn_out
    unit_two, factor_two = norm_forward(residual_mid)
    normed_two = (unit_two * gffn).astype(BF)

    hid_ids = my_group * hid + jnp.arange(hid, dtype=jnp.int32)
    wanted = (jnp.arange(shards, dtype=jnp.int32)[:, None] * hid_shard + hid_ids).reshape(-1)
    chosen_units = (
        jnp.arange(shards * hid_shard, dtype=jnp.int32)[:, None] == wanted[None, :]
    ).astype(BF)

    def shared_pieces(units):
        cut = [mm(w, units).astype(BF).reshape(part, shards, hid) for w in (s_gate, s_up)]
        return jnp.concatenate(cut, axis=2).transpose(1, 0, 2)

    shared_down = lax.dynamic_slice_in_dim(s_down, my_group * hid, hid, 0)
    work = [
        Fill(shared_pieces, chosen_units),
        Fill(lambda p: grad_rows_of(p, g_all, e_down, capacity), pick),
        Fill(lambda w: mm_nt(g_all.reshape(-1, width), w), shared_down),
    ]
    n2_all = links.gather_all(normed_two, list(enumerate(work, 1))).reshape(
        devices, tokens, width
    )
    gate_up, (grad_rows, grad_inner), shared_grad_inner = (w.result for w in work)
    shared_in = links.spread_shard(gate_up)
    shared_in = jnp.take(shared_in, slot_at, axis=0).reshape(width, 2 * hid)
    probs = jax.nn.sigmoid(mm(normed_two, full_router))
    chosen = jnp.sum(jnp.where(choose, probs[:, None, :], 0.0), axis=-1)
    chosen_total = jnp.sum(chosen, axis=1, keepdims=True)

    shared_pre = mm(
        n2_all.reshape(-1, width), jnp.concatenate([shared_in, full_router], axis=1)
    )
    probs_all = jax.nn.sigmoid(
        shared_pre[:, 2 * hid :].reshape(devices, tokens, experts).transpose(0, 2, 1)
    )
    named = jnp.any(
        (slots_all // capacity)[:, None]
        == jnp.arange(experts, dtype=jnp.int32)[None, :, None, None],
        axis=2,
    )
    totals = jnp.sum(jnp.where(named, probs_all, 0.0), axis=1, keepdims=True)
    local_probs = lax.dynamic_slice_in_dim(probs_all, my_group * EXP_DEV, EXP_DEV, 1)
    local_weights = local_probs / totals * ROUTE_SCALE
    slot_weight = jnp.sum(
        jnp.where(
            pick.reshape(devices, EXP_DEV, capacity, tokens) > 0,
            local_weights[:, :, None, :],
            0.0,
        ),
        axis=3,
    )
    row_weight = slot_weight.transpose(1, 0, 2).reshape(EXP_DEV, devices * capacity, 1)

    s_inner, s_slope_gate, s_slope_up = swish_parts(
        shared_pre[:, :hid], shared_pre[:, hid : 2 * hid]
    )
    shared_inner = s_inner.astype(BF)
    shared_grads = jnp.concatenate(
        [shared_grad_inner * s_slope_gate, shared_grad_inner * s_slope_up], axis=1
    ).astype(BF)

    d_shared_down = mm_tn(shared_inner, g_all.reshape(-1, width)).astype(BF)
    shared_out = mm_tn(shared_grads, n2_all.reshape(-1, width)).astype(BF)
    shared_out = shared_out.reshape(2 * hid, shards, part).transpose(1, 0, 2)
    in_pieces = jnp.take(links.spread_shard(shared_out), slot_at, axis=0)
    row_weight, (d_shared_down, in_pieces) = tie(row_weight, (d_shared_down, in_pieces))
    down_all = lax.all_gather(d_shared_down, "expert", axis=0, tiled=True)
    in_all = lax.all_gather(in_pieces, "expert", axis=0, tiled=False)

    rows, inner_w, grads_b, grad_slot_weight = inner_of(
        pick, n2_all, gate_t, up_t, row_weight, grad_inner, capacity
    )
    dn2_own, dn2_other = back_rows(
        pick, grads_b, gate_t, up_t, shared_grads.reshape(devices, tokens, 2 * hid),
        shared_in.T, capacity, shards // 2,
    )

    def router_back(slot_sums):
        slot_back = slot_sums.reshape(EXP_DEV, devices, capacity).transpose(1, 0, 2)
        slot_back = jnp.take(slot_back.reshape(devices, slots), back_order, axis=0)
        got = exchange(slot_back, BOTH)
        slot_grads = jnp.sum(got.reshape(groups, shards, slots), axis=1).reshape(-1)
        at_slot = slot_of[:, :, None] == jnp.arange(experts * capacity, dtype=jnp.int32)
        grad_weights = jnp.sum(jnp.where(at_slot, slot_grads, 0.0), axis=2)
        grad_chosen = ROUTE_SCALE * (
            grad_weights / chosen_total
            - jnp.sum(grad_weights * chosen, axis=1, keepdims=True)
            / (chosen_total * chosen_total)
        )
        grad_probs = jnp.sum(jnp.where(choose, grad_chosen[:, :, None], 0.0), axis=1)
        return (grad_probs * probs * (1.0 - probs)).astype(BF)

    down_grad = lambda a, b: jnp.einsum("jmf,jmd->jfd", a, b, preferred_element_type=F32)
    ring_shape = (groups, shards // 2, tokens, width)
    work = [
        Fill(router_back, grad_slot_weight),
        Fill(
            lambda a: output_rows_of(
                pick, a, e_down, shared_inner.reshape(devices, tokens, hid), shared_down,
                capacity, shards // 2,
            ),
            inner_w,
        ),
        Fill(lambda b: gate_up_grads(rows, b, inner_units), grads_b),
    ]
    dn2 = links.sum_all(
        dn2_own.reshape(ring_shape),
        dn2_other.reshape(ring_shape),
        [(groups // 2 - i, w) for i, w in enumerate(work)],
    )
    grad_logits, (out_own, out_other), (d_egate, grad_expert_up) = (w.result for w in work)
    logits_back = exchange(
        jnp.broadcast_to(grad_logits.T[None], (devices, experts, tokens)), BOTH
    )
    logits_back = jnp.take(logits_back, order, axis=0)

    grad_normed_two = dn2 + mm_nt(grad_logits, full_router)
    grad_mid_norm, d_gffn = norm_backward(grad_normed_two, gffn, unit_two, factor_two)
    grad_mid = cotangent[0].astype(F32) + grad_mid_norm
    (out_own, out_other), grad_mid_b = tie((out_own, out_other), grad_mid.astype(BF))
    grad_attn = links.gather_shard(grad_mid_b).reshape(length, width)
    work_d = Fill(lambda a: down_grad(a, grad_rows), inner_w)
    routed_shared = links.sum_all(
        out_own.reshape(ring_shape), out_other.reshape(ring_shape),
        [(groups // 2 - 1, work_d)],
    )
    d_edown = work_d.result
    output_rows = residual_mid + routed_shared
    own_columns = lax.dynamic_slice_in_dim(n2_all, my_shard * part, part, 2)
    d_router = mm(
        logits_back.transpose(1, 0, 2).reshape(experts, -1), own_columns.reshape(-1, part)
    ).T

    dn1, dw, dwl, d_out, d_glatent = attention_backward(
        slot_at, grad_attn, glatent, w_out, attended, query, kv, lse, latent, compressed,
        we, wl, wq, n1, cosine, sine_vals, col, row,
    )
    (dn1, dw, dwl, d_out), (in_all, down_all) = tie(
        (dn1, dw, dwl, d_out), (in_all, down_all)
    )
    grad_normed = links.sum_shard(dn1.reshape(shards, tokens, width))
    unit_one, factor_one = norm_forward(residual_in)
    grad_input_norm, d_gattn = norm_backward(
        grad_normed, gattn.reshape(width), unit_one, factor_one
    )
    grad_input = grad_mid + grad_input_norm

    cut = part // groups
    lat = links.sum_shard(dwl).astype(BF).reshape(groups, (KVR + DR) // groups, part)
    by_head = links.blocks(dw.reshape(shards, groups, cut, -1).transpose(1, 0, 2, 3))
    by_row = links.blocks(d_out.reshape(groups, cut, width))
    pluses = [groups // 2, (groups - 1) // 2]
    work_s = Fill(shared_finish, in_all)
    sum_head, sum_row = links.ring_reduce(
        [by_head, by_row], pluses, [(groups // 2 - 1, work_s)]
    )
    (sum_lat,) = links.ring_reduce([links.blocks(lat)], pluses[1:])
    part_sgate, part_sup = work_s.result
    sum_head = links.exchange_shard(sum_head.astype(BF))
    all_head, all_row = links.ring_gather([sum_head, sum_row.astype(BF)], pluses)
    (all_lat,) = links.ring_gather([sum_lat.astype(BF)], pluses[1:])
    part_query, part_expand, part_out = finish(
        links.block_at(), all_head, all_row, heads, width
    )
    part_latent = jnp.take(jnp.stack(all_lat), links.block_at(), axis=0)
    part_latent = part_latent.reshape(KVR + DR, part).astype(F32)

    gain_grads = jnp.concatenate(
        [
            d_gattn.reshape(shards, part),
            d_gffn.reshape(shards, part),
            d_glatent.reshape(shards, latent_part),
        ],
        axis=1,
    )
    got = exchange(
        jnp.broadcast_to(gain_grads[None], (groups,) + gain_grads.shape).reshape(devices, -1),
        BOTH,
    )
    gains = jnp.sum(got, axis=0)
    return (
        output_rows.astype(BF)[None],
        grad_input[None],
        part_query,
        part_latent.T,
        gains[2 * part :],
        part_expand,
        part_out,
        gains[:part],
        gains[part : 2 * part],
        d_router,
        part_sgate,
        part_sup,
        down_all.astype(F32),
        jnp.swapaxes(d_egate, 1, 2),
        jnp.swapaxes(grad_expert_up, 1, 2),
        d_edown,
    )


def solution(mesh):
    return jax.shard_map(
        body,
        mesh=mesh,
        in_specs=(
            P("expert", "shard", None),
            P("expert", "shard", None),
            P("expert", None),
            P("expert", "shard", None),
            P("shard", None),
            P("shard", None),
            P("shard"),
            P("shard", None),
            P("shard", None),
            P("shard"),
            P("shard"),
            P("shard", None),
            P("shard", None),
            P("shard", None),
            P("shard", None),
            P("expert", None, "shard"),
            P("expert", None, "shard"),
            P("expert", "shard", None),
        ),
        out_specs=(
            P("expert", "shard", None),
            P("expert", "shard", None),
            P("shard", None),
            P("shard", None),
            P("shard"),
            P("shard", None),
            P("shard", None),
            P("shard"),
            P("shard"),
            P("shard", None),
            P("shard", None),
            P("shard", None),
            P("shard", None),
            P("expert", None, "shard"),
            P("expert", None, "shard"),
            P("expert", "shard", None),
        ),
        check_vma=False,
    )
```

```python
import functools

import jax
import jax.numpy as jnp
from jax import lax
from jax.experimental import pallas as pl
from jax.experimental.pallas import tpu as pltpu
from jax.sharding import PartitionSpec as P

H = 16
DN = 128
DR = 64
DV = 128
KVR = 512
TOP = 6
EXP_DEV = 4

EPS = 1e-06
ROUTE_SCALE = 2.446
ROPE_BASE = 50000.0
SCORE_SCALE = (DN + DR) ** (-0.5)
BF = jnp.bfloat16
F32 = jnp.float32
BOTH = ("expert", "shard")
VMEM_BYTES = 56 * 1024 * 1024


def mm(a, b):
    return jnp.dot(a, b, preferred_element_type=F32)


def mm_tn(a, b):
    return lax.dot_general(a, b, (((0,), (0,)), ((), ())), preferred_element_type=F32)


def mm_nt(a, b):
    return lax.dot_general(a, b, (((1,), (1,)), ((), ())), preferred_element_type=F32)


def rope_angles(positions):
    half_width = DR // 2
    inverse = ROPE_BASE ** (-jnp.arange(half_width).astype(F32) / half_width)
    angles = positions.astype(F32)[:, None] * inverse[None, :]
    return (jnp.cos(angles), jnp.sin(angles))


def rotate(values, cosine, sine_vals):
    half_width = DR // 2
    first_half = values[..., :half_width]
    second_half = values[..., half_width:]
    return jnp.concatenate(
        [
            first_half * cosine - second_half * sine_vals,
            second_half * cosine + first_half * sine_vals,
        ],
        axis=-1,
    )


def norm_forward(values):
    factor = lax.rsqrt(jnp.mean(values * values, axis=-1, keepdims=True) + EPS)
    return values * factor, factor


def norm_backward(grad_out, gain_vec, unit_vals, factor):
    grad_unit = grad_out * gain_vec
    grad_in = factor * (
        grad_unit - unit_vals * jnp.mean(grad_unit * unit_vals, axis=-1, keepdims=True)
    )
    return (grad_in, jnp.sum(grad_out * unit_vals, axis=0))


def swish_parts(gate, up):
    sig = jax.nn.sigmoid(gate)
    silu = gate * sig
    return silu * up, up * sig * (1.0 + gate * (1.0 - sig)), silu


def exchange(values, axis):
    return lax.all_to_all(values, axis, split_axis=0, concat_axis=0, tiled=True)


def tie(streams, extra):
    return lax.optimization_barrier((streams, extra))


class Fill:
    def __init__(self, work, *inputs):
        self.work, self.given, self.result = work, inputs, None

    @property
    def inputs(self):
        return tuple(v() if callable(v) else v for v in self.given)


class Links:
    def __init__(self):
        self.groups = lax.axis_size("expert")
        self.shards = lax.axis_size("shard")
        self.rows = self.shards // 2
        n = self.groups
        self.ring = list(range(0, n, 2)) + list(range(n - 1, 0, -2))
        shard = lax.axis_index("shard")
        self.x = shard // 2
        self.core = shard % 2
        group = lax.axis_index("expert")
        places = [self.ring.index(e) for e in range(n)]
        self.place = jnp.sum(
            jnp.where(jnp.arange(n) == group, jnp.array(places, jnp.int32), 0)
        )

    def send(self, values, target):
        pairs = []
        for e in range(self.groups):
            for s in range(self.shards):
                pairs.append((e * self.shards + s, target(e, s)))
        return lax.ppermute(values, BOTH, pairs)

    def around(self, values, step):
        n = self.groups
        return self.send(
            values,
            lambda e, s: self.ring[(self.ring.index(e) + step) % n] * self.shards + s,
        )

    def along_x(self, values, step):
        return self.send(
            values,
            lambda e, s: e * self.shards + ((s // 2 + step) % self.rows) * 2 + s % 2,
        )

    def partner(self, values):
        return self.send(values, lambda e, s: e * self.shards + (s ^ 1))

    def shard_at(self):
        xs = (self.x - jnp.arange(self.rows, dtype=jnp.int32)) % self.rows
        cores = jnp.stack([self.core, 1 - self.core]).astype(jnp.int32)
        return (xs[:, None] * 2 + cores[None, :]).reshape(-1).astype(jnp.int32)

    def slot_at(self):
        shard = jnp.arange(self.shards, dtype=jnp.int32)
        back = (self.x - shard // 2) % self.rows
        return (back * 2 + (shard % 2 != self.core)).astype(jnp.int32)

    def gather_shard(self, values):
        out = []
        for k in range(self.rows):
            own = values if k == 0 else self.along_x(values, k)
            out += [own, self.partner(own)]
        return jnp.stack(out)

    def spread_shard(self, pieces):
        take = lambda v, i: lax.dynamic_index_in_dim(v, i, 0, keepdims=False)
        pairs = pieces.reshape((self.rows, 2) + pieces.shape[1:])
        out = []
        for k in range(self.rows):
            got = take(pairs, (self.x + k) % self.rows)
            got = got if k == 0 else self.along_x(got, k)
            out += [take(got, self.core), self.partner(take(got, 1 - self.core))]
        return jnp.stack(out)

    def spread_shard_ring(self, pieces):
        n, rows = self.groups, self.rows
        take = lambda v, i, axis: lax.dynamic_index_in_dim(v, i, axis, keepdims=False)
        part, wide = pieces.shape[1:]
        pairs = pieces.reshape(rows, 2, n, part // n, wide)
        mine = take(pairs, self.place, 2)
        out = []
        for k in range(rows):
            if k == 0:
                got = take(pairs, self.x, 0)
            else:
                far = self.along_x(take(mine, (self.x + k) % rows, 0), k)
                (far,) = self.ring_gather([far], [n // 2])
                got = jnp.take(jnp.stack(far, axis=1), self.block_at(), axis=1)
            got = got.reshape(2, part, wide)
            out += [take(got, self.core, 0), self.partner(take(got, 1 - self.core, 0))]
        return jnp.stack(out)

    def exchange_shard(self, values):
        pairs = values.reshape((self.rows, 2) + values.shape[1:])
        out = []
        for k in range(self.rows):
            got = pairs[k] if k == 0 else self.along_x(pairs[k], -k)
            out += [got[0], self.partner(got[1])]
        xs = (self.x + jnp.arange(self.rows, dtype=jnp.int32)) % self.rows
        shard = jnp.arange(self.shards, dtype=jnp.int32)
        ahead = (shard // 2 - self.x) % self.rows
        slot = ahead * 2 + (shard % 2 != self.core)
        return jnp.take(jnp.stack(out), slot, axis=0)

    def sum_shard(self, values, fill=None):
        pairs = values.reshape((self.rows, 2) + values.shape[1:])
        both = [
            pairs[k, 0].astype(F32) + self.partner(pairs[k, 1]).astype(F32)
            for k in range(self.rows)
        ]
        far = [v.astype(BF) for v in both[1:]]
        if fill is not None:
            _, inputs = tie(far, fill.inputs)
        far = [self.along_x(v, -k - 1) for k, v in enumerate(far)]
        if fill is not None:
            far, fill.result = tie(far, fill.work(*inputs))
        total = both[0]
        for v in far:
            total = total + v.astype(F32)
        return total

    def ring_gather(self, values, pluses, fills=()):
        n = self.groups
        fills = dict(fills)
        outs = [[v] + [None] * (n - 1) for v in values]
        ahead, back = list(values), list(values)
        for r in range(1, n):
            moves = [(i, 1) for i, p in enumerate(pluses) if r <= p]
            moves += [(i, -1) for i, p in enumerate(pluses) if r <= n - 1 - p]
            if not moves:
                break
            streams = [ahead[i] if step > 0 else back[i] for i, step in moves]
            streams = self.step(streams, [step for _, step in moves], fills.get(r))
            for (i, step), got in zip(moves, streams):
                if step > 0:
                    ahead[i] = outs[i][r] = got
                else:
                    back[i] = outs[i][n - r] = got
        return outs

    def step(self, streams, steps, fill):
        if fill is None:
            return [self.around(v, s) for v, s in zip(streams, steps)]
        streams, inputs = tie(streams, fill.inputs)
        streams = [self.around(v, s) for v, s in zip(streams, steps)]
        streams, fill.result = tie(streams, fill.work(*inputs))
        return streams

    def ring_reduce(self, parts, pluses, fills=()):
        n = self.groups
        fills = dict(fills)
        ahead = [p[plus] for p, plus in zip(parts, pluses)]
        back = [p[plus + 1] for p, plus in zip(parts, pluses)]
        most = max(max(p, n - 1 - p) for p in pluses)
        for r in range(most, 0, -1):
            moves = [(i, 1) for i, p in enumerate(pluses) if r <= p]
            moves += [(i, -1) for i, p in enumerate(pluses) if r <= n - 1 - p]
            streams = [ahead[i] if step > 0 else back[i] for i, step in moves]
            streams = self.step(streams, [-step for _, step in moves], fills.get(r))
            for (i, step), got in zip(moves, streams):
                here = parts[i][r - 1 if step > 0 else (n - r + 1) % n]
                if r > 1:
                    got = (got.astype(F32) + here.astype(F32)).astype(BF)
                if step > 0:
                    ahead[i] = got
                else:
                    back[i] = got
        return [
            p[0].astype(F32) + a.astype(F32) + b.astype(F32)
            for p, a, b in zip(parts, ahead, back)
        ]

    def block_at(self):
        return (self.place - jnp.arange(self.groups, dtype=jnp.int32)) % self.groups

    def blocks(self, values):
        return [
            lax.dynamic_index_in_dim(
                values, (self.place - r) % self.groups, 0, keepdims=False
            )
            for r in range(self.groups)
        ]

    def order(self):
        n = self.groups
        ring = jnp.array(self.ring, jnp.int32)
        groups = jnp.sum(
            jnp.where(self.block_at()[:, None] == jnp.arange(n)[None, :], ring[None, :], 0),
            axis=1,
        )
        shard = self.shard_at().reshape(self.rows, 2).T.reshape(-1)
        all_of = groups[:, None] * self.shards + shard[None, :]
        return all_of.reshape(-1).astype(jnp.int32)

    def gather_all(self, values, fills=()):
        n, rows = self.groups, self.rows
        tokens, width = values.shape
        half = tokens // 2
        first, second = values[:half], values[half:]
        spread = jnp.stack([first] + [self.along_x(first, k) for k in range(1, rows)])
        upper, lower = self.ring_gather(
            [spread, second], [n // 2, (n - 1) // 2], fills
        )
        out = jnp.zeros((n, 2, rows, tokens, width), values.dtype)
        steps = [0] + [r for k in range(1, n // 2 + 1) for r in dict.fromkeys((k, n - k))]
        for r in steps:
            low = jnp.stack(
                [lower[r]] + [self.along_x(lower[r], k) for k in range(1, rows)]
            )
            own = jnp.concatenate([upper[r], low], axis=1)
            out = lax.dynamic_update_slice(out, own[None, None], (r, 0, 0, 0, 0))
            out = lax.dynamic_update_slice(
                out, self.partner(own)[None, None], (r, 1, 0, 0, 0)
            )
        return out

    def sum_core(self, own, other):
        both = (own.astype(F32) + self.partner(other).astype(F32)).astype(BF)
        return [both[r] for r in range(self.groups)]

    def sum_x(self, top):
        total = top[0]
        for k in range(1, self.rows):
            total = total + self.along_x(top[k].astype(BF), -k).astype(F32)
        return total


def params(**kw):
    return pltpu.CompilerParams(vmem_limit_bytes=VMEM_BYTES, **kw)


SMEM = pl.BlockSpec(memory_space=pltpu.SMEM)
VMEM = pl.BlockSpec(memory_space=pltpu.VMEM)


def allowed_mask(seg_col, seg_row, pos_col, pos_row):
    return (seg_col == seg_row) & (pos_row <= pos_col)


def attention_forward_kernel(
    slot_ref, x_ref, gattn_ref, glat_ref, wq_ref, wl_ref, we_ref, wo_ref,
    cos_ref, sin_ref, col_ref, row_ref,
    out_ref, n1_ref, c_ref, lat_ref, o_ref, q_ref, kv_ref, lse_ref,
):
    shards, part = wq_ref.shape[0], wq_ref.shape[1]
    heads = q_ref.shape[0]
    tokens = x_ref.shape[0] // shards
    for b in range(shards):
        at = slice(b * tokens, (b + 1) * tokens)
        unit, _ = norm_forward(x_ref[at].astype(F32))
        n1_ref[at] = (unit * gattn_ref[...]).astype(BF)
    queries, compressed, kv_all = None, None, None
    for s in range(shards):
        left = n1_ref[:, s * part : (s + 1) * part]
        one = mm(left, wq_ref[slot_ref[s]])
        queries = one if s == 0 else queries + one
        one = mm_nt(left, wl_ref[slot_ref[s]])
        compressed = one if s == 0 else compressed + one
    c_ref[...] = compressed
    unit, _ = norm_forward(compressed[:, :KVR])
    lat_ref[:, :KVR] = (unit * glat_ref[...]).astype(BF)
    lat_ref[:, KVR:] = rotate(compressed[:, KVR:], cos_ref[...], sin_ref[...]).astype(BF)
    part = KVR // shards
    for s in range(shards):
        one = mm(lat_ref[:, s * part : (s + 1) * part], we_ref[slot_ref[s]])
        kv_all = one if s == 0 else kv_all + one
    kv_ref[...] = kv_all.astype(BF)
    ok = allowed_mask(
        col_ref[:, :1], row_ref[:1, :], col_ref[:, 1:2], row_ref[1:2, :]
    )
    key_rot = lat_ref[:, KVR:]
    for h in range(heads):
        at = h * (DN + DR)
        query = jnp.concatenate(
            [
                queries[:, at : at + DN],
                rotate(queries[:, at + DN : at + DN + DR], cos_ref[...], sin_ref[...]),
            ],
            axis=1,
        ).astype(BF)
        q_ref[h] = query
        at = h * (DN + DV)
        keys = kv_ref[:, at : at + DN]
        values = kv_ref[:, at + DN : at + DN + DV]
        scores = mm_nt(query[:, :DN], keys) + mm_nt(query[:, DN:], key_rot)
        scores = jnp.where(ok, scores * SCORE_SCALE, -1e30)
        top = jnp.max(scores, axis=1, keepdims=True)
        expo = jnp.exp(scores - top)
        total = jnp.sum(expo, axis=1, keepdims=True)
        lse_ref[h] = top + jnp.log(total)
        weights = (expo / total).astype(BF)
        o_ref[:, h * DV : (h + 1) * DV] = mm(weights, values).astype(BF)
    out_ref[...] = mm(o_ref[...], wo_ref[...]).astype(BF)


def attention_forward(slot, x, gattn, glat, wq, wl, we, wo, cosine, sine_vals, col, row):
    length, width = x.shape
    heads = wo.shape[0] // DV
    return pl.pallas_call(
        attention_forward_kernel,
        in_specs=[SMEM] + [VMEM] * 11,
        out_shape=[
            jax.ShapeDtypeStruct((length, width), BF),
            jax.ShapeDtypeStruct((length, width), BF),
            jax.ShapeDtypeStruct((length, KVR + DR), F32),
            jax.ShapeDtypeStruct((length, KVR + DR), BF),
            jax.ShapeDtypeStruct((length, heads * DV), BF),
            jax.ShapeDtypeStruct((heads, length, DN + DR), BF),
            jax.ShapeDtypeStruct((length, heads * (DN + DV)), BF),
            jax.ShapeDtypeStruct((heads, length, 1), F32),
        ],
        compiler_params=params(),
        name="attention_forward",
    )(slot, x, gattn, glat, wq, wl, we, wo, cosine, sine_vals, col, row)


def attention_backward_kernel(
    slot_ref, dh_ref, glat_ref, wo_ref, o_ref, q_ref, kv_ref, lse_ref, lat_ref, c_ref,
    we_ref, wl_ref, wq_ref, n1_ref, cos_ref, sin_ref, col_ref, row_ref,
    dn1_ref, dw_ref, dwl_ref, dwo_ref, dgl_ref,
    go_ref, gq_ref, gkv_ref, gc_ref,
):
    shards, part = wq_ref.shape[0], wq_ref.shape[1]
    heads = q_ref.shape[0]
    go_ref[...] = mm_nt(dh_ref[...], wo_ref[...]).astype(BF)
    dwo_ref[...] = mm_tn(o_ref[...], dh_ref[...]).astype(BF)
    ok = allowed_mask(
        col_ref[:, :1], row_ref[:1, :], col_ref[:, 1:2], row_ref[1:2, :]
    )
    key_rot = lat_ref[:, KVR:]
    grad_kr = None
    for h in range(heads):
        at = h * (DN + DV)
        keys = kv_ref[:, at : at + DN]
        values = kv_ref[:, at + DN : at + DN + DV]
        query = q_ref[h]
        grad_o = go_ref[:, h * DV : (h + 1) * DV]
        scores = mm_nt(query[:, :DN], keys) + mm_nt(query[:, DN:], key_rot)
        weights = jnp.where(ok, jnp.exp(scores * SCORE_SCALE - lse_ref[h]), 0.0)
        grad_w = mm_nt(grad_o, values)
        delta = jnp.sum(weights * grad_w, axis=1, keepdims=True)
        grad_s = (weights * (grad_w - delta) * SCORE_SCALE).astype(BF)
        gkv_ref[:, at : at + DN] = mm_tn(grad_s, query[:, :DN]).astype(BF)
        gkv_ref[:, at + DN : at + DN + DV] = mm_tn(weights.astype(BF), grad_o).astype(BF)
        one = mm_tn(grad_s, query[:, DN:])
        grad_kr = one if h == 0 else grad_kr + one
        at = h * (DN + DR)
        grad_qr = rotate(mm(grad_s, key_rot), cos_ref[...], -sin_ref[...])
        gq_ref[:, at : at + DN + DR] = jnp.concatenate(
            [mm(grad_s, keys), grad_qr], axis=1
        ).astype(BF)
    latent_part = KVR // shards
    query_wide = heads * (DN + DR)
    ratio = part // latent_part
    piece = heads * (DN + DV) // ratio
    grad_lat = []
    for s in range(shards):
        at = slice(s * latent_part, (s + 1) * latent_part)
        grad_lat.append(mm_nt(gkv_ref[...], we_ref[slot_ref[s]]))
        one = mm_tn(lat_ref[:, at], gkv_ref[...]).astype(BF)
        for i in range(ratio):
            dw_ref[slot_ref[s], i * latent_part : (i + 1) * latent_part, query_wide:] = one[
                :, i * piece : (i + 1) * piece
            ]
    grad_lat = jnp.concatenate(grad_lat, axis=1)
    unit, factor = norm_forward(c_ref[:, :KVR])
    grad_norm, grad_gain = norm_backward(grad_lat, glat_ref[...], unit, factor)
    dgl_ref[...] = grad_gain.reshape(1, KVR)
    gc_ref[:, :KVR] = grad_norm.astype(BF)
    gc_ref[:, KVR:] = rotate(grad_kr, cos_ref[...], -sin_ref[...]).astype(BF)
    for s in range(shards):
        at = slice(s * part, (s + 1) * part)
        dn1_ref[:, at] = (
            mm_nt(gq_ref[...], wq_ref[slot_ref[s]]) + mm(gc_ref[...], wl_ref[slot_ref[s]])
        ).astype(BF)
        dw_ref[slot_ref[s], :, :query_wide] = mm_tn(n1_ref[:, at], gq_ref[...]).astype(BF)
        dwl_ref[slot_ref[s]] = mm_tn(gc_ref[...], n1_ref[:, at]).astype(BF)


def attention_backward(
    slot, dh, glat, wo, o, query, kv, lse, latent, compressed, we, wl, wq, n1,
    cosine, sine_vals, col, row,
):
    length, width = n1.shape
    heads = query.shape[0]
    shards, part = wq.shape[0], wq.shape[1]
    wide = heads * (DN + DR) + heads * (DN + DV) * KVR // width
    return pl.pallas_call(
        attention_backward_kernel,
        in_specs=[SMEM] + [VMEM] * 17,
        out_shape=[
            jax.ShapeDtypeStruct((length, width), BF),
            jax.ShapeDtypeStruct((shards, part, wide), BF),
            jax.ShapeDtypeStruct(wl.shape, BF),
            jax.ShapeDtypeStruct((heads * DV, width), BF),
            jax.ShapeDtypeStruct((1, KVR), F32),
        ],
        scratch_shapes=[
            pltpu.VMEM((length, heads * DV), BF),
            pltpu.VMEM((length, heads * (DN + DR)), BF),
            pltpu.VMEM((length, heads * (DN + DV)), BF),
            pltpu.VMEM((length, KVR + DR), BF),
        ],
        compiler_params=params(),
        name="attention_backward",
    )(
        slot, dh, glat, wo, o, query, kv, lse, latent, compressed, we, wl, wq, n1,
        cosine, sine_vals, col, row,
    )


def finish_kernel(groups, shards, per, piece, *refs):
    place_ref = refs[0]
    by_head, by_row = (refs[1 + i * groups : 1 + (i + 1) * groups] for i in range(2))
    query_ref, expand_ref, out_ref = refs[1 + 2 * groups :]
    cut = by_row[0].shape[0]
    wide = by_head[0].shape[2] - piece
    expand_wide = expand_ref.shape[1] // shards
    for r in range(groups):
        at = place_ref[r]
        rows = pl.ds(pl.multiple_of(at * cut, cut), cut)
        out_ref[rows, :] = by_row[r][...].astype(F32)
        low = pl.ds(pl.multiple_of((at % per) * cut, cut), cut)
        for s in range(shards):
            query_ref[rows, s * wide : (s + 1) * wide] = by_head[r][s, :, :wide].astype(F32)
            lanes = pl.ds(
                pl.multiple_of(s * expand_wide + (at // per) * piece, piece), piece
            )
            expand_ref[low, lanes] = by_head[r][s, :, wide:].astype(F32)


def finish(place, by_head, by_row, heads, width):
    groups, shards = len(by_head), by_head[0].shape[0]
    latent_part = KVR // shards
    part = width // shards
    per = groups * latent_part // part
    piece = heads * (DN + DV) * latent_part // part
    return pl.pallas_call(
        functools.partial(finish_kernel, groups, shards, per, piece),
        in_specs=[SMEM] + [VMEM] * (2 * groups),
        out_shape=[
            jax.ShapeDtypeStruct((part, H * (DN + DR)), F32),
            jax.ShapeDtypeStruct((latent_part, H * (DN + DV)), F32),
            jax.ShapeDtypeStruct((part, width), F32),
        ],
        compiler_params=params(),
        name="finish",
    )(place, *by_head, *by_row)


def shared_finish_kernel(x_ref, gate_ref, up_ref, hold_ref):
    groups, shards, hid = x_ref.shape[0], x_ref.shape[1], x_ref.shape[2] // 2
    for i, out_ref in ((0, gate_ref), (1, up_ref)):
        for s in range(shards):
            for g in range(groups):
                at = (s * groups + g) * hid
                hold_ref[at : at + hid] = x_ref[g, s, i * hid : (i + 1) * hid].astype(F32)
        out_ref[...] = hold_ref[...].T


def shared_finish(pieces):
    groups, shards, two, part = pieces.shape
    wide = groups * shards * two // 2
    return pl.pallas_call(
        shared_finish_kernel,
        in_specs=[VMEM],
        out_shape=[jax.ShapeDtypeStruct((part, wide), F32)] * 2,
        scratch_shapes=[pltpu.VMEM((wide, part), F32)],
        compiler_params=params(),
        name="shared_finish",
    )(pieces)


STEP = 8
PAD = 128


def pick_into(out_ref, pick, rows_of, i, step):
    capacity = out_ref.shape[1] // step
    rows = mm(pick, rows_of).astype(BF)
    out_ref[:, i * capacity : (i + 1) * capacity, :] = rows.reshape(
        EXP_DEV, capacity, rows.shape[1]
    )


def place_from(rows_ref, pick, i, step):
    capacity = rows_ref.shape[1] // step
    rows = rows_ref[:, i * capacity : (i + 1) * capacity, :]
    return mm_tn(pick, rows.reshape(EXP_DEV * capacity, rows.shape[2]))


def resident(shape):
    return pl.BlockSpec(
        shape, lambda *_: (0,) * len(shape), pipeline_mode=pl.Buffered(1)
    )


def grad_rows_kernel(order_ref, pick_ref, down_ref, *refs):
    rows_ref, inner_ref = refs[STEP:]
    inner = down_ref.shape[1]
    for i in range(STEP):
        pick_into(rows_ref, pick_ref[i], refs[i][0], i, STEP)
    for j in range(EXP_DEV):
        inner_ref[j, :, :inner] = mm_nt(rows_ref[j], down_ref[j])


def grad_rows_of(pick, g_all, order, down, capacity):
    devices, slots, tokens = pick.shape
    width, inner = g_all.shape[2], down.shape[1]
    lanes = inner + -inner % PAD
    rows = STEP * capacity
    at = lambda i: pl.BlockSpec((1, tokens, width), lambda d, o: (o[d * STEP + i], 0, 0))
    return pl.pallas_call(
        grad_rows_kernel,
        grid_spec=pltpu.PrefetchScalarGridSpec(
            num_scalar_prefetch=1,
            grid=(devices // STEP,),
            in_specs=[
                pl.BlockSpec((STEP, slots, tokens), lambda d, o: (d, 0, 0)),
                resident(down.shape),
            ]
            + [at(i) for i in range(STEP)],
            out_specs=[
                pl.BlockSpec((EXP_DEV, rows, width), lambda d, o: (0, d, 0)),
                pl.BlockSpec((EXP_DEV, rows, lanes), lambda d, o: (0, d, 0)),
            ],
        ),
        out_shape=[
            jax.ShapeDtypeStruct((EXP_DEV, devices * capacity, width), BF),
            jax.ShapeDtypeStruct((EXP_DEV, devices * capacity, lanes), F32),
        ],
        compiler_params=params(),
        name="grad_rows",
    )(order, pick, down, *([g_all] * STEP))


def stack_weights(w_ref, gate_ref, up_ref):
    inner, lanes = gate_ref.shape[1], w_ref.shape[1] // 2

    @pl.when(pl.program_id(0) == 0)
    def _():
        for j in range(EXP_DEV):
            for i, ref in ((0, gate_ref), (1, up_ref)):
                w_ref[j, i * lanes : i * lanes + inner] = ref[j]
                if lanes > inner:
                    w_ref[j, i * lanes + inner : (i + 1) * lanes] = jnp.zeros(
                        (lanes - inner, w_ref.shape[2]), BF
                    )


def inner_kernel(
    pick_ref, x_ref, gate_ref, up_ref, weight_ref, grad_ref,
    rows_ref, inner_ref, grads_ref, slot_ref, w_ref,
):
    lanes = grad_ref.shape[2]
    inner = inner_ref.shape[2]
    stack_weights(w_ref, gate_ref, up_ref)
    for i in range(STEP):
        pick_into(rows_ref, pick_ref[i], x_ref[i], i, STEP)
    for j in range(EXP_DEV):
        both = mm_nt(rows_ref[j], w_ref[j])
        gate, up = both[:, :inner], both[:, lanes : lanes + inner]
        act, slope_gate, slope_up = swish_parts(gate, up)
        weight = weight_ref[j]
        grad = grad_ref[j, :, :inner]
        slot_ref[j] = jnp.sum(act.astype(BF).astype(F32) * grad, axis=1, keepdims=True)
        inner_ref[j] = (weight * act).astype(BF)
        grad = weight * grad
        if lanes > inner:
            grads_ref[j] = jnp.zeros(grads_ref.shape[1:], BF)
        grads_ref[j, :, :inner] = (grad * slope_gate).astype(BF)
        grads_ref[j, :, lanes : lanes + inner] = (grad * slope_up).astype(BF)


def inner_of(pick, x_all, gate, up, weight, grad, capacity):
    devices, slots, tokens = pick.shape
    width, lanes, inner = x_all.shape[2], grad.shape[2], gate.shape[1]
    rows = STEP * capacity
    total = devices * capacity
    by_rows = lambda n: pl.BlockSpec((EXP_DEV, rows, n), lambda d: (0, d, 0))
    return pl.pallas_call(
        inner_kernel,
        grid=(devices // STEP,),
        in_specs=[
            pl.BlockSpec((STEP, slots, tokens), lambda d: (d, 0, 0)),
            pl.BlockSpec((STEP, tokens, width), lambda d: (d, 0, 0)),
            resident(gate.shape),
            resident(up.shape),
            by_rows(1),
            by_rows(lanes),
        ],
        out_specs=[by_rows(width), by_rows(inner), by_rows(2 * lanes), by_rows(1)],
        out_shape=[
            jax.ShapeDtypeStruct((EXP_DEV, total, width), BF),
            jax.ShapeDtypeStruct((EXP_DEV, total, inner), BF),
            jax.ShapeDtypeStruct((EXP_DEV, total, 2 * lanes), BF),
            jax.ShapeDtypeStruct((EXP_DEV, total, 1), F32),
        ],
        scratch_shapes=[pltpu.VMEM((EXP_DEV, 2 * lanes, width), BF)],
        compiler_params=params(),
        name="inner",
    )(pick, x_all, gate, up, weight, grad)


def back_kernel(
    rows, pick_ref, grads_ref, gate_ref, up_ref, left_ref, right_ref,
    own_ref, other_ref, hold_ref, w_ref,
):
    stack_weights(w_ref, gate_ref, up_ref)
    for j in range(EXP_DEV):
        hold_ref[j] = mm(grads_ref[j], w_ref[j]).astype(BF)
    for i in range(STEP):
        total = place_from(hold_ref, pick_ref[i], i, STEP) + mm(left_ref[i], right_ref[...])
        out_ref = own_ref if i // rows % 2 == 0 else other_ref
        out_ref[i // (2 * rows) * rows + i % rows] = total.astype(BF)


def back_rows(pick, grads, gate, up, left, right, capacity, x_rows):
    devices, slots, tokens = pick.shape
    width, inner = gate.shape[2], left.shape[2]
    rows = STEP * capacity
    return pl.pallas_call(
        functools.partial(back_kernel, x_rows),
        grid=(devices // STEP,),
        in_specs=[
            pl.BlockSpec((STEP, slots, tokens), lambda d: (d, 0, 0)),
            pl.BlockSpec((EXP_DEV, rows, grads.shape[2]), lambda d: (0, d, 0)),
            resident(gate.shape),
            resident(up.shape),
            pl.BlockSpec((STEP, tokens, inner), lambda d: (d, 0, 0)),
            resident(right.shape),
        ],
        out_specs=[pl.BlockSpec((STEP // 2, tokens, width), lambda d: (d, 0, 0))] * 2,
        out_shape=[jax.ShapeDtypeStruct((devices // 2, tokens, width), BF)] * 2,
        scratch_shapes=[
            pltpu.VMEM((EXP_DEV, rows, width), BF),
            pltpu.VMEM((EXP_DEV, grads.shape[2], width), BF),
        ],
        compiler_params=params(),
        name="back_rows",
    )(pick, grads, gate, up, left, right)


def gate_up_kernel(rows_ref, grads_ref, gate_ref, up_ref):
    inner = gate_ref.shape[1]
    both = mm_tn(grads_ref[0], rows_ref[0])
    gate_ref[0] = both[:inner]
    at = grads_ref.shape[2] // 2
    up_ref[0] = both[at : at + inner]


def gate_up_grads(rows, grads, inner):
    _, total, width = rows.shape
    tile = width // 4
    out = pl.BlockSpec((1, inner, tile), lambda j, i: (j, 0, i))
    return pl.pallas_call(
        gate_up_kernel,
        grid=(EXP_DEV, 4),
        in_specs=[
            pl.BlockSpec((1, total, tile), lambda j, i: (j, 0, i)),
            pl.BlockSpec((1, total, grads.shape[2]), lambda j, i: (j, 0, 0)),
        ],
        out_specs=[out, out],
        out_shape=[jax.ShapeDtypeStruct((EXP_DEV, inner, width), F32)] * 2,
        compiler_params=params(),
        name="gate_up_grads",
    )(rows, grads)


def output_kernel(
    x_rows, pick_ref, inner_ref, down_ref, left_ref, right_ref, own_ref, other_ref, hold_ref
):
    for j in range(EXP_DEV):
        hold_ref[j] = mm(inner_ref[j], down_ref[j]).astype(BF)
    for i in range(STEP):
        total = place_from(hold_ref, pick_ref[i], i, STEP) + mm(left_ref[i], right_ref[...])
        out_ref = own_ref if i // x_rows % 2 == 0 else other_ref
        out_ref[i // (2 * x_rows) * x_rows + i % x_rows] = total.astype(BF)


def output_rows_of(pick, inner, down, left, right, capacity, x_rows):
    devices, slots, tokens = pick.shape
    width = down.shape[2]
    rows = STEP * capacity
    return pl.pallas_call(
        functools.partial(output_kernel, x_rows),
        grid=(devices // STEP,),
        in_specs=[
            pl.BlockSpec((STEP, slots, tokens), lambda d: (d, 0, 0)),
            pl.BlockSpec((EXP_DEV, rows, inner.shape[2]), lambda d: (0, d, 0)),
            resident(down.shape),
            pl.BlockSpec((STEP, tokens, left.shape[2]), lambda d: (d, 0, 0)),
            resident(right.shape),
        ],
        out_specs=[pl.BlockSpec((STEP // 2, tokens, width), lambda d: (d, 0, 0))] * 2,
        out_shape=[jax.ShapeDtypeStruct((devices // 2, tokens, width), BF)] * 2,
        scratch_shapes=[pltpu.VMEM((EXP_DEV, rows, width), BF)],
        compiler_params=params(),
        name="output_rows",
    )(pick, inner, down, left, right)


def body(
    hidden,
    cotangent,
    segments,
    routes,
    w_query,
    w_latent,
    g_latent,
    w_expand,
    w_out,
    g_attn,
    g_ffn,
    w_router,
    s_gate,
    s_up,
    s_down,
    e_gate,
    expert_up_weight,
    e_down,
):
    tokens = hidden.shape[1]
    width = hidden.shape[2]
    links = Links()
    shards, groups = links.shards, links.groups
    devices = groups * shards
    experts = EXP_DEV * groups
    capacity = max(2, tokens * TOP * 4 // (3 * experts))
    heads = H // shards
    length = tokens * shards
    part = width // shards
    my_shard = lax.axis_index("shard")
    my_group = lax.axis_index("expert")
    hid_shard = s_down.shape[0]
    hid = hid_shard // groups
    latent_part = KVR // shards
    shard_at, slot_at = links.shard_at(), links.slot_at()

    g_all = lax.all_gather(cotangent[0], BOTH, axis=0, tiled=False)
    router_rows = part * experts // width
    small_rows = jnp.concatenate([g_attn, g_ffn, g_latent])
    small_rows = jnp.pad(small_rows, (0, -small_rows.shape[0] % width)).reshape(-1, width)
    packed = jnp.concatenate([w_router.reshape(router_rows, width), small_rows])
    packed = links.gather_shard(jnp.pad(packed, ((0, -packed.shape[0] % 16), (0, 0))))
    hidden_all = links.gather_shard(hidden[0]).reshape(length, width)
    pieces = lambda w: jnp.stack(jnp.split(w, shards, axis=1))
    wl = links.gather_shard(w_latent.T)
    wq = links.spread_shard_ring(pieces(w_query))
    we = links.spread_shard(pieces(w_expand))
    packed = jnp.take(packed, slot_at, axis=0)
    full_router = packed[:, :router_rows].reshape(width, experts)
    gains_in = packed[:, router_rows:].reshape(shards, -1)
    gattn = gains_in[:, :part].reshape(1, width).astype(F32)
    gffn = gains_in[:, part : 2 * part].reshape(width).astype(F32)
    glatent = gains_in[:, 2 * part : 2 * part + latent_part].reshape(1, KVR).astype(F32)

    order = links.order()
    same = jnp.arange(devices, dtype=jnp.int32)
    back_order = jnp.sum(
        jnp.where(order[:, None] == same[None, :], same[:, None], 0), axis=0
    ).astype(jnp.int32)
    local_routes = routes[0]
    flat_routes = local_routes.reshape(-1)
    choose = local_routes[:, :, None] == jnp.arange(experts, dtype=jnp.int32)[None, None, :]
    hits = choose.reshape(-1, experts).astype(F32)
    pair_count = tokens * TOP
    before_it = (
        lax.broadcasted_iota(jnp.int32, (pair_count, pair_count), 1)
        < lax.broadcasted_iota(jnp.int32, (pair_count, pair_count), 0)
    ).astype(BF)
    before = mm(before_it, hits.astype(BF))
    slot_rank = jnp.sum(before * hits, axis=1).astype(jnp.int32)
    slot_of = (flat_routes * capacity + slot_rank).reshape(tokens, TOP)
    slots = EXP_DEV * capacity
    slot_rows = jnp.pad(slot_of.T, ((0, 8 - TOP), (0, 0)), constant_values=-1)
    slots_all = exchange(jnp.broadcast_to(slot_rows[None], (devices, 8, tokens)), BOTH)
    slots_all = jnp.take(slots_all, order, axis=0)[:, :TOP]
    slot_ids = my_group * slots + jnp.arange(slots, dtype=jnp.int32)
    pick = jnp.any(
        slots_all[:, None] == slot_ids[None, :, None, None], axis=2
    ).astype(BF)

    positions = (shard_at[:, None] * tokens + jnp.arange(tokens, dtype=jnp.int32)).reshape(-1)
    cosine, sine_vals = rope_angles(positions)
    segs = jnp.take(segments.reshape(shards, tokens), shard_at, axis=0).reshape(-1)
    col = jnp.stack([segs, positions], axis=1)
    row = jnp.stack([segs, positions], axis=0)
    attn_part, n1, compressed, latent, attended, query, kv, lse = attention_forward(
        slot_at, hidden_all, gattn, glatent, wq, wl, we, w_out, cosine, sine_vals, col, row
    )
    inner_units = e_gate.shape[2]
    gate_t, up_t = jnp.swapaxes(e_gate, 1, 2), jnp.swapaxes(expert_up_weight, 1, 2)
    attn_out = links.sum_shard(attn_part.reshape(shards, tokens, width))

    residual_in = hidden[0].astype(F32)
    residual_mid = residual_in + attn_out
    unit_two, factor_two = norm_forward(residual_mid)
    normed_two = (unit_two * gffn).astype(BF)

    hid_ids = my_group * hid + jnp.arange(hid, dtype=jnp.int32)
    wanted = (jnp.arange(shards, dtype=jnp.int32)[:, None] * hid_shard + hid_ids).reshape(-1)
    chosen_units = (
        jnp.arange(shards * hid_shard, dtype=jnp.int32)[:, None] == wanted[None, :]
    ).astype(BF)

    def shared_pieces(units):
        cut = [mm(w, units).astype(BF).reshape(part, shards, hid) for w in (s_gate, s_up)]
        return jnp.concatenate(cut, axis=2).transpose(1, 0, 2)

    shared_down = lax.dynamic_slice_in_dim(s_down, my_group * hid, hid, 0)
    work = [
        Fill(shared_pieces, chosen_units),
        Fill(lambda p: grad_rows_of(p, g_all, order, e_down, capacity), pick),
        Fill(lambda w: mm_nt(g_all.reshape(-1, width), w), shared_down),
    ]
    n2_all = links.gather_all(normed_two, list(enumerate(work, 1))).reshape(
        devices, tokens, width
    )
    gate_up, (grad_rows, grad_inner), shared_grad_inner = (w.result for w in work)
    shared_grad_inner = jnp.take(
        shared_grad_inner.reshape(devices, tokens, hid), order, axis=0
    ).reshape(-1, hid)
    shared_in = links.spread_shard(gate_up)
    shared_in = jnp.take(shared_in, slot_at, axis=0).reshape(width, 2 * hid)
    probs = jax.nn.sigmoid(mm(normed_two, full_router))
    chosen = jnp.sum(jnp.where(choose, probs[:, None, :], 0.0), axis=-1)
    chosen_total = jnp.sum(chosen, axis=1, keepdims=True)

    shared_pre = mm(
        n2_all.reshape(-1, width), jnp.concatenate([shared_in, full_router], axis=1)
    )
    probs_all = jax.nn.sigmoid(
        shared_pre[:, 2 * hid :].reshape(devices, tokens, experts).transpose(0, 2, 1)
    )
    named = jnp.any(
        (slots_all // capacity)[:, None]
        == jnp.arange(experts, dtype=jnp.int32)[None, :, None, None],
        axis=2,
    )
    totals = jnp.sum(jnp.where(named, probs_all, 0.0), axis=1, keepdims=True)
    local_probs = lax.dynamic_slice_in_dim(probs_all, my_group * EXP_DEV, EXP_DEV, 1)
    local_weights = local_probs / totals * ROUTE_SCALE
    slot_weight = jnp.sum(
        jnp.where(
            pick.reshape(devices, EXP_DEV, capacity, tokens) > 0,
            local_weights[:, :, None, :],
            0.0,
        ),
        axis=3,
    )
    row_weight = slot_weight.transpose(1, 0, 2).reshape(EXP_DEV, devices * capacity, 1)

    s_inner, s_slope_gate, s_slope_up = swish_parts(
        shared_pre[:, :hid], shared_pre[:, hid : 2 * hid]
    )
    shared_inner = s_inner.astype(BF)
    shared_grads = jnp.concatenate(
        [shared_grad_inner * s_slope_gate, shared_grad_inner * s_slope_up], axis=1
    ).astype(BF)

    shared_inner_back = jnp.take(
        shared_inner.reshape(devices, tokens, hid), back_order, axis=0
    ).reshape(-1, hid)
    d_shared_down = mm_tn(shared_inner_back, g_all.reshape(-1, width)).astype(BF)
    shared_out = mm_tn(shared_grads, n2_all.reshape(-1, width)).astype(BF)
    shared_out = shared_out.reshape(2 * hid, shards, part).transpose(1, 0, 2)
    in_pieces = jnp.take(links.spread_shard(shared_out), slot_at, axis=0)
    row_weight, (d_shared_down, in_pieces) = tie(row_weight, (d_shared_down, in_pieces))
    down_all = lax.all_gather(d_shared_down, "expert", axis=0, tiled=True)
    in_all = lax.all_gather(in_pieces, "expert", axis=0, tiled=False)

    rows, inner_w, grads_b, grad_slot_weight = inner_of(
        pick, n2_all, gate_t, up_t, row_weight, grad_inner, capacity
    )
    dn2_own, dn2_other = back_rows(
        pick, grads_b, gate_t, up_t, shared_grads.reshape(devices, tokens, 2 * hid),
        shared_in.T, capacity, shards // 2,
    )

    def router_back(slot_sums):
        slot_back = slot_sums.reshape(EXP_DEV, devices, capacity).transpose(1, 0, 2)
        slot_back = jnp.take(slot_back.reshape(devices, slots), back_order, axis=0)
        got = exchange(slot_back, BOTH)
        slot_grads = jnp.sum(got.reshape(groups, shards, slots), axis=1).reshape(-1)
        at_slot = slot_of[:, :, None] == jnp.arange(experts * capacity, dtype=jnp.int32)
        grad_weights = jnp.sum(jnp.where(at_slot, slot_grads, 0.0), axis=2)
        grad_chosen = ROUTE_SCALE * (
            grad_weights / chosen_total
            - jnp.sum(grad_weights * chosen, axis=1, keepdims=True)
            / (chosen_total * chosen_total)
        )
        grad_probs = jnp.sum(jnp.where(choose, grad_chosen[:, :, None], 0.0), axis=1)
        return (grad_probs * probs * (1.0 - probs)).astype(BF)

    down_grad = lambda a, b: jnp.einsum("jmf,jmd->jfd", a, b, preferred_element_type=F32)
    ring_shape = (groups, shards // 2, tokens, width)
    half = groups // 2

    def output_parts(inner_of):
        own, other = output_rows_of(
            pick, inner_of, e_down, shared_inner.reshape(devices, tokens, hid), shared_down,
            capacity, shards // 2,
        )
        return links.sum_core(own.reshape(ring_shape), other.reshape(ring_shape))

    work = [
        Fill(
            lambda a, b: (router_back(a), down_grad(b, grad_rows)),
            grad_slot_weight, inner_w,
        ),
        Fill(output_parts, inner_w),
        Fill(lambda b: gate_up_grads(rows, b, inner_units), grads_b),
    ]
    (dn2,) = links.ring_reduce(
        [links.sum_core(dn2_own.reshape(ring_shape), dn2_other.reshape(ring_shape))],
        [half],
        [(half - i, w) for i, w in enumerate(work)],
    )
    (grad_logits, d_edown), out_parts, (d_egate, grad_expert_up) = (w.result for w in work)

    def back_to_attention(top, logits):
        grad_normed_two = links.sum_x(top) + mm_nt(logits, full_router)
        grad_mid_norm, d_gffn = norm_backward(grad_normed_two, gffn, unit_two, factor_two)
        grad_mid = cotangent[0].astype(F32) + grad_mid_norm
        grad_attn = links.gather_shard(grad_mid.astype(BF)).reshape(length, width)
        return grad_mid, d_gffn, grad_attn

    backward = lambda grad_attn: attention_backward(
        slot_at, grad_attn, glatent, w_out, attended, query, kv, lse, latent, compressed,
        we, wl, wq, n1, cosine, sine_vals, col, row,
    )
    first = Fill(back_to_attention, dn2, grad_logits)
    second = Fill(
        lambda grad, *_: backward(grad), lambda: first.result[2], in_all, down_all
    )
    (routed_shared,) = links.ring_reduce([out_parts], [half], [(half, first), (half - 1, second)])
    routed_shared = links.sum_x(routed_shared)
    grad_mid, d_gffn, _ = first.result
    dn1, dw, dwl, d_out, d_glatent = second.result
    output_rows = residual_mid + routed_shared
    logits_back = exchange(
        jnp.broadcast_to(grad_logits.T[None], (devices, experts, tokens)), BOTH
    )
    logits_back = jnp.take(logits_back, order, axis=0)
    own_columns = lax.dynamic_slice_in_dim(n2_all, my_shard * part, part, 2)
    d_router = mm(
        logits_back.transpose(1, 0, 2).reshape(experts, -1), own_columns.reshape(-1, part)
    ).T
    grad_normed = links.sum_shard(dn1.reshape(shards, tokens, width))
    unit_one, factor_one = norm_forward(residual_in)
    grad_input_norm, d_gattn = norm_backward(
        grad_normed, gattn.reshape(width), unit_one, factor_one
    )
    grad_input = grad_mid + grad_input_norm

    cut = part // groups
    lat = links.sum_shard(dwl).astype(BF).reshape(groups, (KVR + DR) // groups, part)
    by_head = links.blocks(dw.reshape(shards, groups, cut, -1).transpose(1, 0, 2, 3))
    by_row = links.blocks(d_out.reshape(groups, cut, width))
    pluses = [groups // 2, (groups - 1) // 2]
    work_s = Fill(shared_finish, in_all)
    sum_head, sum_row = links.ring_reduce(
        [by_head, by_row], pluses, [(groups // 2 - 1, work_s)]
    )
    (sum_lat,) = links.ring_reduce([links.blocks(lat)], pluses[1:])
    part_sgate, part_sup = work_s.result
    sum_head = links.exchange_shard(sum_head.astype(BF))
    all_head, all_row = links.ring_gather([sum_head, sum_row.astype(BF)], pluses)
    (all_lat,) = links.ring_gather([sum_lat.astype(BF)], pluses[1:])
    part_query, part_expand, part_out = finish(
        links.block_at(), all_head, all_row, heads, width
    )
    part_latent = jnp.take(jnp.stack(all_lat), links.block_at(), axis=0)
    part_latent = part_latent.reshape(KVR + DR, part).astype(F32)

    gain_grads = jnp.concatenate(
        [
            d_gattn.reshape(shards, part),
            d_gffn.reshape(shards, part),
            d_glatent.reshape(shards, latent_part),
        ],
        axis=1,
    )
    got = exchange(
        jnp.broadcast_to(gain_grads[None], (groups,) + gain_grads.shape).reshape(devices, -1),
        BOTH,
    )
    gains = jnp.sum(got, axis=0)
    return (
        output_rows.astype(BF)[None],
        grad_input[None],
        part_query,
        part_latent.T,
        gains[2 * part :],
        part_expand,
        part_out,
        gains[:part],
        gains[part : 2 * part],
        d_router,
        part_sgate,
        part_sup,
        down_all.astype(F32),
        jnp.swapaxes(d_egate, 1, 2),
        jnp.swapaxes(grad_expert_up, 1, 2),
        d_edown,
    )


def solution(mesh):
    return jax.shard_map(
        body,
        mesh=mesh,
        in_specs=(
            P("expert", "shard", None),
            P("expert", "shard", None),
            P("expert", None),
            P("expert", "shard", None),
            P("shard", None),
            P("shard", None),
            P("shard"),
            P("shard", None),
            P("shard", None),
            P("shard"),
            P("shard"),
            P("shard", None),
            P("shard", None),
            P("shard", None),
            P("shard", None),
            P("expert", None, "shard"),
            P("expert", None, "shard"),
            P("expert", "shard", None),
        ),
        out_specs=(
            P("expert", "shard", None),
            P("expert", "shard", None),
            P("shard", None),
            P("shard", None),
            P("shard"),
            P("shard", None),
            P("shard", None),
            P("shard"),
            P("shard"),
            P("shard", None),
            P("shard", None),
            P("shard", None),
            P("shard", None),
            P("expert", None, "shard"),
            P("expert", None, "shard"),
            P("expert", "shard", None),
        ),
        check_vma=False,
    )
```

```python
import functools

import jax
import jax.numpy as jnp
from jax import lax
from jax.experimental import pallas as pl
from jax.experimental.pallas import tpu as pltpu
from jax.sharding import PartitionSpec as P

H = 16
DN = 128
DR = 64
DV = 128
KVR = 512
TOP = 6
EXP_DEV = 4

EPS = 1e-06
ROUTE_SCALE = 2.446
ROPE_BASE = 50000.0
SCORE_SCALE = (DN + DR) ** (-0.5)
BF = jnp.bfloat16
F32 = jnp.float32
BOTH = ("expert", "shard")
VMEM_BYTES = 56 * 1024 * 1024


def mm(a, b):
    return jnp.dot(a, b, preferred_element_type=F32)


def mm_tn(a, b):
    return lax.dot_general(a, b, (((0,), (0,)), ((), ())), preferred_element_type=F32)


def mm_nt(a, b):
    return lax.dot_general(a, b, (((1,), (1,)), ((), ())), preferred_element_type=F32)


def rope_angles(positions):
    half_width = DR // 2
    inverse = ROPE_BASE ** (-jnp.arange(half_width).astype(F32) / half_width)
    angles = positions.astype(F32)[:, None] * inverse[None, :]
    return (jnp.cos(angles), jnp.sin(angles))


def rotate(values, cosine, sine_vals):
    half_width = DR // 2
    first_half = values[..., :half_width]
    second_half = values[..., half_width:]
    return jnp.concatenate(
        [
            first_half * cosine - second_half * sine_vals,
            second_half * cosine + first_half * sine_vals,
        ],
        axis=-1,
    )


def norm_forward(values):
    factor = lax.rsqrt(jnp.mean(values * values, axis=-1, keepdims=True) + EPS)
    return values * factor, factor


def norm_backward(grad_out, gain_vec, unit_vals, factor):
    grad_unit = grad_out * gain_vec
    grad_in = factor * (
        grad_unit - unit_vals * jnp.mean(grad_unit * unit_vals, axis=-1, keepdims=True)
    )
    return (grad_in, jnp.sum(grad_out * unit_vals, axis=0))


def swish_parts(gate, up):
    sig = jax.nn.sigmoid(gate)
    silu = gate * sig
    return silu * up, up * sig * (1.0 + gate * (1.0 - sig)), silu


def exchange(values, axis):
    return lax.all_to_all(values, axis, split_axis=0, concat_axis=0, tiled=True)


def tie(streams, extra):
    return lax.optimization_barrier((streams, extra))


class Fill:
    def __init__(self, work, *inputs, mark=None):
        self.work, self.given, self.result, self.mark = work, inputs, None, mark

    @property
    def inputs(self):
        return tuple(v() if callable(v) else v for v in self.given)


class Links:
    def __init__(self):
        self.groups = lax.axis_size("expert")
        self.shards = lax.axis_size("shard")
        self.rows = self.shards // 2
        n = self.groups
        self.ring = list(range(0, n, 2)) + list(range(n - 1, 0, -2))
        shard = lax.axis_index("shard")
        self.x = shard // 2
        self.core = shard % 2
        group = lax.axis_index("expert")
        places = [self.ring.index(e) for e in range(n)]
        self.place = jnp.sum(
            jnp.where(jnp.arange(n) == group, jnp.array(places, jnp.int32), 0)
        )

    def send(self, values, target):
        pairs = []
        for e in range(self.groups):
            for s in range(self.shards):
                pairs.append((e * self.shards + s, target(e, s)))
        return lax.ppermute(values, BOTH, pairs)

    def around(self, values, step):
        n = self.groups
        return self.send(
            values,
            lambda e, s: self.ring[(self.ring.index(e) + step) % n] * self.shards + s,
        )

    def along_x(self, values, step):
        return self.send(
            values,
            lambda e, s: e * self.shards + ((s // 2 + step) % self.rows) * 2 + s % 2,
        )

    def partner(self, values):
        return self.send(values, lambda e, s: e * self.shards + (s ^ 1))

    def shard_at(self):
        xs = (self.x - jnp.arange(self.rows, dtype=jnp.int32)) % self.rows
        cores = jnp.stack([self.core, 1 - self.core]).astype(jnp.int32)
        return (xs[:, None] * 2 + cores[None, :]).reshape(-1).astype(jnp.int32)

    def slot_at(self):
        shard = jnp.arange(self.shards, dtype=jnp.int32)
        back = (self.x - shard // 2) % self.rows
        return (back * 2 + (shard % 2 != self.core)).astype(jnp.int32)

    def gather_shard(self, values):
        out = []
        for k in range(self.rows):
            own = values if k == 0 else self.along_x(values, k)
            out += [own, self.partner(own)]
        return jnp.stack(out)

    def spread_shard(self, pieces):
        take = lambda v, i: lax.dynamic_index_in_dim(v, i, 0, keepdims=False)
        pairs = pieces.reshape((self.rows, 2) + pieces.shape[1:])
        out = []
        for k in range(self.rows):
            got = take(pairs, (self.x + k) % self.rows)
            got = got if k == 0 else self.along_x(got, k)
            out += [take(got, self.core), self.partner(take(got, 1 - self.core))]
        return jnp.stack(out)

    def spread_shard_ring(self, pieces):
        n, rows = self.groups, self.rows
        take = lambda v, i, axis: lax.dynamic_index_in_dim(v, i, axis, keepdims=False)
        part, wide = pieces.shape[1:]
        pairs = pieces.reshape(rows, 2, n, part // n, wide)
        mine = take(pairs, self.place, 2)
        out = []
        for k in range(rows):
            if k == 0:
                got = take(pairs, self.x, 0)
            else:
                far = self.along_x(take(mine, (self.x + k) % rows, 0), k)
                (far,) = self.ring_gather([far], [n // 2])
                got = jnp.take(jnp.stack(far, axis=1), self.block_at(), axis=1)
            got = got.reshape(2, part, wide)
            out += [take(got, self.core, 0), self.partner(take(got, 1 - self.core, 0))]
        return jnp.stack(out)

    def exchange_shard(self, values):
        pairs = values.reshape((self.rows, 2) + values.shape[1:])
        out = []
        for k in range(self.rows):
            got = pairs[k] if k == 0 else self.along_x(pairs[k], -k)
            out += [got[0], self.partner(got[1])]
        xs = (self.x + jnp.arange(self.rows, dtype=jnp.int32)) % self.rows
        shard = jnp.arange(self.shards, dtype=jnp.int32)
        ahead = (shard // 2 - self.x) % self.rows
        slot = ahead * 2 + (shard % 2 != self.core)
        return jnp.take(jnp.stack(out), slot, axis=0)

    def sum_shard(self, values, fill=None):
        pairs = values.reshape((self.rows, 2) + values.shape[1:])
        both = [
            pairs[k, 0].astype(F32) + self.partner(pairs[k, 1]).astype(F32)
            for k in range(self.rows)
        ]
        far = [v.astype(BF) for v in both[1:]]
        if fill is not None:
            _, inputs = tie(far, fill.inputs)
        far = [self.along_x(v, -k - 1) for k, v in enumerate(far)]
        if fill is not None:
            far, fill.result = tie(far, fill.work(*inputs))
        total = both[0]
        for v in far:
            total = total + v.astype(F32)
        return total

    def ring_gather(self, values, pluses, fills=(), outs=None):
        n = self.groups
        fills = dict(fills)
        outs = [] if outs is None else outs
        outs += [[v] + [None] * (n - 1) for v in values]
        ahead, back = list(values), list(values)
        for r in range(1, n):
            moves = [(i, 1) for i, p in enumerate(pluses) if r <= p]
            moves += [(i, -1) for i, p in enumerate(pluses) if r <= n - 1 - p]
            if not moves:
                break
            streams = [ahead[i] if step > 0 else back[i] for i, step in moves]
            streams = self.step(streams, [step for _, step in moves], fills.get(r))
            for (i, step), got in zip(moves, streams):
                if step > 0:
                    ahead[i] = outs[i][r] = got
                else:
                    back[i] = outs[i][n - r] = got
        return outs

    def step(self, streams, steps, fill):
        if fill is None:
            return [self.around(v, s) for v, s in zip(streams, steps)]
        streams, inputs = tie(streams, fill.inputs)
        streams = [self.around(v, s) for v, s in zip(streams, steps)]
        result = fill.work(*inputs)
        if fill.mark is None:
            streams, fill.result = tie(streams, result)
        else:
            fill.result = list(result)
            streams, fill.result[fill.mark] = tie(streams, result[fill.mark])
        return streams

    def ring_reduce(self, parts, pluses, fills=()):
        n = self.groups
        fills = dict(fills)
        ahead = [p[plus] for p, plus in zip(parts, pluses)]
        back = [p[plus + 1] for p, plus in zip(parts, pluses)]
        most = max(max(p, n - 1 - p) for p in pluses)
        for r in range(most, 0, -1):
            moves = [(i, 1) for i, p in enumerate(pluses) if r <= p]
            moves += [(i, -1) for i, p in enumerate(pluses) if r <= n - 1 - p]
            streams = [ahead[i] if step > 0 else back[i] for i, step in moves]
            streams = self.step(streams, [-step for _, step in moves], fills.get(r))
            for (i, step), got in zip(moves, streams):
                here = parts[i][r - 1 if step > 0 else (n - r + 1) % n]
                if r > 1:
                    got = (got.astype(F32) + here.astype(F32)).astype(BF)
                if step > 0:
                    ahead[i] = got
                else:
                    back[i] = got
        return [
            p[0].astype(F32) + a.astype(F32) + b.astype(F32)
            for p, a, b in zip(parts, ahead, back)
        ]

    def block_at(self):
        return (self.place - jnp.arange(self.groups, dtype=jnp.int32)) % self.groups

    def blocks(self, values):
        return [
            lax.dynamic_index_in_dim(
                values, (self.place - r) % self.groups, 0, keepdims=False
            )
            for r in range(self.groups)
        ]

    def arrival(self):
        n = self.groups
        return [0] + [r for k in range(1, n // 2 + 1) for r in dict.fromkeys((k, n - k))]

    def order(self):
        n = self.groups
        ring = jnp.array(self.ring, jnp.int32)
        groups = jnp.sum(
            jnp.where(
                self.block_at()[jnp.array(self.arrival())][:, None] == jnp.arange(n)[None, :],
                ring[None, :],
                0,
            ),
            axis=1,
        )
        shard = self.shard_at().reshape(self.rows, 2).T.reshape(-1)
        all_of = groups[:, None] * self.shards + shard[None, :]
        return all_of.reshape(-1).astype(jnp.int32)

    def sum_core(self, own, other):
        both = (own.astype(F32) + self.partner(other).astype(F32)).astype(BF)
        return [both[self.arrival().index(r)] for r in range(self.groups)]

    def sum_x(self, top):
        total = top[0]
        for k in range(1, self.rows):
            total = total + self.along_x(top[k].astype(BF), -k).astype(F32)
        return total


def params(**kw):
    return pltpu.CompilerParams(vmem_limit_bytes=VMEM_BYTES, **kw)


SMEM = pl.BlockSpec(memory_space=pltpu.SMEM)
VMEM = pl.BlockSpec(memory_space=pltpu.VMEM)


def allowed_mask(seg_col, seg_row, pos_col, pos_row):
    return (seg_col == seg_row) & (pos_row <= pos_col)


def attention_forward_kernel(
    slot_ref, x_ref, gattn_ref, glat_ref, wq_ref, wl_ref, we_ref, wo_ref,
    cos_ref, sin_ref, col_ref, row_ref,
    out_ref, n1_ref, c_ref, lat_ref, o_ref, q_ref, kv_ref, lse_ref,
):
    shards, part = wq_ref.shape[0], wq_ref.shape[1]
    heads = q_ref.shape[0]
    tokens = x_ref.shape[0] // shards
    for b in range(shards):
        at = slice(b * tokens, (b + 1) * tokens)
        unit, _ = norm_forward(x_ref[at].astype(F32))
        n1_ref[at] = (unit * gattn_ref[...]).astype(BF)
    queries, compressed, kv_all = None, None, None
    for s in range(shards):
        left = n1_ref[:, s * part : (s + 1) * part]
        one = mm(left, wq_ref[slot_ref[s]])
        queries = one if s == 0 else queries + one
        one = mm_nt(left, wl_ref[slot_ref[s]])
        compressed = one if s == 0 else compressed + one
    c_ref[...] = compressed
    unit, _ = norm_forward(compressed[:, :KVR])
    lat_ref[:, :KVR] = (unit * glat_ref[...]).astype(BF)
    lat_ref[:, KVR:] = rotate(compressed[:, KVR:], cos_ref[...], sin_ref[...]).astype(BF)
    part = KVR // shards
    for s in range(shards):
        one = mm(lat_ref[:, s * part : (s + 1) * part], we_ref[slot_ref[s]])
        kv_all = one if s == 0 else kv_all + one
    kv_ref[...] = kv_all.astype(BF)
    ok = allowed_mask(
        col_ref[:, :1], row_ref[:1, :], col_ref[:, 1:2], row_ref[1:2, :]
    )
    key_rot = lat_ref[:, KVR:]
    for h in range(heads):
        at = h * (DN + DR)
        query = jnp.concatenate(
            [
                queries[:, at : at + DN],
                rotate(queries[:, at + DN : at + DN + DR], cos_ref[...], sin_ref[...]),
            ],
            axis=1,
        ).astype(BF)
        q_ref[h] = query
        at = h * (DN + DV)
        keys = kv_ref[:, at : at + DN]
        values = kv_ref[:, at + DN : at + DN + DV]
        scores = mm_nt(query[:, :DN], keys) + mm_nt(query[:, DN:], key_rot)
        scores = jnp.where(ok, scores * SCORE_SCALE, -1e30)
        top = jnp.max(scores, axis=1, keepdims=True)
        expo = jnp.exp(scores - top)
        total = jnp.sum(expo, axis=1, keepdims=True)
        lse_ref[h] = top + jnp.log(total)
        weights = (expo / total).astype(BF)
        o_ref[:, h * DV : (h + 1) * DV] = mm(weights, values).astype(BF)
    out_ref[...] = mm(o_ref[...], wo_ref[...]).astype(BF)


def attention_forward(slot, x, gattn, glat, wq, wl, we, wo, cosine, sine_vals, col, row):
    length, width = x.shape
    heads = wo.shape[0] // DV
    return pl.pallas_call(
        attention_forward_kernel,
        in_specs=[SMEM] + [VMEM] * 11,
        out_shape=[
            jax.ShapeDtypeStruct((length, width), BF),
            jax.ShapeDtypeStruct((length, width), BF),
            jax.ShapeDtypeStruct((length, KVR + DR), F32),
            jax.ShapeDtypeStruct((length, KVR + DR), BF),
            jax.ShapeDtypeStruct((length, heads * DV), BF),
            jax.ShapeDtypeStruct((heads, length, DN + DR), BF),
            jax.ShapeDtypeStruct((length, heads * (DN + DV)), BF),
            jax.ShapeDtypeStruct((heads, length, 1), F32),
        ],
        compiler_params=params(),
        name="attention_forward",
    )(slot, x, gattn, glat, wq, wl, we, wo, cosine, sine_vals, col, row)


def attention_backward_kernel(
    slot_ref, dh_ref, glat_ref, wo_ref, o_ref, q_ref, kv_ref, lse_ref, lat_ref, c_ref,
    we_ref, wl_ref, wq_ref, n1_ref, cos_ref, sin_ref, col_ref, row_ref,
    dn1_ref, dw_ref, dwl_ref, dwo_ref, dgl_ref,
    go_ref, gq_ref, gkv_ref, gc_ref,
):
    shards, part = wq_ref.shape[0], wq_ref.shape[1]
    heads = q_ref.shape[0]
    go_ref[...] = mm_nt(dh_ref[...], wo_ref[...]).astype(BF)
    dwo_ref[...] = mm_tn(o_ref[...], dh_ref[...]).astype(BF)
    ok = allowed_mask(
        col_ref[:, :1], row_ref[:1, :], col_ref[:, 1:2], row_ref[1:2, :]
    )
    key_rot = lat_ref[:, KVR:]
    grad_kr = None
    for h in range(heads):
        at = h * (DN + DV)
        keys = kv_ref[:, at : at + DN]
        values = kv_ref[:, at + DN : at + DN + DV]
        query = q_ref[h]
        grad_o = go_ref[:, h * DV : (h + 1) * DV]
        scores = mm_nt(query[:, :DN], keys) + mm_nt(query[:, DN:], key_rot)
        weights = jnp.where(ok, jnp.exp(scores * SCORE_SCALE - lse_ref[h]), 0.0)
        grad_w = mm_nt(grad_o, values)
        delta = jnp.sum(weights * grad_w, axis=1, keepdims=True)
        grad_s = (weights * (grad_w - delta) * SCORE_SCALE).astype(BF)
        gkv_ref[:, at : at + DN] = mm_tn(grad_s, query[:, :DN]).astype(BF)
        gkv_ref[:, at + DN : at + DN + DV] = mm_tn(weights.astype(BF), grad_o).astype(BF)
        one = mm_tn(grad_s, query[:, DN:])
        grad_kr = one if h == 0 else grad_kr + one
        at = h * (DN + DR)
        grad_qr = rotate(mm(grad_s, key_rot), cos_ref[...], -sin_ref[...])
        gq_ref[:, at : at + DN + DR] = jnp.concatenate(
            [mm(grad_s, keys), grad_qr], axis=1
        ).astype(BF)
    latent_part = KVR // shards
    query_wide = heads * (DN + DR)
    ratio = part // latent_part
    piece = heads * (DN + DV) // ratio
    grad_lat = []
    for s in range(shards):
        at = slice(s * latent_part, (s + 1) * latent_part)
        grad_lat.append(mm_nt(gkv_ref[...], we_ref[slot_ref[s]]))
        one = mm_tn(lat_ref[:, at], gkv_ref[...]).astype(BF)
        for i in range(ratio):
            dw_ref[slot_ref[s], i * latent_part : (i + 1) * latent_part, query_wide:] = one[
                :, i * piece : (i + 1) * piece
            ]
    grad_lat = jnp.concatenate(grad_lat, axis=1)
    unit, factor = norm_forward(c_ref[:, :KVR])
    grad_norm, grad_gain = norm_backward(grad_lat, glat_ref[...], unit, factor)
    dgl_ref[...] = grad_gain.reshape(1, KVR)
    gc_ref[:, :KVR] = grad_norm.astype(BF)
    gc_ref[:, KVR:] = rotate(grad_kr, cos_ref[...], -sin_ref[...]).astype(BF)
    for s in range(shards):
        at = slice(s * part, (s + 1) * part)
        dn1_ref[:, at] = (
            mm_nt(gq_ref[...], wq_ref[slot_ref[s]]) + mm(gc_ref[...], wl_ref[slot_ref[s]])
        ).astype(BF)
        dw_ref[slot_ref[s], :, :query_wide] = mm_tn(n1_ref[:, at], gq_ref[...]).astype(BF)
        dwl_ref[slot_ref[s]] = mm_tn(gc_ref[...], n1_ref[:, at]).astype(BF)


def attention_backward(
    slot, dh, glat, wo, o, query, kv, lse, latent, compressed, we, wl, wq, n1,
    cosine, sine_vals, col, row,
):
    length, width = n1.shape
    heads = query.shape[0]
    shards, part = wq.shape[0], wq.shape[1]
    wide = heads * (DN + DR) + heads * (DN + DV) * KVR // width
    return pl.pallas_call(
        attention_backward_kernel,
        in_specs=[SMEM] + [VMEM] * 17,
        out_shape=[
            jax.ShapeDtypeStruct((length, width), BF),
            jax.ShapeDtypeStruct((shards, part, wide), BF),
            jax.ShapeDtypeStruct(wl.shape, BF),
            jax.ShapeDtypeStruct((heads * DV, width), BF),
            jax.ShapeDtypeStruct((1, KVR), F32),
        ],
        scratch_shapes=[
            pltpu.VMEM((length, heads * DV), BF),
            pltpu.VMEM((length, heads * (DN + DR)), BF),
            pltpu.VMEM((length, heads * (DN + DV)), BF),
            pltpu.VMEM((length, KVR + DR), BF),
        ],
        compiler_params=params(),
        name="attention_backward",
    )(
        slot, dh, glat, wo, o, query, kv, lse, latent, compressed, we, wl, wq, n1,
        cosine, sine_vals, col, row,
    )


def finish_kernel(groups, shards, per, piece, *refs):
    place_ref = refs[0]
    by_head, by_row = (refs[1 + i * groups : 1 + (i + 1) * groups] for i in range(2))
    query_ref, expand_ref, out_ref = refs[1 + 2 * groups :]
    cut = by_row[0].shape[0]
    wide = by_head[0].shape[2] - piece
    expand_wide = expand_ref.shape[1] // shards
    for r in range(groups):
        at = place_ref[r]
        rows = pl.ds(pl.multiple_of(at * cut, cut), cut)
        out_ref[rows, :] = by_row[r][...].astype(F32)
        low = pl.ds(pl.multiple_of((at % per) * cut, cut), cut)
        for s in range(shards):
            query_ref[rows, s * wide : (s + 1) * wide] = by_head[r][s, :, :wide].astype(F32)
            lanes = pl.ds(
                pl.multiple_of(s * expand_wide + (at // per) * piece, piece), piece
            )
            expand_ref[low, lanes] = by_head[r][s, :, wide:].astype(F32)


def finish(place, by_head, by_row, heads, width):
    groups, shards = len(by_head), by_head[0].shape[0]
    latent_part = KVR // shards
    part = width // shards
    per = groups * latent_part // part
    piece = heads * (DN + DV) * latent_part // part
    return pl.pallas_call(
        functools.partial(finish_kernel, groups, shards, per, piece),
        in_specs=[SMEM] + [VMEM] * (2 * groups),
        out_shape=[
            jax.ShapeDtypeStruct((part, H * (DN + DR)), F32),
            jax.ShapeDtypeStruct((latent_part, H * (DN + DV)), F32),
            jax.ShapeDtypeStruct((part, width), F32),
        ],
        compiler_params=params(),
        name="finish",
    )(place, *by_head, *by_row)


def shared_finish_kernel(x_ref, gate_ref, up_ref, hold_ref):
    groups, shards, hid = x_ref.shape[0], x_ref.shape[1], x_ref.shape[2] // 2
    for i, out_ref in ((0, gate_ref), (1, up_ref)):
        for s in range(shards):
            for g in range(groups):
                at = (s * groups + g) * hid
                hold_ref[at : at + hid] = x_ref[g, s, i * hid : (i + 1) * hid].astype(F32)
        out_ref[...] = hold_ref[...].T


def shared_finish(pieces):
    groups, shards, two, part = pieces.shape
    wide = groups * shards * two // 2
    return pl.pallas_call(
        shared_finish_kernel,
        in_specs=[VMEM],
        out_shape=[jax.ShapeDtypeStruct((part, wide), F32)] * 2,
        scratch_shapes=[pltpu.VMEM((wide, part), F32)],
        compiler_params=params(),
        name="shared_finish",
    )(pieces)


STEP = 8
PAD = 128


def pick_into(out_ref, pick, rows_of, i, step):
    capacity = out_ref.shape[1] // step
    rows = mm(pick, rows_of).astype(BF)
    out_ref[:, i * capacity : (i + 1) * capacity, :] = rows.reshape(
        EXP_DEV, capacity, rows.shape[1]
    )


def place_from(rows_ref, pick, i, step):
    capacity = rows_ref.shape[1] // step
    rows = rows_ref[:, i * capacity : (i + 1) * capacity, :]
    return mm_tn(pick, rows.reshape(EXP_DEV * capacity, rows.shape[2]))


def resident(shape):
    return pl.BlockSpec(
        shape, lambda *_: (0,) * len(shape), pipeline_mode=pl.Buffered(1)
    )


def grad_rows_kernel(order_ref, pick_ref, down_ref, *refs):
    rows_ref, inner_ref = refs[STEP:]
    inner = down_ref.shape[1]
    for i in range(STEP):
        pick_into(rows_ref, pick_ref[i], refs[i][0], i, STEP)
    for j in range(EXP_DEV):
        inner_ref[j, :, :inner] = mm_nt(rows_ref[j], down_ref[j])


def grad_rows_of(pick, g_all, order, down, capacity):
    devices, slots, tokens = pick.shape
    width, inner = g_all.shape[2], down.shape[1]
    lanes = inner + -inner % PAD
    rows = STEP * capacity
    at = lambda i: pl.BlockSpec((1, tokens, width), lambda d, o: (o[d * STEP + i], 0, 0))
    return pl.pallas_call(
        grad_rows_kernel,
        grid_spec=pltpu.PrefetchScalarGridSpec(
            num_scalar_prefetch=1,
            grid=(devices // STEP,),
            in_specs=[
                pl.BlockSpec((STEP, slots, tokens), lambda d, o: (d, 0, 0)),
                resident(down.shape),
            ]
            + [at(i) for i in range(STEP)],
            out_specs=[
                pl.BlockSpec((EXP_DEV, rows, width), lambda d, o: (0, d, 0)),
                pl.BlockSpec((EXP_DEV, rows, lanes), lambda d, o: (0, d, 0)),
            ],
        ),
        out_shape=[
            jax.ShapeDtypeStruct((EXP_DEV, devices * capacity, width), BF),
            jax.ShapeDtypeStruct((EXP_DEV, devices * capacity, lanes), F32),
        ],
        compiler_params=params(),
        name="grad_rows",
    )(order, pick, down, *([g_all] * STEP))


def stack_weights(w_ref, gate_ref, up_ref):
    inner, lanes = gate_ref.shape[1], w_ref.shape[1] // 2

    @pl.when(pl.program_id(0) == 0)
    def _():
        for j in range(EXP_DEV):
            for i, ref in ((0, gate_ref), (1, up_ref)):
                w_ref[j, i * lanes : i * lanes + inner] = ref[j]
                if lanes > inner:
                    w_ref[j, i * lanes + inner : (i + 1) * lanes] = jnp.zeros(
                        (lanes - inner, w_ref.shape[2]), BF
                    )


def inner_kernel(
    count, group_ref, pick_ref, named_ref, *refs
):
    x_refs = refs[:count]
    (
        gate_ref, up_ref, shared_ref, grad_ref, shared_grad_ref,
        rows_ref, inner_ref, grads_ref, slot_ref, shared_grads_ref, shared_inner_ref, sum_ref,
    ) = refs[count : count + 5] + refs[-9:-2]
    w_ref, weight_ref = refs[-2:]
    before_ref = refs[-10] if len(refs) == count + 5 + 16 else None
    lanes, inner = grad_ref.shape[2], inner_ref.shape[2]
    hid, pad = shared_grad_ref.shape[1], shared_inner_ref.shape[2]
    x_rows, tokens = x_refs[0].shape[0], x_refs[0].shape[1]
    capacity = rows_ref.shape[1] // STEP
    experts = named_ref.shape[2]
    stack_weights(w_ref, gate_ref, up_ref)
    slots = EXP_DEV * capacity
    mine = group_ref[0] * EXP_DEV + lax.broadcasted_iota(
        jnp.int32, (slots, 3 * experts), 0
    ) // capacity
    at_mine = lax.broadcasted_iota(jnp.int32, (slots, 3 * experts), 1) % experts == mine
    total = None
    for i in range(STEP):
        x = x_refs[i // x_rows][i % x_rows]
        pick_into(rows_ref, pick_ref[i], x, i, STEP)
        both = mm(x, shared_ref[...])
        probs = jax.nn.sigmoid(both[:, 2 * pad : 2 * pad + experts])
        named = named_ref[i]
        weight = probs / jnp.sum(probs * named, axis=1, keepdims=True) * ROUTE_SCALE
        high = weight.astype(BF)
        rest = weight - high.astype(F32)
        middle = rest.astype(BF)
        low = (rest - middle.astype(F32)).astype(BF)
        at_slots = mm(pick_ref[i], jnp.concatenate([high, middle, low], axis=1))
        at_slots = jnp.sum(jnp.where(at_mine, at_slots, 0.0), axis=1, keepdims=True)
        weight_ref[:, i * capacity : (i + 1) * capacity] = at_slots.reshape(
            EXP_DEV, capacity, 1
        )
        act, slope_gate, slope_up = swish_parts(both[:, :hid], both[:, pad : pad + hid])
        grad = shared_grad_ref[i * tokens : (i + 1) * tokens]
        zeros = jnp.zeros((tokens, pad - hid), BF)
        join = lambda v: v.astype(BF) if pad == hid else jnp.concatenate(
            [v.astype(BF), zeros], axis=1
        )
        shared_inner_ref[i] = join(act)
        shared_grads_ref[i, :, :pad] = join(grad * slope_gate)
        shared_grads_ref[i, :, pad:] = join(grad * slope_up)
        one = mm_tn(shared_grads_ref[i], x)
        total = one if total is None else total + one
    sum_ref[...] = total if before_ref is None else total + before_ref[...]
    for j in range(EXP_DEV):
        both = mm_nt(rows_ref[j], w_ref[j])
        gate, up = both[:, :inner], both[:, lanes : lanes + inner]
        act, slope_gate, slope_up = swish_parts(gate, up)
        weight = weight_ref[j]
        grad = grad_ref[j, :, :inner]
        slot_ref[j] = jnp.sum(act.astype(BF).astype(F32) * grad, axis=1, keepdims=True)
        inner_ref[j] = (weight * act).astype(BF)
        grad = weight * grad
        if lanes > inner:
            grads_ref[j] = jnp.zeros(grads_ref.shape[1:], BF)
        grads_ref[j, :, :inner] = (grad * slope_gate).astype(BF)
        grads_ref[j, :, lanes : lanes + inner] = (grad * slope_up).astype(BF)


def inner_of(
    chunk, before, group, pick, named, arrays, gate, up, shared, grad, shared_grad, pad, capacity
):
    devices, slots, tokens = pick.shape
    width, lanes, inner = arrays[0].shape[2], grad.shape[2], gate.shape[1]
    hid, experts = shared_grad.shape[1], named.shape[2]
    rows = STEP * capacity
    total = devices * capacity
    by_rows = lambda n: pl.BlockSpec((EXP_DEV, rows, n), lambda _: (0, chunk, 0))
    by_device = lambda *n: pl.BlockSpec((STEP,) + n, lambda _: (chunk, 0, 0))
    whole = lambda v: resident(v.shape)
    any_spec = pl.BlockSpec(memory_space=pl.ANY)
    in_specs = (
        [SMEM, by_device(slots, tokens), by_device(tokens, experts)]
        + [whole(v) for v in arrays]
        + [
            whole(gate),
            whole(up),
            whole(shared),
            by_rows(lanes),
            pl.BlockSpec((STEP * tokens, hid), lambda _: (chunk, 0)),
        ]
    )
    operands = [group, pick, named, *arrays, gate, up, shared, grad, shared_grad]
    aliases = {}
    if before is not None:
        aliases = {len(operands) + i: i for i in range(6)}
        operands += before
        in_specs += [any_spec] * 6 + [pl.BlockSpec((2 * pad, width), lambda _: (0, 0))]
    return pl.pallas_call(
        functools.partial(inner_kernel, len(arrays)),
        grid=(1,),
        in_specs=in_specs,
        out_specs=[
            by_rows(width),
            by_rows(inner),
            by_rows(2 * lanes),
            by_rows(1),
            by_device(tokens, 2 * pad),
            by_device(tokens, pad),
            pl.BlockSpec((2 * pad, width), lambda _: (0, 0)),
        ],
        out_shape=[
            jax.ShapeDtypeStruct((EXP_DEV, total, width), BF),
            jax.ShapeDtypeStruct((EXP_DEV, total, inner), BF),
            jax.ShapeDtypeStruct((EXP_DEV, total, 2 * lanes), BF),
            jax.ShapeDtypeStruct((EXP_DEV, total, 1), F32),
            jax.ShapeDtypeStruct((devices, tokens, 2 * pad), BF),
            jax.ShapeDtypeStruct((devices, tokens, pad), BF),
            jax.ShapeDtypeStruct((2 * pad, width), F32),
        ],
        scratch_shapes=[
            pltpu.VMEM((EXP_DEV, 2 * lanes, width), BF),
            pltpu.VMEM((EXP_DEV, rows, 1), F32),
        ],
        input_output_aliases=aliases,
        compiler_params=params(),
        name="inner",
    )(*operands)


def back_kernel(
    rows, pick_ref, grads_ref, gate_ref, up_ref, left_ref, right_ref,
    own_ref, other_ref, hold_ref, w_ref,
):
    stack_weights(w_ref, gate_ref, up_ref)
    for j in range(EXP_DEV):
        hold_ref[j] = mm(grads_ref[j], w_ref[j]).astype(BF)
    for i in range(STEP):
        total = place_from(hold_ref, pick_ref[i], i, STEP) + mm(left_ref[i], right_ref[...])
        out_ref = own_ref if i // rows % 2 == 0 else other_ref
        out_ref[i // (2 * rows) * rows + i % rows] = total.astype(BF)


def back_rows(pick, grads, gate, up, left, right, capacity, x_rows):
    devices, slots, tokens = pick.shape
    width, inner = gate.shape[2], left.shape[2]
    rows = STEP * capacity
    return pl.pallas_call(
        functools.partial(back_kernel, x_rows),
        grid=(devices // STEP,),
        in_specs=[
            pl.BlockSpec((STEP, slots, tokens), lambda d: (d, 0, 0)),
            pl.BlockSpec((EXP_DEV, rows, grads.shape[2]), lambda d: (0, d, 0)),
            resident(gate.shape),
            resident(up.shape),
            pl.BlockSpec((STEP, tokens, inner), lambda d: (d, 0, 0)),
            resident(right.shape),
        ],
        out_specs=[pl.BlockSpec((STEP // 2, tokens, width), lambda d: (d, 0, 0))] * 2,
        out_shape=[jax.ShapeDtypeStruct((devices // 2, tokens, width), BF)] * 2,
        scratch_shapes=[
            pltpu.VMEM((EXP_DEV, rows, width), BF),
            pltpu.VMEM((EXP_DEV, grads.shape[2], width), BF),
        ],
        compiler_params=params(),
        name="back_rows",
    )(pick, grads, gate, up, left, right)


def gate_up_kernel(rows_ref, grads_ref, gate_ref, up_ref):
    inner = gate_ref.shape[1]
    both = mm_tn(grads_ref[0], rows_ref[0])
    gate_ref[0] = both[:inner]
    at = grads_ref.shape[2] // 2
    up_ref[0] = both[at : at + inner]


def gate_up_grads(rows, grads, inner):
    _, total, width = rows.shape
    tile = width // 4
    out = pl.BlockSpec((1, inner, tile), lambda j, i: (j, 0, i))
    return pl.pallas_call(
        gate_up_kernel,
        grid=(EXP_DEV, 4),
        in_specs=[
            pl.BlockSpec((1, total, tile), lambda j, i: (j, 0, i)),
            pl.BlockSpec((1, total, grads.shape[2]), lambda j, i: (j, 0, 0)),
        ],
        out_specs=[out, out],
        out_shape=[jax.ShapeDtypeStruct((EXP_DEV, inner, width), F32)] * 2,
        compiler_params=params(),
        name="gate_up_grads",
    )(rows, grads)


def output_kernel(
    x_rows, pick_ref, inner_ref, down_ref, left_ref, right_ref, own_ref, other_ref, hold_ref
):
    for j in range(EXP_DEV):
        hold_ref[j] = mm(inner_ref[j], down_ref[j]).astype(BF)
    for i in range(STEP):
        total = place_from(hold_ref, pick_ref[i], i, STEP) + mm(left_ref[i], right_ref[...])
        out_ref = own_ref if i // x_rows % 2 == 0 else other_ref
        out_ref[i // (2 * x_rows) * x_rows + i % x_rows] = total.astype(BF)


def output_rows_of(pick, inner, down, left, right, capacity, x_rows):
    devices, slots, tokens = pick.shape
    width = down.shape[2]
    rows = STEP * capacity
    return pl.pallas_call(
        functools.partial(output_kernel, x_rows),
        grid=(devices // STEP,),
        in_specs=[
            pl.BlockSpec((STEP, slots, tokens), lambda d: (d, 0, 0)),
            pl.BlockSpec((EXP_DEV, rows, inner.shape[2]), lambda d: (0, d, 0)),
            resident(down.shape),
            pl.BlockSpec((STEP, tokens, left.shape[2]), lambda d: (d, 0, 0)),
            resident(right.shape),
        ],
        out_specs=[pl.BlockSpec((STEP // 2, tokens, width), lambda d: (d, 0, 0))] * 2,
        out_shape=[jax.ShapeDtypeStruct((devices // 2, tokens, width), BF)] * 2,
        scratch_shapes=[pltpu.VMEM((EXP_DEV, rows, width), BF)],
        compiler_params=params(),
        name="output_rows",
    )(pick, inner, down, left, right)


def body(
    hidden,
    cotangent,
    segments,
    routes,
    w_query,
    w_latent,
    g_latent,
    w_expand,
    w_out,
    g_attn,
    g_ffn,
    w_router,
    s_gate,
    s_up,
    s_down,
    e_gate,
    expert_up_weight,
    e_down,
):
    tokens = hidden.shape[1]
    width = hidden.shape[2]
    links = Links()
    shards, groups = links.shards, links.groups
    devices = groups * shards
    experts = EXP_DEV * groups
    capacity = max(2, tokens * TOP * 4 // (3 * experts))
    heads = H // shards
    length = tokens * shards
    part = width // shards
    my_shard = lax.axis_index("shard")
    my_group = lax.axis_index("expert")
    hid_shard = s_down.shape[0]
    hid = hid_shard // groups
    latent_part = KVR // shards
    shard_at, slot_at = links.shard_at(), links.slot_at()

    g_all = lax.all_gather(cotangent[0], BOTH, axis=0, tiled=False)
    router_rows = part * experts // width
    small_rows = jnp.concatenate([g_attn, g_ffn, g_latent])
    small_rows = jnp.pad(small_rows, (0, -small_rows.shape[0] % width)).reshape(-1, width)
    packed = jnp.concatenate([w_router.reshape(router_rows, width), small_rows])
    packed = links.gather_shard(jnp.pad(packed, ((0, -packed.shape[0] % 16), (0, 0))))
    hidden_all = links.gather_shard(hidden[0]).reshape(length, width)
    pieces = lambda w: jnp.stack(jnp.split(w, shards, axis=1))
    wl = links.gather_shard(w_latent.T)
    wq = links.spread_shard_ring(pieces(w_query))
    we = links.spread_shard(pieces(w_expand))
    packed = jnp.take(packed, slot_at, axis=0)
    full_router = packed[:, :router_rows].reshape(width, experts)
    gains_in = packed[:, router_rows:].reshape(shards, -1)
    gattn = gains_in[:, :part].reshape(1, width).astype(F32)
    gffn = gains_in[:, part : 2 * part].reshape(width).astype(F32)
    glatent = gains_in[:, 2 * part : 2 * part + latent_part].reshape(1, KVR).astype(F32)

    order = links.order()
    same = jnp.arange(devices, dtype=jnp.int32)
    back_order = jnp.sum(
        jnp.where(order[:, None] == same[None, :], same[:, None], 0), axis=0
    ).astype(jnp.int32)
    local_routes = routes[0]
    flat_routes = local_routes.reshape(-1)
    choose = local_routes[:, :, None] == jnp.arange(experts, dtype=jnp.int32)[None, None, :]
    hits = choose.reshape(-1, experts).astype(F32)
    pair_count = tokens * TOP
    before_it = (
        lax.broadcasted_iota(jnp.int32, (pair_count, pair_count), 1)
        < lax.broadcasted_iota(jnp.int32, (pair_count, pair_count), 0)
    ).astype(BF)
    before = mm(before_it, hits.astype(BF))
    slot_rank = jnp.sum(before * hits, axis=1).astype(jnp.int32)
    slot_of = (flat_routes * capacity + slot_rank).reshape(tokens, TOP)
    slots = EXP_DEV * capacity
    slot_rows = jnp.pad(slot_of.T, ((0, 8 - TOP), (0, 0)), constant_values=-1)
    slots_all = exchange(jnp.broadcast_to(slot_rows[None], (devices, 8, tokens)), BOTH)
    slots_all = jnp.take(slots_all, order, axis=0)[:, :TOP]
    slot_ids = my_group * slots + jnp.arange(slots, dtype=jnp.int32)
    pick = jnp.any(
        slots_all[:, None] == slot_ids[None, :, None, None], axis=2
    ).astype(BF)

    positions = (shard_at[:, None] * tokens + jnp.arange(tokens, dtype=jnp.int32)).reshape(-1)
    cosine, sine_vals = rope_angles(positions)
    segs = jnp.take(segments.reshape(shards, tokens), shard_at, axis=0).reshape(-1)
    col = jnp.stack([segs, positions], axis=1)
    row = jnp.stack([segs, positions], axis=0)
    attn_part, n1, compressed, latent, attended, query, kv, lse = attention_forward(
        slot_at, hidden_all, gattn, glatent, wq, wl, we, w_out, cosine, sine_vals, col, row
    )
    inner_units = e_gate.shape[2]
    gate_t, up_t = jnp.swapaxes(e_gate, 1, 2), jnp.swapaxes(expert_up_weight, 1, 2)
    attn_out = links.sum_shard(attn_part.reshape(shards, tokens, width))

    residual_in = hidden[0].astype(F32)
    residual_mid = residual_in + attn_out
    unit_two, factor_two = norm_forward(residual_mid)
    normed_two = (unit_two * gffn).astype(BF)

    hid_ids = my_group * hid + jnp.arange(hid, dtype=jnp.int32)
    wanted = (jnp.arange(shards, dtype=jnp.int32)[:, None] * hid_shard + hid_ids).reshape(-1)
    chosen_units = (
        jnp.arange(shards * hid_shard, dtype=jnp.int32)[:, None] == wanted[None, :]
    ).astype(BF)

    def shared_pieces(units):
        cut = [mm(w, units).astype(BF).reshape(part, shards, hid) for w in (s_gate, s_up)]
        return jnp.concatenate(cut, axis=2).transpose(1, 0, 2)

    pad = hid + -hid % PAD
    shared_down = lax.dynamic_slice_in_dim(s_down, my_group * hid, hid, 0)
    gate_up = links.spread_shard(shared_pieces(chosen_units))
    gate_up = jnp.take(gate_up, slot_at, axis=0).reshape(width, 2, hid)
    shared_in = jnp.pad(gate_up, ((0, 0), (0, 0), (0, pad - hid))).reshape(width, 2 * pad)
    shared_all = jnp.concatenate(
        [shared_in, jnp.pad(full_router, ((0, 0), (0, -experts % PAD)))], axis=1
    )
    route_of = slots_all // capacity
    named = jnp.any(
        route_of.transpose(0, 2, 1)[:, :, :, None]
        == jnp.arange(experts, dtype=jnp.int32)[None, None, None, :],
        axis=2,
    ).astype(F32)
    probs = jax.nn.sigmoid(mm(normed_two, full_router))
    chosen = jnp.sum(jnp.where(choose, probs[:, None, :], 0.0), axis=-1)
    chosen_total = jnp.sum(chosen, axis=1, keepdims=True)

    def of_cotangent(pick_of):
        rows_of, inner_grads = grad_rows_of(pick_of, g_all, order, e_down, capacity)
        shared_of = mm_nt(g_all.reshape(-1, width), shared_down)
        shared_of = jnp.take(shared_of.reshape(devices, tokens, hid), order, axis=0)
        return rows_of, inner_grads, shared_of.reshape(-1, hid)

    arrival = links.arrival()
    per_chunk = STEP // shards
    chunks = groups // per_chunk
    slots_in, partners, so_far = [], {}, [None]
    work_g = Fill(of_cotangent, pick, mark=2)

    def one_chunk(c):
        arrays = []
        for r in arrival[c * per_chunk : (c + 1) * per_chunk]:
            partners[r] = links.partner(slots_in[0][r])
            arrays += [slots_in[0][r], partners[r]]
        so_far[0] = inner_of(
            c, so_far[0], my_group.reshape(1), pick, named, arrays, gate_t, up_t, shared_all,
            work_g.result[1], work_g.result[2], pad, capacity,
        )

    def chunks_after(step, done):
        ready = sum(min(r, groups - r) <= step for r in arrival) // per_chunk
        return range(done, ready)

    fills, done = [(1, work_g)], 0
    for r in range(2, groups // 2 + 1):
        some = chunks_after(r - 1, done)
        done += len(some)

        def work_of(some=some, final=r == groups // 2):
            for c in some:
                one_chunk(c)
            return so_far[0]

        if len(some) > 0:
            fill = Fill(work_of, mark=3)
            fills.append((r, fill))
    spread = jnp.stack(
        [normed_two] + [links.along_x(normed_two, k) for k in range(1, shards // 2)]
    )
    links.ring_gather([spread], [groups // 2], fills, slots_in)
    for c in range(done, chunks):
        one_chunk(c)
    grad_rows = work_g.result[0]
    rows, inner_w, grads_b, grad_slot_weight, shared_grads, shared_inner, shared_sum = so_far[0]

    shared_out = jnp.concatenate([shared_sum[:hid], shared_sum[pad : pad + hid]], axis=0)
    shared_out = shared_out.astype(BF).reshape(2 * hid, shards, part).transpose(1, 0, 2)
    in_pieces = jnp.take(links.spread_shard(shared_out), slot_at, axis=0)
    in_all = lax.all_gather(in_pieces, "expert", axis=0, tiled=False)
    shared_down = jnp.pad(shared_down, ((0, pad - hid), (0, 0)))

    def shared_down_grad(inner_of_shared):
        back = jnp.take(inner_of_shared, back_order, axis=0).reshape(-1, pad)
        return mm_tn(back, g_all.reshape(-1, width))[:hid].astype(BF)

    dn2_own, dn2_other = back_rows(
        pick, grads_b, gate_t, up_t, shared_grads, shared_in.T, capacity, shards // 2
    )

    def router_back(slot_sums):
        slot_back = slot_sums.reshape(EXP_DEV, devices, capacity).transpose(1, 0, 2)
        slot_back = jnp.take(slot_back.reshape(devices, slots), back_order, axis=0)
        got = exchange(slot_back, BOTH)
        slot_grads = jnp.sum(got.reshape(groups, shards, slots), axis=1).reshape(-1)
        at_slot = slot_of[:, :, None] == jnp.arange(experts * capacity, dtype=jnp.int32)
        grad_weights = jnp.sum(jnp.where(at_slot, slot_grads, 0.0), axis=2)
        grad_chosen = ROUTE_SCALE * (
            grad_weights / chosen_total
            - jnp.sum(grad_weights * chosen, axis=1, keepdims=True)
            / (chosen_total * chosen_total)
        )
        grad_probs = jnp.sum(jnp.where(choose, grad_chosen[:, :, None], 0.0), axis=1)
        return (grad_probs * probs * (1.0 - probs)).astype(BF)

    down_grad = lambda a, b: jnp.einsum("jmf,jmd->jfd", a, b, preferred_element_type=F32)
    ring_shape = (groups, shards // 2, tokens, width)
    half = groups // 2

    def output_parts(weighted):
        own, other = output_rows_of(
            pick, weighted, e_down, shared_inner, shared_down, capacity, shards // 2
        )
        return links.sum_core(own.reshape(ring_shape), other.reshape(ring_shape))

    work = [
        Fill(
            lambda a, b, _: (shared_down_grad(a), down_grad(b, grad_rows)),
            shared_inner, inner_w, in_pieces,
        ),
        Fill(output_parts, inner_w),
        Fill(
            lambda b, c: (gate_up_grads(rows, b, inner_units), router_back(c)),
            grads_b, grad_slot_weight,
        ),
    ]
    (dn2,) = links.ring_reduce(
        [links.sum_core(dn2_own.reshape(ring_shape), dn2_other.reshape(ring_shape))],
        [half],
        [(half - i, w) for i, w in enumerate(work)],
    )
    (d_shared_down, d_edown), out_parts, ((d_egate, grad_expert_up), grad_logits) = (
        w.result for w in work
    )
    down_all = lax.all_gather(d_shared_down, "expert", axis=0, tiled=True)

    def back_to_attention(top, logits):
        grad_normed_two = links.sum_x(top) + mm_nt(logits, full_router)
        grad_mid_norm, d_gffn = norm_backward(grad_normed_two, gffn, unit_two, factor_two)
        grad_mid = cotangent[0].astype(F32) + grad_mid_norm
        return grad_mid, d_gffn, grad_mid.astype(BF)

    backward = lambda grad_attn: attention_backward(
        slot_at, grad_attn, glatent, w_out, attended, query, kv, lse, latent, compressed,
        we, wl, wq, n1, cosine, sine_vals, col, row,
    )
    first = Fill(back_to_attention, dn2, grad_logits)
    middle = Fill(
        lambda grad: links.gather_shard(grad).reshape(length, width), lambda: first.result[2]
    )
    second = Fill(backward, lambda: middle.result)
    (routed_shared,) = links.ring_reduce(
        [out_parts], [half], [(half, first), (half - 1, middle), (half - 2, second)]
    )
    routed_shared = links.sum_x(routed_shared)
    grad_mid, d_gffn, _ = first.result
    dn1, dw, dwl, d_out, d_glatent = second.result
    output_rows = residual_mid + routed_shared
    (dn1, dw, dwl, d_out), (in_all, down_all, grad_logits) = tie(
        (dn1, dw, dwl, d_out), (in_all, down_all, grad_logits)
    )
    logits_back = exchange(
        jnp.broadcast_to(grad_logits.T[None], (devices, experts, tokens)), BOTH
    )
    logits_back = jnp.take(logits_back, order, axis=0)
    columns = lambda v: lax.dynamic_slice_in_dim(v.reshape(-1, width), my_shard * part, part, 1)
    own_columns = jnp.concatenate(
        [columns(v) for r in arrival for v in (slots_in[0][r], partners[r])], axis=0
    )
    d_router = mm(logits_back.transpose(1, 0, 2).reshape(experts, -1), own_columns).T
    grad_normed = links.sum_shard(dn1.reshape(shards, tokens, width))
    unit_one, factor_one = norm_forward(residual_in)
    grad_input_norm, d_gattn = norm_backward(
        grad_normed, gattn.reshape(width), unit_one, factor_one
    )
    grad_input = grad_mid + grad_input_norm

    cut = part // groups
    lat = links.sum_shard(dwl).astype(BF).reshape(groups, (KVR + DR) // groups, part)
    by_head = links.blocks(dw.reshape(shards, groups, cut, -1).transpose(1, 0, 2, 3))
    by_row = links.blocks(d_out.reshape(groups, cut, width))
    pluses = [groups // 2, (groups - 1) // 2]
    work_s = Fill(shared_finish, in_all)
    sum_head, sum_row = links.ring_reduce(
        [by_head, by_row], pluses, [(groups // 2 - 1, work_s)]
    )
    (sum_lat,) = links.ring_reduce([links.blocks(lat)], pluses[1:])
    part_sgate, part_sup = work_s.result
    sum_head = links.exchange_shard(sum_head.astype(BF))
    all_head, all_row = links.ring_gather([sum_head, sum_row.astype(BF)], pluses)
    (all_lat,) = links.ring_gather([sum_lat.astype(BF)], pluses[1:])
    part_query, part_expand, part_out = finish(
        links.block_at(), all_head, all_row, heads, width
    )
    part_latent = jnp.take(jnp.stack(all_lat), links.block_at(), axis=0)
    part_latent = part_latent.reshape(KVR + DR, part).astype(F32)

    gain_grads = jnp.concatenate(
        [
            d_gattn.reshape(shards, part),
            d_gffn.reshape(shards, part),
            d_glatent.reshape(shards, latent_part),
        ],
        axis=1,
    )
    got = exchange(
        jnp.broadcast_to(gain_grads[None], (groups,) + gain_grads.shape).reshape(devices, -1),
        BOTH,
    )
    gains = jnp.sum(got, axis=0)
    return (
        output_rows.astype(BF)[None],
        grad_input[None],
        part_query,
        part_latent.T,
        gains[2 * part :],
        part_expand,
        part_out,
        gains[:part],
        gains[part : 2 * part],
        d_router,
        part_sgate,
        part_sup,
        down_all.astype(F32),
        jnp.swapaxes(d_egate, 1, 2),
        jnp.swapaxes(grad_expert_up, 1, 2),
        d_edown,
    )


def solution(mesh):
    return jax.shard_map(
        body,
        mesh=mesh,
        in_specs=(
            P("expert", "shard", None),
            P("expert", "shard", None),
            P("expert", None),
            P("expert", "shard", None),
            P("shard", None),
            P("shard", None),
            P("shard"),
            P("shard", None),
            P("shard", None),
            P("shard"),
            P("shard"),
            P("shard", None),
            P("shard", None),
            P("shard", None),
            P("shard", None),
            P("expert", None, "shard"),
            P("expert", None, "shard"),
            P("expert", "shard", None),
        ),
        out_specs=(
            P("expert", "shard", None),
            P("expert", "shard", None),
            P("shard", None),
            P("shard", None),
            P("shard"),
            P("shard", None),
            P("shard", None),
            P("shard"),
            P("shard"),
            P("shard", None),
            P("shard", None),
            P("shard", None),
            P("shard", None),
            P("expert", None, "shard"),
            P("expert", None, "shard"),
            P("expert", "shard", None),
        ),
        check_vma=False,
    )
```

```python
import functools

import jax
import jax.numpy as jnp
from jax import lax
from jax.experimental import pallas as pl
from jax.experimental.pallas import tpu as pltpu
from jax.sharding import PartitionSpec as P

H = 16
DN = 128
DR = 64
DV = 128
KVR = 512
TOP = 6
EXP_DEV = 4

EPS = 1e-06
ROUTE_SCALE = 2.446
ROPE_BASE = 50000.0
SCORE_SCALE = (DN + DR) ** (-0.5)
BF = jnp.bfloat16
F32 = jnp.float32
BOTH = ("expert", "shard")
VMEM_BYTES = 56 * 1024 * 1024


def mm(a, b):
    return jnp.dot(a, b, preferred_element_type=F32)


def mm_tn(a, b):
    return lax.dot_general(a, b, (((0,), (0,)), ((), ())), preferred_element_type=F32)


def mm_nt(a, b):
    return lax.dot_general(a, b, (((1,), (1,)), ((), ())), preferred_element_type=F32)


def rope_angles(positions):
    half_width = DR // 2
    inverse = ROPE_BASE ** (-jnp.arange(half_width).astype(F32) / half_width)
    angles = positions.astype(F32)[:, None] * inverse[None, :]
    return (jnp.cos(angles), jnp.sin(angles))


def rotate(values, cosine, sine_vals):
    half_width = DR // 2
    first_half = values[..., :half_width]
    second_half = values[..., half_width:]
    return jnp.concatenate(
        [
            first_half * cosine - second_half * sine_vals,
            second_half * cosine + first_half * sine_vals,
        ],
        axis=-1,
    )


def norm_forward(values):
    factor = lax.rsqrt(jnp.mean(values * values, axis=-1, keepdims=True) + EPS)
    return values * factor, factor


def norm_backward(grad_out, gain_vec, unit_vals, factor):
    grad_unit = grad_out * gain_vec
    grad_in = factor * (
        grad_unit - unit_vals * jnp.mean(grad_unit * unit_vals, axis=-1, keepdims=True)
    )
    return (grad_in, jnp.sum(grad_out * unit_vals, axis=0))


def swish_parts(gate, up):
    sig = jax.nn.sigmoid(gate)
    silu = gate * sig
    return silu * up, up * sig * (1.0 + gate * (1.0 - sig)), silu


def exchange(values, axis):
    return lax.all_to_all(values, axis, split_axis=0, concat_axis=0, tiled=True)


def tie(streams, extra):
    return lax.optimization_barrier((streams, extra))


class Fill:
    def __init__(self, work, *inputs, mark=None):
        self.work, self.given, self.result, self.mark = work, inputs, None, mark

    @property
    def inputs(self):
        return tuple(v() if callable(v) else v for v in self.given)


class Links:
    def __init__(self):
        self.groups = lax.axis_size("expert")
        self.shards = lax.axis_size("shard")
        self.rows = self.shards // 2
        n = self.groups
        self.ring = list(range(0, n, 2)) + list(range(n - 1, 0, -2))
        shard = lax.axis_index("shard")
        self.x = shard // 2
        self.core = shard % 2
        group = lax.axis_index("expert")
        places = [self.ring.index(e) for e in range(n)]
        self.place = jnp.sum(
            jnp.where(jnp.arange(n) == group, jnp.array(places, jnp.int32), 0)
        )

    def send(self, values, target):
        pairs = []
        for e in range(self.groups):
            for s in range(self.shards):
                pairs.append((e * self.shards + s, target(e, s)))
        return lax.ppermute(values, BOTH, pairs)

    def around(self, values, step):
        n = self.groups
        return self.send(
            values,
            lambda e, s: self.ring[(self.ring.index(e) + step) % n] * self.shards + s,
        )

    def along_x(self, values, step):
        return self.send(
            values,
            lambda e, s: e * self.shards + ((s // 2 + step) % self.rows) * 2 + s % 2,
        )

    def partner(self, values):
        return self.send(values, lambda e, s: e * self.shards + (s ^ 1))

    def shard_at(self):
        xs = (self.x - jnp.arange(self.rows, dtype=jnp.int32)) % self.rows
        cores = jnp.stack([self.core, 1 - self.core]).astype(jnp.int32)
        return (xs[:, None] * 2 + cores[None, :]).reshape(-1).astype(jnp.int32)

    def slot_at(self):
        shard = jnp.arange(self.shards, dtype=jnp.int32)
        back = (self.x - shard // 2) % self.rows
        return (back * 2 + (shard % 2 != self.core)).astype(jnp.int32)

    def gather_shard(self, values):
        out = []
        for k in range(self.rows):
            own = values if k == 0 else self.along_x(values, k)
            out += [own, self.partner(own)]
        return jnp.stack(out)

    def spread_shard(self, pieces):
        take = lambda v, i: lax.dynamic_index_in_dim(v, i, 0, keepdims=False)
        pairs = pieces.reshape((self.rows, 2) + pieces.shape[1:])
        out = []
        for k in range(self.rows):
            got = take(pairs, (self.x + k) % self.rows)
            got = got if k == 0 else self.along_x(got, k)
            out += [take(got, self.core), self.partner(take(got, 1 - self.core))]
        return jnp.stack(out)

    def spread_shard_ring(self, pieces):
        n, rows = self.groups, self.rows
        take = lambda v, i, axis: lax.dynamic_index_in_dim(v, i, axis, keepdims=False)
        part, wide = pieces.shape[1:]
        pairs = pieces.reshape(rows, 2, n, part // n, wide)
        mine = take(pairs, self.place, 2)
        out = []
        for k in range(rows):
            if k == 0:
                got = take(pairs, self.x, 0)
            else:
                far = self.along_x(take(mine, (self.x + k) % rows, 0), k)
                (far,) = self.ring_gather([far], [n // 2])
                got = jnp.take(jnp.stack(far, axis=1), self.block_at(), axis=1)
            got = got.reshape(2, part, wide)
            out += [take(got, self.core, 0), self.partner(take(got, 1 - self.core, 0))]
        return jnp.stack(out)

    def exchange_shard(self, values):
        pairs = values.reshape((self.rows, 2) + values.shape[1:])
        out = []
        for k in range(self.rows):
            got = pairs[k] if k == 0 else self.along_x(pairs[k], -k)
            out += [got[0], self.partner(got[1])]
        xs = (self.x + jnp.arange(self.rows, dtype=jnp.int32)) % self.rows
        shard = jnp.arange(self.shards, dtype=jnp.int32)
        ahead = (shard // 2 - self.x) % self.rows
        slot = ahead * 2 + (shard % 2 != self.core)
        return jnp.take(jnp.stack(out), slot, axis=0)

    def sum_shard(self, values, fill=None):
        pairs = values.reshape((self.rows, 2) + values.shape[1:])
        both = [
            pairs[k, 0].astype(F32) + self.partner(pairs[k, 1]).astype(F32)
            for k in range(self.rows)
        ]
        far = [v.astype(BF) for v in both[1:]]
        if fill is not None:
            _, inputs = tie(far, fill.inputs)
        far = [self.along_x(v, -k - 1) for k, v in enumerate(far)]
        if fill is not None:
            far, fill.result = tie(far, fill.work(*inputs))
        total = both[0]
        for v in far:
            total = total + v.astype(F32)
        return total

    def ring_gather(self, values, pluses, fills=(), outs=None):
        n = self.groups
        fills = dict(fills)
        outs = [] if outs is None else outs
        outs += [[v] + [None] * (n - 1) for v in values]
        ahead, back = list(values), list(values)
        for r in range(1, n):
            moves = [(i, 1) for i, p in enumerate(pluses) if r <= p]
            moves += [(i, -1) for i, p in enumerate(pluses) if r <= n - 1 - p]
            if not moves:
                break
            streams = [ahead[i] if step > 0 else back[i] for i, step in moves]
            streams = self.step(streams, [step for _, step in moves], fills.get(r))
            for (i, step), got in zip(moves, streams):
                if step > 0:
                    ahead[i] = outs[i][r] = got
                else:
                    back[i] = outs[i][n - r] = got
        return outs

    def step(self, streams, steps, fill, free=0):
        if fill is None:
            return [self.around(v, s) for v, s in zip(streams, steps)]
        streams[free:], inputs = tie(streams[free:], fill.inputs)
        streams = [self.around(v, s) for v, s in zip(streams, steps)]
        result = fill.work(*inputs)
        if fill.mark is None:
            streams[free:], fill.result = tie(streams[free:], result)
        else:
            fill.result = list(result)
            streams[free:], fill.result[fill.mark] = tie(
                streams[free:], result[fill.mark]
            )
        return streams

    def ring_reduce(self, parts, pluses, fills=(), free=0, after=None):
        n = self.groups
        fills = dict(fills)
        ahead = [p[plus] for p, plus in zip(parts, pluses)]
        back = [p[plus + 1] for p, plus in zip(parts, pluses)]
        most = max(max(p, n - 1 - p) for p in pluses)
        for r in range(most, 0, -1):
            moves = [(i, 1) for i, p in enumerate(pluses) if r <= p]
            moves += [(i, -1) for i, p in enumerate(pluses) if r <= n - 1 - p]
            moves.sort()
            streams = [ahead[i] if step > 0 else back[i] for i, step in moves]
            streams = self.step(
                streams,
                [-step for _, step in moves],
                fills.get(r),
                len([i for i, _ in moves if i < free]),
            )
            if after is not None:
                after(r, fills.get(r))
            for (i, step), got in zip(moves, streams):
                here = parts[i][r - 1 if step > 0 else (n - r + 1) % n]
                if r > 1:
                    got = (got.astype(F32) + here.astype(F32)).astype(BF)
                if step > 0:
                    ahead[i] = got
                else:
                    back[i] = got
        return [
            p[0].astype(F32) + a.astype(F32) + b.astype(F32)
            for p, a, b in zip(parts, ahead, back)
        ]

    def by_group(self, slots):
        places = jnp.array([self.ring.index(e) for e in range(self.groups)], jnp.int32)
        return jnp.take(jnp.stack(slots), (self.place - places) % self.groups, axis=0)

    def block_at(self):
        return (self.place - jnp.arange(self.groups, dtype=jnp.int32)) % self.groups

    def blocks(self, values):
        return [
            lax.dynamic_index_in_dim(
                values, (self.place - r) % self.groups, 0, keepdims=False
            )
            for r in range(self.groups)
        ]

    def arrival(self):
        n = self.groups
        return [0] + [r for k in range(1, n // 2 + 1) for r in dict.fromkeys((k, n - k))]

    def order(self):
        n = self.groups
        ring = jnp.array(self.ring, jnp.int32)
        groups = jnp.sum(
            jnp.where(
                self.block_at()[jnp.array(self.arrival())][:, None] == jnp.arange(n)[None, :],
                ring[None, :],
                0,
            ),
            axis=1,
        )
        shard = self.shard_at().reshape(self.rows, 2).T.reshape(-1)
        all_of = groups[:, None] * self.shards + shard[None, :]
        return all_of.reshape(-1).astype(jnp.int32)

    def sum_core(self, own, other):
        both = (own.astype(F32) + self.partner(other).astype(F32)).astype(BF)
        return [both[self.arrival().index(r)] for r in range(self.groups)]

    def sum_x(self, top):
        total = top[0]
        for k in range(1, self.rows):
            total = total + self.along_x(top[k].astype(BF), -k).astype(F32)
        return total


def params(**kw):
    return pltpu.CompilerParams(vmem_limit_bytes=VMEM_BYTES, **kw)


SMEM = pl.BlockSpec(memory_space=pltpu.SMEM)
VMEM = pl.BlockSpec(memory_space=pltpu.VMEM)


def allowed_mask(seg_col, seg_row, pos_col, pos_row):
    return (seg_col == seg_row) & (pos_row <= pos_col)


def attention_forward_kernel(
    slot_ref, x_ref, gattn_ref, glat_ref, wq_ref, wl_ref, we_ref, wo_ref,
    cos_ref, sin_ref, col_ref, row_ref,
    out_ref, n1_ref, c_ref, lat_ref, o_ref, q_ref, kv_ref, lse_ref,
):
    shards, part = wq_ref.shape[0], wq_ref.shape[1]
    heads = q_ref.shape[0]
    tokens = x_ref.shape[0] // shards
    for b in range(shards):
        at = slice(b * tokens, (b + 1) * tokens)
        unit, _ = norm_forward(x_ref[at].astype(F32))
        n1_ref[at] = (unit * gattn_ref[...]).astype(BF)
    queries, compressed, kv_all = None, None, None
    for s in range(shards):
        left = n1_ref[:, s * part : (s + 1) * part]
        one = mm(left, wq_ref[slot_ref[s]])
        queries = one if s == 0 else queries + one
        one = mm_nt(left, wl_ref[slot_ref[s]])
        compressed = one if s == 0 else compressed + one
    c_ref[...] = compressed
    unit, _ = norm_forward(compressed[:, :KVR])
    lat_ref[:, :KVR] = (unit * glat_ref[...]).astype(BF)
    lat_ref[:, KVR:] = rotate(compressed[:, KVR:], cos_ref[...], sin_ref[...]).astype(BF)
    part = KVR // shards
    for s in range(shards):
        one = mm(lat_ref[:, s * part : (s + 1) * part], we_ref[slot_ref[s]])
        kv_all = one if s == 0 else kv_all + one
    kv_ref[...] = kv_all.astype(BF)
    ok = allowed_mask(
        col_ref[:, :1], row_ref[:1, :], col_ref[:, 1:2], row_ref[1:2, :]
    )
    key_rot = lat_ref[:, KVR:]
    for h in range(heads):
        at = h * (DN + DR)
        query = jnp.concatenate(
            [
                queries[:, at : at + DN],
                rotate(queries[:, at + DN : at + DN + DR], cos_ref[...], sin_ref[...]),
            ],
            axis=1,
        ).astype(BF)
        q_ref[h] = query
        at = h * (DN + DV)
        keys = kv_ref[:, at : at + DN]
        values = kv_ref[:, at + DN : at + DN + DV]
        scores = mm_nt(query[:, :DN], keys) + mm_nt(query[:, DN:], key_rot)
        scores = jnp.where(ok, scores * SCORE_SCALE, -1e30)
        top = jnp.max(scores, axis=1, keepdims=True)
        expo = jnp.exp(scores - top)
        total = jnp.sum(expo, axis=1, keepdims=True)
        lse_ref[h] = top + jnp.log(total)
        weights = (expo / total).astype(BF)
        o_ref[:, h * DV : (h + 1) * DV] = mm(weights, values).astype(BF)
    out_ref[...] = mm(o_ref[...], wo_ref[...]).astype(BF)


def attention_forward(slot, x, gattn, glat, wq, wl, we, wo, cosine, sine_vals, col, row):
    length, width = x.shape
    heads = wo.shape[0] // DV
    return pl.pallas_call(
        attention_forward_kernel,
        in_specs=[SMEM] + [VMEM] * 11,
        out_shape=[
            jax.ShapeDtypeStruct((length, width), BF),
            jax.ShapeDtypeStruct((length, width), BF),
            jax.ShapeDtypeStruct((length, KVR + DR), F32),
            jax.ShapeDtypeStruct((length, KVR + DR), BF),
            jax.ShapeDtypeStruct((length, heads * DV), BF),
            jax.ShapeDtypeStruct((heads, length, DN + DR), BF),
            jax.ShapeDtypeStruct((length, heads * (DN + DV)), BF),
            jax.ShapeDtypeStruct((heads, length, 1), F32),
        ],
        compiler_params=params(),
        name="attention_forward",
    )(slot, x, gattn, glat, wq, wl, we, wo, cosine, sine_vals, col, row)


def attention_backward_kernel(
    slot_ref, dh_ref, glat_ref, wo_ref, o_ref, q_ref, kv_ref, lse_ref, lat_ref, c_ref,
    we_ref, wl_ref, wq_ref, n1_ref, cos_ref, sin_ref, col_ref, row_ref,
    dn1_ref, dw_ref, dwl_ref, dwo_ref, dgl_ref,
    go_ref, gq_ref, gkv_ref, gc_ref,
):
    shards, part = wq_ref.shape[0], wq_ref.shape[1]
    heads = q_ref.shape[0]
    go_ref[...] = mm_nt(dh_ref[...], wo_ref[...]).astype(BF)
    dwo_ref[...] = mm_tn(o_ref[...], dh_ref[...]).astype(BF)
    ok = allowed_mask(
        col_ref[:, :1], row_ref[:1, :], col_ref[:, 1:2], row_ref[1:2, :]
    )
    key_rot = lat_ref[:, KVR:]
    grad_kr = None
    for h in range(heads):
        at = h * (DN + DV)
        keys = kv_ref[:, at : at + DN]
        values = kv_ref[:, at + DN : at + DN + DV]
        query = q_ref[h]
        grad_o = go_ref[:, h * DV : (h + 1) * DV]
        scores = mm_nt(query[:, :DN], keys) + mm_nt(query[:, DN:], key_rot)
        weights = jnp.where(ok, jnp.exp(scores * SCORE_SCALE - lse_ref[h]), 0.0)
        grad_w = mm_nt(grad_o, values)
        delta = jnp.sum(weights * grad_w, axis=1, keepdims=True)
        grad_s = (weights * (grad_w - delta) * SCORE_SCALE).astype(BF)
        gkv_ref[:, at : at + DN] = mm_tn(grad_s, query[:, :DN]).astype(BF)
        gkv_ref[:, at + DN : at + DN + DV] = mm_tn(weights.astype(BF), grad_o).astype(BF)
        one = mm_tn(grad_s, query[:, DN:])
        grad_kr = one if h == 0 else grad_kr + one
        at = h * (DN + DR)
        grad_qr = rotate(mm(grad_s, key_rot), cos_ref[...], -sin_ref[...])
        gq_ref[:, at : at + DN + DR] = jnp.concatenate(
            [mm(grad_s, keys), grad_qr], axis=1
        ).astype(BF)
    latent_part = KVR // shards
    query_wide = heads * (DN + DR)
    ratio = part // latent_part
    piece = heads * (DN + DV) // ratio
    grad_lat = []
    for s in range(shards):
        at = slice(s * latent_part, (s + 1) * latent_part)
        grad_lat.append(mm_nt(gkv_ref[...], we_ref[slot_ref[s]]))
        one = mm_tn(lat_ref[:, at], gkv_ref[...]).astype(BF)
        for i in range(ratio):
            dw_ref[slot_ref[s], i * latent_part : (i + 1) * latent_part, query_wide:] = one[
                :, i * piece : (i + 1) * piece
            ]
    grad_lat = jnp.concatenate(grad_lat, axis=1)
    unit, factor = norm_forward(c_ref[:, :KVR])
    grad_norm, grad_gain = norm_backward(grad_lat, glat_ref[...], unit, factor)
    dgl_ref[...] = grad_gain.reshape(1, KVR)
    gc_ref[:, :KVR] = grad_norm.astype(BF)
    gc_ref[:, KVR:] = rotate(grad_kr, cos_ref[...], -sin_ref[...]).astype(BF)
    for s in range(shards):
        at = slice(s * part, (s + 1) * part)
        dn1_ref[:, at] = (
            mm_nt(gq_ref[...], wq_ref[slot_ref[s]]) + mm(gc_ref[...], wl_ref[slot_ref[s]])
        ).astype(BF)
        dw_ref[slot_ref[s], :, :query_wide] = mm_tn(n1_ref[:, at], gq_ref[...]).astype(BF)
        dwl_ref[slot_ref[s]] = mm_tn(gc_ref[...], n1_ref[:, at]).astype(BF)


def attention_backward(
    slot, dh, glat, wo, o, query, kv, lse, latent, compressed, we, wl, wq, n1,
    cosine, sine_vals, col, row,
):
    length, width = n1.shape
    heads = query.shape[0]
    shards, part = wq.shape[0], wq.shape[1]
    wide = heads * (DN + DR) + heads * (DN + DV) * KVR // width
    return pl.pallas_call(
        attention_backward_kernel,
        in_specs=[SMEM] + [VMEM] * 17,
        out_shape=[
            jax.ShapeDtypeStruct((length, width), BF),
            jax.ShapeDtypeStruct((shards, part, wide), BF),
            jax.ShapeDtypeStruct(wl.shape, BF),
            jax.ShapeDtypeStruct((heads * DV, width), BF),
            jax.ShapeDtypeStruct((1, KVR), F32),
        ],
        scratch_shapes=[
            pltpu.VMEM((length, heads * DV), BF),
            pltpu.VMEM((length, heads * (DN + DR)), BF),
            pltpu.VMEM((length, heads * (DN + DV)), BF),
            pltpu.VMEM((length, KVR + DR), BF),
        ],
        compiler_params=params(),
        name="attention_backward",
    )(
        slot, dh, glat, wo, o, query, kv, lse, latent, compressed, we, wl, wq, n1,
        cosine, sine_vals, col, row,
    )


def finish_kernel(groups, shards, per, piece, *refs):
    place_ref = refs[0]
    by_head, by_row = (refs[1 + i * groups : 1 + (i + 1) * groups] for i in range(2))
    query_ref, expand_ref, out_ref = refs[1 + 2 * groups :]
    cut = by_row[0].shape[0]
    wide = by_head[0].shape[2] - piece
    expand_wide = expand_ref.shape[1] // shards
    for r in range(groups):
        at = place_ref[r]
        rows = pl.ds(pl.multiple_of(at * cut, cut), cut)
        out_ref[rows, :] = by_row[r][...].astype(F32)
        low = pl.ds(pl.multiple_of((at % per) * cut, cut), cut)
        for s in range(shards):
            query_ref[rows, s * wide : (s + 1) * wide] = by_head[r][s, :, :wide].astype(F32)
            lanes = pl.ds(
                pl.multiple_of(s * expand_wide + (at // per) * piece, piece), piece
            )
            expand_ref[low, lanes] = by_head[r][s, :, wide:].astype(F32)


def finish(place, by_head, by_row, heads, width):
    groups, shards = len(by_head), by_head[0].shape[0]
    latent_part = KVR // shards
    part = width // shards
    per = groups * latent_part // part
    piece = heads * (DN + DV) * latent_part // part
    return pl.pallas_call(
        functools.partial(finish_kernel, groups, shards, per, piece),
        in_specs=[SMEM] + [VMEM] * (2 * groups),
        out_shape=[
            jax.ShapeDtypeStruct((part, H * (DN + DR)), F32),
            jax.ShapeDtypeStruct((latent_part, H * (DN + DV)), F32),
            jax.ShapeDtypeStruct((part, width), F32),
        ],
        compiler_params=params(),
        name="finish",
    )(place, *by_head, *by_row)


def shared_finish_kernel(x_ref, gate_ref, up_ref, hold_ref):
    groups, shards, hid = x_ref.shape[0], x_ref.shape[1], x_ref.shape[2] // 2
    for i, out_ref in ((0, gate_ref), (1, up_ref)):
        for s in range(shards):
            for g in range(groups):
                at = (s * groups + g) * hid
                hold_ref[at : at + hid] = x_ref[g, s, i * hid : (i + 1) * hid].astype(F32)
        out_ref[...] = hold_ref[...].T


def shared_finish(pieces):
    groups, shards, two, part = pieces.shape
    wide = groups * shards * two // 2
    return pl.pallas_call(
        shared_finish_kernel,
        in_specs=[VMEM],
        out_shape=[jax.ShapeDtypeStruct((part, wide), F32)] * 2,
        scratch_shapes=[pltpu.VMEM((wide, part), F32)],
        compiler_params=params(),
        name="shared_finish",
    )(pieces)


STEP = 8
PAD = 128


def pick_into(out_ref, pick, rows_of, i, step):
    capacity = out_ref.shape[1] // step
    rows = mm(pick, rows_of).astype(BF)
    out_ref[:, i * capacity : (i + 1) * capacity, :] = rows.reshape(
        EXP_DEV, capacity, rows.shape[1]
    )


def place_from(rows_ref, pick, i, step):
    capacity = rows_ref.shape[1] // step
    rows = rows_ref[:, i * capacity : (i + 1) * capacity, :]
    return mm_tn(pick, rows.reshape(EXP_DEV * capacity, rows.shape[2]))


def resident(shape):
    return pl.BlockSpec(
        shape, lambda *_: (0,) * len(shape), pipeline_mode=pl.Buffered(1)
    )


def grad_rows_kernel(order_ref, pick_ref, down_ref, *refs):
    rows_ref, inner_ref = refs[STEP:]
    inner = down_ref.shape[1]
    for i in range(STEP):
        pick_into(rows_ref, pick_ref[i], refs[i][0], i, STEP)
    for j in range(EXP_DEV):
        inner_ref[j, :, :inner] = mm_nt(rows_ref[j], down_ref[j])


def grad_rows_of(pick, g_all, order, down, capacity):
    devices, slots, tokens = pick.shape
    width, inner = g_all.shape[2], down.shape[1]
    lanes = inner + -inner % PAD
    rows = STEP * capacity
    at = lambda i: pl.BlockSpec((1, tokens, width), lambda d, o: (o[d * STEP + i], 0, 0))
    return pl.pallas_call(
        grad_rows_kernel,
        grid_spec=pltpu.PrefetchScalarGridSpec(
            num_scalar_prefetch=1,
            grid=(devices // STEP,),
            in_specs=[
                pl.BlockSpec((STEP, slots, tokens), lambda d, o: (d, 0, 0)),
                resident(down.shape),
            ]
            + [at(i) for i in range(STEP)],
            out_specs=[
                pl.BlockSpec((EXP_DEV, rows, width), lambda d, o: (0, d, 0)),
                pl.BlockSpec((EXP_DEV, rows, lanes), lambda d, o: (0, d, 0)),
            ],
        ),
        out_shape=[
            jax.ShapeDtypeStruct((EXP_DEV, devices * capacity, width), BF),
            jax.ShapeDtypeStruct((EXP_DEV, devices * capacity, lanes), F32),
        ],
        compiler_params=params(),
        name="grad_rows",
    )(order, pick, down, *([g_all] * STEP))


def stack_weights(w_ref, gate_ref, up_ref):
    inner, lanes = gate_ref.shape[1], w_ref.shape[1] // 2

    @pl.when(pl.program_id(0) == 0)
    def _():
        for j in range(EXP_DEV):
            for i, ref in ((0, gate_ref), (1, up_ref)):
                w_ref[j, i * lanes : i * lanes + inner] = ref[j]
                if lanes > inner:
                    w_ref[j, i * lanes + inner : (i + 1) * lanes] = jnp.zeros(
                        (lanes - inner, w_ref.shape[2]), BF
                    )


def inner_kernel(
    count, group_ref, pick_ref, named_ref, *refs
):
    x_refs = refs[:count]
    (
        gate_ref, up_ref, shared_ref, grad_ref, shared_grad_ref,
        rows_ref, inner_ref, grads_ref, slot_ref, shared_grads_ref, shared_inner_ref, sum_ref,
    ) = refs[count : count + 5] + refs[-9:-2]
    w_ref, weight_ref = refs[-2:]
    before_ref = refs[-10] if len(refs) == count + 5 + 16 else None
    lanes, inner = grad_ref.shape[2], inner_ref.shape[2]
    hid, pad = shared_grad_ref.shape[1], shared_inner_ref.shape[2]
    x_rows, tokens = x_refs[0].shape[0], x_refs[0].shape[1]
    capacity = rows_ref.shape[1] // STEP
    experts = named_ref.shape[2]
    stack_weights(w_ref, gate_ref, up_ref)
    slots = EXP_DEV * capacity
    mine = group_ref[0] * EXP_DEV + lax.broadcasted_iota(
        jnp.int32, (slots, 3 * experts), 0
    ) // capacity
    at_mine = lax.broadcasted_iota(jnp.int32, (slots, 3 * experts), 1) % experts == mine
    total = None
    for i in range(STEP):
        x = x_refs[i // x_rows][i % x_rows]
        pick_into(rows_ref, pick_ref[i], x, i, STEP)
        both = mm(x, shared_ref[...])
        probs = jax.nn.sigmoid(both[:, 2 * pad : 2 * pad + experts])
        named = named_ref[i]
        weight = probs / jnp.sum(probs * named, axis=1, keepdims=True) * ROUTE_SCALE
        high = weight.astype(BF)
        rest = weight - high.astype(F32)
        middle = rest.astype(BF)
        low = (rest - middle.astype(F32)).astype(BF)
        at_slots = mm(pick_ref[i], jnp.concatenate([high, middle, low], axis=1))
        at_slots = jnp.sum(jnp.where(at_mine, at_slots, 0.0), axis=1, keepdims=True)
        weight_ref[:, i * capacity : (i + 1) * capacity] = at_slots.reshape(
            EXP_DEV, capacity, 1
        )
        act, slope_gate, slope_up = swish_parts(both[:, :hid], both[:, pad : pad + hid])
        grad = shared_grad_ref[i * tokens : (i + 1) * tokens]
        zeros = jnp.zeros((tokens, pad - hid), BF)
        join = lambda v: v.astype(BF) if pad == hid else jnp.concatenate(
            [v.astype(BF), zeros], axis=1
        )
        shared_inner_ref[i] = join(act)
        shared_grads_ref[i, :, :pad] = join(grad * slope_gate)
        shared_grads_ref[i, :, pad:] = join(grad * slope_up)
        one = mm_tn(shared_grads_ref[i], x)
        total = one if total is None else total + one
    sum_ref[...] = total if before_ref is None else total + before_ref[...]
    for j in range(EXP_DEV):
        both = mm_nt(rows_ref[j], w_ref[j])
        gate, up = both[:, :inner], both[:, lanes : lanes + inner]
        act, slope_gate, slope_up = swish_parts(gate, up)
        weight = weight_ref[j]
        grad = grad_ref[j, :, :inner]
        slot_ref[j] = jnp.sum(act.astype(BF).astype(F32) * grad, axis=1, keepdims=True)
        inner_ref[j] = (weight * act).astype(BF)
        grad = weight * grad
        if lanes > inner:
            grads_ref[j] = jnp.zeros(grads_ref.shape[1:], BF)
        grads_ref[j, :, :inner] = (grad * slope_gate).astype(BF)
        grads_ref[j, :, lanes : lanes + inner] = (grad * slope_up).astype(BF)


def inner_of(
    chunk, before, group, pick, named, arrays, gate, up, shared, grad, shared_grad, pad, capacity
):
    devices, slots, tokens = pick.shape
    width, lanes, inner = arrays[0].shape[2], grad.shape[2], gate.shape[1]
    hid, experts = shared_grad.shape[1], named.shape[2]
    rows = STEP * capacity
    total = devices * capacity
    by_rows = lambda n: pl.BlockSpec((EXP_DEV, rows, n), lambda _: (0, chunk, 0))
    by_device = lambda *n: pl.BlockSpec((STEP,) + n, lambda _: (chunk, 0, 0))
    whole = lambda v: resident(v.shape)
    any_spec = pl.BlockSpec(memory_space=pl.ANY)
    in_specs = (
        [SMEM, by_device(slots, tokens), by_device(tokens, experts)]
        + [whole(v) for v in arrays]
        + [
            whole(gate),
            whole(up),
            whole(shared),
            by_rows(lanes),
            pl.BlockSpec((STEP * tokens, hid), lambda _: (chunk, 0)),
        ]
    )
    operands = [group, pick, named, *arrays, gate, up, shared, grad, shared_grad]
    aliases = {}
    if before is not None:
        aliases = {len(operands) + i: i for i in range(6)}
        operands += before
        in_specs += [any_spec] * 6 + [pl.BlockSpec((2 * pad, width), lambda _: (0, 0))]
    return pl.pallas_call(
        functools.partial(inner_kernel, len(arrays)),
        grid=(1,),
        in_specs=in_specs,
        out_specs=[
            by_rows(width),
            by_rows(inner),
            by_rows(2 * lanes),
            by_rows(1),
            by_device(tokens, 2 * pad),
            by_device(tokens, pad),
            pl.BlockSpec((2 * pad, width), lambda _: (0, 0)),
        ],
        out_shape=[
            jax.ShapeDtypeStruct((EXP_DEV, total, width), BF),
            jax.ShapeDtypeStruct((EXP_DEV, total, inner), BF),
            jax.ShapeDtypeStruct((EXP_DEV, total, 2 * lanes), BF),
            jax.ShapeDtypeStruct((EXP_DEV, total, 1), F32),
            jax.ShapeDtypeStruct((devices, tokens, 2 * pad), BF),
            jax.ShapeDtypeStruct((devices, tokens, pad), BF),
            jax.ShapeDtypeStruct((2 * pad, width), F32),
        ],
        scratch_shapes=[
            pltpu.VMEM((EXP_DEV, 2 * lanes, width), BF),
            pltpu.VMEM((EXP_DEV, rows, 1), F32),
        ],
        input_output_aliases=aliases,
        compiler_params=params(),
        name="inner",
    )(*operands)


def back_kernel(
    rows, pick_ref, grads_ref, gate_ref, up_ref, left_ref, right_ref,
    own_ref, other_ref, hold_ref, w_ref,
):
    stack_weights(w_ref, gate_ref, up_ref)
    for j in range(EXP_DEV):
        hold_ref[j] = mm(grads_ref[j], w_ref[j]).astype(BF)
    for i in range(STEP):
        total = place_from(hold_ref, pick_ref[i], i, STEP) + mm(left_ref[i], right_ref[...])
        out_ref = own_ref if i // rows % 2 == 0 else other_ref
        out_ref[i // (2 * rows) * rows + i % rows] = total.astype(BF)


def back_rows(pick, grads, gate, up, left, right, capacity, x_rows):
    devices, slots, tokens = pick.shape
    width, inner = gate.shape[2], left.shape[2]
    rows = STEP * capacity
    return pl.pallas_call(
        functools.partial(back_kernel, x_rows),
        grid=(devices // STEP,),
        in_specs=[
            pl.BlockSpec((STEP, slots, tokens), lambda d: (d, 0, 0)),
            pl.BlockSpec((EXP_DEV, rows, grads.shape[2]), lambda d: (0, d, 0)),
            resident(gate.shape),
            resident(up.shape),
            pl.BlockSpec((STEP, tokens, inner), lambda d: (d, 0, 0)),
            resident(right.shape),
        ],
        out_specs=[pl.BlockSpec((STEP // 2, tokens, width), lambda d: (d, 0, 0))] * 2,
        out_shape=[jax.ShapeDtypeStruct((devices // 2, tokens, width), BF)] * 2,
        scratch_shapes=[
            pltpu.VMEM((EXP_DEV, rows, width), BF),
            pltpu.VMEM((EXP_DEV, grads.shape[2], width), BF),
        ],
        compiler_params=params(),
        name="back_rows",
    )(pick, grads, gate, up, left, right)


def gate_up_kernel(rows_ref, grads_ref, gate_ref, up_ref):
    inner = gate_ref.shape[1]
    both = mm_tn(grads_ref[0], rows_ref[0])
    gate_ref[0] = both[:inner]
    at = grads_ref.shape[2] // 2
    up_ref[0] = both[at : at + inner]


def gate_up_grads(rows, grads, inner):
    _, total, width = rows.shape
    tile = width // 4
    out = pl.BlockSpec((1, inner, tile), lambda j, i: (j, 0, i))
    return pl.pallas_call(
        gate_up_kernel,
        grid=(EXP_DEV, 4),
        in_specs=[
            pl.BlockSpec((1, total, tile), lambda j, i: (j, 0, i)),
            pl.BlockSpec((1, total, grads.shape[2]), lambda j, i: (j, 0, 0)),
        ],
        out_specs=[out, out],
        out_shape=[jax.ShapeDtypeStruct((EXP_DEV, inner, width), F32)] * 2,
        compiler_params=params(),
        name="gate_up_grads",
    )(rows, grads)


def output_kernel(
    x_rows, pick_ref, inner_ref, down_ref, left_ref, right_ref, own_ref, other_ref, hold_ref
):
    for j in range(EXP_DEV):
        hold_ref[j] = mm(inner_ref[j], down_ref[j]).astype(BF)
    for i in range(STEP):
        total = place_from(hold_ref, pick_ref[i], i, STEP) + mm(left_ref[i], right_ref[...])
        out_ref = own_ref if i // x_rows % 2 == 0 else other_ref
        out_ref[i // (2 * x_rows) * x_rows + i % x_rows] = total.astype(BF)


def output_rows_of(pick, inner, down, left, right, capacity, x_rows):
    devices, slots, tokens = pick.shape
    width = down.shape[2]
    rows = STEP * capacity
    return pl.pallas_call(
        functools.partial(output_kernel, x_rows),
        grid=(devices // STEP,),
        in_specs=[
            pl.BlockSpec((STEP, slots, tokens), lambda d: (d, 0, 0)),
            pl.BlockSpec((EXP_DEV, rows, inner.shape[2]), lambda d: (0, d, 0)),
            resident(down.shape),
            pl.BlockSpec((STEP, tokens, left.shape[2]), lambda d: (d, 0, 0)),
            resident(right.shape),
        ],
        out_specs=[pl.BlockSpec((STEP // 2, tokens, width), lambda d: (d, 0, 0))] * 2,
        out_shape=[jax.ShapeDtypeStruct((devices // 2, tokens, width), BF)] * 2,
        scratch_shapes=[pltpu.VMEM((EXP_DEV, rows, width), BF)],
        compiler_params=params(),
        name="output_rows",
    )(pick, inner, down, left, right)


def body(
    hidden,
    cotangent,
    segments,
    routes,
    w_query,
    w_latent,
    g_latent,
    w_expand,
    w_out,
    g_attn,
    g_ffn,
    w_router,
    s_gate,
    s_up,
    s_down,
    e_gate,
    expert_up_weight,
    e_down,
):
    tokens = hidden.shape[1]
    width = hidden.shape[2]
    links = Links()
    shards, groups = links.shards, links.groups
    devices = groups * shards
    experts = EXP_DEV * groups
    capacity = max(2, tokens * TOP * 4 // (3 * experts))
    heads = H // shards
    length = tokens * shards
    part = width // shards
    my_shard = lax.axis_index("shard")
    my_group = lax.axis_index("expert")
    hid_shard = s_down.shape[0]
    hid = hid_shard // groups
    latent_part = KVR // shards
    shard_at, slot_at = links.shard_at(), links.slot_at()

    g_all = lax.all_gather(cotangent[0], BOTH, axis=0, tiled=False)
    router_rows = part * experts // width
    small_rows = jnp.concatenate([g_attn, g_ffn, g_latent])
    small_rows = jnp.pad(small_rows, (0, -small_rows.shape[0] % width)).reshape(-1, width)
    packed = jnp.concatenate([w_router.reshape(router_rows, width), small_rows])
    packed = links.gather_shard(jnp.pad(packed, ((0, -packed.shape[0] % 16), (0, 0))))
    hidden_all = links.gather_shard(hidden[0]).reshape(length, width)
    pieces = lambda w: jnp.stack(jnp.split(w, shards, axis=1))
    wl = links.gather_shard(w_latent.T)
    wq = links.spread_shard_ring(pieces(w_query))
    we = links.spread_shard(pieces(w_expand))
    packed = jnp.take(packed, slot_at, axis=0)
    full_router = packed[:, :router_rows].reshape(width, experts)
    gains_in = packed[:, router_rows:].reshape(shards, -1)
    gattn = gains_in[:, :part].reshape(1, width).astype(F32)
    gffn = gains_in[:, part : 2 * part].reshape(width).astype(F32)
    glatent = gains_in[:, 2 * part : 2 * part + latent_part].reshape(1, KVR).astype(F32)

    order = links.order()
    same = jnp.arange(devices, dtype=jnp.int32)
    back_order = jnp.sum(
        jnp.where(order[:, None] == same[None, :], same[:, None], 0), axis=0
    ).astype(jnp.int32)
    local_routes = routes[0]
    flat_routes = local_routes.reshape(-1)
    choose = local_routes[:, :, None] == jnp.arange(experts, dtype=jnp.int32)[None, None, :]
    hits = choose.reshape(-1, experts).astype(F32)
    pair_count = tokens * TOP
    before_it = (
        lax.broadcasted_iota(jnp.int32, (pair_count, pair_count), 1)
        < lax.broadcasted_iota(jnp.int32, (pair_count, pair_count), 0)
    ).astype(BF)
    before = mm(before_it, hits.astype(BF))
    slot_rank = jnp.sum(before * hits, axis=1).astype(jnp.int32)
    slot_of = (flat_routes * capacity + slot_rank).reshape(tokens, TOP)
    slots = EXP_DEV * capacity
    slot_rows = jnp.pad(slot_of.T, ((0, 8 - TOP), (0, 0)), constant_values=-1)
    slots_all = exchange(jnp.broadcast_to(slot_rows[None], (devices, 8, tokens)), BOTH)
    slots_all = jnp.take(slots_all, order, axis=0)[:, :TOP]
    slot_ids = my_group * slots + jnp.arange(slots, dtype=jnp.int32)
    pick = jnp.any(
        slots_all[:, None] == slot_ids[None, :, None, None], axis=2
    ).astype(BF)

    positions = (shard_at[:, None] * tokens + jnp.arange(tokens, dtype=jnp.int32)).reshape(-1)
    cosine, sine_vals = rope_angles(positions)
    segs = jnp.take(segments.reshape(shards, tokens), shard_at, axis=0).reshape(-1)
    col = jnp.stack([segs, positions], axis=1)
    row = jnp.stack([segs, positions], axis=0)
    attn_part, n1, compressed, latent, attended, query, kv, lse = attention_forward(
        slot_at, hidden_all, gattn, glatent, wq, wl, we, w_out, cosine, sine_vals, col, row
    )
    inner_units = e_gate.shape[2]
    gate_t, up_t = jnp.swapaxes(e_gate, 1, 2), jnp.swapaxes(expert_up_weight, 1, 2)
    attn_out = links.sum_shard(attn_part.reshape(shards, tokens, width))

    residual_in = hidden[0].astype(F32)
    residual_mid = residual_in + attn_out
    unit_two, factor_two = norm_forward(residual_mid)
    normed_two = (unit_two * gffn).astype(BF)

    hid_ids = my_group * hid + jnp.arange(hid, dtype=jnp.int32)
    wanted = (jnp.arange(shards, dtype=jnp.int32)[:, None] * hid_shard + hid_ids).reshape(-1)
    chosen_units = (
        jnp.arange(shards * hid_shard, dtype=jnp.int32)[:, None] == wanted[None, :]
    ).astype(BF)

    def shared_pieces(units):
        cut = [mm(w, units).astype(BF).reshape(part, shards, hid) for w in (s_gate, s_up)]
        return jnp.concatenate(cut, axis=2).transpose(1, 0, 2)

    pad = hid + -hid % PAD
    shared_down = lax.dynamic_slice_in_dim(s_down, my_group * hid, hid, 0)
    gate_up = links.spread_shard(shared_pieces(chosen_units))
    gate_up = jnp.take(gate_up, slot_at, axis=0).reshape(width, 2, hid)
    shared_in = jnp.pad(gate_up, ((0, 0), (0, 0), (0, pad - hid))).reshape(width, 2 * pad)
    shared_all = jnp.concatenate(
        [shared_in, jnp.pad(full_router, ((0, 0), (0, -experts % PAD)))], axis=1
    )
    route_of = slots_all // capacity
    named = jnp.any(
        route_of.transpose(0, 2, 1)[:, :, :, None]
        == jnp.arange(experts, dtype=jnp.int32)[None, None, None, :],
        axis=2,
    ).astype(F32)
    probs = jax.nn.sigmoid(mm(normed_two, full_router))
    chosen = jnp.sum(jnp.where(choose, probs[:, None, :], 0.0), axis=-1)
    chosen_total = jnp.sum(chosen, axis=1, keepdims=True)

    def of_cotangent(pick_of):
        rows_of, inner_grads = grad_rows_of(pick_of, g_all, order, e_down, capacity)
        shared_of = mm_nt(g_all.reshape(-1, width), shared_down)
        shared_of = jnp.take(shared_of.reshape(devices, tokens, hid), order, axis=0)
        return rows_of, inner_grads, shared_of.reshape(-1, hid)

    arrival = links.arrival()
    per_chunk = STEP // shards
    chunks = groups // per_chunk
    slots_in, partners, so_far = [], {}, [None]
    work_g = Fill(of_cotangent, pick, mark=2)

    def one_chunk(c):
        arrays = []
        for r in arrival[c * per_chunk : (c + 1) * per_chunk]:
            partners[r] = links.partner(slots_in[0][r])
            arrays += [slots_in[0][r], partners[r]]
        so_far[0] = inner_of(
            c, so_far[0], my_group.reshape(1), pick, named, arrays, gate_t, up_t, shared_all,
            work_g.result[1], work_g.result[2], pad, capacity,
        )

    def chunks_after(step, done):
        ready = sum(min(r, groups - r) <= step for r in arrival) // per_chunk
        return range(done, ready)

    fills, done = [(1, work_g)], 0
    for r in range(2, groups // 2 + 1):
        some = chunks_after(r - 1, done)
        done += len(some)

        def work_of(some=some, final=r == groups // 2):
            for c in some:
                one_chunk(c)
            return so_far[0]

        if len(some) > 0:
            fill = Fill(work_of, mark=3)
            fills.append((r, fill))
    spread = jnp.stack(
        [normed_two] + [links.along_x(normed_two, k) for k in range(1, shards // 2)]
    )
    links.ring_gather([spread], [groups // 2], fills, slots_in)
    for c in range(done, chunks):
        one_chunk(c)
    grad_rows = work_g.result[0]
    rows, inner_w, grads_b, grad_slot_weight, shared_grads, shared_inner, shared_sum = so_far[0]

    shared_out = jnp.concatenate([shared_sum[:hid], shared_sum[pad : pad + hid]], axis=0)
    shared_out = shared_out.astype(BF).reshape(2 * hid, shards, part).transpose(1, 0, 2)
    in_pieces = jnp.take(links.spread_shard(shared_out), slot_at, axis=0)
    shared_down = jnp.pad(shared_down, ((0, pad - hid), (0, 0)))

    def shared_down_grad(inner_of_shared):
        back = jnp.take(inner_of_shared, back_order, axis=0).reshape(-1, pad)
        return mm_tn(back, g_all.reshape(-1, width))[:hid].astype(BF)

    dn2_own, dn2_other = back_rows(
        pick, grads_b, gate_t, up_t, shared_grads, shared_in.T, capacity, shards // 2
    )

    def router_back(slot_sums):
        slot_back = slot_sums.reshape(EXP_DEV, devices, capacity).transpose(1, 0, 2)
        slot_back = jnp.take(slot_back.reshape(devices, slots), back_order, axis=0)
        got = exchange(slot_back, BOTH)
        slot_grads = jnp.sum(got.reshape(groups, shards, slots), axis=1).reshape(-1)
        at_slot = slot_of[:, :, None] == jnp.arange(experts * capacity, dtype=jnp.int32)
        grad_weights = jnp.sum(jnp.where(at_slot, slot_grads, 0.0), axis=2)
        grad_chosen = ROUTE_SCALE * (
            grad_weights / chosen_total
            - jnp.sum(grad_weights * chosen, axis=1, keepdims=True)
            / (chosen_total * chosen_total)
        )
        grad_probs = jnp.sum(jnp.where(choose, grad_chosen[:, :, None], 0.0), axis=1)
        return (grad_probs * probs * (1.0 - probs)).astype(BF)

    down_grad = lambda a, b: jnp.einsum("jmf,jmd->jfd", a, b, preferred_element_type=F32)
    ring_shape = (groups, shards // 2, tokens, width)
    half = groups // 2

    def output_parts(weighted):
        own, other = output_rows_of(
            pick, weighted, e_down, shared_inner, shared_down, capacity, shards // 2
        )
        return links.sum_core(own.reshape(ring_shape), other.reshape(ring_shape))

    work = [
        Fill(
            lambda a, b, _: (shared_down_grad(a), down_grad(b, grad_rows)),
            shared_inner, inner_w, in_pieces,
        ),
        Fill(output_parts, inner_w),
        Fill(
            lambda b, c: (gate_up_grads(rows, b, inner_units), router_back(c)),
            grads_b, grad_slot_weight,
        ),
    ]
    dn2_parts = links.sum_core(dn2_own.reshape(ring_shape), dn2_other.reshape(ring_shape))
    dn2 = links.ring_reduce(
        [[v[:, : tokens // 2] for v in dn2_parts], [v[:, tokens // 2 :] for v in dn2_parts]],
        [half, half],
        [(half - i, w) for i, w in enumerate(work)],
        free=1,
    )
    dn2 = jnp.concatenate(dn2, axis=1)
    (d_shared_down, d_edown), out_parts, ((d_egate, grad_expert_up), grad_logits) = (
        w.result for w in work
    )

    def back_to_attention(top, logits):
        grad_normed_two = links.sum_x(top) + mm_nt(logits, full_router)
        grad_mid_norm, d_gffn = norm_backward(grad_normed_two, gffn, unit_two, factor_two)
        grad_mid = cotangent[0].astype(F32) + grad_mid_norm
        return grad_mid, d_gffn, grad_mid.astype(BF)

    backward = lambda grad_attn: attention_backward(
        slot_at, grad_attn, glatent, w_out, attended, query, kv, lse, latent, compressed,
        we, wl, wq, n1, cosine, sine_vals, col, row,
    )
    first = Fill(back_to_attention, dn2, grad_logits)
    middle = Fill(
        lambda grad: links.gather_shard(grad).reshape(length, width), lambda: first.result[2]
    )
    second = Fill(backward, lambda: middle.result)
    (routed_shared,) = links.ring_reduce(
        [out_parts], [half], [(half, first), (half - 1, middle), (half - 2, second)]
    )
    routed_shared = links.sum_x(routed_shared)
    grad_mid, d_gffn, _ = first.result
    dn1, dw, dwl, d_out, d_glatent = second.result
    output_rows = residual_mid + routed_shared
    (dn1, dw, dwl, d_out), (in_pieces, d_shared_down, grad_logits) = tie(
        (dn1, dw, dwl, d_out), (in_pieces, d_shared_down, grad_logits)
    )
    logits_back = exchange(
        jnp.broadcast_to(grad_logits.T[None], (devices, experts, tokens)), BOTH
    )
    logits_back = jnp.take(logits_back, order, axis=0)
    columns = lambda v: lax.dynamic_slice_in_dim(v.reshape(-1, width), my_shard * part, part, 1)
    own_columns = jnp.concatenate(
        [columns(v) for r in arrival for v in (slots_in[0][r], partners[r])], axis=0
    )
    d_router = mm(logits_back.transpose(1, 0, 2).reshape(experts, -1), own_columns).T
    grad_normed = links.sum_shard(dn1.reshape(shards, tokens, width))
    unit_one, factor_one = norm_forward(residual_in)
    grad_input_norm, d_gattn = norm_backward(
        grad_normed, gattn.reshape(width), unit_one, factor_one
    )
    grad_input = grad_mid + grad_input_norm

    cut = part // groups
    lat = links.sum_shard(dwl).astype(BF).reshape(groups, (KVR + DR) // groups, part)
    by_head = links.blocks(dw.reshape(shards, groups, cut, -1).transpose(1, 0, 2, 3))
    by_row = links.blocks(d_out.reshape(groups, cut, width))
    pluses = [groups // 2, (groups - 1) // 2]
    shared_slots = [[v] + [None] * (groups - 1) for v in (in_pieces, d_shared_down)]

    def shared_step(k):
        sent = []
        for got, plus in zip(shared_slots, (half, groups - 1 - half)):
            if k <= plus:
                sent.append((got, k, links.around(got[k - 1], 1)))
            if k <= groups - 1 - plus:
                sent.append((got, groups - k, links.around(got[(groups - k + 1) % groups], -1)))
        return sent

    def shared_work(k):
        def work():
            return [v for _, _, v in keep(k)]

        def keep(k):
            sent = shared_step(k)
            kept[k] = [(got, at) for got, at, _ in sent]
            return sent

        return Fill(work)

    kept = {}
    fills = [(half + 1 - k, shared_work(k)) for k in range(1, half + 1)]

    def settle(k, fill):
        for (got, at), v in zip(kept[k], fill.result):
            got[at] = v

    sum_head, sum_row = links.ring_reduce(
        [by_head, by_row], pluses, fills, after=lambda r, fill: settle(half + 1 - r, fill)
    )
    in_all, down_all = (links.by_group(got) for got in shared_slots)
    part_sgate, part_sup = shared_finish(in_all)
    down_all = down_all.reshape(hid_shard, width)
    (sum_lat,) = links.ring_reduce([links.blocks(lat)], pluses[1:])
    sum_head = links.exchange_shard(sum_head.astype(BF))
    all_head, all_row = links.ring_gather([sum_head, sum_row.astype(BF)], pluses)
    (all_lat,) = links.ring_gather([sum_lat.astype(BF)], pluses[1:])
    part_query, part_expand, part_out = finish(
        links.block_at(), all_head, all_row, heads, width
    )
    part_latent = jnp.take(jnp.stack(all_lat), links.block_at(), axis=0)
    part_latent = part_latent.reshape(KVR + DR, part).astype(F32)

    gain_grads = jnp.concatenate(
        [
            d_gattn.reshape(shards, part),
            d_gffn.reshape(shards, part),
            d_glatent.reshape(shards, latent_part),
        ],
        axis=1,
    )
    got = exchange(
        jnp.broadcast_to(gain_grads[None], (groups,) + gain_grads.shape).reshape(devices, -1),
        BOTH,
    )
    gains = jnp.sum(got, axis=0)
    return (
        output_rows.astype(BF)[None],
        grad_input[None],
        part_query,
        part_latent.T,
        gains[2 * part :],
        part_expand,
        part_out,
        gains[:part],
        gains[part : 2 * part],
        d_router,
        part_sgate,
        part_sup,
        down_all.astype(F32),
        jnp.swapaxes(d_egate, 1, 2),
        jnp.swapaxes(grad_expert_up, 1, 2),
        d_edown,
    )


def solution(mesh):
    return jax.shard_map(
        body,
        mesh=mesh,
        in_specs=(
            P("expert", "shard", None),
            P("expert", "shard", None),
            P("expert", None),
            P("expert", "shard", None),
            P("shard", None),
            P("shard", None),
            P("shard"),
            P("shard", None),
            P("shard", None),
            P("shard"),
            P("shard"),
            P("shard", None),
            P("shard", None),
            P("shard", None),
            P("shard", None),
            P("expert", None, "shard"),
            P("expert", None, "shard"),
            P("expert", "shard", None),
        ),
        out_specs=(
            P("expert", "shard", None),
            P("expert", "shard", None),
            P("shard", None),
            P("shard", None),
            P("shard"),
            P("shard", None),
            P("shard", None),
            P("shard"),
            P("shard"),
            P("shard", None),
            P("shard", None),
            P("shard", None),
            P("shard", None),
            P("expert", None, "shard"),
            P("expert", None, "shard"),
            P("expert", "shard", None),
        ),
        check_vma=False,
    )
```

```python
import functools

import jax
import jax.numpy as jnp
from jax import lax
from jax.experimental import pallas as pl
from jax.experimental.pallas import tpu as pltpu
from jax.sharding import PartitionSpec as P

H = 16
DN = 128
DR = 64
DV = 128
KVR = 512
TOP = 6
EXP_DEV = 4

EPS = 1e-06
ROUTE_SCALE = 2.446
ROPE_BASE = 50000.0
SCORE_SCALE = (DN + DR) ** (-0.5)
BF = jnp.bfloat16
F32 = jnp.float32
BOTH = ("expert", "shard")
VMEM_BYTES = 56 * 1024 * 1024


def mm(a, b):
    return jnp.dot(a, b, preferred_element_type=F32)


def mm_tn(a, b):
    return lax.dot_general(a, b, (((0,), (0,)), ((), ())), preferred_element_type=F32)


def mm_nt(a, b):
    return lax.dot_general(a, b, (((1,), (1,)), ((), ())), preferred_element_type=F32)


def rope_angles(positions):
    half_width = DR // 2
    inverse = ROPE_BASE ** (-jnp.arange(half_width).astype(F32) / half_width)
    angles = positions.astype(F32)[:, None] * inverse[None, :]
    return (jnp.cos(angles), jnp.sin(angles))


def rotate(values, cosine, sine_vals):
    half_width = DR // 2
    first_half = values[..., :half_width]
    second_half = values[..., half_width:]
    return jnp.concatenate(
        [
            first_half * cosine - second_half * sine_vals,
            second_half * cosine + first_half * sine_vals,
        ],
        axis=-1,
    )


def norm_forward(values):
    factor = lax.rsqrt(jnp.mean(values * values, axis=-1, keepdims=True) + EPS)
    return values * factor, factor


def norm_backward(grad_out, gain_vec, unit_vals, factor):
    grad_unit = grad_out * gain_vec
    grad_in = factor * (
        grad_unit - unit_vals * jnp.mean(grad_unit * unit_vals, axis=-1, keepdims=True)
    )
    return (grad_in, jnp.sum(grad_out * unit_vals, axis=0))


def swish_parts(gate, up):
    sig = jax.nn.sigmoid(gate)
    silu = gate * sig
    return silu * up, up * sig * (1.0 + gate * (1.0 - sig)), silu


def exchange(values, axis):
    return lax.all_to_all(values, axis, split_axis=0, concat_axis=0, tiled=True)


def tie(streams, extra):
    return lax.optimization_barrier((streams, extra))


class Fill:
    def __init__(self, work, *inputs, mark=None):
        self.work, self.given, self.result, self.mark = work, inputs, None, mark

    @property
    def inputs(self):
        return tuple(v() if callable(v) else v for v in self.given)


class Links:
    def __init__(self):
        self.groups = lax.axis_size("expert")
        self.shards = lax.axis_size("shard")
        self.rows = self.shards // 2
        n = self.groups
        self.ring = list(range(0, n, 2)) + list(range(n - 1, 0, -2))
        shard = lax.axis_index("shard")
        self.x = shard // 2
        self.core = shard % 2
        group = lax.axis_index("expert")
        places = [self.ring.index(e) for e in range(n)]
        self.place = jnp.sum(
            jnp.where(jnp.arange(n) == group, jnp.array(places, jnp.int32), 0)
        )

    def send(self, values, target):
        pairs = []
        for e in range(self.groups):
            for s in range(self.shards):
                pairs.append((e * self.shards + s, target(e, s)))
        return lax.ppermute(values, BOTH, pairs)

    def around(self, values, step):
        n = self.groups
        return self.send(
            values,
            lambda e, s: self.ring[(self.ring.index(e) + step) % n] * self.shards + s,
        )

    def along_x(self, values, step):
        return self.send(
            values,
            lambda e, s: e * self.shards + ((s // 2 + step) % self.rows) * 2 + s % 2,
        )

    def partner(self, values):
        return self.send(values, lambda e, s: e * self.shards + (s ^ 1))

    def shard_at(self):
        xs = (self.x - jnp.arange(self.rows, dtype=jnp.int32)) % self.rows
        cores = jnp.stack([self.core, 1 - self.core]).astype(jnp.int32)
        return (xs[:, None] * 2 + cores[None, :]).reshape(-1).astype(jnp.int32)

    def slot_at(self):
        shard = jnp.arange(self.shards, dtype=jnp.int32)
        back = (self.x - shard // 2) % self.rows
        return (back * 2 + (shard % 2 != self.core)).astype(jnp.int32)

    def gather_shard(self, values):
        out = []
        for k in range(self.rows):
            own = values if k == 0 else self.along_x(values, k)
            out += [own, self.partner(own)]
        return jnp.stack(out)

    def spread_shard(self, pieces):
        take = lambda v, i: lax.dynamic_index_in_dim(v, i, 0, keepdims=False)
        pairs = pieces.reshape((self.rows, 2) + pieces.shape[1:])
        out = []
        for k in range(self.rows):
            got = take(pairs, (self.x + k) % self.rows)
            got = got if k == 0 else self.along_x(got, k)
            out += [take(got, self.core), self.partner(take(got, 1 - self.core))]
        return jnp.stack(out)

    def spread_shard_ring(self, pieces, later):
        n, rows = self.groups, self.rows
        take = lambda v, i, axis: lax.dynamic_index_in_dim(v, i, axis, keepdims=False)
        part, wide = pieces.shape[1:]
        pairs = pieces.reshape(rows, 2, n, part // n, wide)
        mine = take(pairs, self.place, 2)
        out = []
        for k in range(rows):
            if k == 0:
                got = take(pairs, self.x, 0)
            else:
                far = self.along_x(take(mine, (self.x + k) % rows, 0), k)
                far, later = tie(far, later)
                (far,) = self.ring_gather([far], [n // 2])
                got = jnp.take(jnp.stack(far, axis=1), self.block_at(), axis=1)
            got = got.reshape(2, part, wide)
            out += [take(got, self.core, 0), self.partner(take(got, 1 - self.core, 0))]
        return jnp.stack(out), later

    def exchange_shard(self, values):
        pairs = values.reshape((self.rows, 2) + values.shape[1:])
        out = []
        for k in range(self.rows):
            got = pairs[k] if k == 0 else self.along_x(pairs[k], -k)
            out += [got[0], self.partner(got[1])]
        xs = (self.x + jnp.arange(self.rows, dtype=jnp.int32)) % self.rows
        shard = jnp.arange(self.shards, dtype=jnp.int32)
        ahead = (shard // 2 - self.x) % self.rows
        slot = ahead * 2 + (shard % 2 != self.core)
        return jnp.take(jnp.stack(out), slot, axis=0)

    def sum_shard(self, values, fill=None):
        pairs = values.reshape((self.rows, 2) + values.shape[1:])
        both = [
            pairs[k, 0].astype(F32) + self.partner(pairs[k, 1]).astype(F32)
            for k in range(self.rows)
        ]
        far = [v.astype(BF) for v in both[1:]]
        if fill is not None:
            _, inputs = tie(far, fill.inputs)
        far = [self.along_x(v, -k - 1) for k, v in enumerate(far)]
        if fill is not None:
            far, fill.result = tie(far, fill.work(*inputs))
        total = both[0]
        for v in far:
            total = total + v.astype(F32)
        return total

    def ring_gather(self, values, pluses, fills=(), outs=None):
        n = self.groups
        fills = dict(fills)
        outs = [] if outs is None else outs
        outs += [[v] + [None] * (n - 1) for v in values]
        ahead, back = list(values), list(values)
        for r in range(1, n):
            moves = [(i, 1) for i, p in enumerate(pluses) if r <= p]
            moves += [(i, -1) for i, p in enumerate(pluses) if r <= n - 1 - p]
            if not moves:
                break
            streams = [ahead[i] if step > 0 else back[i] for i, step in moves]
            streams = self.step(streams, [step for _, step in moves], fills.get(r))
            for (i, step), got in zip(moves, streams):
                if step > 0:
                    ahead[i] = outs[i][r] = got
                else:
                    back[i] = outs[i][n - r] = got
        return outs

    def step(self, streams, steps, fill, free=0):
        if fill is None:
            return [self.around(v, s) for v, s in zip(streams, steps)]
        streams[free:], inputs = tie(streams[free:], fill.inputs)
        streams = [self.around(v, s) for v, s in zip(streams, steps)]
        result = fill.work(*inputs)
        if fill.mark is None:
            streams[free:], fill.result = tie(streams[free:], result)
        else:
            fill.result = list(result)
            streams[free:], fill.result[fill.mark] = tie(
                streams[free:], result[fill.mark]
            )
        return streams

    def ring_reduce(self, parts, pluses, fills=(), free=0, after=None):
        n = self.groups
        fills = dict(fills)
        ahead = [p[plus] for p, plus in zip(parts, pluses)]
        back = [p[plus + 1] for p, plus in zip(parts, pluses)]
        most = max(max(p, n - 1 - p) for p in pluses)
        for r in range(most, 0, -1):
            moves = [(i, 1) for i, p in enumerate(pluses) if r <= p]
            moves += [(i, -1) for i, p in enumerate(pluses) if r <= n - 1 - p]
            moves.sort()
            streams = [ahead[i] if step > 0 else back[i] for i, step in moves]
            streams = self.step(
                streams,
                [-step for _, step in moves],
                fills.get(r),
                len([i for i, _ in moves if i < free]),
            )
            if after is not None:
                after(r, fills.get(r))
            for (i, step), got in zip(moves, streams):
                here = parts[i][r - 1 if step > 0 else (n - r + 1) % n]
                if r > 1:
                    got = (got.astype(F32) + here.astype(F32)).astype(BF)
                if step > 0:
                    ahead[i] = got
                else:
                    back[i] = got
        return [
            p[0].astype(F32) + a.astype(F32) + b.astype(F32)
            for p, a, b in zip(parts, ahead, back)
        ]

    def by_group(self, slots):
        places = jnp.array([self.ring.index(e) for e in range(self.groups)], jnp.int32)
        return jnp.take(jnp.stack(slots), (self.place - places) % self.groups, axis=0)

    def block_at(self):
        return (self.place - jnp.arange(self.groups, dtype=jnp.int32)) % self.groups

    def blocks(self, values):
        return [
            lax.dynamic_index_in_dim(
                values, (self.place - r) % self.groups, 0, keepdims=False
            )
            for r in range(self.groups)
        ]

    def arrival(self):
        n = self.groups
        return [0] + [r for k in range(1, n // 2 + 1) for r in dict.fromkeys((k, n - k))]

    def order(self):
        n = self.groups
        ring = jnp.array(self.ring, jnp.int32)
        groups = jnp.sum(
            jnp.where(
                self.block_at()[jnp.array(self.arrival())][:, None] == jnp.arange(n)[None, :],
                ring[None, :],
                0,
            ),
            axis=1,
        )
        shard = self.shard_at().reshape(self.rows, 2).T.reshape(-1)
        all_of = groups[:, None] * self.shards + shard[None, :]
        return all_of.reshape(-1).astype(jnp.int32)

    def sum_core(self, own, other):
        both = (own.astype(F32) + self.partner(other).astype(F32)).astype(BF)
        return [both[self.arrival().index(r)] for r in range(self.groups)]

    def sum_x(self, top):
        total = top[0]
        for k in range(1, self.rows):
            total = total + self.along_x(top[k].astype(BF), -k).astype(F32)
        return total


def params(**kw):
    return pltpu.CompilerParams(vmem_limit_bytes=VMEM_BYTES, **kw)


SMEM = pl.BlockSpec(memory_space=pltpu.SMEM)
VMEM = pl.BlockSpec(memory_space=pltpu.VMEM)


def allowed_mask(seg_col, seg_row, pos_col, pos_row):
    return (seg_col == seg_row) & (pos_row <= pos_col)


def attention_forward_kernel(
    slot_ref, x_ref, gattn_ref, glat_ref, wq_ref, wl_ref, we_ref, wo_ref,
    cos_ref, sin_ref, col_ref, row_ref,
    out_ref, n1_ref, c_ref, lat_ref, o_ref, q_ref, kv_ref, lse_ref,
):
    shards, part = wq_ref.shape[0], wq_ref.shape[1]
    heads = q_ref.shape[0]
    tokens = x_ref.shape[0] // shards
    for b in range(shards):
        at = slice(b * tokens, (b + 1) * tokens)
        unit, _ = norm_forward(x_ref[at].astype(F32))
        n1_ref[at] = (unit * gattn_ref[...]).astype(BF)
    queries, compressed, kv_all = None, None, None
    for s in range(shards):
        left = n1_ref[:, s * part : (s + 1) * part]
        one = mm(left, wq_ref[slot_ref[s]])
        queries = one if s == 0 else queries + one
        one = mm_nt(left, wl_ref[slot_ref[s]])
        compressed = one if s == 0 else compressed + one
    c_ref[...] = compressed
    unit, _ = norm_forward(compressed[:, :KVR])
    lat_ref[:, :KVR] = (unit * glat_ref[...]).astype(BF)
    lat_ref[:, KVR:] = rotate(compressed[:, KVR:], cos_ref[...], sin_ref[...]).astype(BF)
    part = KVR // shards
    for s in range(shards):
        one = mm(lat_ref[:, s * part : (s + 1) * part], we_ref[slot_ref[s]])
        kv_all = one if s == 0 else kv_all + one
    kv_ref[...] = kv_all.astype(BF)
    ok = allowed_mask(
        col_ref[:, :1], row_ref[:1, :], col_ref[:, 1:2], row_ref[1:2, :]
    )
    key_rot = lat_ref[:, KVR:]
    for h in range(heads):
        at = h * (DN + DR)
        query = jnp.concatenate(
            [
                queries[:, at : at + DN],
                rotate(queries[:, at + DN : at + DN + DR], cos_ref[...], sin_ref[...]),
            ],
            axis=1,
        ).astype(BF)
        q_ref[h] = query
        at = h * (DN + DV)
        keys = kv_ref[:, at : at + DN]
        values = kv_ref[:, at + DN : at + DN + DV]
        scores = mm_nt(query[:, :DN], keys) + mm_nt(query[:, DN:], key_rot)
        scores = jnp.where(ok, scores * SCORE_SCALE, -1e30)
        top = jnp.max(scores, axis=1, keepdims=True)
        expo = jnp.exp(scores - top)
        total = jnp.sum(expo, axis=1, keepdims=True)
        lse_ref[h] = top + jnp.log(total)
        weights = (expo / total).astype(BF)
        o_ref[:, h * DV : (h + 1) * DV] = mm(weights, values).astype(BF)
    out_ref[...] = mm(o_ref[...], wo_ref[...]).astype(BF)


def attention_forward(slot, x, gattn, glat, wq, wl, we, wo, cosine, sine_vals, col, row):
    length, width = x.shape
    heads = wo.shape[0] // DV
    return pl.pallas_call(
        attention_forward_kernel,
        in_specs=[SMEM] + [VMEM] * 11,
        out_shape=[
            jax.ShapeDtypeStruct((length, width), BF),
            jax.ShapeDtypeStruct((length, width), BF),
            jax.ShapeDtypeStruct((length, KVR + DR), F32),
            jax.ShapeDtypeStruct((length, KVR + DR), BF),
            jax.ShapeDtypeStruct((length, heads * DV), BF),
            jax.ShapeDtypeStruct((heads, length, DN + DR), BF),
            jax.ShapeDtypeStruct((length, heads * (DN + DV)), BF),
            jax.ShapeDtypeStruct((heads, length, 1), F32),
        ],
        compiler_params=params(),
        name="attention_forward",
    )(slot, x, gattn, glat, wq, wl, we, wo, cosine, sine_vals, col, row)


def attention_backward_kernel(
    slot_ref, dh_ref, glat_ref, wo_ref, o_ref, q_ref, kv_ref, lse_ref, lat_ref, c_ref,
    we_ref, wl_ref, wq_ref, n1_ref, cos_ref, sin_ref, col_ref, row_ref,
    dn1_ref, dw_ref, dwl_ref, dwo_ref, dgl_ref,
    go_ref, gq_ref, gkv_ref, gc_ref,
):
    shards, part = wq_ref.shape[0], wq_ref.shape[1]
    heads = q_ref.shape[0]
    go_ref[...] = mm_nt(dh_ref[...], wo_ref[...]).astype(BF)
    dwo_ref[...] = mm_tn(o_ref[...], dh_ref[...]).astype(BF)
    ok = allowed_mask(
        col_ref[:, :1], row_ref[:1, :], col_ref[:, 1:2], row_ref[1:2, :]
    )
    key_rot = lat_ref[:, KVR:]
    grad_kr = None
    for h in range(heads):
        at = h * (DN + DV)
        keys = kv_ref[:, at : at + DN]
        values = kv_ref[:, at + DN : at + DN + DV]
        query = q_ref[h]
        grad_o = go_ref[:, h * DV : (h + 1) * DV]
        scores = mm_nt(query[:, :DN], keys) + mm_nt(query[:, DN:], key_rot)
        weights = jnp.where(ok, jnp.exp(scores * SCORE_SCALE - lse_ref[h]), 0.0)
        grad_w = mm_nt(grad_o, values)
        delta = jnp.sum(weights * grad_w, axis=1, keepdims=True)
        grad_s = (weights * (grad_w - delta) * SCORE_SCALE).astype(BF)
        gkv_ref[:, at : at + DN] = mm_tn(grad_s, query[:, :DN]).astype(BF)
        gkv_ref[:, at + DN : at + DN + DV] = mm_tn(weights.astype(BF), grad_o).astype(BF)
        one = mm_tn(grad_s, query[:, DN:])
        grad_kr = one if h == 0 else grad_kr + one
        at = h * (DN + DR)
        grad_qr = rotate(mm(grad_s, key_rot), cos_ref[...], -sin_ref[...])
        gq_ref[:, at : at + DN + DR] = jnp.concatenate(
            [mm(grad_s, keys), grad_qr], axis=1
        ).astype(BF)
    latent_part = KVR // shards
    query_wide = heads * (DN + DR)
    ratio = part // latent_part
    piece = heads * (DN + DV) // ratio
    grad_lat = []
    for s in range(shards):
        at = slice(s * latent_part, (s + 1) * latent_part)
        grad_lat.append(mm_nt(gkv_ref[...], we_ref[slot_ref[s]]))
        one = mm_tn(lat_ref[:, at], gkv_ref[...]).astype(BF)
        for i in range(ratio):
            dw_ref[slot_ref[s], i * latent_part : (i + 1) * latent_part, query_wide:] = one[
                :, i * piece : (i + 1) * piece
            ]
    grad_lat = jnp.concatenate(grad_lat, axis=1)
    unit, factor = norm_forward(c_ref[:, :KVR])
    grad_norm, grad_gain = norm_backward(grad_lat, glat_ref[...], unit, factor)
    dgl_ref[...] = grad_gain.reshape(1, KVR)
    gc_ref[:, :KVR] = grad_norm.astype(BF)
    gc_ref[:, KVR:] = rotate(grad_kr, cos_ref[...], -sin_ref[...]).astype(BF)
    for s in range(shards):
        at = slice(s * part, (s + 1) * part)
        dn1_ref[:, at] = (
            mm_nt(gq_ref[...], wq_ref[slot_ref[s]]) + mm(gc_ref[...], wl_ref[slot_ref[s]])
        ).astype(BF)
        dw_ref[slot_ref[s], :, :query_wide] = mm_tn(n1_ref[:, at], gq_ref[...]).astype(BF)
        dwl_ref[slot_ref[s]] = mm_tn(gc_ref[...], n1_ref[:, at]).astype(BF)


def attention_backward(
    slot, dh, glat, wo, o, query, kv, lse, latent, compressed, we, wl, wq, n1,
    cosine, sine_vals, col, row,
):
    length, width = n1.shape
    heads = query.shape[0]
    shards, part = wq.shape[0], wq.shape[1]
    wide = heads * (DN + DR) + heads * (DN + DV) * KVR // width
    return pl.pallas_call(
        attention_backward_kernel,
        in_specs=[SMEM] + [VMEM] * 17,
        out_shape=[
            jax.ShapeDtypeStruct((length, width), BF),
            jax.ShapeDtypeStruct((shards, part, wide), BF),
            jax.ShapeDtypeStruct(wl.shape, BF),
            jax.ShapeDtypeStruct((heads * DV, width), BF),
            jax.ShapeDtypeStruct((1, KVR), F32),
        ],
        scratch_shapes=[
            pltpu.VMEM((length, heads * DV), BF),
            pltpu.VMEM((length, heads * (DN + DR)), BF),
            pltpu.VMEM((length, heads * (DN + DV)), BF),
            pltpu.VMEM((length, KVR + DR), BF),
        ],
        compiler_params=params(),
        name="attention_backward",
    )(
        slot, dh, glat, wo, o, query, kv, lse, latent, compressed, we, wl, wq, n1,
        cosine, sine_vals, col, row,
    )


def finish_kernel(groups, shards, per, piece, *refs):
    place_ref = refs[0]
    by_head, by_row = (refs[1 + i * groups : 1 + (i + 1) * groups] for i in range(2))
    query_ref, expand_ref, out_ref = refs[1 + 2 * groups :]
    cut = by_row[0].shape[0]
    wide = by_head[0].shape[2] - piece
    expand_wide = expand_ref.shape[1] // shards
    for r in range(groups):
        at = place_ref[r]
        rows = pl.ds(pl.multiple_of(at * cut, cut), cut)
        out_ref[rows, :] = by_row[r][...].astype(F32)
        low = pl.ds(pl.multiple_of((at % per) * cut, cut), cut)
        for s in range(shards):
            query_ref[rows, s * wide : (s + 1) * wide] = by_head[r][s, :, :wide].astype(F32)
            lanes = pl.ds(
                pl.multiple_of(s * expand_wide + (at // per) * piece, piece), piece
            )
            expand_ref[low, lanes] = by_head[r][s, :, wide:].astype(F32)


def finish(place, by_head, by_row, heads, width):
    groups, shards = len(by_head), by_head[0].shape[0]
    latent_part = KVR // shards
    part = width // shards
    per = groups * latent_part // part
    piece = heads * (DN + DV) * latent_part // part
    return pl.pallas_call(
        functools.partial(finish_kernel, groups, shards, per, piece),
        in_specs=[SMEM] + [VMEM] * (2 * groups),
        out_shape=[
            jax.ShapeDtypeStruct((part, H * (DN + DR)), F32),
            jax.ShapeDtypeStruct((latent_part, H * (DN + DV)), F32),
            jax.ShapeDtypeStruct((part, width), F32),
        ],
        compiler_params=params(),
        name="finish",
    )(place, *by_head, *by_row)


def shared_finish_kernel(x_ref, gate_ref, up_ref, hold_ref):
    groups, shards, hid = x_ref.shape[0], x_ref.shape[1], x_ref.shape[2] // 2
    for i, out_ref in ((0, gate_ref), (1, up_ref)):
        for s in range(shards):
            for g in range(groups):
                at = (s * groups + g) * hid
                hold_ref[at : at + hid] = x_ref[g, s, i * hid : (i + 1) * hid].astype(F32)
        out_ref[...] = hold_ref[...].T


def shared_finish(pieces):
    groups, shards, two, part = pieces.shape
    wide = groups * shards * two // 2
    return pl.pallas_call(
        shared_finish_kernel,
        in_specs=[VMEM],
        out_shape=[jax.ShapeDtypeStruct((part, wide), F32)] * 2,
        scratch_shapes=[pltpu.VMEM((wide, part), F32)],
        compiler_params=params(),
        name="shared_finish",
    )(pieces)


STEP = 8
PAD = 128


def pick_into(out_ref, pick, rows_of, i, step):
    capacity = out_ref.shape[1] // step
    rows = mm(pick, rows_of).astype(BF)
    out_ref[:, i * capacity : (i + 1) * capacity, :] = rows.reshape(
        EXP_DEV, capacity, rows.shape[1]
    )


def place_from(rows_ref, pick, i, step):
    capacity = rows_ref.shape[1] // step
    rows = rows_ref[:, i * capacity : (i + 1) * capacity, :]
    return mm_tn(pick, rows.reshape(EXP_DEV * capacity, rows.shape[2]))


def resident(shape):
    return pl.BlockSpec(
        shape, lambda *_: (0,) * len(shape), pipeline_mode=pl.Buffered(1)
    )


def grad_rows_kernel(order_ref, pick_ref, down_ref, *refs):
    rows_ref, inner_ref = refs[STEP:]
    inner = down_ref.shape[1]
    for i in range(STEP):
        pick_into(rows_ref, pick_ref[i], refs[i][0], i, STEP)
    for j in range(EXP_DEV):
        inner_ref[j, :, :inner] = mm_nt(rows_ref[j], down_ref[j])


def grad_rows_of(pick, g_all, order, down, capacity):
    devices, slots, tokens = pick.shape
    width, inner = g_all.shape[2], down.shape[1]
    lanes = inner + -inner % PAD
    rows = STEP * capacity
    at = lambda i: pl.BlockSpec((1, tokens, width), lambda d, o: (o[d * STEP + i], 0, 0))
    return pl.pallas_call(
        grad_rows_kernel,
        grid_spec=pltpu.PrefetchScalarGridSpec(
            num_scalar_prefetch=1,
            grid=(devices // STEP,),
            in_specs=[
                pl.BlockSpec((STEP, slots, tokens), lambda d, o: (d, 0, 0)),
                resident(down.shape),
            ]
            + [at(i) for i in range(STEP)],
            out_specs=[
                pl.BlockSpec((EXP_DEV, rows, width), lambda d, o: (0, d, 0)),
                pl.BlockSpec((EXP_DEV, rows, lanes), lambda d, o: (0, d, 0)),
            ],
        ),
        out_shape=[
            jax.ShapeDtypeStruct((EXP_DEV, devices * capacity, width), BF),
            jax.ShapeDtypeStruct((EXP_DEV, devices * capacity, lanes), F32),
        ],
        compiler_params=params(),
        name="grad_rows",
    )(order, pick, down, *([g_all] * STEP))


def stack_weights(w_ref, gate_ref, up_ref):
    inner, lanes = gate_ref.shape[1], w_ref.shape[1] // 2

    @pl.when(pl.program_id(0) == 0)
    def _():
        for j in range(EXP_DEV):
            for i, ref in ((0, gate_ref), (1, up_ref)):
                w_ref[j, i * lanes : i * lanes + inner] = ref[j]
                if lanes > inner:
                    w_ref[j, i * lanes + inner : (i + 1) * lanes] = jnp.zeros(
                        (lanes - inner, w_ref.shape[2]), BF
                    )


def inner_kernel(
    count, group_ref, pick_ref, named_ref, *refs
):
    x_refs = refs[:count]
    (
        gate_ref, up_ref, shared_ref, grad_ref, shared_grad_ref,
        rows_ref, inner_ref, grads_ref, slot_ref, shared_grads_ref, shared_inner_ref, sum_ref,
    ) = refs[count : count + 5] + refs[-9:-2]
    w_ref, weight_ref = refs[-2:]
    before_ref = refs[-10] if len(refs) == count + 5 + 16 else None
    lanes, inner = grad_ref.shape[2], inner_ref.shape[2]
    hid, pad = shared_grad_ref.shape[1], shared_inner_ref.shape[2]
    x_rows, tokens = x_refs[0].shape[0], x_refs[0].shape[1]
    capacity = rows_ref.shape[1] // STEP
    experts = named_ref.shape[2]
    stack_weights(w_ref, gate_ref, up_ref)
    slots = EXP_DEV * capacity
    mine = group_ref[0] * EXP_DEV + lax.broadcasted_iota(
        jnp.int32, (slots, 3 * experts), 0
    ) // capacity
    at_mine = lax.broadcasted_iota(jnp.int32, (slots, 3 * experts), 1) % experts == mine
    total = None
    for i in range(STEP):
        x = x_refs[i // x_rows][i % x_rows]
        pick_into(rows_ref, pick_ref[i], x, i, STEP)
        both = mm(x, shared_ref[...])
        probs = jax.nn.sigmoid(both[:, 2 * pad : 2 * pad + experts])
        named = named_ref[i]
        weight = probs / jnp.sum(probs * named, axis=1, keepdims=True) * ROUTE_SCALE
        high = weight.astype(BF)
        rest = weight - high.astype(F32)
        middle = rest.astype(BF)
        low = (rest - middle.astype(F32)).astype(BF)
        at_slots = mm(pick_ref[i], jnp.concatenate([high, middle, low], axis=1))
        at_slots = jnp.sum(jnp.where(at_mine, at_slots, 0.0), axis=1, keepdims=True)
        weight_ref[:, i * capacity : (i + 1) * capacity] = at_slots.reshape(
            EXP_DEV, capacity, 1
        )
        act, slope_gate, slope_up = swish_parts(both[:, :hid], both[:, pad : pad + hid])
        grad = shared_grad_ref[i * tokens : (i + 1) * tokens]
        zeros = jnp.zeros((tokens, pad - hid), BF)
        join = lambda v: v.astype(BF) if pad == hid else jnp.concatenate(
            [v.astype(BF), zeros], axis=1
        )
        shared_inner_ref[i] = join(act)
        shared_grads_ref[i, :, :pad] = join(grad * slope_gate)
        shared_grads_ref[i, :, pad:] = join(grad * slope_up)
        one = mm_tn(shared_grads_ref[i], x)
        total = one if total is None else total + one
    sum_ref[...] = total if before_ref is None else total + before_ref[...]
    for j in range(EXP_DEV):
        both = mm_nt(rows_ref[j], w_ref[j])
        gate, up = both[:, :inner], both[:, lanes : lanes + inner]
        act, slope_gate, slope_up = swish_parts(gate, up)
        weight = weight_ref[j]
        grad = grad_ref[j, :, :inner]
        slot_ref[j] = jnp.sum(act.astype(BF).astype(F32) * grad, axis=1, keepdims=True)
        inner_ref[j] = (weight * act).astype(BF)
        grad = weight * grad
        if lanes > inner:
            grads_ref[j] = jnp.zeros(grads_ref.shape[1:], BF)
        grads_ref[j, :, :inner] = (grad * slope_gate).astype(BF)
        grads_ref[j, :, lanes : lanes + inner] = (grad * slope_up).astype(BF)


def inner_of(
    chunk, before, group, pick, named, arrays, gate, up, shared, grad, shared_grad, pad, capacity
):
    devices, slots, tokens = pick.shape
    width, lanes, inner = arrays[0].shape[2], grad.shape[2], gate.shape[1]
    hid, experts = shared_grad.shape[1], named.shape[2]
    rows = STEP * capacity
    total = devices * capacity
    by_rows = lambda n: pl.BlockSpec((EXP_DEV, rows, n), lambda _: (0, chunk, 0))
    by_device = lambda *n: pl.BlockSpec((STEP,) + n, lambda _: (chunk, 0, 0))
    whole = lambda v: resident(v.shape)
    any_spec = pl.BlockSpec(memory_space=pl.ANY)
    in_specs = (
        [SMEM, by_device(slots, tokens), by_device(tokens, experts)]
        + [whole(v) for v in arrays]
        + [
            whole(gate),
            whole(up),
            whole(shared),
            by_rows(lanes),
            pl.BlockSpec((STEP * tokens, hid), lambda _: (chunk, 0)),
        ]
    )
    operands = [group, pick, named, *arrays, gate, up, shared, grad, shared_grad]
    aliases = {}
    if before is not None:
        aliases = {len(operands) + i: i for i in range(6)}
        operands += before
        in_specs += [any_spec] * 6 + [pl.BlockSpec((2 * pad, width), lambda _: (0, 0))]
    return pl.pallas_call(
        functools.partial(inner_kernel, len(arrays)),
        grid=(1,),
        in_specs=in_specs,
        out_specs=[
            by_rows(width),
            by_rows(inner),
            by_rows(2 * lanes),
            by_rows(1),
            by_device(tokens, 2 * pad),
            by_device(tokens, pad),
            pl.BlockSpec((2 * pad, width), lambda _: (0, 0)),
        ],
        out_shape=[
            jax.ShapeDtypeStruct((EXP_DEV, total, width), BF),
            jax.ShapeDtypeStruct((EXP_DEV, total, inner), BF),
            jax.ShapeDtypeStruct((EXP_DEV, total, 2 * lanes), BF),
            jax.ShapeDtypeStruct((EXP_DEV, total, 1), F32),
            jax.ShapeDtypeStruct((devices, tokens, 2 * pad), BF),
            jax.ShapeDtypeStruct((devices, tokens, pad), BF),
            jax.ShapeDtypeStruct((2 * pad, width), F32),
        ],
        scratch_shapes=[
            pltpu.VMEM((EXP_DEV, 2 * lanes, width), BF),
            pltpu.VMEM((EXP_DEV, rows, 1), F32),
        ],
        input_output_aliases=aliases,
        compiler_params=params(),
        name="inner",
    )(*operands)


def back_kernel(
    rows, pick_ref, grads_ref, gate_ref, up_ref, left_ref, right_ref,
    own_ref, other_ref, hold_ref, w_ref,
):
    stack_weights(w_ref, gate_ref, up_ref)
    for j in range(EXP_DEV):
        hold_ref[j] = mm(grads_ref[j], w_ref[j]).astype(BF)
    for i in range(STEP):
        total = place_from(hold_ref, pick_ref[i], i, STEP) + mm(left_ref[i], right_ref[...])
        out_ref = own_ref if i // rows % 2 == 0 else other_ref
        out_ref[i // (2 * rows) * rows + i % rows] = total.astype(BF)


def back_rows(pick, grads, gate, up, left, right, capacity, x_rows):
    devices, slots, tokens = pick.shape
    width, inner = gate.shape[2], left.shape[2]
    rows = STEP * capacity
    return pl.pallas_call(
        functools.partial(back_kernel, x_rows),
        grid=(devices // STEP,),
        in_specs=[
            pl.BlockSpec((STEP, slots, tokens), lambda d: (d, 0, 0)),
            pl.BlockSpec((EXP_DEV, rows, grads.shape[2]), lambda d: (0, d, 0)),
            resident(gate.shape),
            resident(up.shape),
            pl.BlockSpec((STEP, tokens, inner), lambda d: (d, 0, 0)),
            resident(right.shape),
        ],
        out_specs=[pl.BlockSpec((STEP // 2, tokens, width), lambda d: (d, 0, 0))] * 2,
        out_shape=[jax.ShapeDtypeStruct((devices // 2, tokens, width), BF)] * 2,
        scratch_shapes=[
            pltpu.VMEM((EXP_DEV, rows, width), BF),
            pltpu.VMEM((EXP_DEV, grads.shape[2], width), BF),
        ],
        compiler_params=params(),
        name="back_rows",
    )(pick, grads, gate, up, left, right)


def gate_up_kernel(rows_ref, grads_ref, gate_ref, up_ref):
    inner = gate_ref.shape[1]
    both = mm_tn(grads_ref[0], rows_ref[0])
    gate_ref[0] = both[:inner]
    at = grads_ref.shape[2] // 2
    up_ref[0] = both[at : at + inner]


def gate_up_grads(rows, grads, inner):
    _, total, width = rows.shape
    tile = width // 4
    out = pl.BlockSpec((1, inner, tile), lambda j, i: (j, 0, i))
    return pl.pallas_call(
        gate_up_kernel,
        grid=(EXP_DEV, 4),
        in_specs=[
            pl.BlockSpec((1, total, tile), lambda j, i: (j, 0, i)),
            pl.BlockSpec((1, total, grads.shape[2]), lambda j, i: (j, 0, 0)),
        ],
        out_specs=[out, out],
        out_shape=[jax.ShapeDtypeStruct((EXP_DEV, inner, width), F32)] * 2,
        compiler_params=params(),
        name="gate_up_grads",
    )(rows, grads)


def output_kernel(
    x_rows, pick_ref, inner_ref, down_ref, left_ref, right_ref, own_ref, other_ref, hold_ref
):
    for j in range(EXP_DEV):
        hold_ref[j] = mm(inner_ref[j], down_ref[j]).astype(BF)
    for i in range(STEP):
        total = place_from(hold_ref, pick_ref[i], i, STEP) + mm(left_ref[i], right_ref[...])
        out_ref = own_ref if i // x_rows % 2 == 0 else other_ref
        out_ref[i // (2 * x_rows) * x_rows + i % x_rows] = total.astype(BF)


def output_rows_of(pick, inner, down, left, right, capacity, x_rows):
    devices, slots, tokens = pick.shape
    width = down.shape[2]
    rows = STEP * capacity
    return pl.pallas_call(
        functools.partial(output_kernel, x_rows),
        grid=(devices // STEP,),
        in_specs=[
            pl.BlockSpec((STEP, slots, tokens), lambda d: (d, 0, 0)),
            pl.BlockSpec((EXP_DEV, rows, inner.shape[2]), lambda d: (0, d, 0)),
            resident(down.shape),
            pl.BlockSpec((STEP, tokens, left.shape[2]), lambda d: (d, 0, 0)),
            resident(right.shape),
        ],
        out_specs=[pl.BlockSpec((STEP // 2, tokens, width), lambda d: (d, 0, 0))] * 2,
        out_shape=[jax.ShapeDtypeStruct((devices // 2, tokens, width), BF)] * 2,
        scratch_shapes=[pltpu.VMEM((EXP_DEV, rows, width), BF)],
        compiler_params=params(),
        name="output_rows",
    )(pick, inner, down, left, right)


def body(
    hidden,
    cotangent,
    segments,
    routes,
    w_query,
    w_latent,
    g_latent,
    w_expand,
    w_out,
    g_attn,
    g_ffn,
    w_router,
    s_gate,
    s_up,
    s_down,
    e_gate,
    expert_up_weight,
    e_down,
):
    tokens = hidden.shape[1]
    width = hidden.shape[2]
    links = Links()
    shards, groups = links.shards, links.groups
    devices = groups * shards
    experts = EXP_DEV * groups
    capacity = max(2, tokens * TOP * 4 // (3 * experts))
    heads = H // shards
    length = tokens * shards
    part = width // shards
    my_shard = lax.axis_index("shard")
    my_group = lax.axis_index("expert")
    hid_shard = s_down.shape[0]
    hid = hid_shard // groups
    latent_part = KVR // shards
    shard_at, slot_at = links.shard_at(), links.slot_at()

    g_all = lax.all_gather(cotangent[0], BOTH, axis=0, tiled=False)
    router_rows = part * experts // width
    small_rows = jnp.concatenate([g_attn, g_ffn, g_latent])
    small_rows = jnp.pad(small_rows, (0, -small_rows.shape[0] % width)).reshape(-1, width)
    packed = jnp.concatenate([w_router.reshape(router_rows, width), small_rows])
    packed = links.gather_shard(jnp.pad(packed, ((0, -packed.shape[0] % 16), (0, 0))))
    hidden_all = links.gather_shard(hidden[0]).reshape(length, width)
    pieces = lambda w: jnp.stack(jnp.split(w, shards, axis=1))
    wl = links.gather_shard(w_latent.T)
    wq, expand = links.spread_shard_ring(pieces(w_query), pieces(w_expand))
    we = links.spread_shard(expand)
    packed = jnp.take(packed, slot_at, axis=0)
    full_router = packed[:, :router_rows].reshape(width, experts)
    gains_in = packed[:, router_rows:].reshape(shards, -1)
    gattn = gains_in[:, :part].reshape(1, width).astype(F32)
    gffn = gains_in[:, part : 2 * part].reshape(width).astype(F32)
    glatent = gains_in[:, 2 * part : 2 * part + latent_part].reshape(1, KVR).astype(F32)

    order = links.order()
    same = jnp.arange(devices, dtype=jnp.int32)
    back_order = jnp.sum(
        jnp.where(order[:, None] == same[None, :], same[:, None], 0), axis=0
    ).astype(jnp.int32)
    local_routes = routes[0]
    flat_routes = local_routes.reshape(-1)
    choose = local_routes[:, :, None] == jnp.arange(experts, dtype=jnp.int32)[None, None, :]
    hits = choose.reshape(-1, experts).astype(F32)
    pair_count = tokens * TOP
    before_it = (
        lax.broadcasted_iota(jnp.int32, (pair_count, pair_count), 1)
        < lax.broadcasted_iota(jnp.int32, (pair_count, pair_count), 0)
    ).astype(BF)
    before = mm(before_it, hits.astype(BF))
    slot_rank = jnp.sum(before * hits, axis=1).astype(jnp.int32)
    slot_of = (flat_routes * capacity + slot_rank).reshape(tokens, TOP)
    slots = EXP_DEV * capacity
    slot_rows = jnp.pad(slot_of.T, ((0, 8 - TOP), (0, 0)), constant_values=-1)
    slots_all = exchange(jnp.broadcast_to(slot_rows[None], (devices, 8, tokens)), BOTH)
    slots_all = jnp.take(slots_all, order, axis=0)[:, :TOP]
    slot_ids = my_group * slots + jnp.arange(slots, dtype=jnp.int32)
    pick = jnp.any(
        slots_all[:, None] == slot_ids[None, :, None, None], axis=2
    ).astype(BF)

    hid_ids = my_group * hid + jnp.arange(hid, dtype=jnp.int32)
    wanted = (jnp.arange(shards, dtype=jnp.int32)[:, None] * hid_shard + hid_ids).reshape(-1)
    chosen_units = (
        jnp.arange(shards * hid_shard, dtype=jnp.int32)[:, None] == wanted[None, :]
    ).astype(BF)

    def shared_pieces(units):
        cut = [mm(w, units).astype(BF).reshape(part, shards, hid) for w in (s_gate, s_up)]
        return jnp.concatenate(cut, axis=2).transpose(1, 0, 2)

    wq, chosen_units = tie(wq, chosen_units)

    positions = (shard_at[:, None] * tokens + jnp.arange(tokens, dtype=jnp.int32)).reshape(-1)
    cosine, sine_vals = rope_angles(positions)
    segs = jnp.take(segments.reshape(shards, tokens), shard_at, axis=0).reshape(-1)
    col = jnp.stack([segs, positions], axis=1)
    row = jnp.stack([segs, positions], axis=0)
    attn_part, n1, compressed, latent, attended, query, kv, lse = attention_forward(
        slot_at, hidden_all, gattn, glatent, wq, wl, we, w_out, cosine, sine_vals, col, row
    )
    inner_units = e_gate.shape[2]
    gate_t, up_t = jnp.swapaxes(e_gate, 1, 2), jnp.swapaxes(expert_up_weight, 1, 2)
    attn_out = links.sum_shard(attn_part.reshape(shards, tokens, width))

    residual_in = hidden[0].astype(F32)
    residual_mid = residual_in + attn_out
    unit_two, factor_two = norm_forward(residual_mid)
    normed_two = (unit_two * gffn).astype(BF)

    pad = hid + -hid % PAD
    shared_down = lax.dynamic_slice_in_dim(s_down, my_group * hid, hid, 0)
    gate_up = links.spread_shard(shared_pieces(chosen_units))
    gate_up = jnp.take(gate_up, slot_at, axis=0).reshape(width, 2, hid)
    shared_in = jnp.pad(gate_up, ((0, 0), (0, 0), (0, pad - hid))).reshape(width, 2 * pad)
    shared_all = jnp.concatenate(
        [shared_in, jnp.pad(full_router, ((0, 0), (0, -experts % PAD)))], axis=1
    )
    route_of = slots_all // capacity
    named = jnp.any(
        route_of.transpose(0, 2, 1)[:, :, :, None]
        == jnp.arange(experts, dtype=jnp.int32)[None, None, None, :],
        axis=2,
    ).astype(F32)
    probs = jax.nn.sigmoid(mm(normed_two, full_router))
    chosen = jnp.sum(jnp.where(choose, probs[:, None, :], 0.0), axis=-1)
    chosen_total = jnp.sum(chosen, axis=1, keepdims=True)

    def of_cotangent(pick_of):
        rows_of, inner_grads = grad_rows_of(pick_of, g_all, order, e_down, capacity)
        shared_of = mm_nt(g_all.reshape(-1, width), shared_down)
        shared_of = jnp.take(shared_of.reshape(devices, tokens, hid), order, axis=0)
        return rows_of, inner_grads, shared_of.reshape(-1, hid)

    arrival = links.arrival()
    per_chunk = STEP // shards
    chunks = groups // per_chunk
    slots_in, partners, so_far = [], {}, [None]
    work_g = Fill(of_cotangent, pick, mark=2)

    def one_chunk(c):
        arrays = []
        for r in arrival[c * per_chunk : (c + 1) * per_chunk]:
            partners[r] = links.partner(slots_in[0][r])
            arrays += [slots_in[0][r], partners[r]]
        so_far[0] = inner_of(
            c, so_far[0], my_group.reshape(1), pick, named, arrays, gate_t, up_t, shared_all,
            work_g.result[1], work_g.result[2], pad, capacity,
        )

    def chunks_after(step, done):
        ready = sum(min(r, groups - r) <= step for r in arrival) // per_chunk
        return range(done, ready)

    fills, done = [(1, work_g)], 0
    for r in range(2, groups // 2 + 1):
        some = chunks_after(r - 1, done)
        done += len(some)

        def work_of(some=some, final=r == groups // 2):
            for c in some:
                one_chunk(c)
            return so_far[0]

        if len(some) > 0:
            fill = Fill(work_of, mark=3)
            fills.append((r, fill))
    spread = jnp.stack(
        [normed_two] + [links.along_x(normed_two, k) for k in range(1, shards // 2)]
    )
    links.ring_gather([spread], [groups // 2], fills, slots_in)
    for c in range(done, chunks):
        one_chunk(c)
    grad_rows = work_g.result[0]
    rows, inner_w, grads_b, grad_slot_weight, shared_grads, shared_inner, shared_sum = so_far[0]

    shared_out = jnp.concatenate([shared_sum[:hid], shared_sum[pad : pad + hid]], axis=0)
    shared_out = shared_out.astype(BF).reshape(2 * hid, shards, part).transpose(1, 0, 2)
    in_pieces = jnp.take(links.spread_shard(shared_out), slot_at, axis=0)
    shared_down = jnp.pad(shared_down, ((0, pad - hid), (0, 0)))

    def shared_down_grad(inner_of_shared):
        back = jnp.take(inner_of_shared, back_order, axis=0).reshape(-1, pad)
        return mm_tn(back, g_all.reshape(-1, width))[:hid].astype(BF)

    dn2_own, dn2_other = back_rows(
        pick, grads_b, gate_t, up_t, shared_grads, shared_in.T, capacity, shards // 2
    )

    def router_back(slot_sums):
        slot_back = slot_sums.reshape(EXP_DEV, devices, capacity).transpose(1, 0, 2)
        slot_back = jnp.take(slot_back.reshape(devices, slots), back_order, axis=0)
        got = exchange(slot_back, BOTH)
        slot_grads = jnp.sum(got.reshape(groups, shards, slots), axis=1).reshape(-1)
        at_slot = slot_of[:, :, None] == jnp.arange(experts * capacity, dtype=jnp.int32)
        grad_weights = jnp.sum(jnp.where(at_slot, slot_grads, 0.0), axis=2)
        grad_chosen = ROUTE_SCALE * (
            grad_weights / chosen_total
            - jnp.sum(grad_weights * chosen, axis=1, keepdims=True)
            / (chosen_total * chosen_total)
        )
        grad_probs = jnp.sum(jnp.where(choose, grad_chosen[:, :, None], 0.0), axis=1)
        return (grad_probs * probs * (1.0 - probs)).astype(BF)

    down_grad = lambda a, b: jnp.einsum("jmf,jmd->jfd", a, b, preferred_element_type=F32)
    ring_shape = (groups, shards // 2, tokens, width)
    half = groups // 2

    def output_parts(weighted):
        own, other = output_rows_of(
            pick, weighted, e_down, shared_inner, shared_down, capacity, shards // 2
        )
        return links.sum_core(own.reshape(ring_shape), other.reshape(ring_shape))

    work = [
        Fill(
            lambda a, b: (shared_down_grad(a), down_grad(b, grad_rows)),
            shared_inner, inner_w,
        ),
        Fill(output_parts, inner_w),
        Fill(
            lambda b, c: (gate_up_grads(rows, b, inner_units), router_back(c)),
            grads_b, grad_slot_weight,
        ),
    ]
    dn2_parts = links.sum_core(dn2_own.reshape(ring_shape), dn2_other.reshape(ring_shape))
    dn2 = links.ring_reduce(
        [[v[:, : tokens // 2] for v in dn2_parts], [v[:, tokens // 2 :] for v in dn2_parts]],
        [half, half],
        [(half - i, w) for i, w in enumerate(work)],
        free=1,
    )
    dn2 = jnp.concatenate(dn2, axis=1)
    (d_shared_down, d_edown), out_parts, ((d_egate, grad_expert_up), grad_logits) = (
        w.result for w in work
    )

    def back_to_attention(top, logits):
        grad_normed_two = links.sum_x(top) + mm_nt(logits, full_router)
        grad_mid_norm, d_gffn = norm_backward(grad_normed_two, gffn, unit_two, factor_two)
        grad_mid = cotangent[0].astype(F32) + grad_mid_norm
        return grad_mid, d_gffn, grad_mid.astype(BF)

    backward = lambda grad_attn: attention_backward(
        slot_at, grad_attn, glatent, w_out, attended, query, kv, lse, latent, compressed,
        we, wl, wq, n1, cosine, sine_vals, col, row,
    )
    first = Fill(back_to_attention, dn2, grad_logits)
    middle = Fill(
        lambda grad: links.gather_shard(grad).reshape(length, width), lambda: first.result[2]
    )
    second = Fill(backward, lambda: middle.result)
    (routed_shared,) = links.ring_reduce(
        [out_parts], [half], [(half, first), (half - 1, middle), (half - 2, second)]
    )
    routed_shared = links.sum_x(routed_shared)
    grad_mid, d_gffn, _ = first.result
    dn1, dw, dwl, d_out, d_glatent = second.result
    output_rows = residual_mid + routed_shared
    (dn1, dw, dwl, d_out), (in_pieces, d_shared_down, grad_logits) = tie(
        (dn1, dw, dwl, d_out), (in_pieces, d_shared_down, grad_logits)
    )
    logits_back = exchange(
        jnp.broadcast_to(grad_logits.T[None], (devices, experts, tokens)), BOTH
    )
    logits_back = jnp.take(logits_back, order, axis=0)
    columns = lambda v: lax.dynamic_slice_in_dim(v.reshape(-1, width), my_shard * part, part, 1)
    own_columns = jnp.concatenate(
        [columns(v) for r in arrival for v in (slots_in[0][r], partners[r])], axis=0
    )
    d_router = mm(logits_back.transpose(1, 0, 2).reshape(experts, -1), own_columns).T
    grad_normed = links.sum_shard(dn1.reshape(shards, tokens, width))
    unit_one, factor_one = norm_forward(residual_in)
    grad_input_norm, d_gattn = norm_backward(
        grad_normed, gattn.reshape(width), unit_one, factor_one
    )
    grad_input = grad_mid + grad_input_norm

    cut = part // groups
    lat = links.sum_shard(dwl).astype(BF).reshape(groups, (KVR + DR) // groups, part)
    by_head = links.blocks(dw.reshape(shards, groups, cut, -1).transpose(1, 0, 2, 3))
    by_row = links.blocks(d_out.reshape(groups, cut, width))
    pluses = [groups // 2, (groups - 1) // 2]
    shared_slots = [[v] + [None] * (groups - 1) for v in (in_pieces, d_shared_down)]

    def shared_step(k):
        sent = []
        for got, plus in zip(shared_slots, (half, groups - 1 - half)):
            if k <= plus:
                sent.append((got, k, links.around(got[k - 1], 1)))
            if k <= groups - 1 - plus:
                sent.append((got, groups - k, links.around(got[(groups - k + 1) % groups], -1)))
        return sent

    def shared_work(k):
        def work():
            return [v for _, _, v in keep(k)]

        def keep(k):
            sent = shared_step(k)
            kept[k] = [(got, at) for got, at, _ in sent]
            return sent

        return Fill(work)

    kept = {}
    fills = [(half + 1 - k, shared_work(k)) for k in range(1, half + 1)]

    def settle(k, fill):
        for (got, at), v in zip(kept[k], fill.result):
            got[at] = v

    sum_head, sum_row = links.ring_reduce(
        [by_head, by_row], pluses, fills, after=lambda r, fill: settle(half + 1 - r, fill)
    )
    work_in = Fill(lambda: shared_finish(links.by_group(shared_slots[0])), mark=0)
    work_down = Fill(
        lambda: (links.by_group(shared_slots[1]).reshape(hid_shard, width).astype(F32),),
        mark=0,
    )
    (sum_lat,) = links.ring_reduce([links.blocks(lat)], pluses[1:])
    sum_head = links.exchange_shard(sum_head.astype(BF))
    all_head, all_row = links.ring_gather(
        [sum_head, sum_row.astype(BF)], pluses, [(half - 1, work_in), (half, work_down)]
    )
    part_sgate, part_sup = work_in.result
    (part_sdown,) = work_down.result
    (all_lat,) = links.ring_gather([sum_lat.astype(BF)], pluses[1:])
    part_query, part_expand, part_out = finish(
        links.block_at(), all_head, all_row, heads, width
    )
    part_latent = jnp.take(jnp.stack(all_lat), links.block_at(), axis=0)
    part_latent = part_latent.reshape(KVR + DR, part).astype(F32)

    gain_grads = jnp.concatenate(
        [
            d_gattn.reshape(shards, part),
            d_gffn.reshape(shards, part),
            d_glatent.reshape(shards, latent_part),
        ],
        axis=1,
    )
    got = exchange(
        jnp.broadcast_to(gain_grads[None], (groups,) + gain_grads.shape).reshape(devices, -1),
        BOTH,
    )
    gains = jnp.sum(got, axis=0)
    return (
        output_rows.astype(BF)[None],
        grad_input[None],
        part_query,
        part_latent.T,
        gains[2 * part :],
        part_expand,
        part_out,
        gains[:part],
        gains[part : 2 * part],
        d_router,
        part_sgate,
        part_sup,
        part_sdown,
        jnp.swapaxes(d_egate, 1, 2),
        jnp.swapaxes(grad_expert_up, 1, 2),
        d_edown,
    )


def solution(mesh):
    return jax.shard_map(
        body,
        mesh=mesh,
        in_specs=(
            P("expert", "shard", None),
            P("expert", "shard", None),
            P("expert", None),
            P("expert", "shard", None),
            P("shard", None),
            P("shard", None),
            P("shard"),
            P("shard", None),
            P("shard", None),
            P("shard"),
            P("shard"),
            P("shard", None),
            P("shard", None),
            P("shard", None),
            P("shard", None),
            P("expert", None, "shard"),
            P("expert", None, "shard"),
            P("expert", "shard", None),
        ),
        out_specs=(
            P("expert", "shard", None),
            P("expert", "shard", None),
            P("shard", None),
            P("shard", None),
            P("shard"),
            P("shard", None),
            P("shard", None),
            P("shard"),
            P("shard"),
            P("shard", None),
            P("shard", None),
            P("shard", None),
            P("shard", None),
            P("expert", None, "shard"),
            P("expert", None, "shard"),
            P("expert", "shard", None),
        ),
        check_vma=False,
    )
```

```python
import functools

import jax
import jax.numpy as jnp
from jax import lax
from jax.experimental import pallas as pl
from jax.experimental.pallas import tpu as pltpu
from jax.sharding import PartitionSpec as P

H = 16
DN = 128
DR = 64
DV = 128
KVR = 512
TOP = 6
EXP_DEV = 4

EPS = 1e-06
ROUTE_SCALE = 2.446
ROPE_BASE = 50000.0
SCORE_SCALE = (DN + DR) ** (-0.5)
BF = jnp.bfloat16
F32 = jnp.float32
BOTH = ("expert", "shard")
VMEM_BYTES = 56 * 1024 * 1024


def mm(a, b):
    return jnp.dot(a, b, preferred_element_type=F32)


def mm_tn(a, b):
    return lax.dot_general(a, b, (((0,), (0,)), ((), ())), preferred_element_type=F32)


def mm_nt(a, b):
    return lax.dot_general(a, b, (((1,), (1,)), ((), ())), preferred_element_type=F32)


def rope_angles(positions):
    half_width = DR // 2
    inverse = ROPE_BASE ** (-jnp.arange(half_width).astype(F32) / half_width)
    angles = positions.astype(F32)[:, None] * inverse[None, :]
    return (jnp.cos(angles), jnp.sin(angles))


def rotate(values, cosine, sine_vals):
    half_width = DR // 2
    first_half = values[..., :half_width]
    second_half = values[..., half_width:]
    return jnp.concatenate(
        [
            first_half * cosine - second_half * sine_vals,
            second_half * cosine + first_half * sine_vals,
        ],
        axis=-1,
    )


def norm_forward(values):
    factor = lax.rsqrt(jnp.mean(values * values, axis=-1, keepdims=True) + EPS)
    return values * factor, factor


def norm_backward(grad_out, gain_vec, unit_vals, factor):
    grad_unit = grad_out * gain_vec
    grad_in = factor * (
        grad_unit - unit_vals * jnp.mean(grad_unit * unit_vals, axis=-1, keepdims=True)
    )
    return (grad_in, jnp.sum(grad_out * unit_vals, axis=0))


def swish_parts(gate, up):
    sig = jax.nn.sigmoid(gate)
    silu = gate * sig
    return silu * up, up * sig * (1.0 + gate * (1.0 - sig)), silu


def exchange(values, axis):
    return lax.all_to_all(values, axis, split_axis=0, concat_axis=0, tiled=True)


def tie(streams, extra):
    return lax.optimization_barrier((streams, extra))


class Fill:
    def __init__(self, work, *inputs, mark=None):
        self.work, self.given, self.result, self.mark = work, inputs, None, mark

    @property
    def inputs(self):
        return tuple(v() if callable(v) else v for v in self.given)


class Links:
    def __init__(self):
        self.groups = lax.axis_size("expert")
        self.shards = lax.axis_size("shard")
        self.rows = self.shards // 2
        n = self.groups
        self.ring = list(range(0, n, 2)) + list(range(n - 1, 0, -2))
        shard = lax.axis_index("shard")
        self.x = shard // 2
        self.core = shard % 2
        group = lax.axis_index("expert")
        places = [self.ring.index(e) for e in range(n)]
        self.place = jnp.sum(
            jnp.where(jnp.arange(n) == group, jnp.array(places, jnp.int32), 0)
        )

    def send(self, values, target):
        pairs = []
        for e in range(self.groups):
            for s in range(self.shards):
                pairs.append((e * self.shards + s, target(e, s)))
        return lax.ppermute(values, BOTH, pairs)

    def around(self, values, step):
        n = self.groups
        return self.send(
            values,
            lambda e, s: self.ring[(self.ring.index(e) + step) % n] * self.shards + s,
        )

    def along_x(self, values, step):
        return self.send(
            values,
            lambda e, s: e * self.shards + ((s // 2 + step) % self.rows) * 2 + s % 2,
        )

    def partner(self, values):
        return self.send(values, lambda e, s: e * self.shards + (s ^ 1))

    def shard_at(self):
        xs = (self.x - jnp.arange(self.rows, dtype=jnp.int32)) % self.rows
        cores = jnp.stack([self.core, 1 - self.core]).astype(jnp.int32)
        return (xs[:, None] * 2 + cores[None, :]).reshape(-1).astype(jnp.int32)

    def slot_at(self):
        shard = jnp.arange(self.shards, dtype=jnp.int32)
        back = (self.x - shard // 2) % self.rows
        return (back * 2 + (shard % 2 != self.core)).astype(jnp.int32)

    def gather_shard(self, values):
        out = []
        for k in range(self.rows):
            own = values if k == 0 else self.along_x(values, k)
            out += [own, self.partner(own)]
        return jnp.stack(out)

    def spread_shard(self, pieces):
        take = lambda v, i: lax.dynamic_index_in_dim(v, i, 0, keepdims=False)
        pairs = pieces.reshape((self.rows, 2) + pieces.shape[1:])
        out = []
        for k in range(self.rows):
            got = take(pairs, (self.x + k) % self.rows)
            got = got if k == 0 else self.along_x(got, k)
            out += [take(got, self.core), self.partner(take(got, 1 - self.core))]
        return jnp.stack(out)

    def spread_shard_ring(self, pieces, later):
        n, rows = self.groups, self.rows
        take = lambda v, i, axis: lax.dynamic_index_in_dim(v, i, axis, keepdims=False)
        part, wide = pieces.shape[1:]
        pairs = pieces.reshape(rows, 2, n, part // n, wide)
        mine = take(pairs, self.place, 2)
        out = []
        for k in range(rows):
            if k == 0:
                got = take(pairs, self.x, 0)
            else:
                far = self.along_x(take(mine, (self.x + k) % rows, 0), k)
                far, later = tie(far, later)
                (far,) = self.ring_gather([far], [n // 2])
                got = jnp.take(jnp.stack(far, axis=1), self.block_at(), axis=1)
            got = got.reshape(2, part, wide)
            out += [take(got, self.core, 0), self.partner(take(got, 1 - self.core, 0))]
        return jnp.stack(out), later

    def exchange_shard(self, values):
        pairs = values.reshape((self.rows, 2) + values.shape[1:])
        out = []
        for k in range(self.rows):
            got = pairs[k] if k == 0 else self.along_x(pairs[k], -k)
            out += [got[0], self.partner(got[1])]
        xs = (self.x + jnp.arange(self.rows, dtype=jnp.int32)) % self.rows
        shard = jnp.arange(self.shards, dtype=jnp.int32)
        ahead = (shard // 2 - self.x) % self.rows
        slot = ahead * 2 + (shard % 2 != self.core)
        return jnp.take(jnp.stack(out), slot, axis=0)

    def sum_shard(self, values, fill=None):
        pairs = values.reshape((self.rows, 2) + values.shape[1:])
        both = [
            pairs[k, 0].astype(F32) + self.partner(pairs[k, 1]).astype(F32)
            for k in range(self.rows)
        ]
        far = [v.astype(BF) for v in both[1:]]
        if fill is not None:
            _, inputs = tie(far, fill.inputs)
        far = [self.along_x(v, -k - 1) for k, v in enumerate(far)]
        if fill is not None:
            far, fill.result = tie(far, fill.work(*inputs))
        total = both[0]
        for v in far:
            total = total + v.astype(F32)
        return total

    def ring_gather(self, values, pluses, fills=(), outs=None):
        n = self.groups
        fills = dict(fills)
        outs = [] if outs is None else outs
        outs += [[v] + [None] * (n - 1) for v in values]
        ahead, back = list(values), list(values)
        for r in range(1, n):
            moves = [(i, 1) for i, p in enumerate(pluses) if r <= p]
            moves += [(i, -1) for i, p in enumerate(pluses) if r <= n - 1 - p]
            if not moves:
                break
            streams = [ahead[i] if step > 0 else back[i] for i, step in moves]
            streams = self.step(streams, [step for _, step in moves], fills.get(r))
            for (i, step), got in zip(moves, streams):
                if step > 0:
                    ahead[i] = outs[i][r] = got
                else:
                    back[i] = outs[i][n - r] = got
        return outs

    def step(self, streams, steps, fill, free=0):
        if fill is None:
            return [self.around(v, s) for v, s in zip(streams, steps)]
        streams[free:], inputs = tie(streams[free:], fill.inputs)
        streams = [self.around(v, s) for v, s in zip(streams, steps)]
        result = fill.work(*inputs)
        if fill.mark is None:
            streams[free:], fill.result = tie(streams[free:], result)
        else:
            fill.result = list(result)
            streams[free:], fill.result[fill.mark] = tie(
                streams[free:], result[fill.mark]
            )
        return streams

    def ring_reduce(self, parts, pluses, fills=(), free=0, after=None):
        n = self.groups
        fills = dict(fills)
        ahead = [p[plus] for p, plus in zip(parts, pluses)]
        back = [p[plus + 1] for p, plus in zip(parts, pluses)]
        most = max(max(p, n - 1 - p) for p in pluses)
        for r in range(most, 0, -1):
            moves = [(i, 1) for i, p in enumerate(pluses) if r <= p]
            moves += [(i, -1) for i, p in enumerate(pluses) if r <= n - 1 - p]
            moves.sort()
            streams = [ahead[i] if step > 0 else back[i] for i, step in moves]
            streams = self.step(
                streams,
                [-step for _, step in moves],
                fills.get(r),
                len([i for i, _ in moves if i < free]),
            )
            if after is not None:
                after(r, fills.get(r))
            for (i, step), got in zip(moves, streams):
                here = parts[i][r - 1 if step > 0 else (n - r + 1) % n]
                if r > 1:
                    got = (got.astype(F32) + here.astype(F32)).astype(BF)
                if step > 0:
                    ahead[i] = got
                else:
                    back[i] = got
        return [
            p[0].astype(F32) + a.astype(F32) + b.astype(F32)
            for p, a, b in zip(parts, ahead, back)
        ]

    def by_group(self, slots):
        places = jnp.array([self.ring.index(e) for e in range(self.groups)], jnp.int32)
        return jnp.take(jnp.stack(slots), (self.place - places) % self.groups, axis=0)

    def block_at(self):
        return (self.place - jnp.arange(self.groups, dtype=jnp.int32)) % self.groups

    def blocks(self, values):
        return [
            lax.dynamic_index_in_dim(
                values, (self.place - r) % self.groups, 0, keepdims=False
            )
            for r in range(self.groups)
        ]

    def arrival(self):
        n = self.groups
        return [0] + [r for k in range(1, n // 2 + 1) for r in dict.fromkeys((k, n - k))]

    def order(self):
        n = self.groups
        ring = jnp.array(self.ring, jnp.int32)
        groups = jnp.sum(
            jnp.where(
                self.block_at()[jnp.array(self.arrival())][:, None] == jnp.arange(n)[None, :],
                ring[None, :],
                0,
            ),
            axis=1,
        )
        shard = self.shard_at().reshape(self.rows, 2).T.reshape(-1)
        all_of = groups[:, None] * self.shards + shard[None, :]
        return all_of.reshape(-1).astype(jnp.int32)

    def sum_core(self, own, other):
        both = (own.astype(F32) + self.partner(other).astype(F32)).astype(BF)
        return [both[self.arrival().index(r)] for r in range(self.groups)]

    def sum_x(self, top):
        total = top[0]
        for k in range(1, self.rows):
            total = total + self.along_x(top[k].astype(BF), -k).astype(F32)
        return total


def params(**kw):
    return pltpu.CompilerParams(vmem_limit_bytes=VMEM_BYTES, **kw)


SMEM = pl.BlockSpec(memory_space=pltpu.SMEM)
VMEM = pl.BlockSpec(memory_space=pltpu.VMEM)


def allowed_mask(seg_col, seg_row, pos_col, pos_row):
    return (seg_col == seg_row) & (pos_row <= pos_col)


def attention_forward_kernel(
    slot_ref, x_ref, gattn_ref, glat_ref, wq_ref, wl_ref, we_ref, wo_ref,
    cos_ref, sin_ref, col_ref, row_ref,
    out_ref, n1_ref, c_ref, lat_ref, o_ref, q_ref, kv_ref, lse_ref,
):
    shards, part = wq_ref.shape[0], wq_ref.shape[1]
    heads = q_ref.shape[0]
    tokens = x_ref.shape[0] // shards
    for b in range(shards):
        at = slice(b * tokens, (b + 1) * tokens)
        unit, _ = norm_forward(x_ref[at].astype(F32))
        n1_ref[at] = (unit * gattn_ref[...]).astype(BF)
    queries, compressed, kv_all = None, None, None
    for s in range(shards):
        left = n1_ref[:, s * part : (s + 1) * part]
        one = mm(left, wq_ref[slot_ref[s]])
        queries = one if s == 0 else queries + one
        one = mm_nt(left, wl_ref[slot_ref[s]])
        compressed = one if s == 0 else compressed + one
    c_ref[...] = compressed
    unit, _ = norm_forward(compressed[:, :KVR])
    lat_ref[:, :KVR] = (unit * glat_ref[...]).astype(BF)
    lat_ref[:, KVR:] = rotate(compressed[:, KVR:], cos_ref[...], sin_ref[...]).astype(BF)
    part = KVR // shards
    for s in range(shards):
        one = mm(lat_ref[:, s * part : (s + 1) * part], we_ref[slot_ref[s]])
        kv_all = one if s == 0 else kv_all + one
    kv_ref[...] = kv_all.astype(BF)
    ok = allowed_mask(
        col_ref[:, :1], row_ref[:1, :], col_ref[:, 1:2], row_ref[1:2, :]
    )
    key_rot = lat_ref[:, KVR:]
    for h in range(heads):
        at = h * (DN + DR)
        query = jnp.concatenate(
            [
                queries[:, at : at + DN],
                rotate(queries[:, at + DN : at + DN + DR], cos_ref[...], sin_ref[...]),
            ],
            axis=1,
        ).astype(BF)
        q_ref[h] = query
        at = h * (DN + DV)
        keys = kv_ref[:, at : at + DN]
        values = kv_ref[:, at + DN : at + DN + DV]
        scores = mm_nt(query[:, :DN], keys) + mm_nt(query[:, DN:], key_rot)
        scores = jnp.where(ok, scores * SCORE_SCALE, -1e30)
        top = jnp.max(scores, axis=1, keepdims=True)
        expo = jnp.exp(scores - top)
        total = jnp.sum(expo, axis=1, keepdims=True)
        lse_ref[h] = top + jnp.log(total)
        weights = (expo / total).astype(BF)
        o_ref[:, h * DV : (h + 1) * DV] = mm(weights, values).astype(BF)
    out_ref[...] = mm(o_ref[...], wo_ref[...]).astype(BF)


def attention_forward(slot, x, gattn, glat, wq, wl, we, wo, cosine, sine_vals, col, row):
    length, width = x.shape
    heads = wo.shape[0] // DV
    return pl.pallas_call(
        attention_forward_kernel,
        in_specs=[SMEM] + [VMEM] * 11,
        out_shape=[
            jax.ShapeDtypeStruct((length, width), BF),
            jax.ShapeDtypeStruct((length, width), BF),
            jax.ShapeDtypeStruct((length, KVR + DR), F32),
            jax.ShapeDtypeStruct((length, KVR + DR), BF),
            jax.ShapeDtypeStruct((length, heads * DV), BF),
            jax.ShapeDtypeStruct((heads, length, DN + DR), BF),
            jax.ShapeDtypeStruct((length, heads * (DN + DV)), BF),
            jax.ShapeDtypeStruct((heads, length, 1), F32),
        ],
        compiler_params=params(),
        name="attention_forward",
    )(slot, x, gattn, glat, wq, wl, we, wo, cosine, sine_vals, col, row)


def attention_backward_kernel(
    slot_ref, dh_ref, glat_ref, wo_ref, o_ref, q_ref, kv_ref, lse_ref, lat_ref, c_ref,
    we_ref, wl_ref, wq_ref, n1_ref, cos_ref, sin_ref, col_ref, row_ref,
    dn1_ref, dw_ref, dwl_ref, dwo_ref, dgl_ref,
    go_ref, gq_ref, gkv_ref, gc_ref,
):
    shards, part = wq_ref.shape[0], wq_ref.shape[1]
    heads = q_ref.shape[0]
    go_ref[...] = mm_nt(dh_ref[...], wo_ref[...]).astype(BF)
    dwo_ref[...] = mm_tn(o_ref[...], dh_ref[...]).astype(BF)
    ok = allowed_mask(
        col_ref[:, :1], row_ref[:1, :], col_ref[:, 1:2], row_ref[1:2, :]
    )
    key_rot = lat_ref[:, KVR:]
    grad_kr = None
    for h in range(heads):
        at = h * (DN + DV)
        keys = kv_ref[:, at : at + DN]
        values = kv_ref[:, at + DN : at + DN + DV]
        query = q_ref[h]
        grad_o = go_ref[:, h * DV : (h + 1) * DV]
        scores = mm_nt(query[:, :DN], keys) + mm_nt(query[:, DN:], key_rot)
        weights = jnp.where(ok, jnp.exp(scores * SCORE_SCALE - lse_ref[h]), 0.0)
        grad_w = mm_nt(grad_o, values)
        delta = jnp.sum(weights * grad_w, axis=1, keepdims=True)
        grad_s = (weights * (grad_w - delta) * SCORE_SCALE).astype(BF)
        gkv_ref[:, at : at + DN] = mm_tn(grad_s, query[:, :DN]).astype(BF)
        gkv_ref[:, at + DN : at + DN + DV] = mm_tn(weights.astype(BF), grad_o).astype(BF)
        one = mm_tn(grad_s, query[:, DN:])
        grad_kr = one if h == 0 else grad_kr + one
        at = h * (DN + DR)
        grad_qr = rotate(mm(grad_s, key_rot), cos_ref[...], -sin_ref[...])
        gq_ref[:, at : at + DN + DR] = jnp.concatenate(
            [mm(grad_s, keys), grad_qr], axis=1
        ).astype(BF)
    latent_part = KVR // shards
    query_wide = heads * (DN + DR)
    ratio = part // latent_part
    piece = heads * (DN + DV) // ratio
    grad_lat = []
    for s in range(shards):
        at = slice(s * latent_part, (s + 1) * latent_part)
        grad_lat.append(mm_nt(gkv_ref[...], we_ref[slot_ref[s]]))
        one = mm_tn(lat_ref[:, at], gkv_ref[...]).astype(BF)
        for i in range(ratio):
            dw_ref[slot_ref[s], i * latent_part : (i + 1) * latent_part, query_wide:] = one[
                :, i * piece : (i + 1) * piece
            ]
    grad_lat = jnp.concatenate(grad_lat, axis=1)
    unit, factor = norm_forward(c_ref[:, :KVR])
    grad_norm, grad_gain = norm_backward(grad_lat, glat_ref[...], unit, factor)
    dgl_ref[...] = grad_gain.reshape(1, KVR)
    gc_ref[:, :KVR] = grad_norm.astype(BF)
    gc_ref[:, KVR:] = rotate(grad_kr, cos_ref[...], -sin_ref[...]).astype(BF)
    for s in range(shards):
        at = slice(s * part, (s + 1) * part)
        dn1_ref[:, at] = (
            mm_nt(gq_ref[...], wq_ref[slot_ref[s]]) + mm(gc_ref[...], wl_ref[slot_ref[s]])
        ).astype(BF)
        dw_ref[slot_ref[s], :, :query_wide] = mm_tn(n1_ref[:, at], gq_ref[...]).astype(BF)
        dwl_ref[slot_ref[s]] = mm_tn(gc_ref[...], n1_ref[:, at]).astype(BF)


def attention_backward(
    slot, dh, glat, wo, o, query, kv, lse, latent, compressed, we, wl, wq, n1,
    cosine, sine_vals, col, row,
):
    length, width = n1.shape
    heads = query.shape[0]
    shards, part = wq.shape[0], wq.shape[1]
    wide = heads * (DN + DR) + heads * (DN + DV) * KVR // width
    return pl.pallas_call(
        attention_backward_kernel,
        in_specs=[SMEM] + [VMEM] * 17,
        out_shape=[
            jax.ShapeDtypeStruct((length, width), BF),
            jax.ShapeDtypeStruct((shards, part, wide), BF),
            jax.ShapeDtypeStruct(wl.shape, BF),
            jax.ShapeDtypeStruct((heads * DV, width), BF),
            jax.ShapeDtypeStruct((1, KVR), F32),
        ],
        scratch_shapes=[
            pltpu.VMEM((length, heads * DV), BF),
            pltpu.VMEM((length, heads * (DN + DR)), BF),
            pltpu.VMEM((length, heads * (DN + DV)), BF),
            pltpu.VMEM((length, KVR + DR), BF),
        ],
        compiler_params=params(),
        name="attention_backward",
    )(
        slot, dh, glat, wo, o, query, kv, lse, latent, compressed, we, wl, wq, n1,
        cosine, sine_vals, col, row,
    )


def finish_kernel(groups, shards, per, piece, *refs):
    place_ref = refs[0]
    by_head, by_row = (refs[1 + i * groups : 1 + (i + 1) * groups] for i in range(2))
    query_ref, expand_ref, out_ref = refs[1 + 2 * groups :]
    cut = by_row[0].shape[0]
    wide = by_head[0].shape[2] - piece
    expand_wide = expand_ref.shape[1] // shards
    for r in range(groups):
        at = place_ref[r]
        rows = pl.ds(pl.multiple_of(at * cut, cut), cut)
        out_ref[rows, :] = by_row[r][...].astype(F32)
        low = pl.ds(pl.multiple_of((at % per) * cut, cut), cut)
        for s in range(shards):
            query_ref[rows, s * wide : (s + 1) * wide] = by_head[r][s, :, :wide].astype(F32)
            lanes = pl.ds(
                pl.multiple_of(s * expand_wide + (at // per) * piece, piece), piece
            )
            expand_ref[low, lanes] = by_head[r][s, :, wide:].astype(F32)


def finish(place, by_head, by_row, heads, width):
    groups, shards = len(by_head), by_head[0].shape[0]
    latent_part = KVR // shards
    part = width // shards
    per = groups * latent_part // part
    piece = heads * (DN + DV) * latent_part // part
    return pl.pallas_call(
        functools.partial(finish_kernel, groups, shards, per, piece),
        in_specs=[SMEM] + [VMEM] * (2 * groups),
        out_shape=[
            jax.ShapeDtypeStruct((part, H * (DN + DR)), F32),
            jax.ShapeDtypeStruct((latent_part, H * (DN + DV)), F32),
            jax.ShapeDtypeStruct((part, width), F32),
        ],
        compiler_params=params(),
        name="finish",
    )(place, *by_head, *by_row)


def shared_finish_kernel(x_ref, gate_ref, up_ref, hold_ref):
    groups, shards, hid = x_ref.shape[0], x_ref.shape[1], x_ref.shape[2] // 2
    for i, out_ref in ((0, gate_ref), (1, up_ref)):
        for s in range(shards):
            for g in range(groups):
                at = (s * groups + g) * hid
                hold_ref[at : at + hid] = x_ref[g, s, i * hid : (i + 1) * hid].astype(F32)
        out_ref[...] = hold_ref[...].T


def shared_finish(pieces):
    groups, shards, two, part = pieces.shape
    wide = groups * shards * two // 2
    return pl.pallas_call(
        shared_finish_kernel,
        in_specs=[VMEM],
        out_shape=[jax.ShapeDtypeStruct((part, wide), F32)] * 2,
        scratch_shapes=[pltpu.VMEM((wide, part), F32)],
        compiler_params=params(),
        name="shared_finish",
    )(pieces)


STEP = 8
PAD = 128


def pick_into(out_ref, pick, rows_of, i, step):
    capacity = out_ref.shape[1] // step
    rows = mm(pick, rows_of).astype(BF)
    out_ref[:, i * capacity : (i + 1) * capacity, :] = rows.reshape(
        EXP_DEV, capacity, rows.shape[1]
    )


def place_from(rows_ref, pick, i, step):
    capacity = rows_ref.shape[1] // step
    rows = rows_ref[:, i * capacity : (i + 1) * capacity, :]
    return mm_tn(pick, rows.reshape(EXP_DEV * capacity, rows.shape[2]))


def resident(shape):
    return pl.BlockSpec(
        shape, lambda *_: (0,) * len(shape), pipeline_mode=pl.Buffered(1)
    )


def grad_rows_kernel(order_ref, pick_ref, down_ref, *refs):
    rows_ref, inner_ref = refs[STEP:]
    inner = down_ref.shape[1]
    for i in range(STEP):
        pick_into(rows_ref, pick_ref[i], refs[i][0], i, STEP)
    for j in range(EXP_DEV):
        inner_ref[j, :, :inner] = mm_nt(rows_ref[j], down_ref[j])


def grad_rows_of(pick, g_all, order, down, capacity):
    devices, slots, tokens = pick.shape
    width, inner = g_all.shape[2], down.shape[1]
    lanes = inner + -inner % PAD
    rows = STEP * capacity
    at = lambda i: pl.BlockSpec((1, tokens, width), lambda d, o: (o[d * STEP + i], 0, 0))
    return pl.pallas_call(
        grad_rows_kernel,
        grid_spec=pltpu.PrefetchScalarGridSpec(
            num_scalar_prefetch=1,
            grid=(devices // STEP,),
            in_specs=[
                pl.BlockSpec((STEP, slots, tokens), lambda d, o: (d, 0, 0)),
                resident(down.shape),
            ]
            + [at(i) for i in range(STEP)],
            out_specs=[
                pl.BlockSpec((EXP_DEV, rows, width), lambda d, o: (0, d, 0)),
                pl.BlockSpec((EXP_DEV, rows, lanes), lambda d, o: (0, d, 0)),
            ],
        ),
        out_shape=[
            jax.ShapeDtypeStruct((EXP_DEV, devices * capacity, width), BF),
            jax.ShapeDtypeStruct((EXP_DEV, devices * capacity, lanes), F32),
        ],
        compiler_params=params(),
        name="grad_rows",
    )(order, pick, down, *([g_all] * STEP))


def stack_weights(w_ref, gate_ref, up_ref):
    inner, lanes = gate_ref.shape[1], w_ref.shape[1] // 2

    @pl.when(pl.program_id(0) == 0)
    def _():
        for j in range(EXP_DEV):
            for i, ref in ((0, gate_ref), (1, up_ref)):
                w_ref[j, i * lanes : i * lanes + inner] = ref[j]
                if lanes > inner:
                    w_ref[j, i * lanes + inner : (i + 1) * lanes] = jnp.zeros(
                        (lanes - inner, w_ref.shape[2]), BF
                    )


def inner_kernel(
    count, group_ref, pick_ref, named_ref, *refs
):
    x_refs = refs[:count]
    (
        gate_ref, up_ref, shared_ref, grad_ref, shared_grad_ref,
        rows_ref, inner_ref, grads_ref, slot_ref, shared_grads_ref, shared_inner_ref, sum_ref,
    ) = refs[count : count + 5] + refs[-9:-2]
    w_ref, weight_ref = refs[-2:]
    before_ref = refs[-10] if len(refs) == count + 5 + 16 else None
    lanes, inner = grad_ref.shape[2], inner_ref.shape[2]
    hid, pad = shared_grad_ref.shape[1], shared_inner_ref.shape[2]
    x_rows, tokens = x_refs[0].shape[0], x_refs[0].shape[1]
    capacity = rows_ref.shape[1] // STEP
    experts = named_ref.shape[2]
    stack_weights(w_ref, gate_ref, up_ref)
    slots = EXP_DEV * capacity
    mine = group_ref[0] * EXP_DEV + lax.broadcasted_iota(
        jnp.int32, (slots, 3 * experts), 0
    ) // capacity
    at_mine = lax.broadcasted_iota(jnp.int32, (slots, 3 * experts), 1) % experts == mine
    total = None
    for i in range(STEP):
        x = x_refs[i // x_rows][i % x_rows]
        pick_into(rows_ref, pick_ref[i], x, i, STEP)
        both = mm(x, shared_ref[...])
        probs = jax.nn.sigmoid(both[:, 2 * pad : 2 * pad + experts])
        named = named_ref[i]
        weight = probs / jnp.sum(probs * named, axis=1, keepdims=True) * ROUTE_SCALE
        high = weight.astype(BF)
        rest = weight - high.astype(F32)
        middle = rest.astype(BF)
        low = (rest - middle.astype(F32)).astype(BF)
        at_slots = mm(pick_ref[i], jnp.concatenate([high, middle, low], axis=1))
        at_slots = jnp.sum(jnp.where(at_mine, at_slots, 0.0), axis=1, keepdims=True)
        weight_ref[:, i * capacity : (i + 1) * capacity] = at_slots.reshape(
            EXP_DEV, capacity, 1
        )
        act, slope_gate, slope_up = swish_parts(both[:, :hid], both[:, pad : pad + hid])
        grad = shared_grad_ref[i * tokens : (i + 1) * tokens]
        zeros = jnp.zeros((tokens, pad - hid), BF)
        join = lambda v: v.astype(BF) if pad == hid else jnp.concatenate(
            [v.astype(BF), zeros], axis=1
        )
        shared_inner_ref[i] = join(act)
        shared_grads_ref[i, :, :pad] = join(grad * slope_gate)
        shared_grads_ref[i, :, pad:] = join(grad * slope_up)
        one = mm_tn(shared_grads_ref[i], x)
        total = one if total is None else total + one
    sum_ref[...] = total if before_ref is None else total + before_ref[...]
    for j in range(EXP_DEV):
        both = mm_nt(rows_ref[j], w_ref[j])
        gate, up = both[:, :inner], both[:, lanes : lanes + inner]
        act, slope_gate, slope_up = swish_parts(gate, up)
        weight = weight_ref[j]
        grad = grad_ref[j, :, :inner]
        slot_ref[j] = jnp.sum(act.astype(BF).astype(F32) * grad, axis=1, keepdims=True)
        inner_ref[j] = (weight * act).astype(BF)
        grad = weight * grad
        if lanes > inner:
            grads_ref[j] = jnp.zeros(grads_ref.shape[1:], BF)
        grads_ref[j, :, :inner] = (grad * slope_gate).astype(BF)
        grads_ref[j, :, lanes : lanes + inner] = (grad * slope_up).astype(BF)


def inner_of(
    chunk, before, group, pick, named, arrays, gate, up, shared, grad, shared_grad, pad, capacity
):
    devices, slots, tokens = pick.shape
    width, lanes, inner = arrays[0].shape[2], grad.shape[2], gate.shape[1]
    hid, experts = shared_grad.shape[1], named.shape[2]
    rows = STEP * capacity
    total = devices * capacity
    by_rows = lambda n: pl.BlockSpec((EXP_DEV, rows, n), lambda _: (0, chunk, 0))
    by_device = lambda *n: pl.BlockSpec((STEP,) + n, lambda _: (chunk, 0, 0))
    whole = lambda v: resident(v.shape)
    any_spec = pl.BlockSpec(memory_space=pl.ANY)
    in_specs = (
        [SMEM, by_device(slots, tokens), by_device(tokens, experts)]
        + [whole(v) for v in arrays]
        + [
            whole(gate),
            whole(up),
            whole(shared),
            by_rows(lanes),
            pl.BlockSpec((STEP * tokens, hid), lambda _: (chunk, 0)),
        ]
    )
    operands = [group, pick, named, *arrays, gate, up, shared, grad, shared_grad]
    aliases = {}
    if before is not None:
        aliases = {len(operands) + i: i for i in range(6)}
        operands += before
        in_specs += [any_spec] * 6 + [pl.BlockSpec((2 * pad, width), lambda _: (0, 0))]
    return pl.pallas_call(
        functools.partial(inner_kernel, len(arrays)),
        grid=(1,),
        in_specs=in_specs,
        out_specs=[
            by_rows(width),
            by_rows(inner),
            by_rows(2 * lanes),
            by_rows(1),
            by_device(tokens, 2 * pad),
            by_device(tokens, pad),
            pl.BlockSpec((2 * pad, width), lambda _: (0, 0)),
        ],
        out_shape=[
            jax.ShapeDtypeStruct((EXP_DEV, total, width), BF),
            jax.ShapeDtypeStruct((EXP_DEV, total, inner), BF),
            jax.ShapeDtypeStruct((EXP_DEV, total, 2 * lanes), BF),
            jax.ShapeDtypeStruct((EXP_DEV, total, 1), F32),
            jax.ShapeDtypeStruct((devices, tokens, 2 * pad), BF),
            jax.ShapeDtypeStruct((devices, tokens, pad), BF),
            jax.ShapeDtypeStruct((2 * pad, width), F32),
        ],
        scratch_shapes=[
            pltpu.VMEM((EXP_DEV, 2 * lanes, width), BF),
            pltpu.VMEM((EXP_DEV, rows, 1), F32),
        ],
        input_output_aliases=aliases,
        compiler_params=params(),
        name="inner",
    )(*operands)


def back_kernel(
    rows, pick_ref, grads_ref, gate_ref, up_ref, left_ref, right_ref,
    own_ref, other_ref, hold_ref, w_ref,
):
    stack_weights(w_ref, gate_ref, up_ref)
    for j in range(EXP_DEV):
        hold_ref[j] = mm(grads_ref[j], w_ref[j]).astype(BF)
    for i in range(STEP):
        total = place_from(hold_ref, pick_ref[i], i, STEP) + mm(left_ref[i], right_ref[...])
        out_ref = own_ref if i // rows % 2 == 0 else other_ref
        out_ref[i // (2 * rows) * rows + i % rows] = total.astype(BF)


def back_rows(pick, grads, gate, up, left, right, capacity, x_rows):
    devices, slots, tokens = pick.shape
    width, inner = gate.shape[2], left.shape[2]
    rows = STEP * capacity
    return pl.pallas_call(
        functools.partial(back_kernel, x_rows),
        grid=(devices // STEP,),
        in_specs=[
            pl.BlockSpec((STEP, slots, tokens), lambda d: (d, 0, 0)),
            pl.BlockSpec((EXP_DEV, rows, grads.shape[2]), lambda d: (0, d, 0)),
            resident(gate.shape),
            resident(up.shape),
            pl.BlockSpec((STEP, tokens, inner), lambda d: (d, 0, 0)),
            resident(right.shape),
        ],
        out_specs=[pl.BlockSpec((STEP // 2, tokens, width), lambda d: (d, 0, 0))] * 2,
        out_shape=[jax.ShapeDtypeStruct((devices // 2, tokens, width), BF)] * 2,
        scratch_shapes=[
            pltpu.VMEM((EXP_DEV, rows, width), BF),
            pltpu.VMEM((EXP_DEV, grads.shape[2], width), BF),
        ],
        compiler_params=params(),
        name="back_rows",
    )(pick, grads, gate, up, left, right)


def gate_up_kernel(rows_ref, grads_ref, gate_ref, up_ref):
    inner = gate_ref.shape[1]
    both = mm_tn(grads_ref[0], rows_ref[0])
    gate_ref[0] = both[:inner]
    at = grads_ref.shape[2] // 2
    up_ref[0] = both[at : at + inner]


def gate_up_grads(rows, grads, inner):
    _, total, width = rows.shape
    tile = width // 4
    out = pl.BlockSpec((1, inner, tile), lambda j, i: (j, 0, i))
    return pl.pallas_call(
        gate_up_kernel,
        grid=(EXP_DEV, 4),
        in_specs=[
            pl.BlockSpec((1, total, tile), lambda j, i: (j, 0, i)),
            pl.BlockSpec((1, total, grads.shape[2]), lambda j, i: (j, 0, 0)),
        ],
        out_specs=[out, out],
        out_shape=[jax.ShapeDtypeStruct((EXP_DEV, inner, width), F32)] * 2,
        compiler_params=params(),
        name="gate_up_grads",
    )(rows, grads)


def output_kernel(
    x_rows, pick_ref, inner_ref, down_ref, left_ref, right_ref, own_ref, other_ref, hold_ref
):
    for j in range(EXP_DEV):
        hold_ref[j] = mm(inner_ref[j], down_ref[j]).astype(BF)
    for i in range(STEP):
        total = place_from(hold_ref, pick_ref[i], i, STEP) + mm(left_ref[i], right_ref[...])
        out_ref = own_ref if i // x_rows % 2 == 0 else other_ref
        out_ref[i // (2 * x_rows) * x_rows + i % x_rows] = total.astype(BF)


def output_rows_of(pick, inner, down, left, right, capacity, x_rows):
    devices, slots, tokens = pick.shape
    width = down.shape[2]
    rows = STEP * capacity
    return pl.pallas_call(
        functools.partial(output_kernel, x_rows),
        grid=(devices // STEP,),
        in_specs=[
            pl.BlockSpec((STEP, slots, tokens), lambda d: (d, 0, 0)),
            pl.BlockSpec((EXP_DEV, rows, inner.shape[2]), lambda d: (0, d, 0)),
            resident(down.shape),
            pl.BlockSpec((STEP, tokens, left.shape[2]), lambda d: (d, 0, 0)),
            resident(right.shape),
        ],
        out_specs=[pl.BlockSpec((STEP // 2, tokens, width), lambda d: (d, 0, 0))] * 2,
        out_shape=[jax.ShapeDtypeStruct((devices // 2, tokens, width), BF)] * 2,
        scratch_shapes=[pltpu.VMEM((EXP_DEV, rows, width), BF)],
        compiler_params=params(),
        name="output_rows",
    )(pick, inner, down, left, right)


def body(
    hidden,
    cotangent,
    segments,
    routes,
    w_query,
    w_latent,
    g_latent,
    w_expand,
    w_out,
    g_attn,
    g_ffn,
    w_router,
    s_gate,
    s_up,
    s_down,
    e_gate,
    expert_up_weight,
    e_down,
):
    tokens = hidden.shape[1]
    width = hidden.shape[2]
    links = Links()
    shards, groups = links.shards, links.groups
    devices = groups * shards
    experts = EXP_DEV * groups
    capacity = max(2, tokens * TOP * 4 // (3 * experts))
    heads = H // shards
    length = tokens * shards
    part = width // shards
    my_shard = lax.axis_index("shard")
    my_group = lax.axis_index("expert")
    hid_shard = s_down.shape[0]
    hid = hid_shard // groups
    latent_part = KVR // shards
    shard_at, slot_at = links.shard_at(), links.slot_at()

    g_all = lax.all_gather(cotangent[0], BOTH, axis=0, tiled=False)
    router_rows = part * experts // width
    small_rows = jnp.concatenate([g_attn, g_ffn, g_latent])
    small_rows = jnp.pad(small_rows, (0, -small_rows.shape[0] % width)).reshape(-1, width)
    packed = jnp.concatenate([w_router.reshape(router_rows, width), small_rows])
    packed = links.gather_shard(jnp.pad(packed, ((0, -packed.shape[0] % 16), (0, 0))))
    hidden_all = links.gather_shard(hidden[0]).reshape(length, width)
    pieces = lambda w: jnp.stack(jnp.split(w, shards, axis=1))
    wl = links.gather_shard(w_latent.T)
    wq, expand = links.spread_shard_ring(pieces(w_query), pieces(w_expand))
    we = links.spread_shard(expand)
    packed = jnp.take(packed, slot_at, axis=0)
    full_router = packed[:, :router_rows].reshape(width, experts)
    gains_in = packed[:, router_rows:].reshape(shards, -1)
    gattn = gains_in[:, :part].reshape(1, width).astype(F32)
    gffn = gains_in[:, part : 2 * part].reshape(width).astype(F32)
    glatent = gains_in[:, 2 * part : 2 * part + latent_part].reshape(1, KVR).astype(F32)

    order = links.order()
    same = jnp.arange(devices, dtype=jnp.int32)
    back_order = jnp.sum(
        jnp.where(order[:, None] == same[None, :], same[:, None], 0), axis=0
    ).astype(jnp.int32)
    local_routes = routes[0]
    flat_routes = local_routes.reshape(-1)
    choose = local_routes[:, :, None] == jnp.arange(experts, dtype=jnp.int32)[None, None, :]
    hits = choose.reshape(-1, experts).astype(F32)
    pair_count = tokens * TOP
    before_it = (
        lax.broadcasted_iota(jnp.int32, (pair_count, pair_count), 1)
        < lax.broadcasted_iota(jnp.int32, (pair_count, pair_count), 0)
    ).astype(BF)
    before = mm(before_it, hits.astype(BF))
    slot_rank = jnp.sum(before * hits, axis=1).astype(jnp.int32)
    slot_of = (flat_routes * capacity + slot_rank).reshape(tokens, TOP)
    slots = EXP_DEV * capacity
    slot_rows = jnp.pad(slot_of.T, ((0, 8 - TOP), (0, 0)), constant_values=-1)
    slots_all = exchange(jnp.broadcast_to(slot_rows[None], (devices, 8, tokens)), BOTH)
    slots_all = jnp.take(slots_all, order, axis=0)[:, :TOP]
    slot_ids = my_group * slots + jnp.arange(slots, dtype=jnp.int32)
    pick = jnp.any(
        slots_all[:, None] == slot_ids[None, :, None, None], axis=2
    ).astype(BF)

    hid_ids = my_group * hid + jnp.arange(hid, dtype=jnp.int32)
    wanted = (jnp.arange(shards, dtype=jnp.int32)[:, None] * hid_shard + hid_ids).reshape(-1)
    chosen_units = (
        jnp.arange(shards * hid_shard, dtype=jnp.int32)[:, None] == wanted[None, :]
    ).astype(BF)

    def shared_pieces(units):
        cut = [mm(w, units).astype(BF).reshape(part, shards, hid) for w in (s_gate, s_up)]
        return jnp.concatenate(cut, axis=2).transpose(1, 0, 2)

    wq, chosen_units = tie(wq, chosen_units)

    positions = (shard_at[:, None] * tokens + jnp.arange(tokens, dtype=jnp.int32)).reshape(-1)
    cosine, sine_vals = rope_angles(positions)
    segs = jnp.take(segments.reshape(shards, tokens), shard_at, axis=0).reshape(-1)
    col = jnp.stack([segs, positions], axis=1)
    row = jnp.stack([segs, positions], axis=0)
    attn_part, n1, compressed, latent, attended, query, kv, lse = attention_forward(
        slot_at, hidden_all, gattn, glatent, wq, wl, we, w_out, cosine, sine_vals, col, row
    )
    inner_units = e_gate.shape[2]
    gate_t, up_t = jnp.swapaxes(e_gate, 1, 2), jnp.swapaxes(expert_up_weight, 1, 2)
    attn_out = links.sum_shard(attn_part.reshape(shards, tokens, width))

    residual_in = hidden[0].astype(F32)
    residual_mid = residual_in + attn_out
    unit_two, factor_two = norm_forward(residual_mid)
    normed_two = (unit_two * gffn).astype(BF)

    pad = hid + -hid % PAD
    shared_down = lax.dynamic_slice_in_dim(s_down, my_group * hid, hid, 0)
    gate_up = links.spread_shard(shared_pieces(chosen_units))
    gate_up = jnp.take(gate_up, slot_at, axis=0).reshape(width, 2, hid)
    shared_in = jnp.pad(gate_up, ((0, 0), (0, 0), (0, pad - hid))).reshape(width, 2 * pad)
    shared_all = jnp.concatenate(
        [shared_in, jnp.pad(full_router, ((0, 0), (0, -experts % PAD)))], axis=1
    )
    route_of = slots_all // capacity
    named = jnp.any(
        route_of.transpose(0, 2, 1)[:, :, :, None]
        == jnp.arange(experts, dtype=jnp.int32)[None, None, None, :],
        axis=2,
    ).astype(F32)
    probs = jax.nn.sigmoid(mm(normed_two, full_router))
    chosen = jnp.sum(jnp.where(choose, probs[:, None, :], 0.0), axis=-1)
    chosen_total = jnp.sum(chosen, axis=1, keepdims=True)

    def of_cotangent(pick_of):
        rows_of, inner_grads = grad_rows_of(pick_of, g_all, order, e_down, capacity)
        shared_of = mm_nt(g_all.reshape(-1, width), shared_down)
        shared_of = jnp.take(shared_of.reshape(devices, tokens, hid), order, axis=0)
        return rows_of, inner_grads, shared_of.reshape(-1, hid)

    arrival = links.arrival()
    per_chunk = STEP // shards
    chunks = groups // per_chunk
    slots_in, partners, so_far = [], {}, [None]
    work_g = Fill(of_cotangent, pick, mark=2)

    def one_chunk(c):
        arrays = []
        for r in arrival[c * per_chunk : (c + 1) * per_chunk]:
            partners[r] = links.partner(slots_in[0][r])
            arrays += [slots_in[0][r], partners[r]]
        so_far[0] = inner_of(
            c, so_far[0], my_group.reshape(1), pick, named, arrays, gate_t, up_t, shared_all,
            work_g.result[1], work_g.result[2], pad, capacity,
        )

    def chunks_after(step, done):
        ready = sum(min(r, groups - r) <= step for r in arrival) // per_chunk
        return range(done, ready)

    fills, done = [(1, work_g)], 0
    for r in range(2, groups // 2 + 1):
        some = chunks_after(r - 1, done)
        done += len(some)

        def work_of(some=some, final=r == groups // 2):
            for c in some:
                one_chunk(c)
            return so_far[0]

        if len(some) > 0:
            fill = Fill(work_of, mark=3)
            fills.append((r, fill))
    spread = jnp.stack(
        [normed_two] + [links.along_x(normed_two, k) for k in range(1, shards // 2)]
    )
    links.ring_gather([spread], [groups // 2], fills, slots_in)
    for c in range(done, chunks):
        one_chunk(c)
    grad_rows = work_g.result[0]
    rows, inner_w, grads_b, grad_slot_weight, shared_grads, shared_inner, shared_sum = so_far[0]

    shared_out = jnp.concatenate([shared_sum[:hid], shared_sum[pad : pad + hid]], axis=0)
    shared_out = shared_out.astype(BF).reshape(2 * hid, shards, part).transpose(1, 0, 2)
    in_pieces = jnp.take(links.spread_shard(shared_out), slot_at, axis=0)
    shared_down = jnp.pad(shared_down, ((0, pad - hid), (0, 0)))

    def shared_down_grad(inner_of_shared):
        back = jnp.take(inner_of_shared, back_order, axis=0).reshape(-1, pad)
        return mm_tn(back, g_all.reshape(-1, width))[:hid].astype(BF)

    dn2_own, dn2_other = back_rows(
        pick, grads_b, gate_t, up_t, shared_grads, shared_in.T, capacity, shards // 2
    )

    def router_back(slot_sums):
        slot_back = slot_sums.reshape(EXP_DEV, devices, capacity).transpose(1, 0, 2)
        slot_back = jnp.take(slot_back.reshape(devices, slots), back_order, axis=0)
        got = exchange(slot_back, BOTH)
        slot_grads = jnp.sum(got.reshape(groups, shards, slots), axis=1).reshape(-1)
        at_slot = slot_of[:, :, None] == jnp.arange(experts * capacity, dtype=jnp.int32)
        grad_weights = jnp.sum(jnp.where(at_slot, slot_grads, 0.0), axis=2)
        grad_chosen = ROUTE_SCALE * (
            grad_weights / chosen_total
            - jnp.sum(grad_weights * chosen, axis=1, keepdims=True)
            / (chosen_total * chosen_total)
        )
        grad_probs = jnp.sum(jnp.where(choose, grad_chosen[:, :, None], 0.0), axis=1)
        return (grad_probs * probs * (1.0 - probs)).astype(BF)

    down_grad = lambda a, b: jnp.einsum("jmf,jmd->jfd", a, b, preferred_element_type=F32)
    ring_shape = (groups, shards // 2, tokens, width)
    half = groups // 2

    def output_parts(weighted):
        own, other = output_rows_of(
            pick, weighted, e_down, shared_inner, shared_down, capacity, shards // 2
        )
        return links.sum_core(own.reshape(ring_shape), other.reshape(ring_shape))

    work = [
        Fill(
            lambda a, b: (shared_down_grad(a), down_grad(b, grad_rows)),
            shared_inner, inner_w,
        ),
        Fill(output_parts, inner_w),
        Fill(
            lambda b, c: (gate_up_grads(rows, b, inner_units), router_back(c)),
            grads_b, grad_slot_weight,
        ),
    ]
    dn2_parts = links.sum_core(dn2_own.reshape(ring_shape), dn2_other.reshape(ring_shape))
    dn2 = links.ring_reduce(
        [[v[:, : tokens // 2] for v in dn2_parts], [v[:, tokens // 2 :] for v in dn2_parts]],
        [half, half],
        [(half - i, w) for i, w in enumerate(work)],
        free=1,
    )
    dn2 = jnp.concatenate(dn2, axis=1)
    dn2, (in_pieces, d_shared_down) = tie(dn2, (in_pieces, work[0].result[0]))
    in_all = lax.all_gather(in_pieces, "expert", axis=0, tiled=False)
    down_all = lax.all_gather(d_shared_down, "expert", axis=0, tiled=True)
    (_, d_edown), out_parts, ((d_egate, grad_expert_up), grad_logits) = (
        w.result for w in work
    )

    def back_to_attention(top, logits):
        grad_normed_two = links.sum_x(top) + mm_nt(logits, full_router)
        grad_mid_norm, d_gffn = norm_backward(grad_normed_two, gffn, unit_two, factor_two)
        grad_mid = cotangent[0].astype(F32) + grad_mid_norm
        return grad_mid, d_gffn, grad_mid.astype(BF)

    backward = lambda grad_attn: attention_backward(
        slot_at, grad_attn, glatent, w_out, attended, query, kv, lse, latent, compressed,
        we, wl, wq, n1, cosine, sine_vals, col, row,
    )
    first = Fill(back_to_attention, dn2, grad_logits)
    middle = Fill(
        lambda grad: links.gather_shard(grad).reshape(length, width), lambda: first.result[2]
    )
    second = Fill(backward, lambda: middle.result)
    (routed_shared,) = links.ring_reduce(
        [out_parts], [half], [(half, first), (half - 1, middle), (half - 2, second)]
    )
    routed_shared = links.sum_x(routed_shared)
    grad_mid, d_gffn, _ = first.result
    dn1, dw, dwl, d_out, d_glatent = second.result
    output_rows = residual_mid + routed_shared
    (dn1, dw, dwl, d_out), grad_logits = tie((dn1, dw, dwl, d_out), grad_logits)
    logits_back = exchange(
        jnp.broadcast_to(grad_logits.T[None], (devices, experts, tokens)), BOTH
    )
    logits_back = jnp.take(logits_back, order, axis=0)
    columns = lambda v: lax.dynamic_slice_in_dim(v.reshape(-1, width), my_shard * part, part, 1)
    own_columns = jnp.concatenate(
        [columns(v) for r in arrival for v in (slots_in[0][r], partners[r])], axis=0
    )
    d_router = mm(logits_back.transpose(1, 0, 2).reshape(experts, -1), own_columns).T
    grad_normed = links.sum_shard(dn1.reshape(shards, tokens, width))
    unit_one, factor_one = norm_forward(residual_in)
    grad_input_norm, d_gattn = norm_backward(
        grad_normed, gattn.reshape(width), unit_one, factor_one
    )
    grad_input = grad_mid + grad_input_norm

    cut = part // groups
    lat = links.sum_shard(dwl).astype(BF).reshape(groups, (KVR + DR) // groups, part)
    by_head = links.blocks(dw.reshape(shards, groups, cut, -1).transpose(1, 0, 2, 3))
    by_row = links.blocks(d_out.reshape(groups, cut, width))
    pluses = [groups // 2, (groups - 1) // 2]
    sum_head, sum_row = links.ring_reduce([by_head, by_row], pluses)
    work_in = Fill(lambda: shared_finish(in_all), mark=0)
    work_down = Fill(lambda: (down_all.astype(F32),), mark=0)
    (sum_lat,) = links.ring_reduce([links.blocks(lat)], pluses[1:])
    sum_head = links.exchange_shard(sum_head.astype(BF))
    all_head, all_row, all_lat = links.ring_gather(
        [sum_head, sum_row.astype(BF), sum_lat.astype(BF)],
        pluses + pluses[1:],
        [(half - 1, work_in), (half, work_down)],
    )
    part_sgate, part_sup = work_in.result
    (part_sdown,) = work_down.result
    part_query, part_expand, part_out = finish(
        links.block_at(), all_head, all_row, heads, width
    )
    part_latent = jnp.take(jnp.stack(all_lat), links.block_at(), axis=0)
    part_latent = part_latent.reshape(KVR + DR, part).astype(F32)

    gain_grads = jnp.concatenate(
        [
            d_gattn.reshape(shards, part),
            d_gffn.reshape(shards, part),
            d_glatent.reshape(shards, latent_part),
        ],
        axis=1,
    )
    got = exchange(
        jnp.broadcast_to(gain_grads[None], (groups,) + gain_grads.shape).reshape(devices, -1),
        BOTH,
    )
    gains = jnp.sum(got, axis=0)
    return (
        output_rows.astype(BF)[None],
        grad_input[None],
        part_query,
        part_latent.T,
        gains[2 * part :],
        part_expand,
        part_out,
        gains[:part],
        gains[part : 2 * part],
        d_router,
        part_sgate,
        part_sup,
        part_sdown,
        jnp.swapaxes(d_egate, 1, 2),
        jnp.swapaxes(grad_expert_up, 1, 2),
        d_edown,
    )


def solution(mesh):
    return jax.shard_map(
        body,
        mesh=mesh,
        in_specs=(
            P("expert", "shard", None),
            P("expert", "shard", None),
            P("expert", None),
            P("expert", "shard", None),
            P("shard", None),
            P("shard", None),
            P("shard"),
            P("shard", None),
            P("shard", None),
            P("shard"),
            P("shard"),
            P("shard", None),
            P("shard", None),
            P("shard", None),
            P("shard", None),
            P("expert", None, "shard"),
            P("expert", None, "shard"),
            P("expert", "shard", None),
        ),
        out_specs=(
            P("expert", "shard", None),
            P("expert", "shard", None),
            P("shard", None),
            P("shard", None),
            P("shard"),
            P("shard", None),
            P("shard", None),
            P("shard"),
            P("shard"),
            P("shard", None),
            P("shard", None),
            P("shard", None),
            P("shard", None),
            P("expert", None, "shard"),
            P("expert", None, "shard"),
            P("expert", "shard", None),
        ),
        check_vma=False,
    )
```
